32 devices in a mesh: head: 4 (over y, core), blk: 8 (over z, x).
Axes of the slice: x: 2, y: 2, z: 4, core: 2. Of those that a mesh axis runs over, the one named last changes fastest.
Arguments:
- tokens: bfloat16 [4096, 2048], P(('head', 'blk')), may hold values from -50 to 50
- out_grad: bfloat16 [4096, 2048], P(('head', 'blk')), may hold values from -6 to 6
- seq_lengths: int32 [8], replicated, may hold values from 1 to 2048, 4096 in all
- block_deal: int32 [16], replicated, may hold values from 0 to 15, as said below
- norm_gain: bfloat16 [2048], P('blk'), may hold values from 0.5 to 1.5
- q_weight: bfloat16 [2048, 2048], P('blk', 'head'), may hold values from -0.125 to 0.125
- key_projection_weight: bfloat16 [2048, 1024], P('blk', 'head'), may hold values from -0.125 to 0.125
- value_projection_weight: bfloat16 [2048, 1024], P('blk', 'head'), may hold values from -0.125 to 0.125
- q_gain: bfloat16 [128], P('blk'), may hold values from 0.5 to 1.5
- k_gain: bfloat16 [128], P('blk'), may hold values from 0.5 to 1.5
- o_weight: bfloat16 [2048, 2048], P('head', 'blk'), may hold values from -0.75 to 0.75
- mlp_gain: bfloat16 [2048], P('blk'), may hold values from 0.5 to 1.5
- gate_weight: bfloat16 [2048, 6144], P('blk', 'head'), may hold values from -0.125 to 0.125
- up_weight: bfloat16 [2048, 6144], P('blk', 'head'), may hold values from -0.125 to 0.125
- down_weight: bfloat16 [6144, 2048], P('head', 'blk'), may hold values from -0.078125 to 0.078125
Outputs:
- block_out: bfloat16 [4096, 2048], P(('head', 'blk'))
- in_grad: float32 [4096, 2048], P(('head', 'blk'))
- norm_gain_grad: float32 [2048], P(('head', 'blk'))
- q_weight_grad: float32 [2048, 2048], P('blk', 'head')
- k_weight_grad: float32 [2048, 1024], P('blk', 'head')
- v_weight_grad: float32 [2048, 1024], P('blk', 'head')
- q_gain_grad: float32 [128], P(('head', 'blk'))
- k_gain_grad: float32 [128], P(('head', 'blk'))
- o_weight_grad: float32 [2048, 2048], P('head', 'blk')
- mlp_gain_grad: float32 [2048], P(('head', 'blk'))
- gate_weight_grad: float32 [2048, 6144], P('blk', 'head')
- up_weight_grad: float32 [2048, 6144], P('blk', 'head')
- down_weight_grad: float32 [6144, 2048], P('head', 'blk')
The draws below stay inside these ranges and needn't reach their ends.
Inputs may be any that keep to these rules, and one draw needn't show every extreme that they name: `seq_lengths`: the lengths sum to 4096; the longest has exactly 2048 tokens. `block_deal`: a permutation of 0 to 15 in which entries 2 b and 2 b + 1 sum to 15.
All inputs are finite; a program needn't handle non-finite values.
Results may differ from the reference program's by a relative error of at most 0.035.
Values may be sent and summed in bfloat16 or wider, within the bound.
No kernel may reach another device: no remote copies, remote signals or barrier semaphores. Data moves between devices by JAX's collectives and lax.ppermute only.
A program may use at most 320 MiB of HBM per device.

```python
import math
import jax
import jax.numpy as jnp
import numpy as np
from jax import lax

MODEL_WIDTH = 2048
QUERY_HEADS = 16
KEY_VALUE_HEADS = 8
HEAD_SIZE = 128
FF = 6144
TOK_DEV = 128
NSEQ = 8
TOKEN_TOTAL = 4096
MAX_LEN = 2048
SPANS = 16
N_HEAD = 4
N_BLK = 8


def draw_tokens(key, part):
    base_key = jax.random.fold_in(key, 21)
    row_key = jax.random.fold_in(key, 22)
    col_key = jax.random.fold_in(key, 23)
    base_draw = jnp.clip(jax.random.normal(base_key, (TOKEN_TOTAL, MODEL_WIDTH), jnp.float32), -5.0, 5.0)
    row_scale = jnp.exp(jax.random.uniform(row_key, (TOKEN_TOTAL, 1), jnp.float32, -1.15, 1.15))
    col_scale = jnp.exp(jax.random.uniform(col_key, (1, MODEL_WIDTH), jnp.float32, -1.15, 1.15))
    return (base_draw * row_scale * col_scale).astype(jnp.bfloat16)


def draw_block_deal(key, part):
    pair_count = SPANS // 2
    pair_order = jax.random.permutation(jax.random.fold_in(key, 11), pair_count).astype(jnp.int32)
    flip_bits = jax.random.randint(jax.random.fold_in(key, 12), (pair_count,), 0, 2)
    first_span = jnp.where(flip_bits == 0, pair_order, SPANS - 1 - pair_order)
    return jnp.stack([first_span, SPANS - 1 - first_span], axis=1).reshape(SPANS).astype(jnp.int32)


def steps_of(key, extent, split, low, high):
    gain = 1.0
    for axis_at, shards_of in split:
        draws = jax.random.uniform(jax.random.fold_in(jax.random.fold_in(key, 6), axis_at), (shards_of,), jnp.float32, low / len(split), high / len(split))
        gain = gain * jnp.repeat(jnp.exp(draws), extent[axis_at] // shards_of).reshape((-1,) + (1,) * (len(extent) - 1 - axis_at))
    return gain


def length_profile(number_of, total, most, lean):
    portions = [(1 << 20) // math.isqrt(grade ** lean) + 1 for grade in range(2, number_of + 1)]
    spare, holding = total - most - (number_of - 1), [1] * (number_of - 1)
    while spare > 0:
        free = [i for i in range(number_of - 1) if holding[i] < most]
        mass, budget = sum([portions[i] for i in free]), spare
        for i in free:
            more = min(most - holding[i], max(1, budget * portions[i] // mass), spare)
            holding[i] = holding[i] + more
            spare = spare - more
    return np.array([most] + holding)


def ragged_sizes(key, number_of, total, reach, skew):
    if number_of == 2:
        one = jax.random.randint(key, (), max(1, total - reach), min(reach, total - 1) + 1)
        return jnp.stack([one, total - one])
    sizes = jnp.asarray(length_profile(number_of, total, reach, skew), jnp.int32)
    couples = (number_of - 1) // 2
    source_of, taker = sizes[1:1 + 2 * couples:2], sizes[2:2 + 2 * couples:2]
    slack = jnp.minimum(source_of - 1, reach - taker)
    moved = jax.random.randint(jax.random.fold_in(key, 1), (couples,), 0, 1 << 20) % (slack + 1)
    sizes = sizes.at[1:1 + 2 * couples:2].set(source_of - moved).at[2:2 + 2 * couples:2].set(taker + moved)
    return sizes[jax.random.permutation(jax.random.fold_in(key, 2), number_of)]


def noise(rng, dims, deviation, limit, pieces=(), kind=jnp.bfloat16):
    values = deviation * jax.random.normal(rng, dims, jnp.float32)
    if pieces:
        values = values * steps_of(rng, dims, pieces, -0.22, 0.18)
    return jnp.clip(values, -limit, limit).astype(kind)


def setup_inputs(seed: int = 0) -> dict:
    key_list = jax.random.split(jax.random.key(seed), 16)
    return {
        "tokens": draw_tokens(jax.random.fold_in(key_list[15], 71), 0),
        "out_grad": noise(key_list[1], (TOKEN_TOTAL, MODEL_WIDTH), 1.0, 6.0, ((0, 32),)),
        "seq_lengths": ragged_sizes(key_list[2], NSEQ, TOKEN_TOTAL, MAX_LEN, 1).astype(jnp.int32),
        "block_deal": draw_block_deal(jax.random.fold_in(key_list[15], 71), 0),
        "norm_gain": jnp.clip(1.0 + 0.1 * jax.random.normal(key_list[4], (MODEL_WIDTH,), jnp.float32), 0.5, 1.5).astype(jnp.bfloat16),
        "q_weight": noise(key_list[5], (MODEL_WIDTH, QUERY_HEADS * HEAD_SIZE), MODEL_WIDTH ** -0.5, 0.125, ((0, 8), (1, 4))),
        "key_projection_weight": noise(key_list[6], (MODEL_WIDTH, KEY_VALUE_HEADS * HEAD_SIZE), MODEL_WIDTH ** -0.5, 0.125, ((0, 8), (1, 4))),
        "value_projection_weight": noise(key_list[7], (MODEL_WIDTH, KEY_VALUE_HEADS * HEAD_SIZE), MODEL_WIDTH ** -0.5, 0.125, ((0, 8), (1, 4))),
        "q_gain": jnp.clip(1.0 + 0.1 * jax.random.normal(key_list[8], (HEAD_SIZE,), jnp.float32), 0.5, 1.5).astype(jnp.bfloat16),
        "k_gain": jnp.clip(1.0 + 0.1 * jax.random.normal(key_list[9], (HEAD_SIZE,), jnp.float32), 0.5, 1.5).astype(jnp.bfloat16),
        "o_weight": noise(key_list[10], (QUERY_HEADS * HEAD_SIZE, MODEL_WIDTH), (HEAD_SIZE // 2) ** -0.5, 0.75, ((0, 4), (1, 8))),
        "mlp_gain": jnp.clip(1.0 + 0.1 * jax.random.normal(key_list[11], (MODEL_WIDTH,), jnp.float32), 0.5, 1.5).astype(jnp.bfloat16),
        "gate_weight": noise(key_list[12], (MODEL_WIDTH, FF), MODEL_WIDTH ** -0.5, 0.125, ((0, 8), (1, 4))),
        "up_weight": noise(key_list[13], (MODEL_WIDTH, FF), MODEL_WIDTH ** -0.5, 0.125, ((0, 8), (1, 4))),
        "down_weight": noise(key_list[14], (FF, MODEL_WIDTH), FF ** -0.5, 0.078125, ((0, 4), (1, 8))),
    }


@jax.custom_vjp
def low(v):
    return lax.optimization_barrier(v.astype(jnp.bfloat16)).astype(jnp.float32)

@jax.custom_vjp
def low_back(v):
    return v

def low_keep(v):
    return (low(v), None)

def low_pass(kept, grad):
    return (grad,)

def back_keep(v):
    return (v, None)

def back_low(kept, grad):
    return (low(grad),)
low.defvjp(low_keep, low_pass)
low_back.defvjp(back_keep, back_low)
EPSILON = 1e-06
ROPE_BASE = 1000000.0
MASKED_SCORE = -1e+30

def rms_norm(values_in, gain_vec):
    mean_square = lax.optimization_barrier(jnp.mean(values_in * values_in, axis=-1, keepdims=True))
    return values_in * lax.rsqrt(mean_square + EPSILON) * gain_vec

def rotate(head_rows, places):
    head_width = head_rows.shape[-1]
    half_width = head_width // 2
    frequency = jnp.power(ROPE_BASE, -jnp.arange(half_width, dtype=jnp.float32) * (2.0 / head_width))
    angles = places.astype(jnp.float32)[:, None] * frequency[None, :]
    cosine = jnp.cos(angles)[:, None, :]
    sine_part = jnp.sin(angles)[:, None, :]
    first_half = head_rows[..., :half_width]
    second = head_rows[..., half_width:]
    return jnp.concatenate([first_half * cosine - second * sine_part, second * cosine + first_half * sine_part], axis=-1)

def head_shape(raw_rows, gain_vec, places, factor):
    row_count = raw_rows.shape[0]
    head_rows = raw_rows.reshape(row_count, -1, gain_vec.shape[0])
    return (rotate(rms_norm(head_rows, gain_vec), places) * factor).reshape(row_count, -1)

def natural_places(blk_ids, group_rows, block_deal, seq_lengths, head_count, tok_dev):
    half_heads = head_count // 2
    source = group_rows // tok_dev
    within = group_rows % tok_dev
    entry_index = 2 * blk_ids + source // half_heads
    span_table = jnp.arange(block_deal.shape[0], dtype=jnp.int32)
    span_ids = lax.optimization_barrier(jnp.sum(jnp.where(entry_index[:, None] == span_table[None, :], block_deal[None, :], 0), axis=1, dtype=jnp.int32))
    natural = span_ids * (half_heads * tok_dev) + source % half_heads * tok_dev + within
    seq_ends = jnp.cumsum(seq_lengths, dtype=jnp.int32)
    seq_start = lax.optimization_barrier(jnp.max(jnp.where(seq_ends[None, :] <= natural[:, None], seq_ends[None, :], 0), axis=1))
    return (natural.astype(jnp.int32), seq_start.astype(jnp.int32))

def product(left_side, right_side):
    return jnp.dot(left_side, right_side, precision=lax.Precision.HIGHEST)

def attend(query_block, block_nat, block_start, natural, key_layout, value_layout):
    allowed = ((natural[None, :] <= block_nat[:, None]) & (natural[None, :] >= block_start[:, None]))[:, None, None, :]
    scores = low_back(jnp.einsum('qjgd,kjd->qjgk', query_block, key_layout, precision=lax.Precision.HIGHEST))
    probabilities = jax.nn.softmax(jnp.where(allowed, scores, MASKED_SCORE), axis=-1)
    return jnp.einsum('qjgk,kjd->qjgd', low(probabilities), value_layout, precision=lax.Precision.HIGHEST)

def reference(tokens, out_grad, seq_lengths, block_deal, norm_gain, q_weight, key_projection_weight, value_projection_weight, q_gain, k_gain, o_weight, mlp_gain, gate_weight, up_weight, down_weight):
    row_ids = jnp.arange(TOKEN_TOTAL, dtype=jnp.int32)
    device_ids = row_ids // TOK_DEV
    natural, seq_start = natural_places(device_ids % N_BLK, device_ids // N_BLK * TOK_DEV + row_ids % TOK_DEV, block_deal, seq_lengths, N_HEAD, TOK_DEV)
    places = natural - seq_start
    rows_per_block = math.gcd(TOKEN_TOTAL, 512)
    block_list = TOKEN_TOTAL // rows_per_block
    nat_blocks = natural.reshape(block_list, rows_per_block)
    start_blocks = seq_start.reshape(block_list, rows_per_block)
    block_fn = jax.checkpoint(attend)

    def block_layer(row_values, gain_one, q_cols, k_cols, v_cols, gain_q, gain_k, o_rows, gain_two, gate_cols, up_cols, down_rows):
        normed = low(rms_norm(row_values, gain_one))
        q_raw = low_back(product(normed, q_cols))
        k_raw = low_back(product(normed, k_cols))
        query_matrix = low_back(low(head_shape(q_raw, gain_q, places, HEAD_SIZE ** (-0.5))))
        rows_of_keys = low_back(low(head_shape(k_raw, gain_k, places, 1.0)))
        value_matrix = low_back(low(product(normed, v_cols)))
        query_layout = query_matrix.reshape(block_list, rows_per_block, KEY_VALUE_HEADS, QUERY_HEADS // KEY_VALUE_HEADS, HEAD_SIZE)
        key_layout = rows_of_keys.reshape(TOKEN_TOTAL, KEY_VALUE_HEADS, HEAD_SIZE)
        value_layout = value_matrix.reshape(TOKEN_TOTAL, KEY_VALUE_HEADS, HEAD_SIZE)
        attended = lax.map(lambda packed: block_fn(packed[0], packed[1], packed[2], natural, key_layout, value_layout), (query_layout, nat_blocks, start_blocks))
        attn_low = low_back(low(attended.reshape(TOKEN_TOTAL, QUERY_HEADS * HEAD_SIZE)))
        residual = row_values + low_back(product(attn_low, o_rows))
        mlp_in = low(rms_norm(residual, gain_two))
        gate_act = low_back(product(mlp_in, gate_cols))
        up_act = low_back(product(mlp_in, up_cols))
        hidden = low(jax.nn.silu(gate_act) * up_act)
        return residual + low_back(product(hidden, down_rows))
    primals = (tokens.astype(jnp.float32), norm_gain.astype(jnp.float32), q_weight.astype(jnp.float32), key_projection_weight.astype(jnp.float32), value_projection_weight.astype(jnp.float32), q_gain.astype(jnp.float32), k_gain.astype(jnp.float32), o_weight.astype(jnp.float32), mlp_gain.astype(jnp.float32), gate_weight.astype(jnp.float32), up_weight.astype(jnp.float32), down_weight.astype(jnp.float32))
    block_out, pull_back = jax.vjp(block_layer, *primals)
    gradients = pull_back(out_grad.astype(jnp.float32))
    return (block_out.astype(jnp.bfloat16), gradients[0], gradients[1], gradients[2], gradients[3], gradients[4], gradients[5], gradients[6], gradients[7], gradients[8], gradients[9], gradients[10], gradients[11])
```

```python
import functools
import math

import jax
import jax.numpy as jnp
from jax import lax
from jax.experimental import pallas as pl
from jax.experimental.pallas import tpu as pltpu
from jax.sharding import Mesh
from jax.sharding import PartitionSpec as P

HEAD_SIZE = 128
KEY_VALUE_HEADS = 8
EPSILON = 1e-06
ROPE_BASE = 1000000.0
F32 = jnp.float32
BF16 = jnp.bfloat16
SWAP = [(0, 1), (1, 0)]
PAIRS_OF_ROWS = (((0,), (0,)), ((), ()))
PAIRS_OF_COLS = (((1,), (1,)), ((), ()))
VMEM = pltpu.MemorySpace.VMEM
SMEM = pltpu.MemorySpace.SMEM


def matmul(left, right):
    return jnp.dot(left, right, preferred_element_type=F32)


def contract_rows(left, right):
    return lax.dot_general(left, right, PAIRS_OF_ROWS, preferred_element_type=F32)


def contract_cols(left, right):
    return lax.dot_general(left, right, PAIRS_OF_COLS, preferred_element_type=F32)


def swap(value, axis):
    return lax.ppermute(value, axis, SWAP)


def attend_kernel(off_ref, tile_ref, q_ref, kv_ref, start_ref, out_ref, inv_ref, acc_ref):
    half = 128
    lane = lax.broadcasted_iota(jnp.int32, (256, 256), 1)
    row = lax.broadcasted_iota(jnp.int32, (256, 256), 0) % half
    ones = jnp.ones((256, HEAD_SIZE), BF16)

    def tile(index, unused):
        first = pl.multiple_of(index * half, half)
        rows = pl.ds(first, half)
        queries = jnp.concatenate([q_ref[rows, :HEAD_SIZE], q_ref[rows, HEAD_SIZE:]], axis=0)
        start = start_ref[rows, :]
        start = jnp.concatenate([start, start], axis=1)
        start = jnp.concatenate([start, start], axis=0)
        places = tile_ref[0, index] * half + row
        acc_ref[...] = jnp.zeros_like(acc_ref)

        def step(block, unused_step):
            low = pl.ds(pl.multiple_of(off_ref[2 * block], half), half)
            high = pl.ds(pl.multiple_of(off_ref[2 * block + 1], half), half)
            keys = jnp.concatenate([kv_ref[low, :HEAD_SIZE], kv_ref[high, :HEAD_SIZE]], axis=0)
            values = jnp.concatenate([kv_ref[low, HEAD_SIZE:], kv_ref[high, HEAD_SIZE:]], axis=0)
            scores = contract_cols(queries, keys)
            natural = block * 256 + lane
            allowed = (natural <= places) & (natural >= start)
            weights = jnp.where(allowed, jnp.exp(scores), 0.0).astype(BF16)
            acc_ref[...] += matmul(weights, jnp.concatenate([values, ones], axis=1))
            return unused_step

        lax.fori_loop(tile_ref[1, index], tile_ref[2, index] + 1, step, 0)
        inverse = 1.0 / acc_ref[:, HEAD_SIZE:]
        attended = (acc_ref[:, :HEAD_SIZE] * inverse).astype(BF16)
        out_ref[rows, :HEAD_SIZE] = attended[:half]
        out_ref[rows, HEAD_SIZE:] = attended[half:]
        inv_ref[index, 0:1, :] = jnp.transpose(inverse[:half])[0:1, :]
        inv_ref[index, 1:2, :] = jnp.transpose(inverse[half:])[0:1, :]
        return unused

    lax.fori_loop(0, q_ref.shape[0] // half, tile, 0)


def attend_back_kernel(
    off_ref, tile_ref, q_ref, kv_ref, start_ref, inv_ref, out_ref, grad_ref, dq_ref, dkv_ref, dk_ref, dv_ref, acc_ref
):
    half = 128
    key_row = lax.broadcasted_iota(jnp.int32, (256, 256), 0)
    query_lane = lax.broadcasted_iota(jnp.int32, (1, 256), 1) % half

    def clear(index, unused):
        rows = pl.ds(pl.multiple_of(index * 256, 256), 256)
        dk_ref[rows, :] = jnp.zeros((256, HEAD_SIZE), F32)
        dv_ref[rows, :] = jnp.zeros((256, HEAD_SIZE), F32)
        return unused

    lax.fori_loop(0, dk_ref.shape[0] // 256, clear, 0)

    def tile(index, unused):
        first = pl.multiple_of(index * half, half)
        rows = pl.ds(first, half)

        def both(ref):
            return jnp.concatenate([ref[rows, :HEAD_SIZE], ref[rows, HEAD_SIZE:]], axis=0)

        def along(ref):
            return jnp.concatenate([ref[index, 0:1, :], ref[index, 1:2, :]], axis=1)

        queries = both(q_ref)
        grads = both(grad_ref)
        products = both(out_ref).astype(F32) * grads.astype(F32)
        deltas = jnp.sum(jnp.transpose(products), axis=0, keepdims=True)
        inverse = along(inv_ref)
        start = along(start_ref)
        places = tile_ref[0, index] * half + query_lane
        acc_ref[...] = jnp.zeros_like(acc_ref)

        def step(block, unused_step):
            low = pl.ds(pl.multiple_of(off_ref[2 * block], half), half)
            high = pl.ds(pl.multiple_of(off_ref[2 * block + 1], half), half)
            keys = jnp.concatenate([kv_ref[low, :HEAD_SIZE], kv_ref[high, :HEAD_SIZE]], axis=0)
            values = jnp.concatenate([kv_ref[low, HEAD_SIZE:], kv_ref[high, HEAD_SIZE:]], axis=0)
            scores = contract_cols(keys, queries)
            natural = block * 256 + key_row
            allowed = (natural <= places) & (natural >= start)
            probs = jnp.where(allowed, jnp.exp(scores) * inverse, 0.0)
            prob_grad = contract_cols(values, grads)
            score_grad = (probs * (prob_grad - deltas)).astype(BF16)
            value_part = matmul(probs.astype(BF16), grads)
            key_part = matmul(score_grad, queries)
            dv_ref[low, :] += value_part[:half]
            dv_ref[high, :] += value_part[half:]
            dk_ref[low, :] += key_part[:half]
            dk_ref[high, :] += key_part[half:]
            acc_ref[...] += contract_rows(score_grad, keys)
            return unused_step

        lax.fori_loop(tile_ref[1, index], tile_ref[2, index] + 1, step, 0)
        query_grad = acc_ref[...].astype(BF16)
        dq_ref[rows, :HEAD_SIZE] = query_grad[:half]
        dq_ref[rows, HEAD_SIZE:] = query_grad[half:]
        return unused

    lax.fori_loop(0, q_ref.shape[0] // half, tile, 0)

    def store(index, unused):
        rows = pl.ds(pl.multiple_of(index * 256, 256), 256)
        dkv_ref[rows, :HEAD_SIZE] = dk_ref[rows, :].astype(BF16)
        dkv_ref[rows, HEAD_SIZE:] = dv_ref[rows, :].astype(BF16)
        return unused

    lax.fori_loop(0, dk_ref.shape[0] // 256, store, 0)


def attend(offsets, tiles, queries, key_values, start_cols):
    rows, width = queries.shape
    keys = key_values.shape[0]
    return pl.pallas_call(
        attend_kernel,
        name="attend",
        out_shape=(
            jax.ShapeDtypeStruct((rows, width), BF16),
            jax.ShapeDtypeStruct((rows // 128, 2, 128), F32),
        ),
        in_specs=[pl.BlockSpec(memory_space=SMEM)] * 2 + [pl.BlockSpec(memory_space=VMEM)] * 3,
        out_specs=[pl.BlockSpec(memory_space=VMEM)] * 2,
        scratch_shapes=[pltpu.VMEM((256, 256), F32)],
        compiler_params=pltpu.CompilerParams(vmem_limit_bytes=8 * 2**20 + keys * 1024),
        cost_estimate=pl.CostEstimate(
            flops=4 * rows * width * 1024 * 2, bytes_accessed=keys * 512 + rows * 2048, transcendentals=rows * 2048
        ),
    )(offsets, tiles, queries, key_values, start_cols)


def attend_back(offsets, tiles, queries, key_values, start_rows, inverse, attended, grads):
    rows, width = queries.shape
    keys = key_values.shape[0]
    return pl.pallas_call(
        attend_back_kernel,
        name="attend_back",
        out_shape=(
            jax.ShapeDtypeStruct((rows, width), BF16),
            jax.ShapeDtypeStruct((keys, width), BF16),
        ),
        in_specs=[pl.BlockSpec(memory_space=SMEM)] * 2 + [pl.BlockSpec(memory_space=VMEM)] * 6,
        out_specs=[pl.BlockSpec(memory_space=VMEM)] * 2,
        scratch_shapes=[
            pltpu.VMEM((keys, HEAD_SIZE), F32),
            pltpu.VMEM((keys, HEAD_SIZE), F32),
            pltpu.VMEM((256, HEAD_SIZE), F32),
        ],
        compiler_params=pltpu.CompilerParams(vmem_limit_bytes=8 * 2**20 + keys * 2560),
        cost_estimate=pl.CostEstimate(
            flops=10 * rows * width * 1024 * 2, bytes_accessed=keys * 1024 + rows * 4096, transcendentals=rows * 2048
        ),
    )(offsets, tiles, queries, key_values, start_rows, inverse, attended, grads)


def shape_kernel(raw_ref, cos_ref, sin_ref, gain_ref, q_ref, kv_ref):
    cosine = cos_ref[...]
    sine = sin_ref[...]

    def shaped(first, gain):
        value = raw_ref[:, first : first + HEAD_SIZE]
        mean_square = jnp.mean(value * value, axis=-1, keepdims=True)
        value = value * lax.rsqrt(mean_square + EPSILON) * gain
        return value * cosine + pltpu.roll(value, HEAD_SIZE // 2, 1) * sine

    for head in range(2):
        columns = slice(head * HEAD_SIZE, (head + 1) * HEAD_SIZE)
        q_ref[:, columns] = (shaped(head * HEAD_SIZE, gain_ref[0:1, :]) * HEAD_SIZE**-0.5).astype(BF16)
    kv_ref[:, :HEAD_SIZE] = shaped(2 * HEAD_SIZE, gain_ref[1:2, :]).astype(BF16)
    kv_ref[:, HEAD_SIZE:] = raw_ref[:, 3 * HEAD_SIZE :].astype(BF16)


def shape_back_kernel(raw_ref, grad_ref, cos_ref, sin_ref, gain_ref, low_ref, gain_grad_ref, *, heads, gain_row, factor):
    @pl.when(pl.program_id(0) == 0)
    def _():
        gain_grad_ref[...] = jnp.zeros_like(gain_grad_ref)

    cosine = cos_ref[...]
    sine = sin_ref[...]
    gain = gain_ref[gain_row : gain_row + 1, :]
    total = jnp.zeros((8, HEAD_SIZE), F32)
    for head in range(heads):
        columns = slice(head * HEAD_SIZE, (head + 1) * HEAD_SIZE)
        value = raw_ref[:, columns]
        grad = grad_ref[:, columns].astype(F32) * factor
        grad = grad * cosine - pltpu.roll(grad, HEAD_SIZE // 2, 1) * sine
        rho = lax.rsqrt(jnp.mean(value * value, axis=-1, keepdims=True) + EPSILON)
        unit = value * rho
        total = total + jnp.sum((grad * unit).reshape(-1, 8, HEAD_SIZE), axis=0)
        scaled = grad * gain
        inner = jnp.mean(scaled * unit, axis=-1, keepdims=True)
        low_ref[:, columns] = (rho * (scaled - unit * inner)).astype(BF16)
    if heads == 1:
        low_ref[:, HEAD_SIZE:] = grad_ref[:, HEAD_SIZE:].astype(BF16)
    gain_grad_ref[...] += total


ROW_TILE = 256


def shape_heads(raw, cosine, sine, gains):
    rows = raw.shape[0]
    block = lambda width: pl.BlockSpec((ROW_TILE, width), lambda i: (i, 0))
    return pl.pallas_call(
        shape_kernel,
        name="shape_heads",
        grid=(rows // ROW_TILE,),
        out_shape=(jax.ShapeDtypeStruct((rows, 256), BF16), jax.ShapeDtypeStruct((rows, 256), BF16)),
        in_specs=[block(512), block(128), block(128), pl.BlockSpec((2, 128), lambda i: (0, 0))],
        out_specs=[block(256), block(256)],
        compiler_params=pltpu.CompilerParams(vmem_limit_bytes=8 * 2**20),
        cost_estimate=pl.CostEstimate(flops=rows * 512 * 20, bytes_accessed=rows * 4096, transcendentals=rows * 3),
    )(raw, cosine, sine, gains)


def shape_back(raw, grads, cosine, sine, gains, heads, column, gain_row, factor):
    rows = raw.shape[0]
    block = lambda width, at=0: pl.BlockSpec((ROW_TILE, width), lambda i: (i, at))
    return pl.pallas_call(
        functools.partial(shape_back_kernel, heads=heads, gain_row=gain_row, factor=factor),
        name="shape_back",
        grid=(rows // ROW_TILE,),
        out_shape=(jax.ShapeDtypeStruct((rows, 256), BF16), jax.ShapeDtypeStruct((8, 128), F32)),
        in_specs=[
            block(heads * 128, column),
            block(256),
            block(128),
            block(128),
            pl.BlockSpec((2, 128), lambda i: (0, 0)),
        ],
        out_specs=[block(256), pl.BlockSpec((8, 128), lambda i: (0, 0))],
        compiler_params=pltpu.CompilerParams(vmem_limit_bytes=8 * 2**20),
        cost_estimate=pl.CostEstimate(flops=rows * 256 * 20, bytes_accessed=rows * 4096, transcendentals=rows * 3),
    )(raw, grads, cosine, sine, gains)


def layer(
    sizes,
    tokens,
    out_grad,
    seq_lengths,
    block_deal,
    norm_gain,
    q_weight,
    k_weight,
    v_weight,
    q_gain,
    k_gain,
    o_weight,
    mlp_gain,
    gate_weight,
    up_weight,
    down_weight,
):
    y_count, core_count, zb_count, za_count, x_count = sizes
    pairwise = sizes == (2, 2, 2, 2, 2)
    all_axes = ("y", "core", "zb", "za", "x")
    y_at, core_at, zb_at, za_at, x_at = (lax.axis_index(name) for name in all_axes)
    tok_dev, width = tokens.shape
    blk_rows = q_weight.shape[0]
    group_count = zb_count * x_count
    member_count = y_count * core_count * za_count
    head_count = y_count * core_count
    rows = member_count * tok_dev
    piece = za_count * blk_rows


    def gather_rows(value):
        if not pairwise:
            return lax.all_gather(value, ("y", "core", "za"), axis=0, tiled=True)
        half = tok_dev // 2
        along_y = swap(value, "y")
        along_z = swap(value, "za")
        parts = [value, along_y, along_z, swap(along_z[:half], "y"), swap(along_y[half:], "za")]
        mine = jnp.concatenate(parts, axis=0)
        return jnp.concatenate([mine, swap(mine, "core")], axis=0)

    def scatter_rows(part_of):
        if not pairwise:
            full = part_of(slice(0, rows)).astype(BF16)
            return lax.psum_scatter(full, ("y", "core", "za"), scatter_dimension=0, tiled=True).astype(F32)
        middle = rows // 2
        half = tok_dev // 2
        given = swap(part_of(slice(middle, rows)).astype(BF16), "core")
        kept = part_of(slice(0, middle)) + given.astype(F32)
        own, to_y, to_z, far = (kept[i * tok_dev : (i + 1) * tok_dev] for i in range(4))
        far = far.astype(BF16)
        from_y = swap(far[:half], "y").astype(F32)
        from_z = swap(far[half:], "za").astype(F32)
        z_sum = jnp.concatenate([to_z[:half] + from_y, to_z[half:]], axis=0).astype(BF16)
        y_sum = jnp.concatenate([to_y[:half], to_y[half:] + from_z], axis=0).astype(BF16)
        return own + swap(y_sum, "y").astype(F32) + swap(z_sum, "za").astype(F32)


    def gather_pieces(own, axis):
        if not pairwise:
            return lax.all_gather(own, ("zb", "x"), axis=axis, tiled=True)
        along_z = swap(own, "zb")
        return jnp.concatenate([own, along_z, swap(own, "x"), swap(along_z, "x")], axis=axis)

    def scatter_pieces(part_of, length, axis):
        if not pairwise:
            full = part_of(0, length).astype(BF16)
            return lax.psum_scatter(full, ("zb", "x"), scatter_dimension=axis, tiled=True).astype(F32)
        half, quarter = length // 2, length // 4
        given = swap(part_of(half, length).astype(BF16), "x")
        kept = part_of(0, half) + given.astype(F32)
        given = swap(lax.slice_in_dim(kept, quarter, half, axis=axis).astype(BF16), "zb")
        return lax.slice_in_dim(kept, 0, quarter, axis=axis) + given.astype(F32)

    def in_order(mine, other, axis):
        first = jnp.where(za_at == 0, mine, other)
        second = jnp.where(za_at == 0, other, mine)
        return jnp.concatenate([first, second], axis=axis)

    def gather_weight(part_of, axis):
        mine = part_of(za_at)
        if za_count > 1:
            mine = in_order(mine, swap(part_of(1 - za_at), "za"), axis)
        return gather_pieces(mine, axis)

    def scatter_weight(part_of, axis):
        part = scatter_pieces(part_of, width, axis)
        if za_count == 1:
            return [part]
        first = lax.slice_in_dim(part, 0, blk_rows, axis=axis)
        second = lax.slice_in_dim(part, blk_rows, 2 * blk_rows, axis=axis)
        mine = jnp.where(za_at == 0, first, second)
        other = swap(jnp.where(za_at == 0, second, first).astype(BF16), "za").astype(F32)
        return [jnp.where(za_at == 0, mine, other), jnp.where(za_at == 0, other, mine)]

    def half_of(weight, at, axis):
        size = weight.shape[axis] // za_count
        return lax.dynamic_slice_in_dim(weight, at * size, size, axis=axis)


    def piece_group(index):
        if pairwise:
            return zb_at ^ (index % 2), x_at ^ (index // 2)
        return index // x_count, index % x_count

    def to_pieces(value):
        blocks = []
        for index in range(group_count):
            zb_of, x_of = piece_group(index)
            for za_of in range(za_count):
                block = (zb_of * za_count + za_of) * x_count + x_of
                blocks.append(lax.dynamic_slice_in_dim(value, block * blk_rows, blk_rows, axis=1))
        return jnp.concatenate(blocks, axis=1) if pairwise else value

    def from_pieces(value):
        if not pairwise:
            return value
        blocks = []
        for block in range(group_count * za_count):
            zb_of, za_of, x_of = block // 4, block // 2 % 2, block % 2
            index = (x_at ^ x_of) * 2 + (zb_at ^ zb_of)
            blocks.append(lax.dynamic_slice_in_dim(value, (index * 2 + za_of) * blk_rows, blk_rows, axis=1))
        return jnp.concatenate(blocks, axis=1)


    per_span = head_count // 2
    member = jnp.arange(member_count, dtype=jnp.int32)
    if pairwise:
        member_y, member_za, member_core = y_at ^ (member % 2), za_at ^ (member // 2 % 2), core_at ^ (member // 4)
    else:
        member_za = member % za_count
        member_core = member // za_count % core_count
        member_y = member // (za_count * core_count)
    group = jnp.arange(group_count, dtype=jnp.int32)
    group_zb, group_x = piece_group(group)
    member_head = member_y * core_count + member_core
    span_table = jnp.arange(block_deal.shape[0], dtype=jnp.int32)

    def natural_tile(zb_of, x_of):
        blk = (zb_of * za_count + member_za) * x_count + x_of
        entry = 2 * blk + member_head // per_span
        span = jnp.sum(
            jnp.where(entry[..., None] == span_table, block_deal, 0), axis=-1, dtype=jnp.int32
        )
        return span * per_span + member_head % per_span

    query_tile = natural_tile(zb_at, x_at)
    key_tile = natural_tile(group_zb[:, None], group_x[:, None]).reshape(-1)
    tile_ids = jnp.arange(key_tile.shape[0], dtype=jnp.int32)
    offsets = jnp.sum(
        jnp.where(key_tile[None, :] == tile_ids[:, None], tile_ids[None, :] * tok_dev, 0), axis=1, dtype=jnp.int32
    )
    natural = query_tile[:, None] * tok_dev + jnp.arange(tok_dev, dtype=jnp.int32)[None, :]
    seq_ids = jnp.arange(seq_lengths.shape[0], dtype=jnp.int32)
    seq_ends = jnp.sum(jnp.where(seq_ids[None, :] <= seq_ids[:, None], seq_lengths[None, :], 0), axis=1, dtype=jnp.int32)
    starts = jnp.max(jnp.where(seq_ends <= natural[..., None], seq_ends, 0), axis=-1)
    tiles = jnp.stack([query_tile, starts[:, 0] // (2 * tok_dev), query_tile // 2])
    start_rows = jnp.stack([starts, starts], axis=1)
    start_cols = jnp.broadcast_to(starts.reshape(rows, 1), (rows, 128))
    places = (natural - starts).reshape(rows)
    half_width = HEAD_SIZE // 2
    frequency = jnp.power(ROPE_BASE, -jnp.arange(half_width, dtype=F32) * (2.0 / HEAD_SIZE))
    angles = places.astype(F32)[:, None] * frequency[None, :]
    cosine = jnp.cos(angles)
    sine = jnp.sin(angles)
    cosine = jnp.concatenate([cosine, cosine], axis=1)
    sine = jnp.concatenate([-sine, sine], axis=1)


    q_width = q_weight.shape[1] // za_count
    k_width = k_weight.shape[1] // za_count
    qkv_width = q_width + 2 * k_width
    gain_pad = 16

    gain_row = jnp.concatenate([norm_gain, mlp_gain])
    head_gains = jnp.concatenate([q_gain, k_gain])

    def gain_rows():
        top = jnp.pad(gain_row, (0, qkv_width - gain_row.shape[0]))[None]
        bottom = jnp.pad(head_gains, (0, qkv_width - head_gains.shape[0]))[None]
        return jnp.concatenate([top, bottom, jnp.zeros((gain_pad - 2, qkv_width), BF16)], axis=0)

    def qkv_part(at):
        return jnp.concatenate(
            [half_of(q_weight, at, 1), half_of(k_weight, at, 1), half_of(v_weight, at, 1), ], axis=1
        )

    padded = blk_rows + gain_pad
    own_gain_rows = gain_rows()
    qkv_all = gather_weight(lambda at: jnp.concatenate([qkv_part(at), own_gain_rows], axis=0), 0)
    qkv_all = qkv_all.reshape(group_count * za_count, padded, qkv_width)
    qkv_cols = qkv_all[:, :blk_rows].reshape(width, qkv_width)
    gains = qkv_all[:, blk_rows, : 2 * blk_rows].astype(F32)
    gain_one = gains[:, :blk_rows].reshape(1, width)
    gain_two = gains[:, blk_rows:].reshape(1, width)
    small = q_gain.shape[0]
    head_parts = qkv_all[:, blk_rows + 1, : 2 * small].astype(F32).reshape(group_count * za_count, 2, small)

    def head_gain(which):
        return from_small(head_parts[:, which])

    def from_small(parts):
        if not pairwise:
            return parts.reshape(1, -1)
        rows_of = []
        for block in range(8):
            zb_of, za_of, x_of = block // 4, block // 2 % 2, block % 2
            index = ((x_at ^ x_of) * 2 + (zb_at ^ zb_of)) * 2 + za_of
            rows_of.append(lax.dynamic_slice_in_dim(parts, index, 1, axis=0))
        return jnp.concatenate(rows_of, axis=1)

    qk_gains = jnp.concatenate([head_gain(0), head_gain(1)], axis=0)


    local_low = to_pieces(tokens)
    local_rows = local_low.astype(F32)
    input_rows = gather_rows(local_low).astype(F32)
    o_cols = gather_weight(lambda at: half_of(o_weight, at, 0), 1)
    gu_cols = gather_weight(
        lambda at: jnp.concatenate([half_of(gate_weight, at, 1), half_of(up_weight, at, 1)], axis=1), 0
    )
    down_cols = gather_weight(lambda at: half_of(down_weight, at, 0), 1)
    grad_local = to_pieces(out_grad)
    grad_rows = gather_rows(grad_local)

    def unit_rows(value):
        return value * lax.rsqrt(jnp.mean(value * value, axis=-1, keepdims=True) + EPSILON)

    input_unit = unit_rows(input_rows)
    normed = (input_unit * gain_one).astype(BF16)
    raw = matmul(normed, qkv_cols)
    queries, kv_own = shape_heads(raw, cosine, sine, qk_gains)
    key_values = gather_pieces(kv_own, 0)
    attn_low, inverse = attend(offsets, tiles, queries, key_values, start_cols)
    residual = local_rows + scatter_rows(lambda at: matmul(attn_low[at], o_cols))


    rho_two = lax.rsqrt(jnp.mean(residual * residual, axis=-1, keepdims=True) + EPSILON)
    unit_two = residual * rho_two
    mlp_rows = gather_rows((unit_two * gain_two).astype(BF16))
    ff = gu_cols.shape[1] // 2
    gate_up = matmul(mlp_rows, gu_cols)
    gate_act, up_act = gate_up[:, :ff], gate_up[:, ff:]
    sig = jax.nn.sigmoid(gate_act)
    silu = gate_act * sig
    hidden = (silu * up_act).astype(BF16)
    hidden_grad = contract_cols(grad_rows, down_cols)
    gate_low = (hidden_grad * up_act * (sig * (1.0 + gate_act * (1.0 - sig)))).astype(BF16)
    up_low = (hidden_grad * silu).astype(BF16)
    gu_low = jnp.concatenate([gate_low, up_low], axis=1)
    mlp_in_grad = scatter_rows(lambda at: contract_cols(gu_low[at], gu_cols))

    down_parts = scatter_weight(lambda lo, hi: contract_rows(hidden, grad_rows[:, lo:hi]), 1)
    gate_parts = scatter_weight(lambda lo, hi: contract_rows(mlp_rows[:, lo:hi], gate_low), 0)
    up_parts = scatter_weight(lambda lo, hi: contract_rows(mlp_rows[:, lo:hi], up_low), 0)
    block_out = residual + scatter_rows(lambda at: matmul(hidden[at], down_cols))

    gain_two_part = jnp.sum(mlp_in_grad * unit_two, axis=0, keepdims=True)
    scaled = mlp_in_grad * gain_two
    inner = jnp.mean(scaled * unit_two, axis=-1, keepdims=True)
    residual_grad = grad_local.astype(F32) + rho_two * (scaled - unit_two * inner)


    branch_rows = gather_rows(residual_grad.astype(BF16))
    attn_grad = contract_cols(branch_rows, o_cols).astype(BF16)
    query_grad, kv_grads = attend_back(
        offsets, tiles, queries, key_values, start_rows, inverse, attn_low, attn_grad
    )
    o_parts = scatter_weight(lambda lo, hi: contract_rows(attn_low, branch_rows[:, lo:hi]), 1)
    kv_grad = scatter_pieces(lambda lo, hi: kv_grads[lo:hi].astype(F32), kv_grads.shape[0], 0).astype(BF16)
    q_low, q_gain_part = shape_back(raw, query_grad, cosine, sine, qk_gains, 2, 0, 0, HEAD_SIZE**-0.5)
    kv_low, k_gain_part = shape_back(raw, kv_grad, cosine, sine, qk_gains, 1, 2, 1, 1.0)
    low = jnp.concatenate([q_low, kv_low], axis=1)

    gain_one_parts = []

    def input_terms(at):
        terms = contract_cols(low[at], qkv_cols)
        gain_one_parts.append(jnp.sum(terms * input_unit[at], axis=0, keepdims=True))
        return terms

    input_grad = scatter_rows(input_terms)
    qkv_parts = scatter_weight(lambda lo, hi: contract_rows(normed[:, lo:hi], low), 0)

    gain_sum = jnp.concatenate(
        [
            from_pieces(sum(gain_one_parts)),
            from_pieces(gain_two_part),
            jnp.sum(q_gain_part, axis=0, keepdims=True),
            jnp.sum(k_gain_part, axis=0, keepdims=True),
        ],
        axis=1,
    )
    if pairwise:
        for name in ("core", "y", "za", "x", "zb"):
            gain_sum = gain_sum + swap(gain_sum, name)
    else:
        gain_sum = lax.psum(gain_sum, all_axes)

    unit_one = local_rows * (rho_one := lax.rsqrt(jnp.mean(local_rows * local_rows, axis=-1, keepdims=True) + EPSILON))
    scaled = input_grad * gain_one
    inner = jnp.mean(scaled * unit_one, axis=-1, keepdims=True)
    in_grad = residual_grad + rho_one * (scaled - unit_one * inner)

    device = (((y_at * core_count + core_at) * zb_count + zb_at) * za_count + za_at) * x_count + x_at
    device_count = head_count * zb_count * za_count * x_count

    def own_slice(first, length):
        share = length // device_count
        return lax.dynamic_slice_in_dim(gain_sum[0], first + device * share, share, axis=0)

    def join(parts, lo, hi, axis):
        cut = [lax.slice_in_dim(part, lo, hi, axis=axis) for part in parts]
        return jnp.concatenate(cut, axis=axis)

    return (
        from_pieces(block_out).astype(BF16),
        from_pieces(in_grad),
        own_slice(0, width),
        join(qkv_parts, 0, q_width, 1),
        join(qkv_parts, q_width, q_width + k_width, 1),
        join(qkv_parts, q_width + k_width, qkv_width, 1),
        own_slice(2 * width, HEAD_SIZE),
        own_slice(2 * width + HEAD_SIZE, HEAD_SIZE),
        jnp.concatenate(o_parts, axis=0),
        own_slice(width, width),
        jnp.concatenate(gate_parts, axis=1),
        jnp.concatenate(up_parts, axis=1),
        jnp.concatenate(down_parts, axis=0),
    )


def solution(mesh):
    heads, blks = mesh.shape["head"], mesh.shape["blk"]
    za_count = KEY_VALUE_HEADS // heads
    side = math.isqrt(blks // za_count)
    sizes = (heads // 2, 2, side, za_count, side)
    names = ("y", "core", "zb", "za", "x")
    devices = mesh.devices.reshape(sizes)
    inner = Mesh(devices, names)
    head, blk = ("y", "core"), ("zb", "za", "x")
    rows, in_weight, out_weight, gain = P(names, None), P(blk, head), P(head, blk), P(blk)
    return jax.shard_map(
        functools.partial(layer, sizes),
        mesh=inner,
        in_specs=(
            rows,
            rows,
            P(),
            P(),
            gain,
            in_weight,
            in_weight,
            in_weight,
            gain,
            gain,
            out_weight,
            gain,
            in_weight,
            in_weight,
            out_weight,
        ),
        out_specs=(
            rows,
            rows,
            P(names),
            in_weight,
            in_weight,
            in_weight,
            P(names),
            P(names),
            out_weight,
            P(names),
            in_weight,
            in_weight,
            out_weight,
        ),
        check_vma=False,
    )
```

```python
import functools
import math

import jax
import jax.numpy as jnp
from jax import lax
from jax.experimental import pallas as pl
from jax.experimental.pallas import tpu as pltpu
from jax.sharding import Mesh
from jax.sharding import PartitionSpec as P

HEAD_SIZE = 128
KEY_VALUE_HEADS = 8
EPSILON = 1e-06
ROPE_BASE = 1000000.0
F32 = jnp.float32
BF16 = jnp.bfloat16
SWAP = [(0, 1), (1, 0)]
PAIRS_OF_ROWS = (((0,), (0,)), ((), ()))
PAIRS_OF_COLS = (((1,), (1,)), ((), ()))
VMEM = pltpu.MemorySpace.VMEM
SMEM = pltpu.MemorySpace.SMEM


def matmul(left, right):
    return jnp.dot(left, right, preferred_element_type=F32)


def contract_rows(left, right):
    return lax.dot_general(left, right, PAIRS_OF_ROWS, preferred_element_type=F32)


def contract_cols(left, right):
    return lax.dot_general(left, right, PAIRS_OF_COLS, preferred_element_type=F32)


def swap(value, axis):
    return lax.ppermute(value, axis, SWAP)


def attend_kernel(off_ref, tile_ref, low_ref, q_ref, kv_ref, start_ref, out_ref, inv_ref, acc_ref):
    half = 128
    lane = lax.broadcasted_iota(jnp.int32, (256, 256), 1)
    row = lax.broadcasted_iota(jnp.int32, (256, 256), 0) % half
    ones = jnp.ones((256, HEAD_SIZE), BF16)

    def tile(index, unused):
        first = pl.multiple_of(index * half, half)
        rows = pl.ds(first, half)
        queries = jnp.concatenate([q_ref[rows, :HEAD_SIZE], q_ref[rows, HEAD_SIZE:]], axis=0)
        start = start_ref[rows, :]
        start = jnp.concatenate([start, start], axis=1)
        start = jnp.concatenate([start, start], axis=0)
        places = tile_ref[index] * half + row
        acc_ref[...] = jnp.zeros_like(acc_ref)

        def step(block, unused_step):
            low = pl.ds(pl.multiple_of(off_ref[2 * block], half), half)
            high = pl.ds(pl.multiple_of(off_ref[2 * block + 1], half), half)
            keys = jnp.concatenate([kv_ref[low, :HEAD_SIZE], kv_ref[high, :HEAD_SIZE]], axis=0)
            values = jnp.concatenate([kv_ref[low, HEAD_SIZE:], kv_ref[high, HEAD_SIZE:]], axis=0)
            scores = contract_cols(queries, keys)
            natural = block * 256 + lane
            allowed = (natural <= places) & (natural >= start)
            weights = jnp.where(allowed, jnp.exp(scores), 0.0).astype(BF16)
            acc_ref[...] += matmul(weights, jnp.concatenate([values, ones], axis=1))
            return unused_step

        lax.fori_loop(low_ref[index], tile_ref[index] // 2 + 1, step, 0)
        inverse = 1.0 / acc_ref[:, HEAD_SIZE:]
        attended = (acc_ref[:, :HEAD_SIZE] * inverse).astype(BF16)
        out_ref[rows, :HEAD_SIZE] = attended[:half]
        out_ref[rows, HEAD_SIZE:] = attended[half:]
        inv_ref[index, 0:1, :] = jnp.transpose(inverse[:half])[0:1, :]
        inv_ref[index, 1:2, :] = jnp.transpose(inverse[half:])[0:1, :]
        return unused

    lax.fori_loop(0, q_ref.shape[0] // half, tile, 0)


def attend_back_kernel(
    off_ref, tile_ref, low_ref, q_ref, kv_ref, start_ref, inv_ref, out_ref, grad_ref, dq_ref, dkv_ref, dk_ref, dv_ref, acc_ref
):
    half = 128
    key_row = lax.broadcasted_iota(jnp.int32, (256, 256), 0)
    query_lane = lax.broadcasted_iota(jnp.int32, (1, 256), 1) % half

    def clear(index, unused):
        rows = pl.ds(pl.multiple_of(index * 256, 256), 256)
        dk_ref[rows, :] = jnp.zeros((256, HEAD_SIZE), F32)
        dv_ref[rows, :] = jnp.zeros((256, HEAD_SIZE), F32)
        return unused

    lax.fori_loop(0, dk_ref.shape[0] // 256, clear, 0)

    def tile(index, unused):
        first = pl.multiple_of(index * half, half)
        rows = pl.ds(first, half)

        def both(ref):
            return jnp.concatenate([ref[rows, :HEAD_SIZE], ref[rows, HEAD_SIZE:]], axis=0)

        def along(ref):
            return jnp.concatenate([ref[index, 0:1, :], ref[index, 1:2, :]], axis=1)

        queries = both(q_ref)
        grads = both(grad_ref)
        products = both(out_ref).astype(F32) * grads.astype(F32)
        deltas = jnp.sum(jnp.transpose(products), axis=0, keepdims=True)
        inverse = along(inv_ref)
        start = along(start_ref)
        places = tile_ref[index] * half + query_lane
        acc_ref[...] = jnp.zeros_like(acc_ref)

        def step(block, unused_step):
            low = pl.ds(pl.multiple_of(off_ref[2 * block], half), half)
            high = pl.ds(pl.multiple_of(off_ref[2 * block + 1], half), half)
            keys = jnp.concatenate([kv_ref[low, :HEAD_SIZE], kv_ref[high, :HEAD_SIZE]], axis=0)
            values = jnp.concatenate([kv_ref[low, HEAD_SIZE:], kv_ref[high, HEAD_SIZE:]], axis=0)
            scores = contract_cols(keys, queries)
            natural = block * 256 + key_row
            allowed = (natural <= places) & (natural >= start)
            probs = jnp.where(allowed, jnp.exp(scores) * inverse, 0.0)
            prob_grad = contract_cols(values, grads)
            score_grad = (probs * (prob_grad - deltas)).astype(BF16)
            value_part = matmul(probs.astype(BF16), grads)
            key_part = matmul(score_grad, queries)
            dv_ref[low, :] += value_part[:half]
            dv_ref[high, :] += value_part[half:]
            dk_ref[low, :] += key_part[:half]
            dk_ref[high, :] += key_part[half:]
            acc_ref[...] += contract_rows(score_grad, keys)
            return unused_step

        lax.fori_loop(low_ref[index], tile_ref[index] // 2 + 1, step, 0)
        query_grad = acc_ref[...].astype(BF16)
        dq_ref[rows, :HEAD_SIZE] = query_grad[:half]
        dq_ref[rows, HEAD_SIZE:] = query_grad[half:]
        return unused

    lax.fori_loop(0, q_ref.shape[0] // half, tile, 0)

    def store(index, unused):
        rows = pl.ds(pl.multiple_of(index * 256, 256), 256)
        dkv_ref[rows, :HEAD_SIZE] = dk_ref[rows, :].astype(BF16)
        dkv_ref[rows, HEAD_SIZE:] = dv_ref[rows, :].astype(BF16)
        return unused

    lax.fori_loop(0, dk_ref.shape[0] // 256, store, 0)


def attend(offsets, tiles, queries, key_values, start_cols):
    rows, width = queries.shape
    keys = key_values.shape[0]
    return pl.pallas_call(
        attend_kernel,
        name="attend",
        out_shape=(
            jax.ShapeDtypeStruct((rows, width), BF16),
            jax.ShapeDtypeStruct((rows // 128, 2, 128), F32),
        ),
        in_specs=[pl.BlockSpec(memory_space=SMEM)] * 3 + [pl.BlockSpec(memory_space=VMEM)] * 3,
        out_specs=[pl.BlockSpec(memory_space=VMEM)] * 2,
        scratch_shapes=[pltpu.VMEM((256, 256), F32)],
        compiler_params=pltpu.CompilerParams(vmem_limit_bytes=8 * 2**20 + keys * 1024),
        cost_estimate=pl.CostEstimate(
            flops=4 * rows * width * 1024 * 2, bytes_accessed=keys * 512 + rows * 2048, transcendentals=rows * 2048
        ),
    )(offsets, *tiles, queries, key_values, start_cols)


def attend_back(offsets, tiles, queries, key_values, start_rows, inverse, attended, grads):
    rows, width = queries.shape
    keys = key_values.shape[0]
    return pl.pallas_call(
        attend_back_kernel,
        name="attend_back",
        out_shape=(
            jax.ShapeDtypeStruct((rows, width), BF16),
            jax.ShapeDtypeStruct((keys, width), BF16),
        ),
        in_specs=[pl.BlockSpec(memory_space=SMEM)] * 3 + [pl.BlockSpec(memory_space=VMEM)] * 6,
        out_specs=[pl.BlockSpec(memory_space=VMEM)] * 2,
        scratch_shapes=[
            pltpu.VMEM((keys, HEAD_SIZE), F32),
            pltpu.VMEM((keys, HEAD_SIZE), F32),
            pltpu.VMEM((256, HEAD_SIZE), F32),
        ],
        compiler_params=pltpu.CompilerParams(vmem_limit_bytes=8 * 2**20 + keys * 2560),
        cost_estimate=pl.CostEstimate(
            flops=10 * rows * width * 1024 * 2, bytes_accessed=keys * 1024 + rows * 4096, transcendentals=rows * 2048
        ),
    )(offsets, *tiles, queries, key_values, start_rows, inverse, attended, grads)


def shape_kernel(raw_ref, cos_ref, sin_ref, gain_ref, q_ref, kv_ref):
    cosine = cos_ref[...]
    sine = sin_ref[...]

    def shaped(first, gain):
        value = raw_ref[:, first : first + HEAD_SIZE]
        mean_square = jnp.mean(value * value, axis=-1, keepdims=True)
        value = value * lax.rsqrt(mean_square + EPSILON) * gain
        return value * cosine + pltpu.roll(value, HEAD_SIZE // 2, 1) * sine

    for head in range(2):
        columns = slice(head * HEAD_SIZE, (head + 1) * HEAD_SIZE)
        q_ref[:, columns] = (shaped(head * HEAD_SIZE, gain_ref[0:1, :]) * HEAD_SIZE**-0.5).astype(BF16)
    kv_ref[:, :HEAD_SIZE] = shaped(2 * HEAD_SIZE, gain_ref[1:2, :]).astype(BF16)
    kv_ref[:, HEAD_SIZE:] = raw_ref[:, 3 * HEAD_SIZE :].astype(BF16)


def shape_back_kernel(raw_ref, grad_ref, cos_ref, sin_ref, gain_ref, low_ref, gain_grad_ref, *, heads, gain_row, factor):
    @pl.when(pl.program_id(0) == 0)
    def _():
        gain_grad_ref[...] = jnp.zeros_like(gain_grad_ref)

    cosine = cos_ref[...]
    sine = sin_ref[...]
    gain = gain_ref[gain_row : gain_row + 1, :]
    total = jnp.zeros((8, HEAD_SIZE), F32)
    for head in range(heads):
        columns = slice(head * HEAD_SIZE, (head + 1) * HEAD_SIZE)
        value = raw_ref[:, columns]
        grad = grad_ref[:, columns].astype(F32) * factor
        grad = grad * cosine - pltpu.roll(grad, HEAD_SIZE // 2, 1) * sine
        rho = lax.rsqrt(jnp.mean(value * value, axis=-1, keepdims=True) + EPSILON)
        unit = value * rho
        total = total + jnp.sum((grad * unit).reshape(-1, 8, HEAD_SIZE), axis=0)
        scaled = grad * gain
        inner = jnp.mean(scaled * unit, axis=-1, keepdims=True)
        low_ref[:, columns] = (rho * (scaled - unit * inner)).astype(BF16)
    if heads == 1:
        low_ref[:, HEAD_SIZE:] = grad_ref[:, HEAD_SIZE:].astype(BF16)
    gain_grad_ref[...] += total


ROW_TILE = 256


def shape_heads(raw, cosine, sine, gains):
    rows = raw.shape[0]
    block = lambda width: pl.BlockSpec((ROW_TILE, width), lambda i: (i, 0))
    return pl.pallas_call(
        shape_kernel,
        name="shape_heads",
        grid=(rows // ROW_TILE,),
        out_shape=(jax.ShapeDtypeStruct((rows, 256), BF16), jax.ShapeDtypeStruct((rows, 256), BF16)),
        in_specs=[block(512), block(128), block(128), pl.BlockSpec((2, 128), lambda i: (0, 0))],
        out_specs=[block(256), block(256)],
        compiler_params=pltpu.CompilerParams(vmem_limit_bytes=8 * 2**20),
        cost_estimate=pl.CostEstimate(flops=rows * 512 * 20, bytes_accessed=rows * 4096, transcendentals=rows * 3),
    )(raw, cosine, sine, gains)


def shape_back(raw, grads, cosine, sine, gains, heads, column, gain_row, factor):
    rows = raw.shape[0]
    block = lambda width, at=0: pl.BlockSpec((ROW_TILE, width), lambda i: (i, at))
    return pl.pallas_call(
        functools.partial(shape_back_kernel, heads=heads, gain_row=gain_row, factor=factor),
        name="shape_back",
        grid=(rows // ROW_TILE,),
        out_shape=(jax.ShapeDtypeStruct((rows, 256), BF16), jax.ShapeDtypeStruct((8, 128), F32)),
        in_specs=[
            block(heads * 128, column),
            block(256),
            block(128),
            block(128),
            pl.BlockSpec((2, 128), lambda i: (0, 0)),
        ],
        out_specs=[block(256), pl.BlockSpec((8, 128), lambda i: (0, 0))],
        compiler_params=pltpu.CompilerParams(vmem_limit_bytes=8 * 2**20),
        cost_estimate=pl.CostEstimate(flops=rows * 256 * 20, bytes_accessed=rows * 4096, transcendentals=rows * 3),
    )(raw, grads, cosine, sine, gains)


def reorder_kernel(order_ref, *refs):
    half = len(refs) // 2
    for source, target in zip(refs[:half], refs[half:]):
        target[...] = source[...].astype(target.dtype)


def reorder(order, values, types):
    rows, width = values[0].shape
    blocks = order.shape[0]
    size = width // blocks
    taken = pl.BlockSpec((rows, size), lambda i, order_ref: (0, order_ref[i]))
    put = pl.BlockSpec((rows, size), lambda i, order_ref: (0, i))
    return pl.pallas_call(
        reorder_kernel,
        name="reorder",
        grid_spec=pltpu.PrefetchScalarGridSpec(
            num_scalar_prefetch=1,
            grid=(blocks,),
            in_specs=[taken] * len(values),
            out_specs=[put] * len(values),
        ),
        out_shape=[jax.ShapeDtypeStruct(value.shape, kind) for value, kind in zip(values, types)],
        compiler_params=pltpu.CompilerParams(vmem_limit_bytes=8 * 2**20),
        cost_estimate=pl.CostEstimate(
            flops=rows * width, bytes_accessed=sum(value.size * 6 for value in values), transcendentals=0
        ),
    )(order, *values)


def after(token, values):
    return lax.optimization_barrier((token, values))[1]


def meet(token, values):
    return lax.optimization_barrier((token, values))


def trade(token, sends):
    held = after(token, [value for value, unused in sends])
    return [swap(value, axis) for value, (unused, axis) in zip(held, sends)]


def places_of(query_tile, key_tile, seq_lengths, tok_dev):
    rows = query_tile.shape[0] * tok_dev
    tile_ids = jnp.arange(key_tile.shape[0], dtype=jnp.int32)
    offsets = jnp.sum(
        jnp.where(key_tile[None, :] == tile_ids[:, None], tile_ids[None, :] * tok_dev, 0), axis=1, dtype=jnp.int32
    )
    natural = query_tile[:, None] * tok_dev + jnp.arange(tok_dev, dtype=jnp.int32)[None, :]
    seq_ids = jnp.arange(seq_lengths.shape[0], dtype=jnp.int32)
    seq_ends = jnp.sum(jnp.where(seq_ids[None, :] <= seq_ids[:, None], seq_lengths[None, :], 0), axis=1, dtype=jnp.int32)
    starts = jnp.max(jnp.where(seq_ends <= natural[..., None], seq_ends, 0), axis=-1)
    tiles = (query_tile, jnp.max(jnp.where(seq_ends <= (query_tile * tok_dev)[:, None], seq_ends, 0), axis=-1) // (2 * tok_dev))
    start_rows = jnp.stack([starts, starts], axis=1)
    start_cols = jnp.broadcast_to(starts.reshape(rows, 1), (rows, 128))
    places = (natural - starts).reshape(rows)
    half_width = HEAD_SIZE // 2
    frequency = jnp.power(ROPE_BASE, -jnp.arange(half_width, dtype=F32) * (2.0 / HEAD_SIZE))
    angles = places.astype(F32)[:, None] * frequency[None, :]
    cosine = jnp.cos(angles)
    sine = jnp.sin(angles)
    cosine = jnp.concatenate([cosine, cosine], axis=1)
    sine = jnp.concatenate([-sine, sine], axis=1)
    return offsets, tiles, start_rows, start_cols, cosine, sine


FAR = 96


def paired_layer(
    tokens,
    out_grad,
    seq_lengths,
    block_deal,
    norm_gain,
    q_weight,
    k_weight,
    v_weight,
    q_gain,
    k_gain,
    o_weight,
    mlp_gain,
    gate_weight,
    up_weight,
    down_weight,
):
    y_at, core_at, zb_at, za_at, x_at = (lax.axis_index(name) for name in ("y", "core", "zb", "za", "x"))
    tok_dev, width = tokens.shape
    blk_rows = q_weight.shape[0]
    rows = 8 * tok_dev
    middle = rows // 2
    half, quarter = width // 2, width // 4
    token = seq_lengths


    place_ids = jnp.arange(8, dtype=jnp.int32)
    to_order = ((zb_at ^ (place_ids // 2 % 2)) * 2 + place_ids % 2) * 2 + (x_at ^ (place_ids // 4))
    from_order = ((x_at ^ (place_ids % 2)) * 2 + (zb_at ^ (place_ids // 4))) * 2 + place_ids // 2 % 2

    def in_order(mine, other, axis):
        first = jnp.where(za_at == 0, mine, other)
        second = jnp.where(za_at == 0, other, mine)
        return jnp.concatenate([first, second], axis=axis)

    def half_of(weight, at, axis):
        size = weight.shape[axis] // 2
        return lax.dynamic_slice_in_dim(weight, at * size, size, axis=axis)


    def near(value):
        return [(value, "y"), (value, "za")]

    def far(from_y, from_z):
        sends = [(from_z[:FAR], "y")]
        return sends + ([(from_y[FAR:], "za")] if FAR < tok_dev else [])

    def mine_of(value, from_y, from_z, fars):
        return jnp.concatenate([value, from_y, from_z] + fars, axis=0)

    def far_sums(kept):
        block = kept[3 * tok_dev :].astype(BF16)
        return [(block[:FAR], "y")] + ([(block[FAR:], "za")] if FAR < tok_dev else [])

    def near_sums(kept, fars):
        to_y, to_z = kept[tok_dev : 2 * tok_dev], kept[2 * tok_dev : 3 * tok_dev]
        if FAR == tok_dev:
            to_z = to_z + fars[0].astype(F32)
        else:
            to_z = jnp.concatenate([to_z[:FAR] + fars[0].astype(F32), to_z[FAR:]], axis=0)
            to_y = jnp.concatenate([to_y[:FAR], to_y[FAR:] + fars[1].astype(F32)], axis=0)
        return [(to_y.astype(BF16), "y"), (to_z.astype(BF16), "za")]

    def own_sum(kept, nears):
        return kept[:tok_dev] + nears[0].astype(F32) + nears[1].astype(F32)


    def za_parts(part, axis):
        first = lax.slice_in_dim(part, 0, blk_rows, axis=axis)
        second = lax.slice_in_dim(part, blk_rows, 2 * blk_rows, axis=axis)
        return jnp.where(za_at == 0, first, second), jnp.where(za_at == 0, second, first).astype(BF16)

    def za_join(mine, other):
        other = other.astype(F32)
        return [jnp.where(za_at == 0, mine, other), jnp.where(za_at == 0, other, mine)]


    member = jnp.arange(8, dtype=jnp.int32)
    member_y, member_za, member_core = y_at ^ (member % 2), za_at ^ (member // 2 % 2), core_at ^ (member // 4)
    group = jnp.arange(4, dtype=jnp.int32)
    span_table = jnp.arange(block_deal.shape[0], dtype=jnp.int32)

    def natural_tile(zb_of, x_of):
        entry = 2 * ((zb_of * 2 + member_za) * 2 + x_of) + member_y
        span = jnp.sum(jnp.where(entry[..., None] == span_table, block_deal, 0), axis=-1, dtype=jnp.int32)
        return span * 2 + member_core

    query_tile = natural_tile(zb_at, x_at)
    key_tile = natural_tile(zb_at ^ (group % 2)[:, None], x_at ^ (group // 2)[:, None]).reshape(-1)
    offsets, tiles, start_rows, start_cols, cosine, sine = places_of(query_tile, key_tile, seq_lengths, tok_dev)


    local_low, grad_local = reorder(to_order, [tokens, out_grad], [BF16, BF16])
    local_rows = local_low.astype(F32)
    q_width, k_width = q_weight.shape[1] // 2, k_weight.shape[1] // 2
    qkv_width = q_width + 2 * k_width
    small = q_gain.shape[0]
    top = jnp.concatenate([norm_gain, mlp_gain])[None]
    spread = jnp.where(
        jnp.arange(HEAD_SIZE, dtype=jnp.int32) // small == (zb_at * 2 + za_at) * 2 + x_at,
        jnp.concatenate([jnp.concatenate([q_gain] * 8)[None], jnp.concatenate([k_gain] * 8)[None]], axis=0),
        0,
    )
    bottom = jnp.concatenate([spread[:1], spread[1:], jnp.zeros((1, qkv_width - 2 * HEAD_SIZE), BF16)], axis=1)
    gain_rows = jnp.concatenate([top, bottom, jnp.zeros((14, qkv_width), BF16)], axis=0)

    def qkv_part(at):
        parts = [half_of(q_weight, at, 1), half_of(k_weight, at, 1), half_of(v_weight, at, 1)]
        return jnp.concatenate([jnp.concatenate(parts, axis=1), gain_rows], axis=0)

    qkv_keep = qkv_part(za_at)
    qkv_give = qkv_part(1 - za_at)
    qkv_far, z_keep, x_keep, tokens_y = trade(
        token, [(qkv_give, "za"), (qkv_keep, "zb"), (qkv_keep, "x"), (local_low, "y")]
    )
    o_give = half_of(o_weight, 1 - za_at, 0)
    token, (qkv_far, z_keep, x_keep, tokens_y) = meet(token, (qkv_far, z_keep, x_keep, tokens_y))
    z_far, tokens_z, x_far, xz_keep = trade(
        token, [(qkv_far, "zb"), (local_low, "za"), (qkv_far, "x"), (z_keep, "x")]
    )
    token, (z_far, tokens_z, x_far, xz_keep) = meet(token, (z_far, tokens_z, x_far, xz_keep))
    xz_far, *fars = trade(token, [(z_far, "x")] + far(tokens_y, tokens_z) + [(o_give, "za")])
    o_far = fars.pop()
    token, (xz_far, fars, o_far) = meet(token, (xz_far, fars, o_far))
    mine = mine_of(local_low, tokens_y, tokens_z, fars)
    o_pair = in_order(half_of(o_weight, za_at, 0), o_far, 1)
    gate_give, up_give = half_of(gate_weight, 1 - za_at, 1), half_of(up_weight, 1 - za_at, 1)
    down_give = half_of(down_weight, 1 - za_at, 0)
    theirs, o_z = trade(token, [(mine, "core"), (o_pair, "zb")])
    (gate_far,) = trade(token, [(gate_give, "za")])
    qkv_all = jnp.concatenate(
        [
            in_order(qkv_keep, qkv_far, 0),
            in_order(z_keep, z_far, 0),
            in_order(x_keep, x_far, 0),
            in_order(xz_keep, xz_far, 0),
        ],
        axis=0,
    ).reshape(8, blk_rows + 16, qkv_width)
    qkv_cols = qkv_all[:, :blk_rows].reshape(width, qkv_width)
    gains = qkv_all[:, blk_rows, : 2 * blk_rows].astype(F32)
    gain_one = gains[:, :blk_rows].reshape(1, width)
    gain_two = gains[:, blk_rows:].reshape(1, width)
    head_sum = jnp.sum(qkv_all[:, blk_rows + 1, : 2 * HEAD_SIZE].astype(F32), axis=0, keepdims=True)
    qk_gains = jnp.concatenate([head_sum[:, :HEAD_SIZE], head_sum[:, HEAD_SIZE:]], axis=0)
    token, (theirs, qkv_cols, gain_one, qk_gains) = meet(token, (theirs, qkv_cols, gain_one, qk_gains))


    input_rows = jnp.concatenate([mine, theirs], axis=0).astype(F32)
    input_unit = input_rows * lax.rsqrt(jnp.mean(input_rows * input_rows, axis=-1, keepdims=True) + EPSILON)
    normed = (input_unit * gain_one).astype(BF16)
    raw = matmul(normed, qkv_cols)
    queries, kv_own = shape_heads(raw, cosine, sine, qk_gains)
    token, (queries, kv_own, o_z, gate_far) = meet(token, (queries, kv_own, o_z, gate_far))
    gate_pair = in_order(half_of(gate_weight, za_at, 1), gate_far, 0)

    kv_z, kv_x, grads_y, up_far = trade(
        token, [(kv_own, "zb"), (kv_own, "x"), (grad_local, "y"), (up_give, "za")]
    )
    token, (kv_z, kv_x, grads_y, up_far) = meet(token, (kv_z, kv_x, grads_y, up_far))
    up_pair = in_order(half_of(up_weight, za_at, 1), up_far, 0)
    kv_xz, gate_z = trade(token, [(kv_z, "x"), (gate_pair, "zb")])
    token, (kv_xz,) = meet(token, (kv_xz,))
    key_values = jnp.concatenate([kv_own, kv_z, kv_x, kv_xz], axis=0)
    o_x, o_xz, down_far, grads_z = trade(
        token, [(o_pair, "x"), (o_z, "x"), (down_give, "za"), (grad_local, "za")]
    )
    attn_low, inverse = attend(offsets, tiles, queries, key_values, start_cols)
    token, (attn_low, o_x, o_xz, gate_z, down_far, grads_z) = meet(
        token, (attn_low, o_x, o_xz, gate_z, down_far, grads_z)
    )
    down_pair = in_order(half_of(down_weight, za_at, 0), down_far, 1)
    o_cols = jnp.concatenate([o_pair, o_z, o_x, o_xz], axis=1)
    given = matmul(attn_low[middle:], o_cols).astype(BF16)
    token, (given,) = meet(token, (given,))
    given, up_z, gate_x = trade(token, [(given, "core"), (up_pair, "zb"), (gate_pair, "x")])
    kept = matmul(attn_low[:middle], o_cols)
    token, (given, kept) = meet(token, (given, kept))
    kept = kept + given.astype(F32)
    fars = trade(token, far_sums(kept))
    (gate_xz,) = trade(token, [(gate_z, "x")])
    token, (fars, kept, gate_x) = meet(token, (fars, kept, gate_x))
    nears = trade(token, near_sums(kept, fars))
    (up_x,) = trade(token, [(up_pair, "x")])
    token, (nears, kept, gate_xz) = meet(token, (nears, kept, gate_xz))
    residual = local_rows + own_sum(kept, nears)


    rho_two = lax.rsqrt(jnp.mean(residual * residual, axis=-1, keepdims=True) + EPSILON)
    unit_two = residual * rho_two
    mlp_low = (unit_two * gain_two).astype(BF16)
    token, (mlp_low, up_x, up_z) = meet(token, (mlp_low, up_x, up_z))
    mlp_y, mlp_z, down_z0, up_xz = trade(token, near(mlp_low) + [(down_pair[:middle], "zb"), (up_z, "x")])
    token, (mlp_y, mlp_z, down_z0, up_xz) = meet(token, (mlp_y, mlp_z, down_z0, up_xz))
    fars = trade(token, far(mlp_y, mlp_z))
    down_z1, down_x = trade(token, [(down_pair[middle:], "zb"), (down_pair, "x")])
    token, (fars,) = meet(token, (fars,))
    mlp_mine = mine_of(mlp_low, mlp_y, mlp_z, fars)
    (mlp_theirs,) = trade(token, [(mlp_mine, "core")])
    (down_xz0,) = trade(token, [(down_z0, "x")])
    gate_cols = jnp.concatenate([gate_pair, gate_z, gate_x, gate_xz], axis=0)
    up_cols = jnp.concatenate([up_pair, up_z, up_x, up_xz], axis=0)
    token, (mlp_theirs, gate_cols, up_cols, down_z1, down_x) = meet(
        token, (mlp_theirs, gate_cols, up_cols, down_z1, down_x)
    )
    (down_xz1, *grads_far) = trade(token, [(down_z1, "x")] + far(grads_y, grads_z))
    mlp_rows = jnp.concatenate([mlp_mine, mlp_theirs], axis=0)
    gate_act = matmul(mlp_rows, gate_cols)
    up_act = matmul(mlp_rows, up_cols)
    sig = jax.nn.sigmoid(gate_act)
    silu = gate_act * sig
    hidden = (silu * up_act).astype(BF16)
    gate_slope = (up_act * (sig * (1.0 + gate_act * (1.0 - sig)))).astype(BF16)
    up_slope = silu.astype(BF16)
    token, (grads_far,) = meet(token, (grads_far,))
    grad_mine = mine_of(grad_local, grads_y, grads_z, grads_far)
    (grad_theirs,) = trade(token, [(grad_mine, "core")])
    token, (hidden, gate_slope, up_slope, down_xz0, down_xz1, grad_theirs) = meet(
        token, (hidden, gate_slope, up_slope, down_xz0, down_xz1, grad_theirs)
    )
    grad_rows = jnp.concatenate([grad_mine, grad_theirs], axis=0)
    down_3 = contract_rows(hidden, grad_rows[:, 3 * quarter :]).astype(BF16)
    down_cols = jnp.concatenate(
        [down_pair, jnp.concatenate([down_z0, down_z1], axis=0), down_x, jnp.concatenate([down_xz0, down_xz1], axis=0)],
        axis=1,
    )
    token, (down_3, down_cols) = meet(token, (down_3, down_cols))
    (down_3,) = trade(token, [(down_3, "x")])
    hidden_grad = contract_cols(grad_rows, after(token, down_cols))
    gate_low = (hidden_grad * gate_slope.astype(F32)).astype(BF16)
    up_low = (hidden_grad * up_slope.astype(F32)).astype(BF16)

    def mlp_terms(at):
        return contract_cols(gate_low[at], gate_cols) + contract_cols(up_low[at], up_cols)

    def columns_of(value, piece):
        return value[:, piece * quarter : (piece + 1) * quarter]

    given = mlp_terms(slice(middle, rows)).astype(BF16)
    token, (given, gate_low, up_low) = meet(token, (given, gate_low, up_low))
    (given,) = trade(token, [(given, "core")])
    kept = mlp_terms(slice(0, middle))
    down_2 = contract_rows(hidden, columns_of(grad_rows, 2)).astype(BF16)
    down_1 = contract_rows(hidden, columns_of(grad_rows, 1))
    token, (given, kept, down_1, down_2, down_3) = meet(token, (given, kept, down_1, down_2, down_3))
    kept = kept + given.astype(F32)
    down_1 = (down_1 + down_3.astype(F32)).astype(BF16)
    fars = trade(token, far_sums(kept))
    down_1a, down_2 = trade(token, [(down_1[:middle], "zb"), (down_2, "x")])
    gate_3 = contract_rows(columns_of(mlp_rows, 3), gate_low).astype(BF16)
    token, (fars, kept, gate_3) = meet(token, (fars, kept, gate_3))
    nears = trade(token, near_sums(kept, fars))
    (gate_3,) = trade(token, [(gate_3, "x")])
    up_3 = contract_rows(columns_of(mlp_rows, 3), up_low).astype(BF16)
    gate_1 = contract_rows(columns_of(mlp_rows, 1), gate_low)
    token, (nears, kept, down_1a, down_2, up_3, gate_1) = meet(token, (nears, kept, down_1a, down_2, up_3, gate_1))
    mlp_in_grad = own_sum(kept, nears)
    gain_two_part = jnp.sum(mlp_in_grad * unit_two, axis=0, keepdims=True)
    scaled = mlp_in_grad * gain_two
    inner = jnp.mean(scaled * unit_two, axis=-1, keepdims=True)
    residual_grad = grad_local.astype(F32) + rho_two * (scaled - unit_two * inner)


    branch_low = residual_grad.astype(BF16)
    token, (branch_low, residual_grad, gain_two_part) = meet(token, (branch_low, residual_grad, gain_two_part))
    branch_y, branch_z, down_1b, up_3 = trade(
        token, near(branch_low) + [(down_1[middle:], "zb"), (up_3, "x")]
    )
    down_0 = contract_rows(hidden, columns_of(grad_rows, 0)) + down_2.astype(F32)
    gate_2 = contract_rows(columns_of(mlp_rows, 2), gate_low).astype(BF16)
    out_given = matmul(hidden[middle:], down_cols).astype(BF16)
    token, (branch_y, branch_z, down_1b, gate_3, down_0, gate_2, out_given) = meet(
        token, (branch_y, branch_z, down_1b, gate_3, down_0, gate_2, out_given)
    )
    gate_1 = (gate_1 + gate_3.astype(F32)).astype(BF16)
    cut = 352
    fars = trade(token, far(branch_y, branch_z))
    gate_1a, gate_2 = trade(token, [(gate_1[:cut], "zb"), (gate_2, "x")])
    out_kept = matmul(hidden[:middle], down_cols)
    token, (fars, out_kept, up_3) = meet(token, (fars, out_kept, up_3))
    branch_mine = mine_of(branch_low, branch_y, branch_z, fars)
    branch_theirs, out_given = trade(token, [(branch_mine, "core"), (out_given, "core")])
    up_1 = contract_rows(columns_of(mlp_rows, 1), up_low) + up_3.astype(F32)
    token, (branch_theirs, out_given, up_1) = meet(token, (branch_theirs, out_given, up_1))
    up_1 = up_1.astype(BF16)
    attn_grad = jnp.concatenate(
        [contract_cols(branch_mine, o_cols).astype(BF16), contract_cols(branch_theirs, o_cols).astype(BF16)], axis=0
    )
    o_3 = (
        contract_rows(attn_low[:middle], columns_of(branch_mine, 3))
        + contract_rows(attn_low[middle:], columns_of(branch_theirs, 3))
    ).astype(BF16)
    up_2 = contract_rows(columns_of(mlp_rows, 2), up_low).astype(BF16)
    token, (attn_grad, o_3, up_2, gate_1a, gate_2) = meet(token, (attn_grad, o_3, up_2, gate_1a, gate_2))
    down_part = down_0 + jnp.concatenate([down_1a, down_1b], axis=0).astype(F32)
    down_mine, down_give = za_parts(down_part, 1)
    gate_1b, up_1a, up_2, o_3, down_give = trade(
        token, [(gate_1[cut:], "zb"), (up_1[:176], "zb"), (up_2, "x"), (o_3, "x"), (down_give, "za")]
    )
    query_grad, kv_grads = attend_back(
        offsets, tiles, queries, key_values, start_rows, inverse, attn_low, attn_grad
    )
    token, (query_grad, kv_grads, gate_1b, up_1a, up_2, o_3, down_give) = meet(
        token, (query_grad, kv_grads, gate_1b, up_1a, up_2, o_3, down_give)
    )
    out_kept = out_kept + out_given.astype(F32)
    gate_0 = contract_rows(columns_of(mlp_rows, 0), gate_low) + gate_2.astype(F32)
    gate_part = gate_0 + jnp.concatenate([gate_1a, gate_1b], axis=0).astype(F32)
    gate_mine, gate_give = za_parts(gate_part, 0)

    def piece_of(value, piece):
        return value[piece * rows : (piece + 1) * rows]

    kv_3, up_1b = trade(token, [(piece_of(kv_grads, 3), "x"), (up_1[176:cut], "zb")])
    out_fars = trade(token, far_sums(out_kept))
    q_low, q_gain_part = shape_back(raw, query_grad, cosine, sine, qk_gains, 2, 0, 0, HEAD_SIZE**-0.5)
    q_3 = contract_rows(columns_of(normed, 3), q_low).astype(BF16)
    q_2 = contract_rows(columns_of(normed, 2), q_low).astype(BF16)
    q_1 = contract_rows(columns_of(normed, 1), q_low)
    token, (kv_3, q_3, q_2, q_1, q_low, q_gain_part, out_fars, gate_give, gate_mine, up_1b) = meet(
        token, (kv_3, q_3, q_2, q_1, q_low, q_gain_part, out_fars, gate_give, gate_mine, up_1b)
    )
    kv_1 = (piece_of(kv_grads, 1).astype(F32) + kv_3.astype(F32)).astype(BF16)
    kv_1, kv_2, q_3, *out_nears = trade(
        token, [(kv_1, "zb"), (piece_of(kv_grads, 2), "x"), (q_3, "x")] + near_sums(out_kept, out_fars)
    )
    o_1 = (
        contract_rows(attn_low[:middle], columns_of(branch_mine, 1))
        + contract_rows(attn_low[middle:], columns_of(branch_theirs, 1))
    ) + o_3.astype(F32)
    o_2 = (
        contract_rows(attn_low[:middle], columns_of(branch_mine, 2))
        + contract_rows(attn_low[middle:], columns_of(branch_theirs, 2))
    ).astype(BF16)
    up_0 = contract_rows(columns_of(mlp_rows, 0), up_low) + up_2.astype(F32)
    q_0 = contract_rows(columns_of(normed, 0), q_low)
    q_terms = contract_cols(q_low[middle:], qkv_cols[:, :q_width])
    token, (kv_1, kv_2, q_3, out_nears, o_1, o_2, up_0, q_0, q_terms) = meet(
        token, (kv_1, kv_2, q_3, out_nears, o_1, o_2, up_0, q_0, q_terms)
    )
    block_out = residual + own_sum(out_kept, out_nears)
    kv_grad = (piece_of(kv_grads, 0).astype(F32) + kv_1.astype(F32) + kv_2.astype(F32)).astype(BF16)
    kv_low, k_gain_part = shape_back(raw, kv_grad, cosine, sine, qk_gains, 1, 2, 1, 1.0)
    terms = q_terms + contract_cols(kv_low[middle:], qkv_cols[:, q_width:])
    gain_one_part = jnp.sum(terms * input_unit[middle:], axis=0, keepdims=True)
    given = terms.astype(BF16)
    token, (given, gain_one_part, kv_low) = meet(token, (given, gain_one_part, kv_low))
    q_1 = (q_1 + q_3.astype(F32)).astype(BF16)
    given, up_1c, o_2, q_2, gate_give = trade(
        token, [(given, "core"), (up_1[cut:], "zb"), (o_2, "x"), (q_2, "x"), (gate_give, "za")]
    )
    terms = contract_cols(q_low[:middle], qkv_cols[:, :q_width]) + contract_cols(kv_low[:middle], qkv_cols[:, q_width:])
    gain_one_part = gain_one_part + jnp.sum(terms * input_unit[:middle], axis=0, keepdims=True)
    gain_sum = jnp.concatenate(
        [
            *reorder(from_order, [gain_one_part, gain_two_part], [F32, F32]),
            jnp.sum(q_gain_part, axis=0, keepdims=True),
            jnp.sum(k_gain_part, axis=0, keepdims=True),
        ],
        axis=1,
    )
    w_3 = contract_rows(columns_of(normed, 3), kv_low).astype(BF16)
    token, (given, terms, gain_sum, w_3) = meet(token, (given, terms, gain_sum, w_3))
    kept = terms + given.astype(F32)
    fars = trade(token, far_sums(kept))
    q_1, w_3, gain_x = trade(token, [(q_1, "zb"), (w_3, "x"), (gain_sum, "core")])
    w_1 = contract_rows(columns_of(normed, 1), kv_low)
    w_2 = contract_rows(columns_of(normed, 2), kv_low).astype(BF16)
    token, (fars, kept, w_3, w_1, w_2, gain_x, up_1c, o_2, q_2, gate_give) = meet(
        token, (fars, kept, w_3, w_1, w_2, gain_x, up_1c, o_2, q_2, gate_give)
    )
    gain_sum = gain_sum + gain_x
    w_1 = (w_1 + w_3.astype(F32)).astype(BF16)
    up_part = up_0 + jnp.concatenate([up_1a, up_1b, up_1c], axis=0).astype(F32)
    up_mine, up_give = za_parts(up_part, 0)
    nears = trade(token, near_sums(kept, fars))
    w_1, w_2, gain_y = trade(token, [(w_1, "zb"), (w_2, "x"), (gain_sum, "y")])
    o_0 = (
        contract_rows(attn_low[:middle], columns_of(branch_mine, 0))
        + contract_rows(attn_low[middle:], columns_of(branch_theirs, 0))
    ) + o_2.astype(F32)
    w_0 = contract_rows(columns_of(normed, 0), kv_low)
    token, (nears, kept, q_1, w_0, o_0, gain_y, w_1, w_2) = meet(token, (nears, kept, q_1, w_0, o_0, gain_y, w_1, w_2))
    gain_sum = gain_sum + gain_y
    qkv_part_grad = jnp.concatenate(
        [q_0 + q_2.astype(F32) + q_1.astype(F32), w_0 + w_2.astype(F32) + w_1.astype(F32)], axis=1
    )
    qkv_mine, qkv_give = za_parts(qkv_part_grad, 0)
    o_1, qkv_give, up_give, gain_x = trade(
        token, [(o_1.astype(BF16), "zb"), (qkv_give, "za"), (up_give, "za"), (gain_sum, "x")]
    )
    input_grad = own_sum(kept, nears)
    unit_one = local_rows * (rho_one := lax.rsqrt(jnp.mean(local_rows * local_rows, axis=-1, keepdims=True) + EPSILON))
    scaled = input_grad * gain_one
    inner = jnp.mean(scaled * unit_one, axis=-1, keepdims=True)
    in_grad = residual_grad + rho_one * (scaled - unit_one * inner)
    block_out, in_grad = reorder(from_order, [block_out, in_grad], [BF16, F32])
    token, (o_1, qkv_give, up_give, gain_x) = meet(token, (o_1, qkv_give, up_give, gain_x))
    o_mine, o_give = za_parts(o_0 + o_1.astype(F32), 1)
    o_give = swap(o_give, "za")
    gain_sum = gain_sum + gain_x
    for name in ("zb", "za"):
        gain_sum = gain_sum + swap(gain_sum, name)
    device = (((y_at * 2 + core_at) * 2 + zb_at) * 2 + za_at) * 2 + x_at

    def own_slice(first, length):
        share = length // 32
        return lax.dynamic_slice_in_dim(gain_sum[0], first + device * share, share, axis=0)

    qkv_parts = za_join(qkv_mine, qkv_give)

    def columns(lo, hi):
        return jnp.concatenate([part[:, lo:hi] for part in qkv_parts], axis=1)

    return (
        block_out,
        in_grad,
        own_slice(0, width),
        columns(0, q_width),
        columns(q_width, q_width + k_width),
        columns(q_width + k_width, qkv_width),
        own_slice(2 * width, HEAD_SIZE),
        own_slice(2 * width + HEAD_SIZE, HEAD_SIZE),
        jnp.concatenate(za_join(o_mine, o_give), axis=0),
        own_slice(width, width),
        jnp.concatenate(za_join(gate_mine, gate_give), axis=1),
        jnp.concatenate(za_join(up_mine, up_give), axis=1),
        jnp.concatenate(za_join(down_mine, down_give), axis=0),
    )


def layer(
    sizes,
    tokens,
    out_grad,
    seq_lengths,
    block_deal,
    norm_gain,
    q_weight,
    k_weight,
    v_weight,
    q_gain,
    k_gain,
    o_weight,
    mlp_gain,
    gate_weight,
    up_weight,
    down_weight,
):
    y_count, core_count, zb_count, za_count, x_count = sizes
    pairwise = sizes == (2, 2, 2, 2, 2)
    all_axes = ("y", "core", "zb", "za", "x")
    y_at, core_at, zb_at, za_at, x_at = (lax.axis_index(name) for name in all_axes)
    tok_dev, width = tokens.shape
    blk_rows = q_weight.shape[0]
    group_count = zb_count * x_count
    member_count = y_count * core_count * za_count
    head_count = y_count * core_count
    rows = member_count * tok_dev
    piece = za_count * blk_rows


    def gather_rows(value):
        if not pairwise:
            return lax.all_gather(value, ("y", "core", "za"), axis=0, tiled=True)
        half = tok_dev // 2
        along_y = swap(value, "y")
        along_z = swap(value, "za")
        parts = [value, along_y, along_z, swap(along_z[:half], "y"), swap(along_y[half:], "za")]
        mine = jnp.concatenate(parts, axis=0)
        return jnp.concatenate([mine, swap(mine, "core")], axis=0)

    def scatter_rows(part_of):
        if not pairwise:
            full = part_of(slice(0, rows)).astype(BF16)
            return lax.psum_scatter(full, ("y", "core", "za"), scatter_dimension=0, tiled=True).astype(F32)
        middle = rows // 2
        half = tok_dev // 2
        given = swap(part_of(slice(middle, rows)).astype(BF16), "core")
        kept = part_of(slice(0, middle)) + given.astype(F32)
        own, to_y, to_z, far = (kept[i * tok_dev : (i + 1) * tok_dev] for i in range(4))
        far = far.astype(BF16)
        from_y = swap(far[:half], "y").astype(F32)
        from_z = swap(far[half:], "za").astype(F32)
        z_sum = jnp.concatenate([to_z[:half] + from_y, to_z[half:]], axis=0).astype(BF16)
        y_sum = jnp.concatenate([to_y[:half], to_y[half:] + from_z], axis=0).astype(BF16)
        return own + swap(y_sum, "y").astype(F32) + swap(z_sum, "za").astype(F32)


    def gather_pieces(own, axis):
        if not pairwise:
            return lax.all_gather(own, ("zb", "x"), axis=axis, tiled=True)
        along_z = swap(own, "zb")
        return jnp.concatenate([own, along_z, swap(own, "x"), swap(along_z, "x")], axis=axis)

    def scatter_pieces(part_of, length, axis):
        if not pairwise:
            full = part_of(0, length).astype(BF16)
            return lax.psum_scatter(full, ("zb", "x"), scatter_dimension=axis, tiled=True).astype(F32)
        half, quarter = length // 2, length // 4
        given = swap(part_of(half, length).astype(BF16), "x")
        kept = part_of(0, half) + given.astype(F32)
        given = swap(lax.slice_in_dim(kept, quarter, half, axis=axis).astype(BF16), "zb")
        return lax.slice_in_dim(kept, 0, quarter, axis=axis) + given.astype(F32)

    def in_order(mine, other, axis):
        first = jnp.where(za_at == 0, mine, other)
        second = jnp.where(za_at == 0, other, mine)
        return jnp.concatenate([first, second], axis=axis)

    def gather_weight(part_of, axis):
        mine = part_of(za_at)
        if za_count > 1:
            mine = in_order(mine, swap(part_of(1 - za_at), "za"), axis)
        return gather_pieces(mine, axis)

    def scatter_weight(part_of, axis):
        part = scatter_pieces(part_of, width, axis)
        if za_count == 1:
            return [part]
        first = lax.slice_in_dim(part, 0, blk_rows, axis=axis)
        second = lax.slice_in_dim(part, blk_rows, 2 * blk_rows, axis=axis)
        mine = jnp.where(za_at == 0, first, second)
        other = swap(jnp.where(za_at == 0, second, first).astype(BF16), "za").astype(F32)
        return [jnp.where(za_at == 0, mine, other), jnp.where(za_at == 0, other, mine)]

    def half_of(weight, at, axis):
        size = weight.shape[axis] // za_count
        return lax.dynamic_slice_in_dim(weight, at * size, size, axis=axis)


    def piece_group(index):
        if pairwise:
            return zb_at ^ (index % 2), x_at ^ (index // 2)
        return index // x_count, index % x_count

    def to_pieces(value):
        blocks = []
        for index in range(group_count):
            zb_of, x_of = piece_group(index)
            for za_of in range(za_count):
                block = (zb_of * za_count + za_of) * x_count + x_of
                blocks.append(lax.dynamic_slice_in_dim(value, block * blk_rows, blk_rows, axis=1))
        return jnp.concatenate(blocks, axis=1) if pairwise else value

    def from_pieces(value):
        if not pairwise:
            return value
        blocks = []
        for block in range(group_count * za_count):
            zb_of, za_of, x_of = block // 4, block // 2 % 2, block % 2
            index = (x_at ^ x_of) * 2 + (zb_at ^ zb_of)
            blocks.append(lax.dynamic_slice_in_dim(value, (index * 2 + za_of) * blk_rows, blk_rows, axis=1))
        return jnp.concatenate(blocks, axis=1)


    per_span = head_count // 2
    member = jnp.arange(member_count, dtype=jnp.int32)
    if pairwise:
        member_y, member_za, member_core = y_at ^ (member % 2), za_at ^ (member // 2 % 2), core_at ^ (member // 4)
    else:
        member_za = member % za_count
        member_core = member // za_count % core_count
        member_y = member // (za_count * core_count)
    group = jnp.arange(group_count, dtype=jnp.int32)
    group_zb, group_x = piece_group(group)
    member_head = member_y * core_count + member_core
    span_table = jnp.arange(block_deal.shape[0], dtype=jnp.int32)

    def natural_tile(zb_of, x_of):
        blk = (zb_of * za_count + member_za) * x_count + x_of
        entry = 2 * blk + member_head // per_span
        span = jnp.sum(
            jnp.where(entry[..., None] == span_table, block_deal, 0), axis=-1, dtype=jnp.int32
        )
        return span * per_span + member_head % per_span

    query_tile = natural_tile(zb_at, x_at)
    key_tile = natural_tile(group_zb[:, None], group_x[:, None]).reshape(-1)
    tile_ids = jnp.arange(key_tile.shape[0], dtype=jnp.int32)
    offsets = jnp.sum(
        jnp.where(key_tile[None, :] == tile_ids[:, None], tile_ids[None, :] * tok_dev, 0), axis=1, dtype=jnp.int32
    )
    natural = query_tile[:, None] * tok_dev + jnp.arange(tok_dev, dtype=jnp.int32)[None, :]
    seq_ids = jnp.arange(seq_lengths.shape[0], dtype=jnp.int32)
    seq_ends = jnp.sum(jnp.where(seq_ids[None, :] <= seq_ids[:, None], seq_lengths[None, :], 0), axis=1, dtype=jnp.int32)
    starts = jnp.max(jnp.where(seq_ends <= natural[..., None], seq_ends, 0), axis=-1)
    tiles = (query_tile, starts[:, 0] // (2 * tok_dev))
    start_rows = jnp.stack([starts, starts], axis=1)
    start_cols = jnp.broadcast_to(starts.reshape(rows, 1), (rows, 128))
    places = (natural - starts).reshape(rows)
    half_width = HEAD_SIZE // 2
    frequency = jnp.power(ROPE_BASE, -jnp.arange(half_width, dtype=F32) * (2.0 / HEAD_SIZE))
    angles = places.astype(F32)[:, None] * frequency[None, :]
    cosine = jnp.cos(angles)
    sine = jnp.sin(angles)
    cosine = jnp.concatenate([cosine, cosine], axis=1)
    sine = jnp.concatenate([-sine, sine], axis=1)


    q_width = q_weight.shape[1] // za_count
    k_width = k_weight.shape[1] // za_count
    qkv_width = q_width + 2 * k_width
    gain_pad = 16

    gain_row = jnp.concatenate([norm_gain, mlp_gain])
    head_gains = jnp.concatenate([q_gain, k_gain])

    def gain_rows():
        top = jnp.pad(gain_row, (0, qkv_width - gain_row.shape[0]))[None]
        bottom = jnp.pad(head_gains, (0, qkv_width - head_gains.shape[0]))[None]
        return jnp.concatenate([top, bottom, jnp.zeros((gain_pad - 2, qkv_width), BF16)], axis=0)

    def qkv_part(at):
        return jnp.concatenate(
            [half_of(q_weight, at, 1), half_of(k_weight, at, 1), half_of(v_weight, at, 1), ], axis=1
        )

    padded = blk_rows + gain_pad
    own_gain_rows = gain_rows()
    qkv_all = gather_weight(lambda at: jnp.concatenate([qkv_part(at), own_gain_rows], axis=0), 0)
    qkv_all = qkv_all.reshape(group_count * za_count, padded, qkv_width)
    qkv_cols = qkv_all[:, :blk_rows].reshape(width, qkv_width)
    gains = qkv_all[:, blk_rows, : 2 * blk_rows].astype(F32)
    gain_one = gains[:, :blk_rows].reshape(1, width)
    gain_two = gains[:, blk_rows:].reshape(1, width)
    small = q_gain.shape[0]
    head_parts = qkv_all[:, blk_rows + 1, : 2 * small].astype(F32).reshape(group_count * za_count, 2, small)

    def head_gain(which):
        return from_small(head_parts[:, which])

    def from_small(parts):
        if not pairwise:
            return parts.reshape(1, -1)
        rows_of = []
        for block in range(8):
            zb_of, za_of, x_of = block // 4, block // 2 % 2, block % 2
            index = ((x_at ^ x_of) * 2 + (zb_at ^ zb_of)) * 2 + za_of
            rows_of.append(lax.dynamic_slice_in_dim(parts, index, 1, axis=0))
        return jnp.concatenate(rows_of, axis=1)

    qk_gains = jnp.concatenate([head_gain(0), head_gain(1)], axis=0)


    local_low = to_pieces(tokens)
    local_rows = local_low.astype(F32)
    input_rows = gather_rows(local_low).astype(F32)
    o_cols = gather_weight(lambda at: half_of(o_weight, at, 0), 1)
    gu_cols = gather_weight(
        lambda at: jnp.concatenate([half_of(gate_weight, at, 1), half_of(up_weight, at, 1)], axis=1), 0
    )
    down_cols = gather_weight(lambda at: half_of(down_weight, at, 0), 1)
    grad_local = to_pieces(out_grad)
    grad_rows = gather_rows(grad_local)

    def unit_rows(value):
        return value * lax.rsqrt(jnp.mean(value * value, axis=-1, keepdims=True) + EPSILON)

    input_unit = unit_rows(input_rows)
    normed = (input_unit * gain_one).astype(BF16)
    raw = matmul(normed, qkv_cols)
    queries, kv_own = shape_heads(raw, cosine, sine, qk_gains)
    key_values = gather_pieces(kv_own, 0)
    attn_low, inverse = attend(offsets, tiles, queries, key_values, start_cols)
    residual = local_rows + scatter_rows(lambda at: matmul(attn_low[at], o_cols))


    rho_two = lax.rsqrt(jnp.mean(residual * residual, axis=-1, keepdims=True) + EPSILON)
    unit_two = residual * rho_two
    mlp_rows = gather_rows((unit_two * gain_two).astype(BF16))
    ff = gu_cols.shape[1] // 2
    gate_up = matmul(mlp_rows, gu_cols)
    gate_act, up_act = gate_up[:, :ff], gate_up[:, ff:]
    sig = jax.nn.sigmoid(gate_act)
    silu = gate_act * sig
    hidden = (silu * up_act).astype(BF16)
    hidden_grad = contract_cols(grad_rows, down_cols)
    gate_low = (hidden_grad * up_act * (sig * (1.0 + gate_act * (1.0 - sig)))).astype(BF16)
    up_low = (hidden_grad * silu).astype(BF16)
    gu_low = jnp.concatenate([gate_low, up_low], axis=1)
    mlp_in_grad = scatter_rows(lambda at: contract_cols(gu_low[at], gu_cols))

    down_parts = scatter_weight(lambda lo, hi: contract_rows(hidden, grad_rows[:, lo:hi]), 1)
    gate_parts = scatter_weight(lambda lo, hi: contract_rows(mlp_rows[:, lo:hi], gate_low), 0)
    up_parts = scatter_weight(lambda lo, hi: contract_rows(mlp_rows[:, lo:hi], up_low), 0)
    block_out = residual + scatter_rows(lambda at: matmul(hidden[at], down_cols))

    gain_two_part = jnp.sum(mlp_in_grad * unit_two, axis=0, keepdims=True)
    scaled = mlp_in_grad * gain_two
    inner = jnp.mean(scaled * unit_two, axis=-1, keepdims=True)
    residual_grad = grad_local.astype(F32) + rho_two * (scaled - unit_two * inner)


    branch_rows = gather_rows(residual_grad.astype(BF16))
    attn_grad = contract_cols(branch_rows, o_cols).astype(BF16)
    query_grad, kv_grads = attend_back(
        offsets, tiles, queries, key_values, start_rows, inverse, attn_low, attn_grad
    )
    o_parts = scatter_weight(lambda lo, hi: contract_rows(attn_low, branch_rows[:, lo:hi]), 1)
    kv_grad = scatter_pieces(lambda lo, hi: kv_grads[lo:hi].astype(F32), kv_grads.shape[0], 0).astype(BF16)
    q_low, q_gain_part = shape_back(raw, query_grad, cosine, sine, qk_gains, 2, 0, 0, HEAD_SIZE**-0.5)
    kv_low, k_gain_part = shape_back(raw, kv_grad, cosine, sine, qk_gains, 1, 2, 1, 1.0)
    low = jnp.concatenate([q_low, kv_low], axis=1)

    gain_one_parts = []

    def input_terms(at):
        terms = contract_cols(low[at], qkv_cols)
        gain_one_parts.append(jnp.sum(terms * input_unit[at], axis=0, keepdims=True))
        return terms

    input_grad = scatter_rows(input_terms)
    qkv_parts = scatter_weight(lambda lo, hi: contract_rows(normed[:, lo:hi], low), 0)

    gain_sum = jnp.concatenate(
        [
            from_pieces(sum(gain_one_parts)),
            from_pieces(gain_two_part),
            jnp.sum(q_gain_part, axis=0, keepdims=True),
            jnp.sum(k_gain_part, axis=0, keepdims=True),
        ],
        axis=1,
    )
    if pairwise:
        for name in ("core", "y", "za", "x", "zb"):
            gain_sum = gain_sum + swap(gain_sum, name)
    else:
        gain_sum = lax.psum(gain_sum, all_axes)

    unit_one = local_rows * (rho_one := lax.rsqrt(jnp.mean(local_rows * local_rows, axis=-1, keepdims=True) + EPSILON))
    scaled = input_grad * gain_one
    inner = jnp.mean(scaled * unit_one, axis=-1, keepdims=True)
    in_grad = residual_grad + rho_one * (scaled - unit_one * inner)

    device = (((y_at * core_count + core_at) * zb_count + zb_at) * za_count + za_at) * x_count + x_at
    device_count = head_count * zb_count * za_count * x_count

    def own_slice(first, length):
        share = length // device_count
        return lax.dynamic_slice_in_dim(gain_sum[0], first + device * share, share, axis=0)

    def join(parts, lo, hi, axis):
        cut = [lax.slice_in_dim(part, lo, hi, axis=axis) for part in parts]
        return jnp.concatenate(cut, axis=axis)

    return (
        from_pieces(block_out).astype(BF16),
        from_pieces(in_grad),
        own_slice(0, width),
        join(qkv_parts, 0, q_width, 1),
        join(qkv_parts, q_width, q_width + k_width, 1),
        join(qkv_parts, q_width + k_width, qkv_width, 1),
        own_slice(2 * width, HEAD_SIZE),
        own_slice(2 * width + HEAD_SIZE, HEAD_SIZE),
        jnp.concatenate(o_parts, axis=0),
        own_slice(width, width),
        jnp.concatenate(gate_parts, axis=1),
        jnp.concatenate(up_parts, axis=1),
        jnp.concatenate(down_parts, axis=0),
    )


def solution(mesh):
    heads, blks = mesh.shape["head"], mesh.shape["blk"]
    za_count = KEY_VALUE_HEADS // heads
    side = math.isqrt(blks // za_count)
    sizes = (heads // 2, 2, side, za_count, side)
    names = ("y", "core", "zb", "za", "x")
    devices = mesh.devices.reshape(sizes)
    inner = Mesh(devices, names)
    head, blk = ("y", "core"), ("zb", "za", "x")
    rows, in_weight, out_weight, gain = P(names, None), P(blk, head), P(head, blk), P(blk)
    return jax.shard_map(
        paired_layer if sizes == (2, 2, 2, 2, 2) else functools.partial(layer, sizes),
        mesh=inner,
        in_specs=(
            rows,
            rows,
            P(),
            P(),
            gain,
            in_weight,
            in_weight,
            in_weight,
            gain,
            gain,
            out_weight,
            gain,
            in_weight,
            in_weight,
            out_weight,
        ),
        out_specs=(
            rows,
            rows,
            P(names),
            in_weight,
            in_weight,
            in_weight,
            P(names),
            P(names),
            out_weight,
            P(names),
            in_weight,
            in_weight,
            out_weight,
        ),
        check_vma=False,
    )
```

```python
import functools
import math

import jax
import jax.numpy as jnp
from jax import lax
from jax.experimental import pallas as pl
from jax.experimental.pallas import tpu as pltpu
from jax.sharding import Mesh
from jax.sharding import PartitionSpec as P

HEAD_SIZE = 128
KEY_VALUE_HEADS = 8
EPSILON = 1e-06
ROPE_BASE = 1000000.0
F32 = jnp.float32
BF16 = jnp.bfloat16
SWAP = [(0, 1), (1, 0)]
PAIRS_OF_ROWS = (((0,), (0,)), ((), ()))
PAIRS_OF_COLS = (((1,), (1,)), ((), ()))
VMEM = pltpu.MemorySpace.VMEM
LIGHT = pl.CostEstimate(flops=1000, bytes_accessed=1000, transcendentals=0)
SMEM = pltpu.MemorySpace.SMEM


def matmul(left, right):
    return jnp.dot(left, right, preferred_element_type=F32)


def contract_rows(left, right):
    return lax.dot_general(left, right, PAIRS_OF_ROWS, preferred_element_type=F32)


def contract_cols(left, right):
    return lax.dot_general(left, right, PAIRS_OF_COLS, preferred_element_type=F32)


def swap(value, axis):
    return lax.ppermute(value, axis, SWAP)


def attend_kernel(off_ref, tile_ref, low_ref, q_ref, start_ref, *refs, parts, first, last):
    half = 128
    kv_refs, refs = refs[:parts], refs[parts:]
    if not first:
        before_ref, refs = refs[0], refs[1:]
    if last:
        out_ref, inv_ref, kv_ref, acc_ref = refs
    else:
        after_ref, kv_ref, acc_ref = refs
    share = kv_refs[0].shape[0]
    for part, ref in enumerate(kv_refs):
        kv_ref[part * share : (part + 1) * share, :] = ref[...]
    lane = lax.broadcasted_iota(jnp.int32, (256, 256), 1)
    row = lax.broadcasted_iota(jnp.int32, (256, 256), 0) % half
    ones = jnp.ones((256, HEAD_SIZE), BF16)

    def tile(index, unused):
        rows = pl.ds(pl.multiple_of(index * half, half), half)
        queries = jnp.concatenate([q_ref[rows, :HEAD_SIZE], q_ref[rows, HEAD_SIZE:]], axis=0)
        start = start_ref[rows, :]
        start = jnp.concatenate([start, start], axis=1)
        start = jnp.concatenate([start, start], axis=0)
        places = tile_ref[index] * half + row
        acc_ref[...] = jnp.zeros_like(acc_ref) if first else before_ref[index]

        def step(block, unused_step):
            at = off_ref[2 * block]

            @pl.when(at >= 0)
            def _():
                low = pl.ds(pl.multiple_of(at, half), half)
                high = pl.ds(pl.multiple_of(off_ref[2 * block + 1], half), half)
                keys = jnp.concatenate([kv_ref[low, :HEAD_SIZE], kv_ref[high, :HEAD_SIZE]], axis=0)
                values = jnp.concatenate([kv_ref[low, HEAD_SIZE:], kv_ref[high, HEAD_SIZE:]], axis=0)
                scores = contract_cols(queries, keys)
                natural = block * 256 + lane
                allowed = (natural <= places) & (natural >= start)
                weights = jnp.where(allowed, jnp.exp(scores), 0.0).astype(BF16)
                acc_ref[...] += matmul(weights, jnp.concatenate([values, ones], axis=1))

            return unused_step

        lax.fori_loop(low_ref[index], tile_ref[index] // 2 + 1, step, 0)
        if last:
            inverse = 1.0 / acc_ref[:, HEAD_SIZE:]
            attended = (acc_ref[:, :HEAD_SIZE] * inverse).astype(BF16)
            out_ref[rows, :HEAD_SIZE] = attended[:half]
            out_ref[rows, HEAD_SIZE:] = attended[half:]
            inv_ref[index, 0:1, :] = jnp.transpose(inverse[:half])[0:1, :]
            inv_ref[index, 1:2, :] = jnp.transpose(inverse[half:])[0:1, :]
        else:
            after_ref[index] = acc_ref[...]
        return unused

    lax.fori_loop(0, q_ref.shape[0] // half, tile, 0)


def attend_back_kernel(
    off_ref, tile_ref, low_ref, q_ref, start_ref, inv_ref, out_ref, grad_ref, *refs, parts, first, last
):
    half = 128
    kv_refs, refs = refs[:parts], refs[parts:]
    if not first:
        before_ref, refs = refs[0], refs[1:]
    dq_ref, *dkv_refs = refs[: 1 + parts]
    kv_ref, dk_ref, dv_ref, acc_ref = refs[1 + parts :]
    share = kv_refs[0].shape[0]
    for part, ref in enumerate(kv_refs):
        kv_ref[part * share : (part + 1) * share, :] = ref[...]
    key_row = lax.broadcasted_iota(jnp.int32, (256, 256), 0)
    query_lane = lax.broadcasted_iota(jnp.int32, (1, 256), 1) % half

    def clear(index, unused):
        rows = pl.ds(pl.multiple_of(index * 256, 256), 256)
        dk_ref[rows, :] = jnp.zeros((256, HEAD_SIZE), F32)
        dv_ref[rows, :] = jnp.zeros((256, HEAD_SIZE), F32)
        return unused

    lax.fori_loop(0, dk_ref.shape[0] // 256, clear, 0)

    def tile(index, unused):
        rows = pl.ds(pl.multiple_of(index * half, half), half)

        def both(ref):
            return jnp.concatenate([ref[rows, :HEAD_SIZE], ref[rows, HEAD_SIZE:]], axis=0)

        def along(ref):
            return jnp.concatenate([ref[index, 0:1, :], ref[index, 1:2, :]], axis=1)

        queries = both(q_ref)
        grads = both(grad_ref)
        products = both(out_ref).astype(F32) * grads.astype(F32)
        deltas = jnp.sum(jnp.transpose(products), axis=0, keepdims=True)
        inverse = along(inv_ref)
        start = along(start_ref)
        places = tile_ref[index] * half + query_lane
        acc_ref[...] = jnp.zeros_like(acc_ref) if first else both(before_ref)

        def step(block, unused_step):
            at = off_ref[2 * block]

            @pl.when(at >= 0)
            def _():
                low = pl.ds(pl.multiple_of(at, half), half)
                high = pl.ds(pl.multiple_of(off_ref[2 * block + 1], half), half)
                keys = jnp.concatenate([kv_ref[low, :HEAD_SIZE], kv_ref[high, :HEAD_SIZE]], axis=0)
                values = jnp.concatenate([kv_ref[low, HEAD_SIZE:], kv_ref[high, HEAD_SIZE:]], axis=0)
                scores = contract_cols(keys, queries)
                natural = block * 256 + key_row
                allowed = (natural <= places) & (natural >= start)
                probs = jnp.where(allowed, jnp.exp(scores) * inverse, 0.0)
                prob_grad = contract_cols(values, grads)
                score_grad = (probs * (prob_grad - deltas)).astype(BF16)
                value_part = matmul(probs.astype(BF16), grads)
                key_part = matmul(score_grad, queries)
                dv_ref[low, :] += value_part[:half]
                dv_ref[high, :] += value_part[half:]
                dk_ref[low, :] += key_part[:half]
                dk_ref[high, :] += key_part[half:]
                acc_ref[...] += contract_rows(score_grad, keys)

            return unused_step

        lax.fori_loop(low_ref[index], tile_ref[index] // 2 + 1, step, 0)
        dq_ref[rows, :HEAD_SIZE] = acc_ref[:half, :].astype(dq_ref.dtype)
        dq_ref[rows, HEAD_SIZE:] = acc_ref[half:, :].astype(dq_ref.dtype)
        return unused

    lax.fori_loop(0, q_ref.shape[0] // half, tile, 0)

    for part, ref in enumerate(dkv_refs):

        def store(index, unused):
            target = pl.ds(pl.multiple_of(index * 256, 256), 256)
            source = pl.ds(pl.multiple_of(part * share + index * 256, 256), 256)
            ref[target, :HEAD_SIZE] = dk_ref[source, :].astype(BF16)
            ref[target, HEAD_SIZE:] = dv_ref[source, :].astype(BF16)
            return unused

        lax.fori_loop(0, share // 256, store, 0)


def attend(offsets, tiles, queries, start_cols, kv_parts, before=None, last=True):
    rows, width = queries.shape
    parts, share = len(kv_parts), kv_parts[0].shape[0]
    keys = parts * share
    first = before is None
    extra = () if first else (before,)
    whole = (
        (jax.ShapeDtypeStruct((rows, width), BF16), jax.ShapeDtypeStruct((rows // 128, 2, 128), F32))
        if last
        else (jax.ShapeDtypeStruct((rows // 128, 256, 256), F32),)
    )
    return pl.pallas_call(
        functools.partial(attend_kernel, parts=parts, first=first, last=last),
        name="attend",
        out_shape=whole,
        in_specs=[pl.BlockSpec(memory_space=SMEM)] * 3 + [pl.BlockSpec(memory_space=VMEM)] * (2 + parts + len(extra)),
        out_specs=[pl.BlockSpec(memory_space=VMEM)] * len(whole),
        scratch_shapes=[pltpu.VMEM((keys, width), BF16), pltpu.VMEM((256, 256), F32)],
        compiler_params=pltpu.CompilerParams(vmem_limit_bytes=12 * 2**20 + keys * 1536),
        cost_estimate=LIGHT,
    )(offsets, *tiles, queries, start_cols, *kv_parts, *extra)


def attend_back(offsets, tiles, queries, start_rows, inverse, attended, grads, kv_parts, before=None, last=True):
    rows, width = queries.shape
    parts, share = len(kv_parts), kv_parts[0].shape[0]
    keys = parts * share
    first = before is None
    extra = () if first else (before,)
    return pl.pallas_call(
        functools.partial(attend_back_kernel, parts=parts, first=first, last=last),
        name="attend_back",
        out_shape=(jax.ShapeDtypeStruct((rows, width), BF16 if last else F32),)
        + tuple(jax.ShapeDtypeStruct((share, width), BF16) for unused in kv_parts),
        in_specs=[pl.BlockSpec(memory_space=SMEM)] * 3 + [pl.BlockSpec(memory_space=VMEM)] * (5 + parts + len(extra)),
        out_specs=[pl.BlockSpec(memory_space=VMEM)] * (1 + parts),
        scratch_shapes=[
            pltpu.VMEM((keys, width), BF16),
            pltpu.VMEM((keys, HEAD_SIZE), F32),
            pltpu.VMEM((keys, HEAD_SIZE), F32),
            pltpu.VMEM((256, HEAD_SIZE), F32),
        ],
        compiler_params=pltpu.CompilerParams(vmem_limit_bytes=12 * 2**20 + keys * 2816),
        cost_estimate=LIGHT,
    )(offsets, *tiles, queries, start_rows, inverse, attended, grads, *kv_parts, *extra)


def shape_kernel(raw_ref, cos_ref, sin_ref, gain_ref, q_ref, kv_ref):
    cosine = cos_ref[...]
    sine = sin_ref[...]

    def shaped(first, gain):
        value = raw_ref[:, first : first + HEAD_SIZE]
        mean_square = jnp.mean(value * value, axis=-1, keepdims=True)
        value = value * lax.rsqrt(mean_square + EPSILON) * gain
        return value * cosine + pltpu.roll(value, HEAD_SIZE // 2, 1) * sine

    for head in range(2):
        columns = slice(head * HEAD_SIZE, (head + 1) * HEAD_SIZE)
        q_ref[:, columns] = (shaped(head * HEAD_SIZE, gain_ref[0:1, :]) * HEAD_SIZE**-0.5).astype(BF16)
    kv_ref[:, :HEAD_SIZE] = shaped(2 * HEAD_SIZE, gain_ref[1:2, :]).astype(BF16)
    kv_ref[:, HEAD_SIZE:] = raw_ref[:, 3 * HEAD_SIZE :].astype(BF16)


def shape_back_kernel(raw_ref, grad_ref, cos_ref, sin_ref, gain_ref, low_ref, gain_grad_ref, *, heads, gain_row, factor):
    @pl.when(pl.program_id(0) == 0)
    def _():
        gain_grad_ref[...] = jnp.zeros_like(gain_grad_ref)

    cosine = cos_ref[...]
    sine = sin_ref[...]
    gain = gain_ref[gain_row : gain_row + 1, :]
    total = jnp.zeros((8, HEAD_SIZE), F32)
    for head in range(heads):
        columns = slice(head * HEAD_SIZE, (head + 1) * HEAD_SIZE)
        value = raw_ref[:, columns]
        grad = grad_ref[:, columns].astype(F32) * factor
        grad = grad * cosine - pltpu.roll(grad, HEAD_SIZE // 2, 1) * sine
        rho = lax.rsqrt(jnp.mean(value * value, axis=-1, keepdims=True) + EPSILON)
        unit = value * rho
        total = total + jnp.sum((grad * unit).reshape(-1, 8, HEAD_SIZE), axis=0)
        scaled = grad * gain
        inner = jnp.mean(scaled * unit, axis=-1, keepdims=True)
        low_ref[:, columns] = (rho * (scaled - unit * inner)).astype(BF16)
    if heads == 1:
        low_ref[:, HEAD_SIZE:] = grad_ref[:, HEAD_SIZE:].astype(BF16)
    gain_grad_ref[...] += total


ROW_TILE = 256


def shape_heads(raw, cosine, sine, gains):
    rows = raw.shape[0]
    block = lambda width: pl.BlockSpec((ROW_TILE, width), lambda i: (i, 0))
    return pl.pallas_call(
        shape_kernel,
        name="shape_heads",
        grid=(rows // ROW_TILE,),
        out_shape=(jax.ShapeDtypeStruct((rows, 256), BF16), jax.ShapeDtypeStruct((rows, 256), BF16)),
        in_specs=[block(512), block(128), block(128), pl.BlockSpec((2, 128), lambda i: (0, 0))],
        out_specs=[block(256), block(256)],
        compiler_params=pltpu.CompilerParams(vmem_limit_bytes=8 * 2**20),
        cost_estimate=LIGHT,
    )(raw, cosine, sine, gains)


def shape_back(raw, grads, cosine, sine, gains, heads, column, gain_row, factor):
    rows = raw.shape[0]
    block = lambda width, at=0: pl.BlockSpec((ROW_TILE, width), lambda i: (i, at))
    return pl.pallas_call(
        functools.partial(shape_back_kernel, heads=heads, gain_row=gain_row, factor=factor),
        name="shape_back",
        grid=(rows // ROW_TILE,),
        out_shape=(jax.ShapeDtypeStruct((rows, 256), BF16), jax.ShapeDtypeStruct((8, 128), F32)),
        in_specs=[
            block(heads * 128, column),
            block(256),
            block(128),
            block(128),
            pl.BlockSpec((2, 128), lambda i: (0, 0)),
        ],
        out_specs=[block(256), pl.BlockSpec((8, 128), lambda i: (0, 0))],
        compiler_params=pltpu.CompilerParams(vmem_limit_bytes=8 * 2**20),
        cost_estimate=LIGHT,
    )(raw, grads, cosine, sine, gains)


def reorder_kernel(order_ref, *refs):
    half = len(refs) // 2
    for source, target in zip(refs[:half], refs[half:]):
        target[...] = source[...].astype(target.dtype)


def reorder(order, values, types):
    rows, width = values[0].shape
    blocks = order.shape[0]
    size = width // blocks
    taken = pl.BlockSpec((rows, size), lambda i, order_ref: (0, order_ref[i]))
    put = pl.BlockSpec((rows, size), lambda i, order_ref: (0, i))
    return pl.pallas_call(
        reorder_kernel,
        name="reorder",
        grid_spec=pltpu.PrefetchScalarGridSpec(
            num_scalar_prefetch=1,
            grid=(blocks,),
            in_specs=[taken] * len(values),
            out_specs=[put] * len(values),
        ),
        out_shape=[jax.ShapeDtypeStruct(value.shape, kind) for value, kind in zip(values, types)],
        compiler_params=pltpu.CompilerParams(vmem_limit_bytes=8 * 2**20),
        cost_estimate=LIGHT,
    )(order, *values)


def pack_kernel(at_ref, q_ref, k_ref, v_ref, norm_ref, mlp_ref, head_ref, keep_ref, give_ref):
    rows, q_width = q_ref.shape[0], q_ref.shape[1] // 2
    k_width = k_ref.shape[1] // 2
    total = q_width + 2 * k_width
    small = head_ref.shape[1]
    place = lax.broadcasted_iota(jnp.int32, (small, HEAD_SIZE), 1) - lax.broadcasted_iota(
        jnp.int32, (small, HEAD_SIZE), 0
    )
    spread = matmul(head_ref[...], (place == at_ref[1] * small).astype(BF16)).astype(BF16)
    extra = jnp.concatenate(
        [
            jnp.concatenate([norm_ref[...], mlp_ref[...]], axis=1),
            jnp.concatenate([spread[0:1], spread[1:2], jnp.zeros((1, total - 2 * HEAD_SIZE), BF16)], axis=1),
            jnp.zeros((14, total), BF16),
        ],
        axis=0,
    )
    for target, at in ((keep_ref, at_ref[0]), (give_ref, 1 - at_ref[0])):
        target[:rows, :q_width] = q_ref[:, pl.ds(pl.multiple_of(at * q_width, 128), q_width)]
        target[:rows, q_width : q_width + k_width] = k_ref[:, pl.ds(pl.multiple_of(at * k_width, 128), k_width)]
        target[:rows, q_width + k_width :] = v_ref[:, pl.ds(pl.multiple_of(at * k_width, 128), k_width)]
        target[rows:, :] = extra


def pack(at, q_weight, k_weight, v_weight, norm_gain, mlp_gain, head_gains):
    shape = jax.ShapeDtypeStruct((q_weight.shape[0] + 16, (q_weight.shape[1] + 2 * k_weight.shape[1]) // 2), BF16)
    return pl.pallas_call(
        pack_kernel,
        name="pack",
        out_shape=(shape, shape),
        grid=(1,),
        in_specs=[pl.BlockSpec(memory_space=SMEM)]
        + [
            pl.BlockSpec(value.shape, lambda i: (0, 0))
            for value in (q_weight, k_weight, v_weight, norm_gain, mlp_gain, head_gains)
        ],
        out_specs=[pl.BlockSpec(shape.shape, lambda i: (0, 0))] * 2,
        compiler_params=pltpu.CompilerParams(vmem_limit_bytes=8 * 2**20),
        cost_estimate=LIGHT,
    )(at, q_weight, k_weight, v_weight, norm_gain, mlp_gain, head_gains)


def after(token, values):
    return lax.optimization_barrier((token, values))[1]


def meet(token, values):
    return lax.optimization_barrier((token, values))


def trade(token, sends):
    held = after(token, [value for value, unused in sends])
    return [swap(value, axis) for value, (unused, axis) in zip(held, sends)]


def places_of(query_tile, key_tile, seq_lengths, tok_dev):
    rows = query_tile.shape[0] * tok_dev
    tile_ids = jnp.arange(key_tile.shape[0], dtype=jnp.int32)
    shares = (tile_ids // 16) * 8 + tile_ids % 8
    found = key_tile[None, :] == tile_ids[:, None]

    def offsets_of(parity):
        mine = found & (tile_ids // 8 % 2 == parity)[None, :]
        return jnp.sum(jnp.where(mine, shares * tok_dev + 1, 0), axis=1, dtype=jnp.int32) - 1

    offsets = (offsets_of(0), offsets_of(1))
    natural = query_tile[:, None] * tok_dev + jnp.arange(tok_dev, dtype=jnp.int32)[None, :]
    seq_ids = jnp.arange(seq_lengths.shape[0], dtype=jnp.int32)
    seq_ends = jnp.sum(jnp.where(seq_ids[None, :] <= seq_ids[:, None], seq_lengths[None, :], 0), axis=1, dtype=jnp.int32)
    starts = jnp.max(jnp.where(seq_ends <= natural[..., None], seq_ends, 0), axis=-1)
    tiles = (query_tile, jnp.max(jnp.where(seq_ends <= (query_tile * tok_dev)[:, None], seq_ends, 0), axis=-1) // (2 * tok_dev))
    start_rows = jnp.stack([starts, starts], axis=1)
    start_cols = jnp.broadcast_to(starts.reshape(rows, 1), (rows, 128))
    places = (natural - starts).reshape(rows)
    half_width = HEAD_SIZE // 2
    frequency = jnp.power(ROPE_BASE, -jnp.arange(half_width, dtype=F32) * (2.0 / HEAD_SIZE))
    angles = places.astype(F32)[:, None] * frequency[None, :]
    cosine = jnp.cos(angles)
    sine = jnp.sin(angles)
    cosine = jnp.concatenate([cosine, cosine], axis=1)
    sine = jnp.concatenate([-sine, sine], axis=1)
    return offsets, tiles, start_rows, start_cols, cosine, sine


FAR = 96


def paired_layer(
    tokens,
    out_grad,
    seq_lengths,
    block_deal,
    norm_gain,
    q_weight,
    k_weight,
    v_weight,
    q_gain,
    k_gain,
    o_weight,
    mlp_gain,
    gate_weight,
    up_weight,
    down_weight,
):
    y_at, core_at, zb_at, za_at, x_at = (lax.axis_index(name) for name in ("y", "core", "zb", "za", "x"))
    tok_dev, width = tokens.shape
    blk_rows = q_weight.shape[0]
    rows = 8 * tok_dev
    middle = rows // 2
    half, quarter = width // 2, width // 4
    token = seq_lengths


    place_ids = jnp.arange(8, dtype=jnp.int32)
    to_order = ((zb_at ^ (place_ids // 2 % 2)) * 2 + place_ids % 2) * 2 + (x_at ^ (place_ids // 4))
    from_order = ((x_at ^ (place_ids % 2)) * 2 + (zb_at ^ (place_ids // 4))) * 2 + place_ids // 2 % 2

    def in_order(mine, other, axis):
        first = jnp.where(za_at == 0, mine, other)
        second = jnp.where(za_at == 0, other, mine)
        return jnp.concatenate([first, second], axis=axis)

    def half_of(weight, at, axis):
        size = weight.shape[axis] // 2
        return lax.dynamic_slice_in_dim(weight, at * size, size, axis=axis)


    def near(value):
        return [(value, "y"), (value, "za")]

    def far(from_y, from_z):
        sends = [(from_z[:FAR], "y")]
        return sends + ([(from_y[FAR:], "za")] if FAR < tok_dev else [])

    def mine_of(value, from_y, from_z, fars):
        return jnp.concatenate([value, from_y, from_z] + fars, axis=0)

    def far_sums(kept):
        block = kept[3 * tok_dev :].astype(BF16)
        return [(block[:FAR], "y")] + ([(block[FAR:], "za")] if FAR < tok_dev else [])

    def near_sums(kept, fars):
        to_y, to_z = kept[tok_dev : 2 * tok_dev], kept[2 * tok_dev : 3 * tok_dev]
        if FAR == tok_dev:
            to_z = to_z + fars[0].astype(F32)
        else:
            to_z = jnp.concatenate([to_z[:FAR] + fars[0].astype(F32), to_z[FAR:]], axis=0)
            to_y = jnp.concatenate([to_y[:FAR], to_y[FAR:] + fars[1].astype(F32)], axis=0)
        return [(to_y.astype(BF16), "y"), (to_z.astype(BF16), "za")]

    def own_sum(kept, nears):
        return kept[:tok_dev] + nears[0].astype(F32) + nears[1].astype(F32)


    def za_parts(part, axis):
        first = lax.slice_in_dim(part, 0, blk_rows, axis=axis)
        second = lax.slice_in_dim(part, blk_rows, 2 * blk_rows, axis=axis)
        return jnp.where(za_at == 0, first, second), jnp.where(za_at == 0, second, first).astype(BF16)

    def za_join(mine, other):
        other = other.astype(F32)
        return [jnp.where(za_at == 0, mine, other), jnp.where(za_at == 0, other, mine)]


    member = jnp.arange(8, dtype=jnp.int32)
    member_y, member_za, member_core = y_at ^ (member % 2), za_at ^ (member // 2 % 2), core_at ^ (member // 4)
    group = jnp.arange(4, dtype=jnp.int32)
    span_table = jnp.arange(block_deal.shape[0], dtype=jnp.int32)

    def natural_tile(zb_of, x_of):
        entry = 2 * ((zb_of * 2 + member_za) * 2 + x_of) + member_y
        span = jnp.sum(jnp.where(entry[..., None] == span_table, block_deal, 0), axis=-1, dtype=jnp.int32)
        return span * 2 + member_core

    query_tile = natural_tile(zb_at, x_at)
    key_tile = natural_tile(zb_at ^ (group % 2)[:, None], x_at ^ (group // 2)[:, None]).reshape(-1)
    offsets, tiles, start_rows, start_cols, cosine, sine = places_of(query_tile, key_tile, seq_lengths, tok_dev)


    local_low, grad_local = reorder(to_order, [tokens, out_grad], [BF16, BF16])
    local_rows = local_low.astype(F32)
    q_width, k_width = q_weight.shape[1] // 2, k_weight.shape[1] // 2
    qkv_width = q_width + 2 * k_width
    qkv_keep, qkv_give = pack(
        jnp.stack([za_at, (zb_at * 2 + za_at) * 2 + x_at]),
        q_weight,
        k_weight,
        v_weight,
        norm_gain[None],
        mlp_gain[None],
        jnp.stack([q_gain, k_gain]),
    )
    o_give = half_of(o_weight, 1 - za_at, 0)
    z_keep, qkv_far, x_keep = swap(qkv_keep, "zb"), swap(qkv_give, "za"), swap(qkv_keep, "x")
    tokens_y, o_far = swap(local_low, "y"), swap(o_give, "za")
    token, (qkv_far, z_keep, x_keep, tokens_y) = meet(token, (qkv_far, z_keep, x_keep, tokens_y))
    tokens_z, z_far, xz_keep, x_far = trade(
        token, [(local_low, "za"), (qkv_far, "zb"), (z_keep, "x"), (qkv_far, "x")]
    )
    token, (z_far, tokens_z, xz_keep, x_far, o_far) = meet(token, (z_far, tokens_z, xz_keep, x_far, o_far))
    o_pair = in_order(half_of(o_weight, za_at, 0), o_far, 1)
    *fars, xz_far, o_z = trade(token, far(tokens_y, tokens_z) + [(z_far, "x"), (o_pair, "zb")])
    token, (xz_far, fars) = meet(token, (xz_far, fars))
    mine = mine_of(local_low, tokens_y, tokens_z, fars)
    gate_keep, up_keep = half_of(gate_weight, za_at, 1), half_of(up_weight, za_at, 1)
    gate_give, up_give = half_of(gate_weight, 1 - za_at, 1), half_of(up_weight, 1 - za_at, 1)
    down_keep, down_give = half_of(down_weight, za_at, 0), half_of(down_weight, 1 - za_at, 0)
    theirs, gate_zk, gate_far, o_x = trade(token, [(mine, "core"), (gate_keep, "zb"), (gate_give, "za"), (o_pair, "x")])
    qkv_all = jnp.concatenate(
        [
            in_order(qkv_keep, qkv_far, 0),
            in_order(z_keep, z_far, 0),
            in_order(x_keep, x_far, 0),
            in_order(xz_keep, xz_far, 0),
        ],
        axis=0,
    ).reshape(8, blk_rows + 16, qkv_width)
    qkv_cols = qkv_all[:, :blk_rows].reshape(width, qkv_width)
    gains = qkv_all[:, blk_rows, : 2 * blk_rows].astype(F32)
    gain_one = gains[:, :blk_rows].reshape(1, width)
    gain_two = gains[:, blk_rows:].reshape(1, width)
    head_sum = jnp.sum(qkv_all[:, blk_rows + 1, : 2 * HEAD_SIZE].astype(F32), axis=0, keepdims=True)
    qk_gains = jnp.concatenate([head_sum[:, :HEAD_SIZE], head_sum[:, HEAD_SIZE:]], axis=0)
    token, (theirs, qkv_cols, gain_one, qk_gains) = meet(token, (theirs, qkv_cols, gain_one, qk_gains))


    input_rows = jnp.concatenate([mine, theirs], axis=0).astype(F32)
    input_unit = input_rows * lax.rsqrt(jnp.mean(input_rows * input_rows, axis=-1, keepdims=True) + EPSILON)
    normed = (input_unit * gain_one).astype(BF16)
    raw = matmul(normed, qkv_cols)
    queries, kv_own = shape_heads(raw, cosine, sine, qk_gains)
    token, (queries, kv_own, o_z, o_x, gate_zk) = meet(token, (queries, kv_own, o_z, o_x, gate_zk))
    kv_z, kv_x, grads_y = trade(token, [(kv_own, "zb"), (kv_own, "x"), (grad_local, "y")])
    (o_xz,) = trade(token, [(o_z, "x")])
    token, (kv_x, gate_far) = meet(token, (kv_x, gate_far))
    (attn_part,) = attend(offsets[0], tiles, queries, start_cols, [kv_own, kv_x], last=False)
    gate_pair = in_order(gate_keep, gate_far, 0)
    token, (kv_z, attn_part, grads_y, o_xz) = meet(token, (kv_z, attn_part, grads_y, o_xz))
    kv_xz, gate_zf, grads_z = trade(token, [(kv_z, "x"), (gate_far, "zb"), (grad_local, "za")])
    o_cols = jnp.concatenate([o_pair, o_z, o_x, o_xz], axis=1)
    token, (kv_xz, o_cols) = meet(token, (kv_xz, o_cols))
    gate_x, up_far = trade(token, [(gate_pair, "x"), (up_give, "za")])
    attn_low, inverse = attend(offsets[1], tiles, queries, start_cols, [kv_z, kv_xz], before=attn_part)
    given = matmul(attn_low[middle:], o_cols).astype(BF16)
    token, (given, attn_low, gate_zf, grads_z) = meet(token, (given, attn_low, gate_zf, grads_z))
    given, *grads_far = trade(token, [(given, "core")] + far(grads_y, grads_z))
    kept = matmul(attn_low[:middle], o_cols)
    token, (given, kept, up_far) = meet(token, (given, kept, up_far))
    up_pair = in_order(up_keep, up_far, 0)
    kept = kept + given.astype(F32)
    *fars, up_z0, gate_xzk, down_far = trade(
        token, far_sums(kept) + [(up_pair[:blk_rows], "zb"), (gate_zk, "x"), (down_give, "za")]
    )
    token, (fars, kept, gate_x, grads_far) = meet(token, (fars, kept, gate_x, grads_far))
    grad_mine = mine_of(grad_local, grads_y, grads_z, grads_far)
    nears = trade(token, near_sums(kept, fars))
    gate_xzf, up_x = trade(token, [(gate_zf, "x"), (up_pair, "x")])
    token, (nears, kept, up_z0, gate_xzk, down_far) = meet(token, (nears, kept, up_z0, gate_xzk, down_far))
    down_pair = in_order(down_keep, down_far, 1)
    residual = local_rows + own_sum(kept, nears)


    rho_two = lax.rsqrt(jnp.mean(residual * residual, axis=-1, keepdims=True) + EPSILON)
    unit_two = residual * rho_two
    mlp_low = (unit_two * gain_two).astype(BF16)
    token, (mlp_low, gate_xzf, up_x) = meet(token, (mlp_low, gate_xzf, up_x))
    *nears, up_z1, up_xz0 = trade(token, near(mlp_low) + [(up_pair[blk_rows:], "zb"), (up_z0, "x")])
    gate_cols = jnp.concatenate(
        [gate_pair, in_order(gate_zk, gate_zf, 0), gate_x, in_order(gate_xzk, gate_xzf, 0)], axis=0
    )
    token, (nears, up_xz0, gate_cols) = meet(token, (nears, up_xz0, gate_cols))
    mlp_y, mlp_z = nears
    fars = trade(token, far(mlp_y, mlp_z))
    token, (fars, up_z1) = meet(token, (fars, up_z1))
    mlp_mine = mine_of(mlp_low, mlp_y, mlp_z, fars)
    mlp_theirs, up_xz1, down_z0, grad_theirs = trade(
        token, [(mlp_mine, "core"), (up_z1, "x"), (down_pair[:middle], "zb"), (grad_mine, "core")]
    )
    up_cols = jnp.concatenate([up_pair, up_z0, up_z1, up_x, up_xz0, up_xz1], axis=0)
    token, (mlp_theirs, up_cols) = meet(token, (mlp_theirs, up_cols))
    (down_x,) = trade(token, [(down_pair, "x")])
    mlp_rows = jnp.concatenate([mlp_mine, mlp_theirs], axis=0)
    gate_act = matmul(mlp_rows, gate_cols)
    token, (gate_act, down_z0, down_x, grad_theirs) = meet(token, (gate_act, down_z0, down_x, grad_theirs))
    down_z1, down_xz0 = trade(token, [(down_pair[middle:], "zb"), (down_z0, "x")])
    up_act = matmul(mlp_rows, up_cols)
    sig = jax.nn.sigmoid(gate_act)
    silu = gate_act * sig
    hidden = (silu * up_act).astype(BF16)
    gate_slope = (up_act * (sig * (1.0 + gate_act * (1.0 - sig)))).astype(BF16)
    up_slope = silu.astype(BF16)
    token, (hidden, gate_slope, up_slope, down_z1, down_xz0) = meet(
        token, (hidden, gate_slope, up_slope, down_z1, down_xz0)
    )
    grad_rows = jnp.concatenate([grad_mine, grad_theirs], axis=0)

    def columns_of(value, piece):
        return value[:, piece * quarter : (piece + 1) * quarter]

    (down_xz1,) = trade(token, [(down_z1, "x")])
    down_z = jnp.concatenate([down_z0, down_z1], axis=0)
    down_3 = contract_rows(hidden, columns_of(grad_rows, 3)).astype(BF16)
    hidden_part = (
        contract_cols(columns_of(grad_rows, 0), down_pair)
        + contract_cols(columns_of(grad_rows, 1), down_z)
        + contract_cols(columns_of(grad_rows, 2), down_x)
    )
    token, (down_xz1, down_3, hidden_part) = meet(token, (down_xz1, down_3, hidden_part))
    (down_3,) = trade(token, [(down_3, "x")])
    down_xz = jnp.concatenate([down_xz0, down_xz1], axis=0)
    hidden_grad = hidden_part + contract_cols(columns_of(grad_rows, 3), down_xz)
    gate_low = (hidden_grad * gate_slope.astype(F32)).astype(BF16)
    up_low = (hidden_grad * up_slope.astype(F32)).astype(BF16)

    def mlp_terms(at):
        return contract_cols(gate_low[at], gate_cols) + contract_cols(up_low[at], up_cols)

    given = mlp_terms(slice(middle, rows)).astype(BF16)
    token, (given, gate_low, up_low) = meet(token, (given, gate_low, up_low))
    (given,) = trade(token, [(given, "core")])
    kept = mlp_terms(slice(0, middle))
    down_1 = contract_rows(hidden, columns_of(grad_rows, 1))
    token, (given, kept, down_1, down_3) = meet(token, (given, kept, down_1, down_3))
    kept = kept + given.astype(F32)
    down_1 = (down_1 + down_3.astype(F32)).astype(BF16)
    *fars, down_1a = trade(token, far_sums(kept) + [(down_1[:middle], "zb")])
    gate_3 = contract_rows(columns_of(mlp_rows, 3), gate_low).astype(BF16)
    down_2 = contract_rows(hidden, columns_of(grad_rows, 2)).astype(BF16)
    token, (fars, kept, gate_3, down_2) = meet(token, (fars, kept, gate_3, down_2))
    *nears, gate_3 = trade(token, near_sums(kept, fars) + [(gate_3, "x")])
    up_3 = contract_rows(columns_of(mlp_rows, 3), up_low).astype(BF16)
    gate_1 = contract_rows(columns_of(mlp_rows, 1), gate_low)
    token, (nears, kept, down_1a, up_3, gate_1) = meet(token, (nears, kept, down_1a, up_3, gate_1))
    mlp_in_grad = own_sum(kept, nears)
    gain_two_part = jnp.sum(mlp_in_grad * unit_two, axis=0, keepdims=True)
    scaled = mlp_in_grad * gain_two
    inner = jnp.mean(scaled * unit_two, axis=-1, keepdims=True)
    residual_grad = grad_local.astype(F32) + rho_two * (scaled - unit_two * inner)


    branch_low = residual_grad.astype(BF16)
    token, (branch_low, residual_grad, gain_two_part) = meet(token, (branch_low, residual_grad, gain_two_part))
    branch_y, branch_z, down_1b, down_2 = trade(
        token, near(branch_low) + [(down_1[middle:], "zb"), (down_2, "x")]
    )
    gate_2 = contract_rows(columns_of(mlp_rows, 2), gate_low).astype(BF16)
    down_cols = jnp.concatenate([down_pair, down_z, down_x, down_xz], axis=1)
    out_given = matmul(hidden[middle:], down_cols).astype(BF16)
    token, (branch_y, branch_z, down_1b, gate_3, gate_2, out_given) = meet(
        token, (branch_y, branch_z, down_1b, gate_3, gate_2, out_given)
    )
    gate_1 = (gate_1 + gate_3.astype(F32)).astype(BF16)
    cut = 352
    *fars, gate_1a, up_3 = trade(token, far(branch_y, branch_z) + [(gate_1[:128], "zb"), (up_3, "x")])
    out_kept = matmul(hidden[:middle], down_cols)
    token, (fars, out_kept, down_2, gate_1a) = meet(token, (fars, out_kept, down_2, gate_1a))
    branch_mine = mine_of(branch_low, branch_y, branch_z, fars)
    branch_theirs, out_given, gate_1b = trade(
        token, [(branch_mine, "core"), (out_given, "core"), (gate_1[128:384], "zb")]
    )
    token, (branch_theirs, out_given) = meet(token, (branch_theirs, out_given))
    attn_grad = jnp.concatenate(
        [contract_cols(branch_mine, o_cols).astype(BF16), contract_cols(branch_theirs, o_cols).astype(BF16)], axis=0
    )
    token, (attn_grad, gate_1b, up_3) = meet(token, (attn_grad, gate_1b, up_3))
    gate_1c, gate_2 = trade(token, [(gate_1[384:], "zb"), (gate_2, "x")])
    query_part, kv_1, kv_3 = attend_back(
        offsets[1], tiles, queries, start_rows, inverse, attn_low, attn_grad, [kv_z, kv_xz], last=False
    )
    up_1 = (contract_rows(columns_of(mlp_rows, 1), up_low) + up_3.astype(F32)).astype(BF16)
    out_kept = out_kept + out_given.astype(F32)
    token, (query_part, kv_1, kv_3, gate_1c, up_1, out_kept) = meet(
        token, (query_part, kv_1, kv_3, gate_1c, up_1, out_kept)
    )
    kv_3, up_1a, *out_fars = trade(token, [(kv_3, "x"), (up_1[:blk_rows], "zb")] + far_sums(out_kept))
    query_grad, kv_0, kv_2 = attend_back(
        offsets[0],
        tiles,
        queries,
        start_rows,
        inverse,
        attn_low,
        attn_grad,
        [kv_own, kv_x],
        before=query_part,
    )
    token, (query_grad, kv_0, kv_2, kv_3, out_fars, up_1a, gate_2) = meet(
        token, (query_grad, kv_0, kv_2, kv_3, out_fars, up_1a, gate_2)
    )
    kv_1 = (kv_1.astype(F32) + kv_3.astype(F32)).astype(BF16)
    kv_1, kv_2, *out_nears = trade(token, [(kv_1, "zb"), (kv_2, "x")] + near_sums(out_kept, out_fars))
    q_low, q_gain_part = shape_back(raw, query_grad, cosine, sine, qk_gains, 2, 0, 0, HEAD_SIZE**-0.5)
    q_3 = contract_rows(columns_of(normed, 3), q_low).astype(BF16)
    q_1 = contract_rows(columns_of(normed, 1), q_low)
    branch_rows = jnp.concatenate([branch_mine, branch_theirs], axis=0)
    o_3 = contract_rows(attn_low, columns_of(branch_rows, 3)).astype(BF16)
    up_2 = contract_rows(columns_of(mlp_rows, 2), up_low).astype(BF16)
    token, (kv_2, out_nears, q_low, q_gain_part, q_3, q_1, o_3, up_2) = meet(
        token, (kv_2, out_nears, q_low, q_gain_part, q_3, q_1, o_3, up_2)
    )
    q_3, o_3 = trade(token, [(q_3, "x"), (o_3, "x")])
    down_0 = contract_rows(hidden, columns_of(grad_rows, 0)) + down_2.astype(F32)
    down_part = down_0 + jnp.concatenate([down_1a, down_1b], axis=0).astype(F32)
    down_mine, down_give = za_parts(down_part, 1)
    gate_0 = contract_rows(columns_of(mlp_rows, 0), gate_low) + gate_2.astype(F32)
    gate_part = gate_0 + jnp.concatenate([gate_1a, gate_1b, gate_1c], axis=0).astype(F32)
    gate_mine, gate_give = za_parts(gate_part, 0)
    block_out = residual + own_sum(out_kept, out_nears)
    q_terms = contract_cols(q_low[middle:], qkv_cols[:, :q_width])
    token, (kv_1, gate_mine, gate_give, down_mine, down_give, block_out, q_terms) = meet(
        token, (kv_1, gate_mine, gate_give, down_mine, down_give, block_out, q_terms)
    )
    up_1b, up_2, gate_give, down_give = trade(
        token, [(up_1[blk_rows:], "zb"), (up_2, "x"), (gate_give, "za"), (down_give, "za")]
    )
    kv_grad = (kv_0.astype(F32) + kv_1.astype(F32) + kv_2.astype(F32)).astype(BF16)
    kv_low, k_gain_part = shape_back(raw, kv_grad, cosine, sine, qk_gains, 1, 2, 1, 1.0)
    terms = q_terms + contract_cols(kv_low[middle:], qkv_cols[:, q_width:])
    gain_one_part = jnp.sum(terms * input_unit[middle:], axis=0, keepdims=True)
    given = terms.astype(BF16)
    token, (given, gain_one_part, kv_low, q_3, o_3) = meet(token, (given, gain_one_part, kv_low, q_3, o_3))
    q_1 = (q_1 + q_3.astype(F32)).astype(BF16)
    (given,) = trade(token, [(given, "core")])
    terms = contract_cols(q_low[:middle], qkv_cols[:, :q_width]) + contract_cols(kv_low[:middle], qkv_cols[:, q_width:])
    gain_one_part = gain_one_part + jnp.sum(terms * input_unit[:middle], axis=0, keepdims=True)
    token, (given, terms, gain_one_part) = meet(token, (given, terms, gain_one_part))
    kept = terms + given.astype(F32)
    low = jnp.concatenate([q_low, kv_low], axis=1)
    w_3 = contract_rows(columns_of(normed, 3), kv_low).astype(BF16)
    o_1 = (contract_rows(attn_low, columns_of(branch_rows, 1)) + o_3.astype(F32)).astype(BF16)
    gain_sum = jnp.concatenate(
        [
            *reorder(from_order, [gain_one_part, gain_two_part], [F32, F32]),
            jnp.sum(q_gain_part, axis=0, keepdims=True),
            jnp.sum(k_gain_part, axis=0, keepdims=True),
        ],
        axis=1,
    )
    token, (kept, w_3, up_1b, gain_sum) = meet(token, (kept, w_3, up_1b, gain_sum))
    *fars, q_1, w_3, gain_x = trade(token, far_sums(kept) + [(q_1, "zb"), (w_3, "x"), (gain_sum, "core")])
    qw_2 = contract_rows(columns_of(normed, 2), low).astype(BF16)
    w_1 = contract_rows(columns_of(normed, 1), kv_low)
    token, (fars, kept, w_3, qw_2, w_1, o_1, q_1, gain_x, gate_give, down_give, up_2) = meet(
        token, (fars, kept, w_3, qw_2, w_1, o_1, q_1, gain_x, gate_give, down_give, up_2)
    )
    gain_sum = gain_sum + gain_x
    w_1 = (w_1 + w_3.astype(F32)).astype(BF16)
    *nears, w_1, qw_2, gain_x = trade(
        token, near_sums(kept, fars) + [(w_1, "zb"), (qw_2, "x"), (gain_sum, "y")]
    )
    o_2 = contract_rows(attn_low, columns_of(branch_rows, 2)).astype(BF16)
    up_0 = contract_rows(columns_of(mlp_rows, 0), up_low)
    up_part = up_0 + up_2.astype(F32) + jnp.concatenate([up_1a, up_1b], axis=0).astype(F32)
    up_mine, up_give = za_parts(up_part, 0)
    token, (nears, kept, up_mine, up_give, o_2, w_1, gain_x) = meet(
        token, (nears, kept, up_mine, up_give, o_2, w_1, gain_x)
    )
    gain_sum = gain_sum + gain_x
    o_1, o_2, up_give, gain_x = trade(token, [(o_1, "zb"), (o_2, "x"), (up_give, "za"), (gain_sum, "x")])
    input_grad = own_sum(kept, nears)
    unit_one = local_rows * (rho_one := lax.rsqrt(jnp.mean(local_rows * local_rows, axis=-1, keepdims=True) + EPSILON))
    scaled = input_grad * gain_one
    inner = jnp.mean(scaled * unit_one, axis=-1, keepdims=True)
    in_grad = residual_grad + rho_one * (scaled - unit_one * inner)
    block_out, in_grad = reorder(from_order, [block_out, in_grad], [BF16, F32])
    qw_0 = contract_rows(columns_of(normed, 0), low) + qw_2.astype(F32)
    qkv_mine, qkv_give = za_parts(qw_0 + jnp.concatenate([q_1, w_1], axis=1).astype(F32), 0)
    token, (qkv_mine, qkv_give, gain_x) = meet(token, (qkv_mine, qkv_give, gain_x))
    gain_sum = gain_sum + gain_x
    qkv_give, gain_x = trade(token, [(qkv_give, "za"), (gain_sum, "zb")])
    o_part = contract_rows(attn_low, columns_of(branch_rows, 0)) + o_2.astype(F32)
    token, (o_1, gain_x, o_part, up_give) = meet(token, (o_1, gain_x, o_part, up_give))
    gain_sum = gain_sum + gain_x
    o_mine, o_give = za_parts(o_part + o_1.astype(F32), 1)
    o_give, gain_x = trade(token, [(o_give, "za"), (gain_sum, "za")])
    gain_sum = gain_sum + gain_x
    device = (((y_at * 2 + core_at) * 2 + zb_at) * 2 + za_at) * 2 + x_at

    def own_slice(first, length):
        share = length // 32
        return lax.dynamic_slice_in_dim(gain_sum[0], first + device * share, share, axis=0)

    qkv_parts = za_join(qkv_mine, qkv_give)

    def columns(lo, hi):
        return jnp.concatenate([part[:, lo:hi] for part in qkv_parts], axis=1)

    return (
        block_out,
        in_grad,
        own_slice(0, width),
        columns(0, q_width),
        columns(q_width, q_width + k_width),
        columns(q_width + k_width, qkv_width),
        own_slice(2 * width, HEAD_SIZE),
        own_slice(2 * width + HEAD_SIZE, HEAD_SIZE),
        jnp.concatenate(za_join(o_mine, o_give), axis=0),
        own_slice(width, width),
        jnp.concatenate(za_join(gate_mine, gate_give), axis=1),
        jnp.concatenate(za_join(up_mine, up_give), axis=1),
        jnp.concatenate(za_join(down_mine, down_give), axis=0),
    )


def layer(
    sizes,
    tokens,
    out_grad,
    seq_lengths,
    block_deal,
    norm_gain,
    q_weight,
    k_weight,
    v_weight,
    q_gain,
    k_gain,
    o_weight,
    mlp_gain,
    gate_weight,
    up_weight,
    down_weight,
):
    y_count, core_count, zb_count, za_count, x_count = sizes
    pairwise = sizes == (2, 2, 2, 2, 2)
    all_axes = ("y", "core", "zb", "za", "x")
    y_at, core_at, zb_at, za_at, x_at = (lax.axis_index(name) for name in all_axes)
    tok_dev, width = tokens.shape
    blk_rows = q_weight.shape[0]
    group_count = zb_count * x_count
    member_count = y_count * core_count * za_count
    head_count = y_count * core_count
    rows = member_count * tok_dev
    piece = za_count * blk_rows


    def gather_rows(value):
        if not pairwise:
            return lax.all_gather(value, ("y", "core", "za"), axis=0, tiled=True)
        half = tok_dev // 2
        along_y = swap(value, "y")
        along_z = swap(value, "za")
        parts = [value, along_y, along_z, swap(along_z[:half], "y"), swap(along_y[half:], "za")]
        mine = jnp.concatenate(parts, axis=0)
        return jnp.concatenate([mine, swap(mine, "core")], axis=0)

    def scatter_rows(part_of):
        if not pairwise:
            full = part_of(slice(0, rows)).astype(BF16)
            return lax.psum_scatter(full, ("y", "core", "za"), scatter_dimension=0, tiled=True).astype(F32)
        middle = rows // 2
        half = tok_dev // 2
        given = swap(part_of(slice(middle, rows)).astype(BF16), "core")
        kept = part_of(slice(0, middle)) + given.astype(F32)
        own, to_y, to_z, far = (kept[i * tok_dev : (i + 1) * tok_dev] for i in range(4))
        far = far.astype(BF16)
        from_y = swap(far[:half], "y").astype(F32)
        from_z = swap(far[half:], "za").astype(F32)
        z_sum = jnp.concatenate([to_z[:half] + from_y, to_z[half:]], axis=0).astype(BF16)
        y_sum = jnp.concatenate([to_y[:half], to_y[half:] + from_z], axis=0).astype(BF16)
        return own + swap(y_sum, "y").astype(F32) + swap(z_sum, "za").astype(F32)


    def gather_pieces(own, axis):
        if not pairwise:
            return lax.all_gather(own, ("zb", "x"), axis=axis, tiled=True)
        along_z = swap(own, "zb")
        return jnp.concatenate([own, along_z, swap(own, "x"), swap(along_z, "x")], axis=axis)

    def scatter_pieces(part_of, length, axis):
        if not pairwise:
            full = part_of(0, length).astype(BF16)
            return lax.psum_scatter(full, ("zb", "x"), scatter_dimension=axis, tiled=True).astype(F32)
        half, quarter = length // 2, length // 4
        given = swap(part_of(half, length).astype(BF16), "x")
        kept = part_of(0, half) + given.astype(F32)
        given = swap(lax.slice_in_dim(kept, quarter, half, axis=axis).astype(BF16), "zb")
        return lax.slice_in_dim(kept, 0, quarter, axis=axis) + given.astype(F32)

    def in_order(mine, other, axis):
        first = jnp.where(za_at == 0, mine, other)
        second = jnp.where(za_at == 0, other, mine)
        return jnp.concatenate([first, second], axis=axis)

    def gather_weight(part_of, axis):
        mine = part_of(za_at)
        if za_count > 1:
            mine = in_order(mine, swap(part_of(1 - za_at), "za"), axis)
        return gather_pieces(mine, axis)

    def scatter_weight(part_of, axis):
        part = scatter_pieces(part_of, width, axis)
        if za_count == 1:
            return [part]
        first = lax.slice_in_dim(part, 0, blk_rows, axis=axis)
        second = lax.slice_in_dim(part, blk_rows, 2 * blk_rows, axis=axis)
        mine = jnp.where(za_at == 0, first, second)
        other = swap(jnp.where(za_at == 0, second, first).astype(BF16), "za").astype(F32)
        return [jnp.where(za_at == 0, mine, other), jnp.where(za_at == 0, other, mine)]

    def half_of(weight, at, axis):
        size = weight.shape[axis] // za_count
        return lax.dynamic_slice_in_dim(weight, at * size, size, axis=axis)


    def piece_group(index):
        if pairwise:
            return zb_at ^ (index % 2), x_at ^ (index // 2)
        return index // x_count, index % x_count

    def to_pieces(value):
        blocks = []
        for index in range(group_count):
            zb_of, x_of = piece_group(index)
            for za_of in range(za_count):
                block = (zb_of * za_count + za_of) * x_count + x_of
                blocks.append(lax.dynamic_slice_in_dim(value, block * blk_rows, blk_rows, axis=1))
        return jnp.concatenate(blocks, axis=1) if pairwise else value

    def from_pieces(value):
        if not pairwise:
            return value
        blocks = []
        for block in range(group_count * za_count):
            zb_of, za_of, x_of = block // 4, block // 2 % 2, block % 2
            index = (x_at ^ x_of) * 2 + (zb_at ^ zb_of)
            blocks.append(lax.dynamic_slice_in_dim(value, (index * 2 + za_of) * blk_rows, blk_rows, axis=1))
        return jnp.concatenate(blocks, axis=1)


    per_span = head_count // 2
    member = jnp.arange(member_count, dtype=jnp.int32)
    if pairwise:
        member_y, member_za, member_core = y_at ^ (member % 2), za_at ^ (member // 2 % 2), core_at ^ (member // 4)
    else:
        member_za = member % za_count
        member_core = member // za_count % core_count
        member_y = member // (za_count * core_count)
    group = jnp.arange(group_count, dtype=jnp.int32)
    group_zb, group_x = piece_group(group)
    member_head = member_y * core_count + member_core
    span_table = jnp.arange(block_deal.shape[0], dtype=jnp.int32)

    def natural_tile(zb_of, x_of):
        blk = (zb_of * za_count + member_za) * x_count + x_of
        entry = 2 * blk + member_head // per_span
        span = jnp.sum(
            jnp.where(entry[..., None] == span_table, block_deal, 0), axis=-1, dtype=jnp.int32
        )
        return span * per_span + member_head % per_span

    query_tile = natural_tile(zb_at, x_at)
    key_tile = natural_tile(group_zb[:, None], group_x[:, None]).reshape(-1)
    tile_ids = jnp.arange(key_tile.shape[0], dtype=jnp.int32)
    offsets = jnp.sum(
        jnp.where(key_tile[None, :] == tile_ids[:, None], tile_ids[None, :] * tok_dev, 0), axis=1, dtype=jnp.int32
    )
    natural = query_tile[:, None] * tok_dev + jnp.arange(tok_dev, dtype=jnp.int32)[None, :]
    seq_ids = jnp.arange(seq_lengths.shape[0], dtype=jnp.int32)
    seq_ends = jnp.sum(jnp.where(seq_ids[None, :] <= seq_ids[:, None], seq_lengths[None, :], 0), axis=1, dtype=jnp.int32)
    starts = jnp.max(jnp.where(seq_ends <= natural[..., None], seq_ends, 0), axis=-1)
    tiles = (query_tile, starts[:, 0] // (2 * tok_dev))
    start_rows = jnp.stack([starts, starts], axis=1)
    start_cols = jnp.broadcast_to(starts.reshape(rows, 1), (rows, 128))
    places = (natural - starts).reshape(rows)
    half_width = HEAD_SIZE // 2
    frequency = jnp.power(ROPE_BASE, -jnp.arange(half_width, dtype=F32) * (2.0 / HEAD_SIZE))
    angles = places.astype(F32)[:, None] * frequency[None, :]
    cosine = jnp.cos(angles)
    sine = jnp.sin(angles)
    cosine = jnp.concatenate([cosine, cosine], axis=1)
    sine = jnp.concatenate([-sine, sine], axis=1)


    q_width = q_weight.shape[1] // za_count
    k_width = k_weight.shape[1] // za_count
    qkv_width = q_width + 2 * k_width
    gain_pad = 16

    gain_row = jnp.concatenate([norm_gain, mlp_gain])
    head_gains = jnp.concatenate([q_gain, k_gain])

    def gain_rows():
        top = jnp.pad(gain_row, (0, qkv_width - gain_row.shape[0]))[None]
        bottom = jnp.pad(head_gains, (0, qkv_width - head_gains.shape[0]))[None]
        return jnp.concatenate([top, bottom, jnp.zeros((gain_pad - 2, qkv_width), BF16)], axis=0)

    def qkv_part(at):
        return jnp.concatenate(
            [half_of(q_weight, at, 1), half_of(k_weight, at, 1), half_of(v_weight, at, 1), ], axis=1
        )

    padded = blk_rows + gain_pad
    own_gain_rows = gain_rows()
    qkv_all = gather_weight(lambda at: jnp.concatenate([qkv_part(at), own_gain_rows], axis=0), 0)
    qkv_all = qkv_all.reshape(group_count * za_count, padded, qkv_width)
    qkv_cols = qkv_all[:, :blk_rows].reshape(width, qkv_width)
    gains = qkv_all[:, blk_rows, : 2 * blk_rows].astype(F32)
    gain_one = gains[:, :blk_rows].reshape(1, width)
    gain_two = gains[:, blk_rows:].reshape(1, width)
    small = q_gain.shape[0]
    head_parts = qkv_all[:, blk_rows + 1, : 2 * small].astype(F32).reshape(group_count * za_count, 2, small)

    def head_gain(which):
        return from_small(head_parts[:, which])

    def from_small(parts):
        if not pairwise:
            return parts.reshape(1, -1)
        rows_of = []
        for block in range(8):
            zb_of, za_of, x_of = block // 4, block // 2 % 2, block % 2
            index = ((x_at ^ x_of) * 2 + (zb_at ^ zb_of)) * 2 + za_of
            rows_of.append(lax.dynamic_slice_in_dim(parts, index, 1, axis=0))
        return jnp.concatenate(rows_of, axis=1)

    qk_gains = jnp.concatenate([head_gain(0), head_gain(1)], axis=0)


    local_low = to_pieces(tokens)
    local_rows = local_low.astype(F32)
    input_rows = gather_rows(local_low).astype(F32)
    o_cols = gather_weight(lambda at: half_of(o_weight, at, 0), 1)
    gu_cols = gather_weight(
        lambda at: jnp.concatenate([half_of(gate_weight, at, 1), half_of(up_weight, at, 1)], axis=1), 0
    )
    down_cols = gather_weight(lambda at: half_of(down_weight, at, 0), 1)
    grad_local = to_pieces(out_grad)
    grad_rows = gather_rows(grad_local)

    def unit_rows(value):
        return value * lax.rsqrt(jnp.mean(value * value, axis=-1, keepdims=True) + EPSILON)

    input_unit = unit_rows(input_rows)
    normed = (input_unit * gain_one).astype(BF16)
    raw = matmul(normed, qkv_cols)
    queries, kv_own = shape_heads(raw, cosine, sine, qk_gains)
    key_values = gather_pieces(kv_own, 0)
    attn_low, inverse = attend(offsets, tiles, queries, start_cols, [key_values])
    residual = local_rows + scatter_rows(lambda at: matmul(attn_low[at], o_cols))


    rho_two = lax.rsqrt(jnp.mean(residual * residual, axis=-1, keepdims=True) + EPSILON)
    unit_two = residual * rho_two
    mlp_rows = gather_rows((unit_two * gain_two).astype(BF16))
    ff = gu_cols.shape[1] // 2
    gate_up = matmul(mlp_rows, gu_cols)
    gate_act, up_act = gate_up[:, :ff], gate_up[:, ff:]
    sig = jax.nn.sigmoid(gate_act)
    silu = gate_act * sig
    hidden = (silu * up_act).astype(BF16)
    hidden_grad = contract_cols(grad_rows, down_cols)
    gate_low = (hidden_grad * up_act * (sig * (1.0 + gate_act * (1.0 - sig)))).astype(BF16)
    up_low = (hidden_grad * silu).astype(BF16)
    gu_low = jnp.concatenate([gate_low, up_low], axis=1)
    mlp_in_grad = scatter_rows(lambda at: contract_cols(gu_low[at], gu_cols))

    down_parts = scatter_weight(lambda lo, hi: contract_rows(hidden, grad_rows[:, lo:hi]), 1)
    gate_parts = scatter_weight(lambda lo, hi: contract_rows(mlp_rows[:, lo:hi], gate_low), 0)
    up_parts = scatter_weight(lambda lo, hi: contract_rows(mlp_rows[:, lo:hi], up_low), 0)
    block_out = residual + scatter_rows(lambda at: matmul(hidden[at], down_cols))

    gain_two_part = jnp.sum(mlp_in_grad * unit_two, axis=0, keepdims=True)
    scaled = mlp_in_grad * gain_two
    inner = jnp.mean(scaled * unit_two, axis=-1, keepdims=True)
    residual_grad = grad_local.astype(F32) + rho_two * (scaled - unit_two * inner)


    branch_rows = gather_rows(residual_grad.astype(BF16))
    attn_grad = contract_cols(branch_rows, o_cols).astype(BF16)
    query_grad, kv_grads = attend_back(
        offsets, tiles, queries, start_rows, inverse, attn_low, attn_grad, [key_values]
    )
    o_parts = scatter_weight(lambda lo, hi: contract_rows(attn_low, branch_rows[:, lo:hi]), 1)
    kv_grad = scatter_pieces(lambda lo, hi: kv_grads[lo:hi].astype(F32), kv_grads.shape[0], 0).astype(BF16)
    q_low, q_gain_part = shape_back(raw, query_grad, cosine, sine, qk_gains, 2, 0, 0, HEAD_SIZE**-0.5)
    kv_low, k_gain_part = shape_back(raw, kv_grad, cosine, sine, qk_gains, 1, 2, 1, 1.0)
    low = jnp.concatenate([q_low, kv_low], axis=1)

    gain_one_parts = []

    def input_terms(at):
        terms = contract_cols(low[at], qkv_cols)
        gain_one_parts.append(jnp.sum(terms * input_unit[at], axis=0, keepdims=True))
        return terms

    input_grad = scatter_rows(input_terms)
    qkv_parts = scatter_weight(lambda lo, hi: contract_rows(normed[:, lo:hi], low), 0)

    gain_sum = jnp.concatenate(
        [
            from_pieces(sum(gain_one_parts)),
            from_pieces(gain_two_part),
            jnp.sum(q_gain_part, axis=0, keepdims=True),
            jnp.sum(k_gain_part, axis=0, keepdims=True),
        ],
        axis=1,
    )
    if pairwise:
        for name in ("core", "y", "za", "x", "zb"):
            gain_sum = gain_sum + swap(gain_sum, name)
    else:
        gain_sum = lax.psum(gain_sum, all_axes)

    unit_one = local_rows * (rho_one := lax.rsqrt(jnp.mean(local_rows * local_rows, axis=-1, keepdims=True) + EPSILON))
    scaled = input_grad * gain_one
    inner = jnp.mean(scaled * unit_one, axis=-1, keepdims=True)
    in_grad = residual_grad + rho_one * (scaled - unit_one * inner)

    device = (((y_at * core_count + core_at) * zb_count + zb_at) * za_count + za_at) * x_count + x_at
    device_count = head_count * zb_count * za_count * x_count

    def own_slice(first, length):
        share = length // device_count
        return lax.dynamic_slice_in_dim(gain_sum[0], first + device * share, share, axis=0)

    def join(parts, lo, hi, axis):
        cut = [lax.slice_in_dim(part, lo, hi, axis=axis) for part in parts]
        return jnp.concatenate(cut, axis=axis)

    return (
        from_pieces(block_out).astype(BF16),
        from_pieces(in_grad),
        own_slice(0, width),
        join(qkv_parts, 0, q_width, 1),
        join(qkv_parts, q_width, q_width + k_width, 1),
        join(qkv_parts, q_width + k_width, qkv_width, 1),
        own_slice(2 * width, HEAD_SIZE),
        own_slice(2 * width + HEAD_SIZE, HEAD_SIZE),
        jnp.concatenate(o_parts, axis=0),
        own_slice(width, width),
        jnp.concatenate(gate_parts, axis=1),
        jnp.concatenate(up_parts, axis=1),
        jnp.concatenate(down_parts, axis=0),
    )


def solution(mesh):
    heads, blks = mesh.shape["head"], mesh.shape["blk"]
    za_count = KEY_VALUE_HEADS // heads
    side = math.isqrt(blks // za_count)
    sizes = (heads // 2, 2, side, za_count, side)
    names = ("y", "core", "zb", "za", "x")
    devices = mesh.devices.reshape(sizes)
    inner = Mesh(devices, names)
    head, blk = ("y", "core"), ("zb", "za", "x")
    rows, in_weight, out_weight, gain = P(names, None), P(blk, head), P(head, blk), P(blk)
    return jax.shard_map(
        paired_layer if sizes == (2, 2, 2, 2, 2) else functools.partial(layer, sizes),
        mesh=inner,
        in_specs=(
            rows,
            rows,
            P(),
            P(),
            gain,
            in_weight,
            in_weight,
            in_weight,
            gain,
            gain,
            out_weight,
            gain,
            in_weight,
            in_weight,
            out_weight,
        ),
        out_specs=(
            rows,
            rows,
            P(names),
            in_weight,
            in_weight,
            in_weight,
            P(names),
            P(names),
            out_weight,
            P(names),
            in_weight,
            in_weight,
            out_weight,
        ),
        check_vma=False,
    )
```

```python
import functools
import math

import jax
import jax.numpy as jnp
from jax import lax
from jax.experimental import pallas as pl
from jax.experimental.pallas import tpu as pltpu
from jax.sharding import Mesh
from jax.sharding import PartitionSpec as P

HEAD_SIZE = 128
KEY_VALUE_HEADS = 8
EPSILON = 1e-06
ROPE_BASE = 1000000.0
F32 = jnp.float32
BF16 = jnp.bfloat16
SWAP = [(0, 1), (1, 0)]
PAIRS_OF_ROWS = (((0,), (0,)), ((), ()))
PAIRS_OF_COLS = (((1,), (1,)), ((), ()))
VMEM = pltpu.MemorySpace.VMEM
LIGHT = pl.CostEstimate(flops=1000, bytes_accessed=1000, transcendentals=0)
SMEM = pltpu.MemorySpace.SMEM


def matmul(left, right):
    return jnp.dot(left, right, preferred_element_type=F32)


def contract_rows(left, right):
    return lax.dot_general(left, right, PAIRS_OF_ROWS, preferred_element_type=F32)


def contract_cols(left, right):
    return lax.dot_general(left, right, PAIRS_OF_COLS, preferred_element_type=F32)


def swap(value, axis):
    return lax.ppermute(value, axis, SWAP)


def attend_kernel(off_ref, tile_ref, low_ref, q_ref, start_ref, *refs, parts, first, last):
    half = 128
    kv_refs, refs = refs[:parts], refs[parts:]
    if not first:
        before_ref, refs = refs[0], refs[1:]
    if last:
        out_ref, inv_ref, kv_ref, acc_ref = refs
    else:
        after_ref, kv_ref, acc_ref = refs
    share = kv_refs[0].shape[0]
    for part, ref in enumerate(kv_refs):
        kv_ref[part * share : (part + 1) * share, :] = ref[...]
    lane = lax.broadcasted_iota(jnp.int32, (256, 256), 1)
    row = lax.broadcasted_iota(jnp.int32, (256, 256), 0) % half
    ones = jnp.ones((256, HEAD_SIZE), BF16)

    def tile(index, unused):
        rows = pl.ds(pl.multiple_of(index * half, half), half)
        queries = jnp.concatenate([q_ref[rows, :HEAD_SIZE], q_ref[rows, HEAD_SIZE:]], axis=0)
        start = start_ref[rows, :]
        start = jnp.concatenate([start, start], axis=1)
        start = jnp.concatenate([start, start], axis=0)
        places = tile_ref[index] * half + row
        acc_ref[...] = jnp.zeros_like(acc_ref) if first else before_ref[index]

        def step(block, unused_step):
            at = off_ref[2 * block]

            @pl.when(at >= 0)
            def _():
                low = pl.ds(pl.multiple_of(at, half), half)
                high = pl.ds(pl.multiple_of(off_ref[2 * block + 1], half), half)
                keys = jnp.concatenate([kv_ref[low, :HEAD_SIZE], kv_ref[high, :HEAD_SIZE]], axis=0)
                values = jnp.concatenate([kv_ref[low, HEAD_SIZE:], kv_ref[high, HEAD_SIZE:]], axis=0)
                scores = contract_cols(queries, keys)
                natural = block * 256 + lane
                allowed = (natural <= places) & (natural >= start)
                weights = jnp.where(allowed, jnp.exp(scores), 0.0).astype(BF16)
                acc_ref[...] += matmul(weights, jnp.concatenate([values, ones], axis=1))

            return unused_step

        lax.fori_loop(low_ref[index], tile_ref[index] // 2 + 1, step, 0)
        if last:
            inverse = 1.0 / acc_ref[:, HEAD_SIZE:]
            attended = (acc_ref[:, :HEAD_SIZE] * inverse).astype(BF16)
            out_ref[rows, :HEAD_SIZE] = attended[:half]
            out_ref[rows, HEAD_SIZE:] = attended[half:]
            inv_ref[index, 0:1, :] = jnp.transpose(inverse[:half])[0:1, :]
            inv_ref[index, 1:2, :] = jnp.transpose(inverse[half:])[0:1, :]
        else:
            after_ref[index] = acc_ref[...]
        return unused

    lax.fori_loop(0, q_ref.shape[0] // half, tile, 0)


def attend_back_kernel(
    off_ref, tile_ref, low_ref, q_ref, start_ref, inv_ref, out_ref, grad_ref, *refs, parts, first, last
):
    half = 128
    kv_refs, refs = refs[:parts], refs[parts:]
    if not first:
        before_ref, refs = refs[0], refs[1:]
    dq_ref, *dkv_refs = refs[: 1 + parts]
    kv_ref, dk_ref, dv_ref, acc_ref = refs[1 + parts :]
    share = kv_refs[0].shape[0]
    for part, ref in enumerate(kv_refs):
        kv_ref[part * share : (part + 1) * share, :] = ref[...]
    key_row = lax.broadcasted_iota(jnp.int32, (256, 256), 0)
    query_lane = lax.broadcasted_iota(jnp.int32, (1, 256), 1) % half

    def clear(index, unused):
        rows = pl.ds(pl.multiple_of(index * 256, 256), 256)
        dk_ref[rows, :] = jnp.zeros((256, HEAD_SIZE), F32)
        dv_ref[rows, :] = jnp.zeros((256, HEAD_SIZE), F32)
        return unused

    lax.fori_loop(0, dk_ref.shape[0] // 256, clear, 0)

    def tile(index, unused):
        rows = pl.ds(pl.multiple_of(index * half, half), half)

        def both(ref):
            return jnp.concatenate([ref[rows, :HEAD_SIZE], ref[rows, HEAD_SIZE:]], axis=0)

        def along(ref):
            return jnp.concatenate([ref[index, 0:1, :], ref[index, 1:2, :]], axis=1)

        queries = both(q_ref)
        grads = both(grad_ref)
        products = both(out_ref).astype(F32) * grads.astype(F32)
        deltas = jnp.sum(jnp.transpose(products), axis=0, keepdims=True)
        inverse = along(inv_ref)
        start = along(start_ref)
        places = tile_ref[index] * half + query_lane
        acc_ref[...] = jnp.zeros_like(acc_ref) if first else both(before_ref)

        def step(block, unused_step):
            at = off_ref[2 * block]

            @pl.when(at >= 0)
            def _():
                low = pl.ds(pl.multiple_of(at, half), half)
                high = pl.ds(pl.multiple_of(off_ref[2 * block + 1], half), half)
                keys = jnp.concatenate([kv_ref[low, :HEAD_SIZE], kv_ref[high, :HEAD_SIZE]], axis=0)
                values = jnp.concatenate([kv_ref[low, HEAD_SIZE:], kv_ref[high, HEAD_SIZE:]], axis=0)
                scores = contract_cols(keys, queries)
                natural = block * 256 + key_row
                allowed = (natural <= places) & (natural >= start)
                probs = jnp.where(allowed, jnp.exp(scores) * inverse, 0.0)
                prob_grad = contract_cols(values, grads)
                score_grad = (probs * (prob_grad - deltas)).astype(BF16)
                value_part = matmul(probs.astype(BF16), grads)
                key_part = matmul(score_grad, queries)
                dv_ref[low, :] += value_part[:half]
                dv_ref[high, :] += value_part[half:]
                dk_ref[low, :] += key_part[:half]
                dk_ref[high, :] += key_part[half:]
                acc_ref[...] += contract_rows(score_grad, keys)

            return unused_step

        lax.fori_loop(low_ref[index], tile_ref[index] // 2 + 1, step, 0)
        dq_ref[rows, :HEAD_SIZE] = acc_ref[:half, :].astype(dq_ref.dtype)
        dq_ref[rows, HEAD_SIZE:] = acc_ref[half:, :].astype(dq_ref.dtype)
        return unused

    lax.fori_loop(0, q_ref.shape[0] // half, tile, 0)

    for part, ref in enumerate(dkv_refs):

        def store(index, unused):
            target = pl.ds(pl.multiple_of(index * 256, 256), 256)
            source = pl.ds(pl.multiple_of(part * share + index * 256, 256), 256)
            ref[target, :HEAD_SIZE] = dk_ref[source, :].astype(BF16)
            ref[target, HEAD_SIZE:] = dv_ref[source, :].astype(BF16)
            return unused

        lax.fori_loop(0, share // 256, store, 0)


def attend(offsets, tiles, queries, start_cols, kv_parts, before=None, last=True):
    rows, width = queries.shape
    parts, share = len(kv_parts), kv_parts[0].shape[0]
    keys = parts * share
    first = before is None
    extra = () if first else (before,)
    whole = (
        (jax.ShapeDtypeStruct((rows, width), BF16), jax.ShapeDtypeStruct((rows // 128, 2, 128), F32))
        if last
        else (jax.ShapeDtypeStruct((rows // 128, 256, 256), F32),)
    )
    return pl.pallas_call(
        functools.partial(attend_kernel, parts=parts, first=first, last=last),
        name="attend",
        out_shape=whole,
        in_specs=[pl.BlockSpec(memory_space=SMEM)] * 3 + [pl.BlockSpec(memory_space=VMEM)] * (2 + parts + len(extra)),
        out_specs=[pl.BlockSpec(memory_space=VMEM)] * len(whole),
        scratch_shapes=[pltpu.VMEM((keys, width), BF16), pltpu.VMEM((256, 256), F32)],
        compiler_params=pltpu.CompilerParams(vmem_limit_bytes=12 * 2**20 + keys * 1536),
        cost_estimate=LIGHT,
    )(offsets, *tiles, queries, start_cols, *kv_parts, *extra)


def attend_back(offsets, tiles, queries, start_rows, inverse, attended, grads, kv_parts, before=None, last=True):
    rows, width = queries.shape
    parts, share = len(kv_parts), kv_parts[0].shape[0]
    keys = parts * share
    first = before is None
    extra = () if first else (before,)
    return pl.pallas_call(
        functools.partial(attend_back_kernel, parts=parts, first=first, last=last),
        name="attend_back",
        out_shape=(jax.ShapeDtypeStruct((rows, width), BF16 if last else F32),)
        + tuple(jax.ShapeDtypeStruct((share, width), BF16) for unused in kv_parts),
        in_specs=[pl.BlockSpec(memory_space=SMEM)] * 3 + [pl.BlockSpec(memory_space=VMEM)] * (5 + parts + len(extra)),
        out_specs=[pl.BlockSpec(memory_space=VMEM)] * (1 + parts),
        scratch_shapes=[
            pltpu.VMEM((keys, width), BF16),
            pltpu.VMEM((keys, HEAD_SIZE), F32),
            pltpu.VMEM((keys, HEAD_SIZE), F32),
            pltpu.VMEM((256, HEAD_SIZE), F32),
        ],
        compiler_params=pltpu.CompilerParams(vmem_limit_bytes=12 * 2**20 + keys * 2816),
        cost_estimate=LIGHT,
    )(offsets, *tiles, queries, start_rows, inverse, attended, grads, *kv_parts, *extra)


def shape_kernel(raw_ref, cos_ref, sin_ref, gain_ref, q_ref, kv_ref):
    cosine = cos_ref[...]
    sine = sin_ref[...]

    def shaped(first, gain):
        value = raw_ref[:, first : first + HEAD_SIZE]
        mean_square = jnp.mean(value * value, axis=-1, keepdims=True)
        value = value * lax.rsqrt(mean_square + EPSILON) * gain
        return value * cosine + pltpu.roll(value, HEAD_SIZE // 2, 1) * sine

    for head in range(2):
        columns = slice(head * HEAD_SIZE, (head + 1) * HEAD_SIZE)
        q_ref[:, columns] = (shaped(head * HEAD_SIZE, gain_ref[0:1, :]) * HEAD_SIZE**-0.5).astype(BF16)
    kv_ref[:, :HEAD_SIZE] = shaped(2 * HEAD_SIZE, gain_ref[1:2, :]).astype(BF16)
    kv_ref[:, HEAD_SIZE:] = raw_ref[:, 3 * HEAD_SIZE :].astype(BF16)


def shape_back_kernel(raw_ref, grad_ref, cos_ref, sin_ref, gain_ref, low_ref, gain_grad_ref, *, heads, gain_row, factor):
    @pl.when(pl.program_id(0) == 0)
    def _():
        gain_grad_ref[...] = jnp.zeros_like(gain_grad_ref)

    cosine = cos_ref[...]
    sine = sin_ref[...]
    gain = gain_ref[gain_row : gain_row + 1, :]
    total = jnp.zeros((8, HEAD_SIZE), F32)
    for head in range(heads):
        columns = slice(head * HEAD_SIZE, (head + 1) * HEAD_SIZE)
        value = raw_ref[:, columns]
        grad = grad_ref[:, columns].astype(F32) * factor
        grad = grad * cosine - pltpu.roll(grad, HEAD_SIZE // 2, 1) * sine
        rho = lax.rsqrt(jnp.mean(value * value, axis=-1, keepdims=True) + EPSILON)
        unit = value * rho
        total = total + jnp.sum((grad * unit).reshape(-1, 8, HEAD_SIZE), axis=0)
        scaled = grad * gain
        inner = jnp.mean(scaled * unit, axis=-1, keepdims=True)
        low_ref[:, columns] = (rho * (scaled - unit * inner)).astype(BF16)
    if heads == 1:
        low_ref[:, HEAD_SIZE:] = grad_ref[:, HEAD_SIZE:].astype(BF16)
    gain_grad_ref[...] += total


ROW_TILE = 256


def shape_heads(raw, cosine, sine, gains):
    rows = raw.shape[0]
    block = lambda width: pl.BlockSpec((ROW_TILE, width), lambda i: (i, 0))
    return pl.pallas_call(
        shape_kernel,
        name="shape_heads",
        grid=(rows // ROW_TILE,),
        out_shape=(jax.ShapeDtypeStruct((rows, 256), BF16), jax.ShapeDtypeStruct((rows, 256), BF16)),
        in_specs=[block(512), block(128), block(128), pl.BlockSpec((2, 128), lambda i: (0, 0))],
        out_specs=[block(256), block(256)],
        compiler_params=pltpu.CompilerParams(vmem_limit_bytes=8 * 2**20),
        cost_estimate=LIGHT,
    )(raw, cosine, sine, gains)


def shape_back(raw, grads, cosine, sine, gains, heads, column, gain_row, factor):
    rows = raw.shape[0]
    block = lambda width, at=0: pl.BlockSpec((ROW_TILE, width), lambda i: (i, at))
    return pl.pallas_call(
        functools.partial(shape_back_kernel, heads=heads, gain_row=gain_row, factor=factor),
        name="shape_back",
        grid=(rows // ROW_TILE,),
        out_shape=(jax.ShapeDtypeStruct((rows, 256), BF16), jax.ShapeDtypeStruct((8, 128), F32)),
        in_specs=[
            block(heads * 128, column),
            block(256),
            block(128),
            block(128),
            pl.BlockSpec((2, 128), lambda i: (0, 0)),
        ],
        out_specs=[block(256), pl.BlockSpec((8, 128), lambda i: (0, 0))],
        compiler_params=pltpu.CompilerParams(vmem_limit_bytes=8 * 2**20),
        cost_estimate=LIGHT,
    )(raw, grads, cosine, sine, gains)


def reorder_kernel(order_ref, *refs):
    half = len(refs) // 2
    for source, target in zip(refs[:half], refs[half:]):
        target[...] = source[...].astype(target.dtype)


def reorder(order, values, types):
    rows, width = values[0].shape
    blocks = order.shape[0]
    size = width // blocks
    taken = pl.BlockSpec((rows, size), lambda i, order_ref: (0, order_ref[i]))
    put = pl.BlockSpec((rows, size), lambda i, order_ref: (0, i))
    return pl.pallas_call(
        reorder_kernel,
        name="reorder",
        grid_spec=pltpu.PrefetchScalarGridSpec(
            num_scalar_prefetch=1,
            grid=(blocks,),
            in_specs=[taken] * len(values),
            out_specs=[put] * len(values),
        ),
        out_shape=[jax.ShapeDtypeStruct(value.shape, kind) for value, kind in zip(values, types)],
        compiler_params=pltpu.CompilerParams(vmem_limit_bytes=8 * 2**20),
        cost_estimate=LIGHT,
    )(order, *values)


def assemble_kernel(at_ref, *refs, entries, axis):
    out_ref = refs[-1]
    for source, (place, kind) in zip(refs[:-1], entries):
        size = source.shape[axis]
        if kind == 0:
            span = slice(place, place + size)
        else:
            at = at_ref[0] if kind > 0 else 1 - at_ref[0]
            span = pl.ds(pl.multiple_of(place + at * 256, 16 if axis == 0 else 128), size)
        if axis == 0:
            out_ref[span, :] = source[...]
        else:
            out_ref[:, span] = source[...]


def assemble(at, parts, axis):
    values = [value for value, unused, kind in parts]
    total = sum(value.shape[axis] for value in values)
    other = values[0].shape[1 - axis]
    shape = (total, other) if axis == 0 else (other, total)
    return pl.pallas_call(
        functools.partial(assemble_kernel, entries=tuple((place, kind) for unused, place, kind in parts), axis=axis),
        name="assemble",
        out_shape=jax.ShapeDtypeStruct(shape, BF16),
        in_specs=[pl.BlockSpec(memory_space=SMEM)] + [pl.BlockSpec(memory_space=VMEM)] * len(values),
        out_specs=pl.BlockSpec(memory_space=VMEM),
        compiler_params=pltpu.CompilerParams(vmem_limit_bytes=12 * 2**20),
        cost_estimate=LIGHT,
    )(at, *values)


def terms_kernel(left_ref, right_ref, left_cols_ref, right_cols_ref, kept_ref, given_ref):
    total = contract_cols(left_ref[...], left_cols_ref[...]) + contract_cols(right_ref[...], right_cols_ref[...])
    middle = kept_ref.shape[0]
    kept_ref[...] = total[:middle]
    given_ref[...] = total[middle:].astype(BF16)


def two_terms(left, right, left_cols, right_cols):
    rows, depth = left.shape
    width = left_cols.shape[0]
    tile = 512
    value = pl.BlockSpec((rows, depth), lambda i: (0, 0))
    cols = pl.BlockSpec((tile, depth), lambda i: (i, 0))
    half = pl.BlockSpec((rows // 2, tile), lambda i: (0, i))
    return pl.pallas_call(
        terms_kernel,
        name="two_terms",
        grid=(width // tile,),
        out_shape=(jax.ShapeDtypeStruct((rows // 2, width), F32), jax.ShapeDtypeStruct((rows // 2, width), BF16)),
        in_specs=[value, value, cols, cols],
        out_specs=(half, half),
        cost_estimate=LIGHT,
    )(left, right, left_cols, right_cols)


def hidden_kernel(mine_ref, theirs_ref, gate_ref, up_ref, hidden_ref, gate_slope_ref, up_slope_ref):
    middle = mine_ref.shape[0]
    for part, source in ((slice(0, middle), mine_ref), (slice(middle, 2 * middle), theirs_ref)):
        rows = source[...]
        gate = matmul(rows, gate_ref[...])
        up = matmul(rows, up_ref[...])
        sig = 1.0 / (1.0 + jnp.exp(-gate))
        silu = gate * sig
        hidden_ref[part, :] = (silu * up).astype(BF16)
        gate_slope_ref[part, :] = (up * (sig * (1.0 + gate * (1.0 - sig)))).astype(BF16)
        up_slope_ref[part, :] = silu.astype(BF16)


def hidden_units(mine, theirs, gate_cols, up_cols):
    middle, width = mine.shape
    units = gate_cols.shape[1]
    tile = 256
    whole = pl.BlockSpec((middle, width), lambda i: (0, 0))
    cols = pl.BlockSpec((width, tile), lambda i: (0, i))
    out = pl.BlockSpec((2 * middle, tile), lambda i: (0, i))
    return pl.pallas_call(
        hidden_kernel,
        name="hidden_units",
        grid=(units // tile,),
        out_shape=(jax.ShapeDtypeStruct((2 * middle, units), BF16),) * 3,
        in_specs=[whole, whole, cols, cols],
        out_specs=(out,) * 3,
        cost_estimate=LIGHT,
    )(mine, theirs, gate_cols, up_cols)


def prologue_kernel(
    order_ref, at_ref, tokens_ref, grad_ref, q_ref, k_ref, v_ref, norm_ref, mlp_ref, q_gain_ref, k_gain_ref,
    tokens_out, grad_out, keep_ref, give_ref
):
    size = tokens_ref.shape[1] // 8
    for block in range(8):
        source = pl.ds(pl.multiple_of(order_ref[block] * size, 128), size)
        tokens_out[:, block * size : (block + 1) * size] = tokens_ref[:, source]
        grad_out[:, block * size : (block + 1) * size] = grad_ref[:, source]

    rows, q_width = q_ref.shape[0], q_ref.shape[1] // 2
    k_width = k_ref.shape[1] // 2
    total = q_width + 2 * k_width
    small = q_gain_ref.shape[1]
    place = lax.broadcasted_iota(jnp.int32, (small, HEAD_SIZE), 1) - lax.broadcasted_iota(
        jnp.int32, (small, HEAD_SIZE), 0
    )
    put = (place == at_ref[1] * small).astype(BF16)
    extra = jnp.concatenate(
        [
            jnp.concatenate([norm_ref[...], mlp_ref[...]], axis=1),
            jnp.concatenate(
                [
                    matmul(q_gain_ref[...], put).astype(BF16),
                    matmul(k_gain_ref[...], put).astype(BF16),
                    jnp.zeros((1, total - 2 * HEAD_SIZE), BF16),
                ],
                axis=1,
            ),
            jnp.zeros((14, total), BF16),
        ],
        axis=0,
    )
    for target, at in ((keep_ref, at_ref[0]), (give_ref, 1 - at_ref[0])):
        target[:rows, :q_width] = q_ref[:, pl.ds(pl.multiple_of(at * q_width, 128), q_width)]
        target[:rows, q_width : q_width + k_width] = k_ref[:, pl.ds(pl.multiple_of(at * k_width, 128), k_width)]
        target[:rows, q_width + k_width :] = v_ref[:, pl.ds(pl.multiple_of(at * k_width, 128), k_width)]
        target[rows:, :] = extra


def prologue(order, at, tokens, out_grad, q_weight, k_weight, v_weight, gains):
    shape = jax.ShapeDtypeStruct((q_weight.shape[0] + 16, (q_weight.shape[1] + 2 * k_weight.shape[1]) // 2), BF16)
    whole = lambda value: pl.BlockSpec(value.shape, lambda i, order_ref, at_ref: (0, 0))
    fixed = (q_weight, k_weight, v_weight) + gains
    return pl.pallas_call(
        prologue_kernel,
        name="prologue",
        grid_spec=pltpu.PrefetchScalarGridSpec(
            num_scalar_prefetch=2,
            grid=(1,),
            in_specs=[whole(tokens), whole(out_grad)] + [whole(value) for value in fixed],
            out_specs=[whole(tokens), whole(tokens), whole(shape), whole(shape)],
        ),
        out_shape=(jax.ShapeDtypeStruct(tokens.shape, BF16),) * 2 + (shape, shape),
        cost_estimate=LIGHT,
    )(order, at, tokens, out_grad, *fixed)


def after(token, values):
    return lax.optimization_barrier((token, values))[1]


def meet(token, values):
    return lax.optimization_barrier((token, values))


def trade(token, sends):
    held = after(token, [value for value, unused in sends])
    return [swap(value, axis) for value, (unused, axis) in zip(held, sends)]


def places_of(query_tile, key_tile, seq_lengths, tok_dev):
    rows = query_tile.shape[0] * tok_dev
    tile_ids = jnp.arange(key_tile.shape[0], dtype=jnp.int32)
    shares = (tile_ids // 16) * 8 + tile_ids % 8
    found = key_tile[None, :] == tile_ids[:, None]

    def offsets_of(parity):
        mine = found & (tile_ids // 8 % 2 == parity)[None, :]
        return jnp.sum(jnp.where(mine, shares * tok_dev + 1, 0), axis=1, dtype=jnp.int32) - 1

    offsets = (offsets_of(0), offsets_of(1))
    natural = query_tile[:, None] * tok_dev + jnp.arange(tok_dev, dtype=jnp.int32)[None, :]
    seq_ids = jnp.arange(seq_lengths.shape[0], dtype=jnp.int32)
    seq_ends = jnp.sum(jnp.where(seq_ids[None, :] <= seq_ids[:, None], seq_lengths[None, :], 0), axis=1, dtype=jnp.int32)
    starts = jnp.max(jnp.where(seq_ends <= natural[..., None], seq_ends, 0), axis=-1)
    tiles = (query_tile, jnp.max(jnp.where(seq_ends <= (query_tile * tok_dev)[:, None], seq_ends, 0), axis=-1) // (2 * tok_dev))
    start_rows = jnp.stack([starts, starts], axis=1)
    start_cols = jnp.broadcast_to(starts.reshape(rows, 1), (rows, 128))
    places = (natural - starts).reshape(rows)
    half_width = HEAD_SIZE // 2
    frequency = jnp.power(ROPE_BASE, -jnp.arange(half_width, dtype=F32) * (2.0 / HEAD_SIZE))
    angles = places.astype(F32)[:, None] * frequency[None, :]
    cosine = jnp.cos(angles)
    sine = jnp.sin(angles)
    cosine = jnp.concatenate([cosine, cosine], axis=1)
    sine = jnp.concatenate([-sine, sine], axis=1)
    return offsets, tiles, start_rows, start_cols, cosine, sine


FAR = 96
KEEP_ROWS = 128
UP_ROWS = 96


def paired_layer(
    tokens,
    out_grad,
    seq_lengths,
    block_deal,
    norm_gain,
    q_weight,
    k_weight,
    v_weight,
    q_gain,
    k_gain,
    o_weight,
    mlp_gain,
    gate_weight,
    up_weight,
    down_weight,
):
    y_at, core_at, zb_at, za_at, x_at = (lax.axis_index(name) for name in ("y", "core", "zb", "za", "x"))
    tok_dev, width = tokens.shape
    blk_rows = q_weight.shape[0]
    rows = 8 * tok_dev
    middle = rows // 2
    half, quarter = width // 2, width // 4
    token = seq_lengths


    place_ids = jnp.arange(8, dtype=jnp.int32)
    to_order = ((zb_at ^ (place_ids // 2 % 2)) * 2 + place_ids % 2) * 2 + (x_at ^ (place_ids // 4))
    from_order = ((x_at ^ (place_ids % 2)) * 2 + (zb_at ^ (place_ids // 4))) * 2 + place_ids // 2 % 2

    def in_order(mine, other, axis):
        first = jnp.where(za_at == 0, mine, other)
        second = jnp.where(za_at == 0, other, mine)
        return jnp.concatenate([first, second], axis=axis)

    def half_of(weight, at, axis):
        size = weight.shape[axis] // 2
        return lax.dynamic_slice_in_dim(weight, at * size, size, axis=axis)


    def near(value):
        return [(value, "y"), (value, "za")]

    def far(from_y, from_z, rows_y):
        sends = [(from_z[:rows_y], "y")]
        return sends + ([(from_y[rows_y:], "za")] if rows_y < tok_dev else [])

    def mine_of(value, from_y, from_z, fars):
        return jnp.concatenate([value, from_y, from_z] + fars, axis=0)

    def far_sums(kept):
        return [(kept[3 * tok_dev :].astype(BF16), "y")]

    def near_sums(kept, from_y):
        to_y, to_z = kept[tok_dev : 2 * tok_dev], kept[2 * tok_dev : 3 * tok_dev] + from_y.astype(F32)
        return [(to_y.astype(BF16), "y"), (to_z.astype(BF16), "za")]

    def own_sum(kept, nears):
        return kept[:tok_dev] + nears[0].astype(F32) + nears[1].astype(F32)


    def za_parts(part, axis):
        first = lax.slice_in_dim(part, 0, blk_rows, axis=axis)
        second = lax.slice_in_dim(part, blk_rows, 2 * blk_rows, axis=axis)
        return jnp.where(za_at == 0, first, second), jnp.where(za_at == 0, second, first).astype(BF16)

    def za_join(mine, other):
        other = other.astype(F32)
        return [jnp.where(za_at == 0, mine, other), jnp.where(za_at == 0, other, mine)]


    member = jnp.arange(8, dtype=jnp.int32)
    member_y, member_za, member_core = y_at ^ (member % 2), za_at ^ (member // 2 % 2), core_at ^ (member // 4)
    group = jnp.arange(4, dtype=jnp.int32)
    span_table = jnp.arange(block_deal.shape[0], dtype=jnp.int32)

    def natural_tile(zb_of, x_of):
        entry = 2 * ((zb_of * 2 + member_za) * 2 + x_of) + member_y
        span = jnp.sum(jnp.where(entry[..., None] == span_table, block_deal, 0), axis=-1, dtype=jnp.int32)
        return span * 2 + member_core

    query_tile = natural_tile(zb_at, x_at)
    key_tile = natural_tile(zb_at ^ (group % 2)[:, None], x_at ^ (group // 2)[:, None]).reshape(-1)
    offsets, tiles, start_rows, start_cols, cosine, sine = places_of(query_tile, key_tile, seq_lengths, tok_dev)


    q_width, k_width = q_weight.shape[1] // 2, k_weight.shape[1] // 2
    qkv_width = q_width + 2 * k_width
    local_low, grad_local, qkv_keep, qkv_give = prologue(
        to_order,
        jnp.stack([za_at, (zb_at * 2 + za_at) * 2 + x_at]),
        tokens,
        out_grad,
        q_weight,
        k_weight,
        v_weight,
        (norm_gain[None], mlp_gain[None], q_gain[None], k_gain[None]),
    )
    local_rows = local_low.astype(F32)
    o_give = half_of(o_weight, 1 - za_at, 0)
    za_place = za_at[None].astype(jnp.int32)
    z_keep, qkv_far, x_keep = swap(qkv_keep, "zb"), swap(qkv_give, "za"), swap(qkv_keep, "x")
    tokens_y = swap(local_low, "y")
    (o_far,) = trade(qkv_keep, [(o_give, "za")])
    token, (qkv_far, z_keep, x_keep, tokens_y, o_far) = meet(token, (qkv_far, z_keep, x_keep, tokens_y, o_far))
    down_keep = half_of(down_weight, za_at, 0)
    tokens_z, z_far, xz_keep, x_far, down_xk = trade(
        token, [(local_low, "za"), (qkv_far, "zb"), (z_keep, "x"), (qkv_far, "x"), (down_keep, "x")]
    )
    o_pair = in_order(half_of(o_weight, za_at, 0), o_far, 1)
    token, (z_far, tokens_z, xz_keep, x_far, o_pair, down_xk) = meet(
        token, (z_far, tokens_z, xz_keep, x_far, o_pair, down_xk)
    )
    *fars, xz_far, o_x, o_z = trade(
        token, far(tokens_y, tokens_z, FAR) + [(z_far, "x"), (o_pair, "x"), (o_pair, "zb")]
    )
    gate_weight, up_weight, down_weight = after(token, (gate_weight, up_weight, down_weight))
    gate_keep, up_keep = half_of(gate_weight, za_at, 1), half_of(up_weight, za_at, 1)
    gate_give, up_give = half_of(gate_weight, 1 - za_at, 1), half_of(up_weight, 1 - za_at, 1)
    down_give = half_of(down_weight, 1 - za_at, 0)
    token, (xz_far, fars, o_x, o_z) = meet(token, (xz_far, fars, o_x, o_z))
    mine = mine_of(local_low, tokens_y, tokens_z, fars)
    theirs, gate_zk0, gate_far, gate_xk = trade(
        token, [(mine, "core"), (gate_keep[:KEEP_ROWS], "zb"), (gate_give, "za"), (gate_keep, "x")]
    )
    qkv_all = jnp.concatenate(
        [
            in_order(qkv_keep, qkv_far, 0),
            in_order(z_keep, z_far, 0),
            in_order(x_keep, x_far, 0),
            in_order(xz_keep, xz_far, 0),
        ],
        axis=0,
    ).reshape(8, blk_rows + 16, qkv_width)
    qkv_cols = qkv_all[:, :blk_rows].reshape(width, qkv_width)
    gains = qkv_all[:, blk_rows, : 2 * blk_rows].astype(F32)
    gain_one = gains[:, :blk_rows].reshape(1, width)
    gain_two = gains[:, blk_rows:].reshape(1, width)
    head_sum = jnp.sum(qkv_all[:, blk_rows + 1, : 2 * HEAD_SIZE].astype(F32), axis=0, keepdims=True)
    qk_gains = jnp.concatenate([head_sum[:, :HEAD_SIZE], head_sum[:, HEAD_SIZE:]], axis=0)


    input_rows = jnp.concatenate([mine, theirs], axis=0).astype(F32)
    input_unit = input_rows * lax.rsqrt(jnp.mean(input_rows * input_rows, axis=-1, keepdims=True) + EPSILON)
    normed = (input_unit * gain_one).astype(BF16)
    raw = matmul(normed, qkv_cols)
    queries, kv_own = shape_heads(raw, cosine, sine, qk_gains)
    token, (queries, kv_own, gate_zk0, gate_far, gate_xk) = meet(
        token, (queries, kv_own, gate_zk0, gate_far, gate_xk)
    )
    kv_z, kv_x, up_far, grads_y = trade(
        token, [(kv_own, "zb"), (kv_own, "x"), (up_give, "za"), (grad_local, "y")]
    )
    token, (kv_x,) = meet(token, (kv_x,))
    (o_xz,) = trade(token, [(o_z, "x")])
    (attn_part,) = attend(offsets[0], tiles, queries, start_cols, [kv_own, kv_x], last=False)
    gate_pair = in_order(gate_keep, gate_far, 0)
    token, (kv_z, attn_part, grads_y, o_xz, up_far, gate_pair) = meet(
        token, (kv_z, attn_part, grads_y, o_xz, up_far, gate_pair)
    )
    gate_rest = jnp.concatenate([gate_keep[KEEP_ROWS:], gate_far], axis=0)
    token, (gate_rest,) = meet(token, (gate_rest,))
    kv_xz, gate_zr, grads_z = trade(token, [(kv_z, "x"), (gate_rest, "zb"), (grad_local, "za")])
    o_cols = jnp.concatenate([o_pair, o_z, o_x, o_xz], axis=1)
    token, (kv_xz, o_cols) = meet(token, (kv_xz, o_cols))
    (gate_xf,) = trade(token, [(gate_far, "x")])
    attn_low, inverse = attend(offsets[1], tiles, queries, start_cols, [kv_z, kv_xz], before=attn_part)
    given = matmul(attn_low[middle:], o_cols).astype(BF16)
    token, (given, attn_low, gate_xf, gate_zr, grads_z) = meet(token, (given, attn_low, gate_xf, gate_zr, grads_z))
    up_pair = in_order(up_keep, up_far, 0)
    given, up_z0, up_x0, grads_far, down_far = trade(
        token,
        [(given, "core"), (up_pair[:UP_ROWS], "zb"), (up_pair[:blk_rows], "x"), (grads_z, "y"), (down_give, "za")],
    )
    kept = matmul(attn_low[:middle], o_cols)
    token, (given, kept, up_z0, up_x0, up_pair, grads_far, down_far) = meet(
        token, (given, kept, up_z0, up_x0, up_pair, grads_far, down_far)
    )
    grad_mine = mine_of(grad_local, grads_y, grads_z, [grads_far])
    kept = kept + given.astype(F32)
    from_y, up_z1, up_x1 = trade(
        token,
        far_sums(kept) + [(up_pair[UP_ROWS:blk_rows], "zb"), (up_pair[blk_rows:], "x")],
    )
    gate_z = assemble(
        za_place,
        [
            (gate_zk0, 0, 1),
            (gate_zr[: blk_rows - KEEP_ROWS], KEEP_ROWS, 1),
            (gate_zr[blk_rows - KEEP_ROWS :], 0, -1),
        ],
        0,
    )
    token, (from_y, kept, up_x1, gate_z, up_z1, grad_mine) = meet(
        token, (from_y, kept, up_x1, gate_z, up_z1, grad_mine)
    )
    *nears, gate_xz, up_z2, grad_theirs = trade(
        token, near_sums(kept, from_y) + [(gate_z, "x"), (up_pair[blk_rows:], "zb"), (grad_mine, "core")]
    )
    token, (nears, kept, gate_xz, up_z2, grad_theirs) = meet(token, (nears, kept, gate_xz, up_z2, grad_theirs))
    up_z01 = jnp.concatenate([up_z0, up_z1], axis=0)
    residual = local_rows + own_sum(kept, nears)


    rho_two = lax.rsqrt(jnp.mean(residual * residual, axis=-1, keepdims=True) + EPSILON)
    unit_two = residual * rho_two
    mlp_low = (unit_two * gain_two).astype(BF16)
    token, (mlp_low,) = meet(token, (mlp_low,))
    mlp_y, mlp_z, down_zk, down_xf, up_xz0 = trade(
        token, near(mlp_low) + [(down_keep, "zb"), (down_far, "x"), (up_z01, "x")]
    )
    gate_cols = assemble(
        za_place,
        [(gate_pair, 0, 0), (gate_z, quarter, 0), (gate_xk, half, 1), (gate_xf, half, -1)]
        + [(gate_xz, half + quarter, 0)],
        0,
    )
    grad_mine, grad_theirs = after(token, (grad_mine, grad_theirs))
    grad_rows = assemble(za_place, [(grad_mine, 0, 0), (grad_theirs, middle, 0)], 0)
    token, (mlp_y, mlp_z, down_xf, up_xz0, gate_cols, down_zk, grad_rows) = meet(
        token, (mlp_y, mlp_z, down_xf, up_xz0, gate_cols, down_zk, grad_rows)
    )
    *fars, up_xz1, down_zf0 = trade(token, far(mlp_y, mlp_z, FAR) + [(up_z2, "x"), (down_far[:400], "zb")])
    token, (fars, down_zf0, up_xz1) = meet(token, (fars, down_zf0, up_xz1))
    mlp_mine = mine_of(mlp_low, mlp_y, mlp_z, fars)
    mlp_theirs, down_zf1, down_xzk = trade(
        token, [(mlp_mine, "core"), (down_far[400:], "zb"), (down_zk, "x")]
    )
    up_cols = assemble(
        za_place,
        [
            (up_pair, 0, 0),
            (up_z01, quarter, 0),
            (up_z2, quarter + blk_rows, 0),
            (up_x0, half, 0),
            (up_x1, half + blk_rows, 0),
            (up_xz0, half + quarter, 0),
            (up_xz1, half + quarter + blk_rows, 0),
        ],
        0,
    )
    down_zf = jnp.concatenate([down_zf0, down_zf1], axis=0)
    token, (mlp_theirs, up_cols, down_zf, down_xzk) = meet(token, (mlp_theirs, up_cols, down_zf, down_xzk))
    (down_xzf,) = trade(token, [(down_zf, "x")])
    mlp_rows = jnp.concatenate([mlp_mine, mlp_theirs], axis=0)
    gate_act = matmul(mlp_rows, gate_cols)
    token, (gate_act, up_cols, mlp_rows) = meet(token, (gate_act, up_cols, mlp_rows))
    up_act = matmul(mlp_rows, up_cols)
    token, (gate_act, up_act) = meet(token, (gate_act, up_act))
    sig = jax.nn.sigmoid(gate_act)
    silu = gate_act * sig
    hidden = (silu * up_act).astype(BF16)
    gate_slope = (up_act * (sig * (1.0 + gate_act * (1.0 - sig)))).astype(BF16)
    up_slope = silu.astype(BF16)
    token, (hidden, gate_slope, up_slope, grad_rows, down_xzf) = meet(
        token, (hidden, gate_slope, up_slope, grad_rows, down_xzf)
    )

    def columns_of(value, piece):
        return value[:, piece * quarter : (piece + 1) * quarter]

    down_cols = assemble(
        za_place,
        [
            (down_keep, 0, 1),
            (down_far, 0, -1),
            (down_zk, quarter, 1),
            (down_zf, quarter, -1),
            (down_xk, half, 1),
            (down_xf, half, -1),
            (down_xzk, half + quarter, 1),
            (down_xzf, half + quarter, -1),
        ],
        1,
    )
    down_3 = contract_rows(hidden, columns_of(grad_rows, 3)).astype(BF16)
    down_1 = contract_rows(hidden, columns_of(grad_rows, 1))
    token, (down_3, down_1, down_cols) = meet(token, (down_3, down_1, down_cols))
    (down_3,) = trade(token, [(down_3, "x")])
    hidden_grad = contract_cols(grad_rows, down_cols)
    gate_low = (hidden_grad * gate_slope.astype(F32)).astype(BF16)
    up_low = (hidden_grad * up_slope.astype(F32)).astype(BF16)

    kept, given = two_terms(gate_low, up_low, gate_cols, up_cols)
    token, (kept, given, gate_low, up_low, down_3) = meet(token, (kept, given, gate_low, up_low, down_3))
    (given,) = trade(token, [(given, "core")])
    down_1 = (down_1 + down_3.astype(F32)).astype(BF16)
    gate_3 = contract_rows(columns_of(mlp_rows, 3), gate_low).astype(BF16)
    token, (given, kept, down_1, gate_3) = meet(token, (given, kept, down_1, gate_3))
    kept = kept + given.astype(F32)
    token, (kept,) = meet(token, (kept,))
    from_y, down_1a, gate_3 = trade(token, far_sums(kept) + [(down_1[:320], "zb"), (gate_3, "x")])
    down_2 = contract_rows(hidden, columns_of(grad_rows, 2)).astype(BF16)
    up_3 = contract_rows(columns_of(mlp_rows, 3), up_low).astype(BF16)
    gate_1 = contract_rows(columns_of(mlp_rows, 1), gate_low)
    token, (from_y, kept, down_1a, gate_3, down_2, up_3, gate_1) = meet(
        token, (from_y, kept, down_1a, gate_3, down_2, up_3, gate_1)
    )
    *nears, down_1b, up_3 = trade(token, near_sums(kept, from_y) + [(down_1[320:], "zb"), (up_3, "x")])
    gate_1 = (gate_1 + gate_3.astype(F32)).astype(BF16)
    gate_2 = contract_rows(columns_of(mlp_rows, 2), gate_low).astype(BF16)
    up_1 = contract_rows(columns_of(mlp_rows, 1), up_low)
    up_2 = contract_rows(columns_of(mlp_rows, 2), up_low).astype(BF16)
    token, (nears, kept, down_1b, up_3, gate_2, up_1, up_2, gate_1) = meet(
        token, (nears, kept, down_1b, up_3, gate_2, up_1, up_2, gate_1)
    )
    mlp_in_grad = own_sum(kept, nears)
    gain_two_part = jnp.sum(mlp_in_grad * unit_two, axis=0, keepdims=True)
    scaled = mlp_in_grad * gain_two
    inner = jnp.mean(scaled * unit_two, axis=-1, keepdims=True)
    residual_grad = grad_local.astype(F32) + rho_two * (scaled - unit_two * inner)


    branch_low = residual_grad.astype(BF16)
    token, (branch_low, residual_grad, gain_two_part, gate_1) = meet(
        token, (branch_low, residual_grad, gain_two_part, gate_1)
    )
    branch_y, branch_z, gate_1a, gate_2 = trade(
        token, near(branch_low) + [(gate_1[:blk_rows], "zb"), (gate_2, "x")]
    )
    hidden, down_cols = after(token, (hidden, down_cols))
    out_given = matmul(hidden[middle:], down_cols).astype(BF16)
    up_1 = (up_1 + up_3.astype(F32)).astype(BF16)
    token, (branch_y, branch_z, gate_1a, gate_2, out_given, up_1) = meet(
        token, (branch_y, branch_z, gate_1a, gate_2, out_given, up_1)
    )
    *fars, gate_1b, down_2a = trade(
        token, far(branch_y, branch_z, FAR) + [(gate_1[blk_rows:384], "zb"), (down_2[:384], "x")]
    )
    hidden, down_cols = after(token, (hidden, down_cols))
    out_kept = matmul(hidden[:middle], down_cols)
    token, (fars, out_kept, gate_1b, down_2a) = meet(token, (fars, out_kept, gate_1b, down_2a))
    branch_mine = mine_of(branch_low, branch_y, branch_z, fars)
    branch_theirs, gate_1c, down_2b, out_given = trade(
        token,
        [(branch_mine, "core"), (gate_1[384:464], "zb"), (down_2[384:], "x"), (out_given, "core")],
    )
    grad_own = contract_cols(branch_mine, o_cols).astype(BF16)
    attn_grad = jnp.concatenate([grad_own, contract_cols(branch_theirs, o_cols).astype(BF16)], axis=0)
    mixed = jnp.concatenate([gate_1[464:], up_1[:144]], axis=0)
    token, (attn_grad, gate_1c, down_2b, mixed) = meet(token, (attn_grad, gate_1c, down_2b, mixed))
    mixed, up_2a = trade(token, [(mixed, "zb"), (up_2[:blk_rows], "x")])
    query_part, kv_1, kv_3 = attend_back(
        offsets[1], tiles, queries, start_rows, inverse, attn_low, attn_grad, [kv_z, kv_xz], last=False
    )
    out_kept = out_kept + out_given.astype(F32)
    token, (query_part, kv_1, kv_3, mixed, up_2a, out_kept) = meet(
        token, (query_part, kv_1, kv_3, mixed, up_2a, out_kept)
    )
    gate_1d, up_1a = mixed[:48], mixed[48:]
    kv_3, up_1b, out_from = trade(token, [(kv_3, "x"), (up_1[144:336], "zb")] + far_sums(out_kept))
    query_grad, kv_0, kv_2 = attend_back(
        offsets[0],
        tiles,
        queries,
        start_rows,
        inverse,
        attn_low,
        attn_grad,
        [kv_own, kv_x],
        before=query_part,
    )
    token, (query_grad, kv_0, kv_2, kv_3, up_1b, out_from) = meet(
        token, (query_grad, kv_0, kv_2, kv_3, up_1b, out_from)
    )
    kv_1 = (kv_1.astype(F32) + kv_3.astype(F32)).astype(BF16)
    kv_1, kv_2, *out_nears = trade(token, [(kv_1, "zb"), (kv_2, "x")] + near_sums(out_kept, out_from))
    token, (kv_2, branch_mine, branch_theirs, gate_low, up_low, hidden, query_grad) = meet(
        token, (kv_2, branch_mine, branch_theirs, gate_low, up_low, hidden, query_grad)
    )
    q_low, q_gain_part = shape_back(raw, query_grad, cosine, sine, qk_gains, 2, 0, 0, HEAD_SIZE**-0.5)
    q_3 = swap(contract_rows(columns_of(normed, 3), q_low).astype(BF16), "x")
    branch_rows = jnp.concatenate([branch_mine, branch_theirs], axis=0)
    o_3 = contract_rows(attn_low, columns_of(branch_rows, 3)).astype(BF16)
    q_1 = contract_rows(columns_of(normed, 1), q_low)
    gate_part = (
        contract_rows(columns_of(mlp_rows, 0), gate_low)
        + gate_2.astype(F32)
        + jnp.concatenate([gate_1a, gate_1b, gate_1c, gate_1d], axis=0).astype(F32)
    )
    gate_mine, gate_give = za_parts(gate_part, 0)
    down_part = (
        contract_rows(hidden, columns_of(grad_rows, 0))
        + jnp.concatenate([down_2a, down_2b], axis=0).astype(F32)
        + jnp.concatenate([down_1a, down_1b], axis=0).astype(F32)
    )
    down_mine, down_give = za_parts(down_part, 1)
    token, (kv_1, out_nears, q_low, q_gain_part, o_3, gate_mine, gate_give, down_mine, down_give, q_1) = meet(
        token, (kv_1, out_nears, q_low, q_gain_part, o_3, gate_mine, gate_give, down_mine, down_give, q_1)
    )
    gate_give, up_1c, down_give, up_2b = trade(
        token, [(gate_give, "za"), (up_1[336:], "zb"), (down_give, "za"), (up_2[blk_rows:], "x")]
    )
    kv_grad = (kv_0.astype(F32) + kv_1.astype(F32) + kv_2.astype(F32)).astype(BF16)
    kv_low, k_gain_part = shape_back(raw, kv_grad, cosine, sine, qk_gains, 1, 2, 1, 1.0)
    low = jnp.concatenate([q_low, kv_low], axis=1)
    given = contract_cols(low[middle:], qkv_cols).astype(BF16)
    w_3 = contract_rows(columns_of(normed, 3), kv_low).astype(BF16)
    q_1 = (q_1 + q_3.astype(F32)).astype(BF16)
    token, (given, low, kv_low, k_gain_part, w_3, q_1, gate_give, up_1c, up_2b) = meet(
        token, (given, low, kv_low, k_gain_part, w_3, q_1, gate_give, up_1c, up_2b)
    )
    given_low = given
    kv_late, normed, attn_low, branch_rows, low = after(token, (kv_low, normed, attn_low, branch_rows, low))
    given, q_1, w_3, o_3 = trade(token, [(given, "core"), (q_1, "zb"), (w_3, "x"), (o_3, "x")])
    terms = contract_cols(low[:middle], qkv_cols)
    w_1 = contract_rows(columns_of(normed, 1), kv_late)
    o_1 = contract_rows(attn_low, columns_of(branch_rows, 1))
    o_2 = contract_rows(attn_low, columns_of(branch_rows, 2)).astype(BF16)
    token, (given, terms, q_1, w_3, o_3, w_1, o_1, o_2, down_give, up_low) = meet(
        token, (given, terms, q_1, w_3, o_3, w_1, o_1, o_2, down_give, up_low)
    )
    kept = terms + given.astype(F32)
    w_1 = (w_1 + w_3.astype(F32)).astype(BF16)
    token, (kept, w_1) = meet(token, (kept, w_1))
    from_y, w_1, o_2 = trade(token, far_sums(kept) + [(w_1, "zb"), (o_2, "x")])
    o_1 = (o_1 + o_3.astype(F32)).astype(BF16)
    terms_low, given_low, input_unit = after(token, (terms, given_low, input_unit))
    gain_one_part = jnp.sum(
        terms_low * input_unit[:middle] + given_low.astype(F32) * input_unit[middle:], axis=0, keepdims=True
    )
    gain_sum = jnp.concatenate(
        [
            *reorder(from_order, [gain_one_part, gain_two_part], [F32, F32]),
            jnp.sum(q_gain_part, axis=0, keepdims=True),
            jnp.sum(k_gain_part, axis=0, keepdims=True),
        ],
        axis=1,
    )
    qw_2 = contract_rows(columns_of(normed, 2), low).astype(BF16)
    token, (from_y, kept, w_1, o_1, qw_2, o_2, gain_sum, up_low) = meet(
        token, (from_y, kept, w_1, o_1, qw_2, o_2, gain_sum, up_low)
    )
    *nears, o_1, qw_2, gain_x = trade(
        token, near_sums(kept, from_y) + [(o_1, "zb"), (qw_2, "x"), (gain_sum, "core")]
    )
    gain_sum = gain_sum + gain_x
    gain_sum = gain_sum + swap(gain_sum, "y")
    up_part = (
        contract_rows(columns_of(mlp_rows, 0), up_low)
        + jnp.concatenate([up_2a, up_2b], axis=0).astype(F32)
        + jnp.concatenate([up_1a, up_1b, up_1c], axis=0).astype(F32)
    )
    up_mine, up_give = za_parts(up_part, 0)
    qw_0 = contract_rows(columns_of(normed, 0), low)
    o_0 = contract_rows(attn_low, columns_of(branch_rows, 0))
    block_out = residual + own_sum(out_kept, out_nears)
    token, (nears, kept, qw_2, qw_0, o_0, block_out, gain_sum, o_1, up_mine, up_give) = meet(
        token, (nears, kept, qw_2, qw_0, o_0, block_out, gain_sum, o_1, up_mine, up_give)
    )
    qkv_mine, qkv_give = za_parts(qw_0 + qw_2.astype(F32) + jnp.concatenate([q_1, w_1], axis=1).astype(F32), 0)
    o_mine, o_give = za_parts(o_0 + o_2.astype(F32) + o_1.astype(F32), 1)
    token, (qkv_mine, qkv_give, o_mine, o_give) = meet(token, (qkv_mine, qkv_give, o_mine, o_give))
    gain_x, qkv_give, o_give, up_give = trade(
        token, [(gain_sum, "x"), (qkv_give, "za"), (o_give, "za"), (up_give, "za")]
    )
    gain_sum = gain_sum + gain_x
    gain_sum = gain_sum + swap(gain_sum, "zb")
    gain_sum = gain_sum + swap(gain_sum, "za")
    input_grad = own_sum(kept, nears)
    unit_one = local_rows * (rho_one := lax.rsqrt(jnp.mean(local_rows * local_rows, axis=-1, keepdims=True) + EPSILON))
    scaled = input_grad * gain_one
    inner = jnp.mean(scaled * unit_one, axis=-1, keepdims=True)
    in_grad = residual_grad + rho_one * (scaled - unit_one * inner)
    block_out, in_grad = reorder(from_order, [block_out, in_grad], [BF16, F32])
    device = (((y_at * 2 + core_at) * 2 + zb_at) * 2 + za_at) * 2 + x_at

    def own_slice(first, length):
        share = length // 32
        return lax.dynamic_slice_in_dim(gain_sum[0], first + device * share, share, axis=0)

    qkv_parts = za_join(qkv_mine, qkv_give)

    def columns(lo, hi):
        return jnp.concatenate([part[:, lo:hi] for part in qkv_parts], axis=1)

    return (
        block_out,
        in_grad,
        own_slice(0, width),
        columns(0, q_width),
        columns(q_width, q_width + k_width),
        columns(q_width + k_width, qkv_width),
        own_slice(2 * width, HEAD_SIZE),
        own_slice(2 * width + HEAD_SIZE, HEAD_SIZE),
        jnp.concatenate(za_join(o_mine, o_give), axis=0),
        own_slice(width, width),
        jnp.concatenate(za_join(gate_mine, gate_give), axis=1),
        jnp.concatenate(za_join(up_mine, up_give), axis=1),
        jnp.concatenate(za_join(down_mine, down_give), axis=0),
    )


def layer(
    sizes,
    tokens,
    out_grad,
    seq_lengths,
    block_deal,
    norm_gain,
    q_weight,
    k_weight,
    v_weight,
    q_gain,
    k_gain,
    o_weight,
    mlp_gain,
    gate_weight,
    up_weight,
    down_weight,
):
    y_count, core_count, zb_count, za_count, x_count = sizes
    pairwise = sizes == (2, 2, 2, 2, 2)
    all_axes = ("y", "core", "zb", "za", "x")
    y_at, core_at, zb_at, za_at, x_at = (lax.axis_index(name) for name in all_axes)
    tok_dev, width = tokens.shape
    blk_rows = q_weight.shape[0]
    group_count = zb_count * x_count
    member_count = y_count * core_count * za_count
    head_count = y_count * core_count
    rows = member_count * tok_dev
    piece = za_count * blk_rows


    def gather_rows(value):
        if not pairwise:
            return lax.all_gather(value, ("y", "core", "za"), axis=0, tiled=True)
        half = tok_dev // 2
        along_y = swap(value, "y")
        along_z = swap(value, "za")
        parts = [value, along_y, along_z, swap(along_z[:half], "y"), swap(along_y[half:], "za")]
        mine = jnp.concatenate(parts, axis=0)
        return jnp.concatenate([mine, swap(mine, "core")], axis=0)

    def scatter_rows(part_of):
        if not pairwise:
            full = part_of(slice(0, rows)).astype(BF16)
            return lax.psum_scatter(full, ("y", "core", "za"), scatter_dimension=0, tiled=True).astype(F32)
        middle = rows // 2
        half = tok_dev // 2
        given = swap(part_of(slice(middle, rows)).astype(BF16), "core")
        kept = part_of(slice(0, middle)) + given.astype(F32)
        own, to_y, to_z, far = (kept[i * tok_dev : (i + 1) * tok_dev] for i in range(4))
        far = far.astype(BF16)
        from_y = swap(far[:half], "y").astype(F32)
        from_z = swap(far[half:], "za").astype(F32)
        z_sum = jnp.concatenate([to_z[:half] + from_y, to_z[half:]], axis=0).astype(BF16)
        y_sum = jnp.concatenate([to_y[:half], to_y[half:] + from_z], axis=0).astype(BF16)
        return own + swap(y_sum, "y").astype(F32) + swap(z_sum, "za").astype(F32)


    def gather_pieces(own, axis):
        if not pairwise:
            return lax.all_gather(own, ("zb", "x"), axis=axis, tiled=True)
        along_z = swap(own, "zb")
        return jnp.concatenate([own, along_z, swap(own, "x"), swap(along_z, "x")], axis=axis)

    def scatter_pieces(part_of, length, axis):
        if not pairwise:
            full = part_of(0, length).astype(BF16)
            return lax.psum_scatter(full, ("zb", "x"), scatter_dimension=axis, tiled=True).astype(F32)
        half, quarter = length // 2, length // 4
        given = swap(part_of(half, length).astype(BF16), "x")
        kept = part_of(0, half) + given.astype(F32)
        given = swap(lax.slice_in_dim(kept, quarter, half, axis=axis).astype(BF16), "zb")
        return lax.slice_in_dim(kept, 0, quarter, axis=axis) + given.astype(F32)

    def in_order(mine, other, axis):
        first = jnp.where(za_at == 0, mine, other)
        second = jnp.where(za_at == 0, other, mine)
        return jnp.concatenate([first, second], axis=axis)

    def gather_weight(part_of, axis):
        mine = part_of(za_at)
        if za_count > 1:
            mine = in_order(mine, swap(part_of(1 - za_at), "za"), axis)
        return gather_pieces(mine, axis)

    def scatter_weight(part_of, axis):
        part = scatter_pieces(part_of, width, axis)
        if za_count == 1:
            return [part]
        first = lax.slice_in_dim(part, 0, blk_rows, axis=axis)
        second = lax.slice_in_dim(part, blk_rows, 2 * blk_rows, axis=axis)
        mine = jnp.where(za_at == 0, first, second)
        other = swap(jnp.where(za_at == 0, second, first).astype(BF16), "za").astype(F32)
        return [jnp.where(za_at == 0, mine, other), jnp.where(za_at == 0, other, mine)]

    def half_of(weight, at, axis):
        size = weight.shape[axis] // za_count
        return lax.dynamic_slice_in_dim(weight, at * size, size, axis=axis)


    def piece_group(index):
        if pairwise:
            return zb_at ^ (index % 2), x_at ^ (index // 2)
        return index // x_count, index % x_count

    def to_pieces(value):
        blocks = []
        for index in range(group_count):
            zb_of, x_of = piece_group(index)
            for za_of in range(za_count):
                block = (zb_of * za_count + za_of) * x_count + x_of
                blocks.append(lax.dynamic_slice_in_dim(value, block * blk_rows, blk_rows, axis=1))
        return jnp.concatenate(blocks, axis=1) if pairwise else value

    def from_pieces(value):
        if not pairwise:
            return value
        blocks = []
        for block in range(group_count * za_count):
            zb_of, za_of, x_of = block // 4, block // 2 % 2, block % 2
            index = (x_at ^ x_of) * 2 + (zb_at ^ zb_of)
            blocks.append(lax.dynamic_slice_in_dim(value, (index * 2 + za_of) * blk_rows, blk_rows, axis=1))
        return jnp.concatenate(blocks, axis=1)


    per_span = head_count // 2
    member = jnp.arange(member_count, dtype=jnp.int32)
    if pairwise:
        member_y, member_za, member_core = y_at ^ (member % 2), za_at ^ (member // 2 % 2), core_at ^ (member // 4)
    else:
        member_za = member % za_count
        member_core = member // za_count % core_count
        member_y = member // (za_count * core_count)
    group = jnp.arange(group_count, dtype=jnp.int32)
    group_zb, group_x = piece_group(group)
    member_head = member_y * core_count + member_core
    span_table = jnp.arange(block_deal.shape[0], dtype=jnp.int32)

    def natural_tile(zb_of, x_of):
        blk = (zb_of * za_count + member_za) * x_count + x_of
        entry = 2 * blk + member_head // per_span
        span = jnp.sum(
            jnp.where(entry[..., None] == span_table, block_deal, 0), axis=-1, dtype=jnp.int32
        )
        return span * per_span + member_head % per_span

    query_tile = natural_tile(zb_at, x_at)
    key_tile = natural_tile(group_zb[:, None], group_x[:, None]).reshape(-1)
    tile_ids = jnp.arange(key_tile.shape[0], dtype=jnp.int32)
    offsets = jnp.sum(
        jnp.where(key_tile[None, :] == tile_ids[:, None], tile_ids[None, :] * tok_dev, 0), axis=1, dtype=jnp.int32
    )
    natural = query_tile[:, None] * tok_dev + jnp.arange(tok_dev, dtype=jnp.int32)[None, :]
    seq_ids = jnp.arange(seq_lengths.shape[0], dtype=jnp.int32)
    seq_ends = jnp.sum(jnp.where(seq_ids[None, :] <= seq_ids[:, None], seq_lengths[None, :], 0), axis=1, dtype=jnp.int32)
    starts = jnp.max(jnp.where(seq_ends <= natural[..., None], seq_ends, 0), axis=-1)
    tiles = (query_tile, starts[:, 0] // (2 * tok_dev))
    start_rows = jnp.stack([starts, starts], axis=1)
    start_cols = jnp.broadcast_to(starts.reshape(rows, 1), (rows, 128))
    places = (natural - starts).reshape(rows)
    half_width = HEAD_SIZE // 2
    frequency = jnp.power(ROPE_BASE, -jnp.arange(half_width, dtype=F32) * (2.0 / HEAD_SIZE))
    angles = places.astype(F32)[:, None] * frequency[None, :]
    cosine = jnp.cos(angles)
    sine = jnp.sin(angles)
    cosine = jnp.concatenate([cosine, cosine], axis=1)
    sine = jnp.concatenate([-sine, sine], axis=1)


    q_width = q_weight.shape[1] // za_count
    k_width = k_weight.shape[1] // za_count
    qkv_width = q_width + 2 * k_width
    gain_pad = 16

    gain_row = jnp.concatenate([norm_gain, mlp_gain])
    head_gains = jnp.concatenate([q_gain, k_gain])

    def gain_rows():
        top = jnp.pad(gain_row, (0, qkv_width - gain_row.shape[0]))[None]
        bottom = jnp.pad(head_gains, (0, qkv_width - head_gains.shape[0]))[None]
        return jnp.concatenate([top, bottom, jnp.zeros((gain_pad - 2, qkv_width), BF16)], axis=0)

    def qkv_part(at):
        return jnp.concatenate(
            [half_of(q_weight, at, 1), half_of(k_weight, at, 1), half_of(v_weight, at, 1), ], axis=1
        )

    padded = blk_rows + gain_pad
    own_gain_rows = gain_rows()
    qkv_all = gather_weight(lambda at: jnp.concatenate([qkv_part(at), own_gain_rows], axis=0), 0)
    qkv_all = qkv_all.reshape(group_count * za_count, padded, qkv_width)
    qkv_cols = qkv_all[:, :blk_rows].reshape(width, qkv_width)
    gains = qkv_all[:, blk_rows, : 2 * blk_rows].astype(F32)
    gain_one = gains[:, :blk_rows].reshape(1, width)
    gain_two = gains[:, blk_rows:].reshape(1, width)
    small = q_gain.shape[0]
    head_parts = qkv_all[:, blk_rows + 1, : 2 * small].astype(F32).reshape(group_count * za_count, 2, small)

    def head_gain(which):
        return from_small(head_parts[:, which])

    def from_small(parts):
        if not pairwise:
            return parts.reshape(1, -1)
        rows_of = []
        for block in range(8):
            zb_of, za_of, x_of = block // 4, block // 2 % 2, block % 2
            index = ((x_at ^ x_of) * 2 + (zb_at ^ zb_of)) * 2 + za_of
            rows_of.append(lax.dynamic_slice_in_dim(parts, index, 1, axis=0))
        return jnp.concatenate(rows_of, axis=1)

    qk_gains = jnp.concatenate([head_gain(0), head_gain(1)], axis=0)


    local_low = to_pieces(tokens)
    local_rows = local_low.astype(F32)
    input_rows = gather_rows(local_low).astype(F32)
    o_cols = gather_weight(lambda at: half_of(o_weight, at, 0), 1)
    gu_cols = gather_weight(
        lambda at: jnp.concatenate([half_of(gate_weight, at, 1), half_of(up_weight, at, 1)], axis=1), 0
    )
    down_cols = gather_weight(lambda at: half_of(down_weight, at, 0), 1)
    grad_local = to_pieces(out_grad)
    grad_rows = gather_rows(grad_local)

    def unit_rows(value):
        return value * lax.rsqrt(jnp.mean(value * value, axis=-1, keepdims=True) + EPSILON)

    input_unit = unit_rows(input_rows)
    normed = (input_unit * gain_one).astype(BF16)
    raw = matmul(normed, qkv_cols)
    queries, kv_own = shape_heads(raw, cosine, sine, qk_gains)
    key_values = gather_pieces(kv_own, 0)
    attn_low, inverse = attend(offsets, tiles, queries, start_cols, [key_values])
    residual = local_rows + scatter_rows(lambda at: matmul(attn_low[at], o_cols))


    rho_two = lax.rsqrt(jnp.mean(residual * residual, axis=-1, keepdims=True) + EPSILON)
    unit_two = residual * rho_two
    mlp_rows = gather_rows((unit_two * gain_two).astype(BF16))
    ff = gu_cols.shape[1] // 2
    gate_up = matmul(mlp_rows, gu_cols)
    gate_act, up_act = gate_up[:, :ff], gate_up[:, ff:]
    sig = jax.nn.sigmoid(gate_act)
    silu = gate_act * sig
    hidden = (silu * up_act).astype(BF16)
    hidden_grad = contract_cols(grad_rows, down_cols)
    gate_low = (hidden_grad * up_act * (sig * (1.0 + gate_act * (1.0 - sig)))).astype(BF16)
    up_low = (hidden_grad * silu).astype(BF16)
    gu_low = jnp.concatenate([gate_low, up_low], axis=1)
    mlp_in_grad = scatter_rows(lambda at: contract_cols(gu_low[at], gu_cols))

    down_parts = scatter_weight(lambda lo, hi: contract_rows(hidden, grad_rows[:, lo:hi]), 1)
    gate_parts = scatter_weight(lambda lo, hi: contract_rows(mlp_rows[:, lo:hi], gate_low), 0)
    up_parts = scatter_weight(lambda lo, hi: contract_rows(mlp_rows[:, lo:hi], up_low), 0)
    block_out = residual + scatter_rows(lambda at: matmul(hidden[at], down_cols))

    gain_two_part = jnp.sum(mlp_in_grad * unit_two, axis=0, keepdims=True)
    scaled = mlp_in_grad * gain_two
    inner = jnp.mean(scaled * unit_two, axis=-1, keepdims=True)
    residual_grad = grad_local.astype(F32) + rho_two * (scaled - unit_two * inner)


    branch_rows = gather_rows(residual_grad.astype(BF16))
    attn_grad = contract_cols(branch_rows, o_cols).astype(BF16)
    query_grad, kv_grads = attend_back(
        offsets, tiles, queries, start_rows, inverse, attn_low, attn_grad, [key_values]
    )
    o_parts = scatter_weight(lambda lo, hi: contract_rows(attn_low, branch_rows[:, lo:hi]), 1)
    kv_grad = scatter_pieces(lambda lo, hi: kv_grads[lo:hi].astype(F32), kv_grads.shape[0], 0).astype(BF16)
    q_low, q_gain_part = shape_back(raw, query_grad, cosine, sine, qk_gains, 2, 0, 0, HEAD_SIZE**-0.5)
    kv_low, k_gain_part = shape_back(raw, kv_grad, cosine, sine, qk_gains, 1, 2, 1, 1.0)
    low = jnp.concatenate([q_low, kv_low], axis=1)

    gain_one_parts = []

    def input_terms(at):
        terms = contract_cols(low[at], qkv_cols)
        gain_one_parts.append(jnp.sum(terms * input_unit[at], axis=0, keepdims=True))
        return terms

    input_grad = scatter_rows(input_terms)
    qkv_parts = scatter_weight(lambda lo, hi: contract_rows(normed[:, lo:hi], low), 0)

    gain_sum = jnp.concatenate(
        [
            from_pieces(sum(gain_one_parts)),
            from_pieces(gain_two_part),
            jnp.sum(q_gain_part, axis=0, keepdims=True),
            jnp.sum(k_gain_part, axis=0, keepdims=True),
        ],
        axis=1,
    )
    if pairwise:
        for name in ("core", "y", "za", "x", "zb"):
            gain_sum = gain_sum + swap(gain_sum, name)
    else:
        gain_sum = lax.psum(gain_sum, all_axes)

    unit_one = local_rows * (rho_one := lax.rsqrt(jnp.mean(local_rows * local_rows, axis=-1, keepdims=True) + EPSILON))
    scaled = input_grad * gain_one
    inner = jnp.mean(scaled * unit_one, axis=-1, keepdims=True)
    in_grad = residual_grad + rho_one * (scaled - unit_one * inner)

    device = (((y_at * core_count + core_at) * zb_count + zb_at) * za_count + za_at) * x_count + x_at
    device_count = head_count * zb_count * za_count * x_count

    def own_slice(first, length):
        share = length // device_count
        return lax.dynamic_slice_in_dim(gain_sum[0], first + device * share, share, axis=0)

    def join(parts, lo, hi, axis):
        cut = [lax.slice_in_dim(part, lo, hi, axis=axis) for part in parts]
        return jnp.concatenate(cut, axis=axis)

    return (
        from_pieces(block_out).astype(BF16),
        from_pieces(in_grad),
        own_slice(0, width),
        join(qkv_parts, 0, q_width, 1),
        join(qkv_parts, q_width, q_width + k_width, 1),
        join(qkv_parts, q_width + k_width, qkv_width, 1),
        own_slice(2 * width, HEAD_SIZE),
        own_slice(2 * width + HEAD_SIZE, HEAD_SIZE),
        jnp.concatenate(o_parts, axis=0),
        own_slice(width, width),
        jnp.concatenate(gate_parts, axis=1),
        jnp.concatenate(up_parts, axis=1),
        jnp.concatenate(down_parts, axis=0),
    )


def solution(mesh):
    heads, blks = mesh.shape["head"], mesh.shape["blk"]
    za_count = KEY_VALUE_HEADS // heads
    side = math.isqrt(blks // za_count)
    sizes = (heads // 2, 2, side, za_count, side)
    names = ("y", "core", "zb", "za", "x")
    devices = mesh.devices.reshape(sizes)
    inner = Mesh(devices, names)
    head, blk = ("y", "core"), ("zb", "za", "x")
    rows, in_weight, out_weight, gain = P(names, None), P(blk, head), P(head, blk), P(blk)
    return jax.shard_map(
        paired_layer if sizes == (2, 2, 2, 2, 2) else functools.partial(layer, sizes),
        mesh=inner,
        in_specs=(
            rows,
            rows,
            P(),
            P(),
            gain,
            in_weight,
            in_weight,
            in_weight,
            gain,
            gain,
            out_weight,
            gain,
            in_weight,
            in_weight,
            out_weight,
        ),
        out_specs=(
            rows,
            rows,
            P(names),
            in_weight,
            in_weight,
            in_weight,
            P(names),
            P(names),
            out_weight,
            P(names),
            in_weight,
            in_weight,
            out_weight,
        ),
        check_vma=False,
    )
```

```python
import functools
import math

import jax
import jax.numpy as jnp
from jax import lax
from jax.experimental import pallas as pl
from jax.experimental.pallas import tpu as pltpu
from jax.sharding import Mesh
from jax.sharding import PartitionSpec as P

HEAD_SIZE = 128
KEY_VALUE_HEADS = 8
EPSILON = 1e-06
ROPE_BASE = 1000000.0
F32 = jnp.float32
BF16 = jnp.bfloat16
SWAP = [(0, 1), (1, 0)]
PAIRS_OF_ROWS = (((0,), (0,)), ((), ()))
PAIRS_OF_COLS = (((1,), (1,)), ((), ()))
VMEM = pltpu.MemorySpace.VMEM
LIGHT = pl.CostEstimate(flops=1000, bytes_accessed=1000, transcendentals=0)
SMEM = pltpu.MemorySpace.SMEM


def matmul(left, right):
    return jnp.dot(left, right, preferred_element_type=F32)


def contract_rows(left, right):
    return lax.dot_general(left, right, PAIRS_OF_ROWS, preferred_element_type=F32)


def contract_cols(left, right):
    return lax.dot_general(left, right, PAIRS_OF_COLS, preferred_element_type=F32)


def swap(value, axis):
    return lax.ppermute(value, axis, SWAP)


def attend_kernel(off_ref, tile_ref, low_ref, q_ref, start_ref, *refs, parts, first, last):
    half = 128
    kv_refs, refs = refs[:parts], refs[parts:]
    if not first:
        before_ref, refs = refs[0], refs[1:]
    if last:
        out_ref, inv_ref, kv_ref, acc_ref = refs
    else:
        after_ref, kv_ref, acc_ref = refs
    share = kv_refs[0].shape[0]
    for part, ref in enumerate(kv_refs):
        kv_ref[part * share : (part + 1) * share, :] = ref[...]
    lane = lax.broadcasted_iota(jnp.int32, (256, 256), 1)
    row = lax.broadcasted_iota(jnp.int32, (256, 256), 0) % half
    ones = jnp.ones((256, HEAD_SIZE), BF16)

    def tile(index, unused):
        rows = pl.ds(pl.multiple_of(index * half, half), half)
        queries = jnp.concatenate([q_ref[rows, :HEAD_SIZE], q_ref[rows, HEAD_SIZE:]], axis=0)
        start = start_ref[rows, :]
        start = jnp.concatenate([start, start], axis=1)
        start = jnp.concatenate([start, start], axis=0)
        places = tile_ref[index] * half + row
        acc_ref[...] = jnp.zeros_like(acc_ref) if first else before_ref[index]

        def step(block, unused_step):
            at = off_ref[2 * block]

            @pl.when(at >= 0)
            def _():
                low = pl.ds(pl.multiple_of(at, half), half)
                high = pl.ds(pl.multiple_of(off_ref[2 * block + 1], half), half)
                keys = jnp.concatenate([kv_ref[low, :HEAD_SIZE], kv_ref[high, :HEAD_SIZE]], axis=0)
                values = jnp.concatenate([kv_ref[low, HEAD_SIZE:], kv_ref[high, HEAD_SIZE:]], axis=0)
                scores = contract_cols(queries, keys)
                natural = block * 256 + lane
                allowed = (natural <= places) & (natural >= start)
                weights = jnp.where(allowed, jnp.exp(scores), 0.0).astype(BF16)
                acc_ref[...] += matmul(weights, jnp.concatenate([values, ones], axis=1))

            return unused_step

        lax.fori_loop(low_ref[index], tile_ref[index] // 2 + 1, step, 0)
        if last:
            inverse = 1.0 / acc_ref[:, HEAD_SIZE:]
            attended = (acc_ref[:, :HEAD_SIZE] * inverse).astype(BF16)
            out_ref[rows, :HEAD_SIZE] = attended[:half]
            out_ref[rows, HEAD_SIZE:] = attended[half:]
            inv_ref[index, 0:1, :] = jnp.transpose(inverse[:half])[0:1, :]
            inv_ref[index, 1:2, :] = jnp.transpose(inverse[half:])[0:1, :]
        else:
            after_ref[index] = acc_ref[...]
        return unused

    lax.fori_loop(0, q_ref.shape[0] // half, tile, 0)


def attend_back_kernel(
    off_ref, tile_ref, low_ref, q_ref, start_ref, inv_ref, out_ref, grad_ref, *refs, parts, first, last
):
    half = 128
    kv_refs, refs = refs[:parts], refs[parts:]
    if not first:
        before_ref, refs = refs[0], refs[1:]
    dq_ref, *dkv_refs = refs[: 1 + parts]
    kv_ref, dk_ref, dv_ref, acc_ref = refs[1 + parts :]
    share = kv_refs[0].shape[0]
    for part, ref in enumerate(kv_refs):
        kv_ref[part * share : (part + 1) * share, :] = ref[...]
    key_row = lax.broadcasted_iota(jnp.int32, (256, 256), 0)
    query_lane = lax.broadcasted_iota(jnp.int32, (1, 256), 1) % half

    def clear(index, unused):
        rows = pl.ds(pl.multiple_of(index * 256, 256), 256)
        dk_ref[rows, :] = jnp.zeros((256, HEAD_SIZE), F32)
        dv_ref[rows, :] = jnp.zeros((256, HEAD_SIZE), F32)
        return unused

    lax.fori_loop(0, dk_ref.shape[0] // 256, clear, 0)

    def tile(index, unused):
        rows = pl.ds(pl.multiple_of(index * half, half), half)

        def both(ref):
            return jnp.concatenate([ref[rows, :HEAD_SIZE], ref[rows, HEAD_SIZE:]], axis=0)

        def along(ref):
            return jnp.concatenate([ref[index, 0:1, :], ref[index, 1:2, :]], axis=1)

        queries = both(q_ref)
        grads = both(grad_ref)
        products = both(out_ref).astype(F32) * grads.astype(F32)
        deltas = jnp.sum(jnp.transpose(products), axis=0, keepdims=True)
        inverse = along(inv_ref)
        start = along(start_ref)
        places = tile_ref[index] * half + query_lane
        acc_ref[...] = jnp.zeros_like(acc_ref) if first else both(before_ref)

        def step(block, unused_step):
            at = off_ref[2 * block]

            @pl.when(at >= 0)
            def _():
                low = pl.ds(pl.multiple_of(at, half), half)
                high = pl.ds(pl.multiple_of(off_ref[2 * block + 1], half), half)
                keys = jnp.concatenate([kv_ref[low, :HEAD_SIZE], kv_ref[high, :HEAD_SIZE]], axis=0)
                values = jnp.concatenate([kv_ref[low, HEAD_SIZE:], kv_ref[high, HEAD_SIZE:]], axis=0)
                scores = contract_cols(keys, queries)
                natural = block * 256 + key_row
                allowed = (natural <= places) & (natural >= start)
                probs = jnp.where(allowed, jnp.exp(scores) * inverse, 0.0)
                prob_grad = contract_cols(values, grads)
                score_grad = (probs * (prob_grad - deltas)).astype(BF16)
                value_part = matmul(probs.astype(BF16), grads)
                key_part = matmul(score_grad, queries)
                dv_ref[low, :] += value_part[:half]
                dv_ref[high, :] += value_part[half:]
                dk_ref[low, :] += key_part[:half]
                dk_ref[high, :] += key_part[half:]
                acc_ref[...] += contract_rows(score_grad, keys)

            return unused_step

        lax.fori_loop(low_ref[index], tile_ref[index] // 2 + 1, step, 0)
        dq_ref[rows, :HEAD_SIZE] = acc_ref[:half, :].astype(dq_ref.dtype)
        dq_ref[rows, HEAD_SIZE:] = acc_ref[half:, :].astype(dq_ref.dtype)
        return unused

    lax.fori_loop(0, q_ref.shape[0] // half, tile, 0)

    for part, ref in enumerate(dkv_refs):

        def store(index, unused):
            target = pl.ds(pl.multiple_of(index * 256, 256), 256)
            source = pl.ds(pl.multiple_of(part * share + index * 256, 256), 256)
            ref[target, :HEAD_SIZE] = dk_ref[source, :].astype(BF16)
            ref[target, HEAD_SIZE:] = dv_ref[source, :].astype(BF16)
            return unused

        lax.fori_loop(0, share // 256, store, 0)


def attend(offsets, tiles, queries, start_cols, kv_parts, before=None, last=True):
    rows, width = queries.shape
    parts, share = len(kv_parts), kv_parts[0].shape[0]
    keys = parts * share
    first = before is None
    extra = () if first else (before,)
    whole = (
        (jax.ShapeDtypeStruct((rows, width), BF16), jax.ShapeDtypeStruct((rows // 128, 2, 128), F32))
        if last
        else (jax.ShapeDtypeStruct((rows // 128, 256, 256), F32),)
    )
    return pl.pallas_call(
        functools.partial(attend_kernel, parts=parts, first=first, last=last),
        name="attend",
        out_shape=whole,
        in_specs=[pl.BlockSpec(memory_space=SMEM)] * 3 + [pl.BlockSpec(memory_space=VMEM)] * (2 + parts + len(extra)),
        out_specs=[pl.BlockSpec(memory_space=VMEM)] * len(whole),
        scratch_shapes=[pltpu.VMEM((keys, width), BF16), pltpu.VMEM((256, 256), F32)],
        compiler_params=pltpu.CompilerParams(vmem_limit_bytes=12 * 2**20 + keys * 1536),
        cost_estimate=LIGHT,
    )(offsets, *tiles, queries, start_cols, *kv_parts, *extra)


def attend_back(offsets, tiles, queries, start_rows, inverse, attended, grads, kv_parts, before=None, last=True):
    rows, width = queries.shape
    parts, share = len(kv_parts), kv_parts[0].shape[0]
    keys = parts * share
    first = before is None
    extra = () if first else (before,)
    return pl.pallas_call(
        functools.partial(attend_back_kernel, parts=parts, first=first, last=last),
        name="attend_back",
        out_shape=(jax.ShapeDtypeStruct((rows, width), BF16 if last else F32),)
        + tuple(jax.ShapeDtypeStruct((share, width), BF16) for unused in kv_parts),
        in_specs=[pl.BlockSpec(memory_space=SMEM)] * 3 + [pl.BlockSpec(memory_space=VMEM)] * (5 + parts + len(extra)),
        out_specs=[pl.BlockSpec(memory_space=VMEM)] * (1 + parts),
        scratch_shapes=[
            pltpu.VMEM((keys, width), BF16),
            pltpu.VMEM((keys, HEAD_SIZE), F32),
            pltpu.VMEM((keys, HEAD_SIZE), F32),
            pltpu.VMEM((256, HEAD_SIZE), F32),
        ],
        compiler_params=pltpu.CompilerParams(vmem_limit_bytes=12 * 2**20 + keys * 2816),
        cost_estimate=LIGHT,
    )(offsets, *tiles, queries, start_rows, inverse, attended, grads, *kv_parts, *extra)


def shape_kernel(raw_ref, cos_ref, sin_ref, gain_ref, q_ref, kv_ref):
    cosine = cos_ref[...]
    sine = sin_ref[...]

    def shaped(first, gain):
        value = raw_ref[:, first : first + HEAD_SIZE]
        mean_square = jnp.mean(value * value, axis=-1, keepdims=True)
        value = value * lax.rsqrt(mean_square + EPSILON) * gain
        return value * cosine + pltpu.roll(value, HEAD_SIZE // 2, 1) * sine

    for head in range(2):
        columns = slice(head * HEAD_SIZE, (head + 1) * HEAD_SIZE)
        q_ref[:, columns] = (shaped(head * HEAD_SIZE, gain_ref[0:1, :]) * HEAD_SIZE**-0.5).astype(BF16)
    kv_ref[:, :HEAD_SIZE] = shaped(2 * HEAD_SIZE, gain_ref[1:2, :]).astype(BF16)
    kv_ref[:, HEAD_SIZE:] = raw_ref[:, 3 * HEAD_SIZE :].astype(BF16)


def shape_back_kernel(raw_ref, grad_ref, cos_ref, sin_ref, gain_ref, low_ref, gain_grad_ref, *, heads, gain_row, factor):
    @pl.when(pl.program_id(0) == 0)
    def _():
        gain_grad_ref[...] = jnp.zeros_like(gain_grad_ref)

    cosine = cos_ref[...]
    sine = sin_ref[...]
    gain = gain_ref[gain_row : gain_row + 1, :]
    total = jnp.zeros((8, HEAD_SIZE), F32)
    for head in range(heads):
        columns = slice(head * HEAD_SIZE, (head + 1) * HEAD_SIZE)
        value = raw_ref[:, columns]
        grad = grad_ref[:, columns].astype(F32) * factor
        grad = grad * cosine - pltpu.roll(grad, HEAD_SIZE // 2, 1) * sine
        rho = lax.rsqrt(jnp.mean(value * value, axis=-1, keepdims=True) + EPSILON)
        unit = value * rho
        total = total + jnp.sum((grad * unit).reshape(-1, 8, HEAD_SIZE), axis=0)
        scaled = grad * gain
        inner = jnp.mean(scaled * unit, axis=-1, keepdims=True)
        low_ref[:, columns] = (rho * (scaled - unit * inner)).astype(BF16)
    if heads == 1:
        low_ref[:, HEAD_SIZE:] = grad_ref[:, HEAD_SIZE:].astype(BF16)
    gain_grad_ref[...] += total


ROW_TILE = 256


def shape_heads(raw, cosine, sine, gains):
    rows = raw.shape[0]
    block = lambda width: pl.BlockSpec((ROW_TILE, width), lambda i: (i, 0))
    return pl.pallas_call(
        shape_kernel,
        name="shape_heads",
        grid=(rows // ROW_TILE,),
        out_shape=(jax.ShapeDtypeStruct((rows, 256), BF16), jax.ShapeDtypeStruct((rows, 256), BF16)),
        in_specs=[block(512), block(128), block(128), pl.BlockSpec((2, 128), lambda i: (0, 0))],
        out_specs=[block(256), block(256)],
        compiler_params=pltpu.CompilerParams(vmem_limit_bytes=8 * 2**20),
        cost_estimate=LIGHT,
    )(raw, cosine, sine, gains)


def shape_back(raw, grads, cosine, sine, gains, heads, column, gain_row, factor):
    rows = raw.shape[0]
    block = lambda width, at=0: pl.BlockSpec((ROW_TILE, width), lambda i: (i, at))
    return pl.pallas_call(
        functools.partial(shape_back_kernel, heads=heads, gain_row=gain_row, factor=factor),
        name="shape_back",
        grid=(rows // ROW_TILE,),
        out_shape=(jax.ShapeDtypeStruct((rows, 256), BF16), jax.ShapeDtypeStruct((8, 128), F32)),
        in_specs=[
            block(heads * 128, column),
            block(256),
            block(128),
            block(128),
            pl.BlockSpec((2, 128), lambda i: (0, 0)),
        ],
        out_specs=[block(256), pl.BlockSpec((8, 128), lambda i: (0, 0))],
        compiler_params=pltpu.CompilerParams(vmem_limit_bytes=8 * 2**20),
        cost_estimate=LIGHT,
    )(raw, grads, cosine, sine, gains)


def reorder_kernel(order_ref, *refs):
    half = len(refs) // 2
    for source, target in zip(refs[:half], refs[half:]):
        target[...] = source[...].astype(target.dtype)


def reorder(order, values, types):
    rows, width = values[0].shape
    blocks = order.shape[0]
    size = width // blocks
    taken = pl.BlockSpec((rows, size), lambda i, order_ref: (0, order_ref[i]))
    put = pl.BlockSpec((rows, size), lambda i, order_ref: (0, i))
    return pl.pallas_call(
        reorder_kernel,
        name="reorder",
        grid_spec=pltpu.PrefetchScalarGridSpec(
            num_scalar_prefetch=1,
            grid=(blocks,),
            in_specs=[taken] * len(values),
            out_specs=[put] * len(values),
        ),
        out_shape=[jax.ShapeDtypeStruct(value.shape, kind) for value, kind in zip(values, types)],
        compiler_params=pltpu.CompilerParams(vmem_limit_bytes=8 * 2**20),
        cost_estimate=LIGHT,
    )(order, *values)


def assemble_kernel(at_ref, *refs, entries, axis):
    out_ref = refs[-1]
    for source, (place, kind) in zip(refs[:-1], entries):
        size = source.shape[axis]
        if kind == 0:
            span = slice(place, place + size)
        else:
            at = at_ref[0] if kind > 0 else 1 - at_ref[0]
            span = pl.ds(pl.multiple_of(place + at * 256, 16 if axis == 0 else 128), size)
        if axis == 0:
            out_ref[span, :] = source[...]
        else:
            out_ref[:, span] = source[...]


def assemble(at, parts, axis):
    values = [value for value, unused, kind in parts]
    total = sum(value.shape[axis] for value in values)
    other = values[0].shape[1 - axis]
    shape = (total, other) if axis == 0 else (other, total)
    return pl.pallas_call(
        functools.partial(assemble_kernel, entries=tuple((place, kind) for unused, place, kind in parts), axis=axis),
        name="assemble",
        out_shape=jax.ShapeDtypeStruct(shape, BF16),
        in_specs=[pl.BlockSpec(memory_space=SMEM)] + [pl.BlockSpec(memory_space=VMEM)] * len(values),
        out_specs=pl.BlockSpec(memory_space=VMEM),
        compiler_params=pltpu.CompilerParams(vmem_limit_bytes=12 * 2**20),
        cost_estimate=LIGHT,
    )(at, *values)


def terms_kernel(left_ref, right_ref, left_cols_ref, right_cols_ref, kept_ref, given_ref):
    total = contract_cols(left_ref[...], left_cols_ref[...]) + contract_cols(right_ref[...], right_cols_ref[...])
    middle = kept_ref.shape[0]
    kept_ref[...] = total[:middle]
    given_ref[...] = total[middle:].astype(BF16)


def two_terms(left, right, left_cols, right_cols):
    rows, depth = left.shape
    width = left_cols.shape[0]
    tile = 512
    value = pl.BlockSpec((rows, depth), lambda i: (0, 0))
    cols = pl.BlockSpec((tile, depth), lambda i: (i, 0))
    half = pl.BlockSpec((rows // 2, tile), lambda i: (0, i))
    return pl.pallas_call(
        terms_kernel,
        name="two_terms",
        grid=(width // tile,),
        out_shape=(jax.ShapeDtypeStruct((rows // 2, width), F32), jax.ShapeDtypeStruct((rows // 2, width), BF16)),
        in_specs=[value, value, cols, cols],
        out_specs=(half, half),
        cost_estimate=LIGHT,
    )(left, right, left_cols, right_cols)


def hidden_kernel(mine_ref, theirs_ref, gate_ref, up_ref, hidden_ref, gate_slope_ref, up_slope_ref):
    middle = mine_ref.shape[0]
    for part, source in ((slice(0, middle), mine_ref), (slice(middle, 2 * middle), theirs_ref)):
        rows = source[...]
        gate = matmul(rows, gate_ref[...])
        up = matmul(rows, up_ref[...])
        sig = 1.0 / (1.0 + jnp.exp(-gate))
        silu = gate * sig
        hidden_ref[part, :] = (silu * up).astype(BF16)
        gate_slope_ref[part, :] = (up * (sig * (1.0 + gate * (1.0 - sig)))).astype(BF16)
        up_slope_ref[part, :] = silu.astype(BF16)


def hidden_units(mine, theirs, gate_cols, up_cols):
    middle, width = mine.shape
    units = gate_cols.shape[1]
    tile = 256
    whole = pl.BlockSpec((middle, width), lambda i: (0, 0))
    cols = pl.BlockSpec((width, tile), lambda i: (0, i))
    out = pl.BlockSpec((2 * middle, tile), lambda i: (0, i))
    return pl.pallas_call(
        hidden_kernel,
        name="hidden_units",
        grid=(units // tile,),
        out_shape=(jax.ShapeDtypeStruct((2 * middle, units), BF16),) * 3,
        in_specs=[whole, whole, cols, cols],
        out_specs=(out,) * 3,
        cost_estimate=LIGHT,
    )(mine, theirs, gate_cols, up_cols)


def prologue_kernel(
    order_ref, at_ref, tokens_ref, grad_ref, q_ref, k_ref, v_ref, norm_ref, mlp_ref, q_gain_ref, k_gain_ref,
    tokens_out, grad_out, keep_ref, give_ref
):
    size = tokens_ref.shape[1] // 8
    for block in range(8):
        source = pl.ds(pl.multiple_of(order_ref[block] * size, 128), size)
        tokens_out[:, block * size : (block + 1) * size] = tokens_ref[:, source]
        grad_out[:, block * size : (block + 1) * size] = grad_ref[:, source]

    rows, q_width = q_ref.shape[0], q_ref.shape[1] // 2
    k_width = k_ref.shape[1] // 2
    total = q_width + 2 * k_width
    small = q_gain_ref.shape[1]
    place = lax.broadcasted_iota(jnp.int32, (small, HEAD_SIZE), 1) - lax.broadcasted_iota(
        jnp.int32, (small, HEAD_SIZE), 0
    )
    put = (place == at_ref[1] * small).astype(BF16)
    extra = jnp.concatenate(
        [
            jnp.concatenate([norm_ref[...], mlp_ref[...]], axis=1),
            jnp.concatenate(
                [
                    matmul(q_gain_ref[...], put).astype(BF16),
                    matmul(k_gain_ref[...], put).astype(BF16),
                    jnp.zeros((1, total - 2 * HEAD_SIZE), BF16),
                ],
                axis=1,
            ),
            jnp.zeros((14, total), BF16),
        ],
        axis=0,
    )
    for target, at in ((keep_ref, at_ref[0]), (give_ref, 1 - at_ref[0])):
        target[:rows, :q_width] = q_ref[:, pl.ds(pl.multiple_of(at * q_width, 128), q_width)]
        target[:rows, q_width : q_width + k_width] = k_ref[:, pl.ds(pl.multiple_of(at * k_width, 128), k_width)]
        target[:rows, q_width + k_width :] = v_ref[:, pl.ds(pl.multiple_of(at * k_width, 128), k_width)]
        target[rows:, :] = extra


def prologue(order, at, tokens, out_grad, q_weight, k_weight, v_weight, gains):
    shape = jax.ShapeDtypeStruct((q_weight.shape[0] + 16, (q_weight.shape[1] + 2 * k_weight.shape[1]) // 2), BF16)
    whole = lambda value: pl.BlockSpec(value.shape, lambda i, order_ref, at_ref: (0, 0))
    fixed = (q_weight, k_weight, v_weight) + gains
    return pl.pallas_call(
        prologue_kernel,
        name="prologue",
        grid_spec=pltpu.PrefetchScalarGridSpec(
            num_scalar_prefetch=2,
            grid=(1,),
            in_specs=[whole(tokens), whole(out_grad)] + [whole(value) for value in fixed],
            out_specs=[whole(tokens), whole(tokens), whole(shape), whole(shape)],
        ),
        out_shape=(jax.ShapeDtypeStruct(tokens.shape, BF16),) * 2 + (shape, shape),
        cost_estimate=LIGHT,
    )(order, at, tokens, out_grad, *fixed)


def after(token, values):
    return lax.optimization_barrier((token, values))[1]


def meet(token, values):
    return lax.optimization_barrier((token, values))


def trade(token, sends):
    held = after(token, [value for value, unused in sends])
    return [swap(value, axis) for value, (unused, axis) in zip(held, sends)]


def places_of(query_tile, key_tile, seq_lengths, tok_dev):
    rows = query_tile.shape[0] * tok_dev
    tile_ids = jnp.arange(key_tile.shape[0], dtype=jnp.int32)
    shares = (tile_ids // 16) * 8 + tile_ids % 8
    found = key_tile[None, :] == tile_ids[:, None]

    def offsets_of(parity):
        mine = found & (tile_ids // 8 % 2 == parity)[None, :]
        return jnp.sum(jnp.where(mine, shares * tok_dev + 1, 0), axis=1, dtype=jnp.int32) - 1

    offsets = (offsets_of(0), offsets_of(1))
    natural = query_tile[:, None] * tok_dev + jnp.arange(tok_dev, dtype=jnp.int32)[None, :]
    seq_ids = jnp.arange(seq_lengths.shape[0], dtype=jnp.int32)
    seq_ends = jnp.sum(jnp.where(seq_ids[None, :] <= seq_ids[:, None], seq_lengths[None, :], 0), axis=1, dtype=jnp.int32)
    starts = jnp.max(jnp.where(seq_ends <= natural[..., None], seq_ends, 0), axis=-1)
    tiles = (query_tile, jnp.max(jnp.where(seq_ends <= (query_tile * tok_dev)[:, None], seq_ends, 0), axis=-1) // (2 * tok_dev))
    start_rows = jnp.stack([starts, starts], axis=1)
    start_cols = jnp.broadcast_to(starts.reshape(rows, 1), (rows, 128))
    places = (natural - starts).reshape(rows)
    half_width = HEAD_SIZE // 2
    frequency = jnp.power(ROPE_BASE, -jnp.arange(half_width, dtype=F32) * (2.0 / HEAD_SIZE))
    angles = places.astype(F32)[:, None] * frequency[None, :]
    cosine = jnp.cos(angles)
    sine = jnp.sin(angles)
    cosine = jnp.concatenate([cosine, cosine], axis=1)
    sine = jnp.concatenate([-sine, sine], axis=1)
    return offsets, tiles, start_rows, start_cols, cosine, sine


FAR = 96
KEEP_ROWS = 128
UP_ROWS = 96


def paired_layer(
    tokens,
    out_grad,
    seq_lengths,
    block_deal,
    norm_gain,
    q_weight,
    k_weight,
    v_weight,
    q_gain,
    k_gain,
    o_weight,
    mlp_gain,
    gate_weight,
    up_weight,
    down_weight,
):
    y_at, core_at, zb_at, za_at, x_at = (lax.axis_index(name) for name in ("y", "core", "zb", "za", "x"))
    tok_dev, width = tokens.shape
    blk_rows = q_weight.shape[0]
    rows = 8 * tok_dev
    middle = rows // 2
    half, quarter = width // 2, width // 4
    token = seq_lengths


    place_ids = jnp.arange(8, dtype=jnp.int32)
    to_order = ((zb_at ^ (place_ids // 2 % 2)) * 2 + place_ids % 2) * 2 + (x_at ^ (place_ids // 4))
    from_order = ((x_at ^ (place_ids % 2)) * 2 + (zb_at ^ (place_ids // 4))) * 2 + place_ids // 2 % 2

    def in_order(mine, other, axis):
        first = jnp.where(za_at == 0, mine, other)
        second = jnp.where(za_at == 0, other, mine)
        return jnp.concatenate([first, second], axis=axis)

    def half_of(weight, at, axis):
        size = weight.shape[axis] // 2
        return lax.dynamic_slice_in_dim(weight, at * size, size, axis=axis)


    def near(value):
        return [(value, "y"), (value, "za")]

    def far(from_y, from_z, rows_y):
        sends = [(from_z[:rows_y], "y")]
        return sends + ([(from_y[rows_y:], "za")] if rows_y < tok_dev else [])

    def mine_of(value, from_y, from_z, fars):
        return jnp.concatenate([value, from_y, from_z] + fars, axis=0)

    def far_sums(kept):
        return [(kept[3 * tok_dev :].astype(BF16), "y")]

    def near_sums(kept, from_y):
        to_y, to_z = kept[tok_dev : 2 * tok_dev], kept[2 * tok_dev : 3 * tok_dev] + from_y.astype(F32)
        return [(to_y.astype(BF16), "y"), (to_z.astype(BF16), "za")]

    def own_sum(kept, nears):
        return kept[:tok_dev] + nears[0].astype(F32) + nears[1].astype(F32)


    def za_parts(part, axis):
        first = lax.slice_in_dim(part, 0, blk_rows, axis=axis)
        second = lax.slice_in_dim(part, blk_rows, 2 * blk_rows, axis=axis)
        return jnp.where(za_at == 0, first, second), jnp.where(za_at == 0, second, first).astype(BF16)

    def za_join(mine, other):
        other = other.astype(F32)
        return [jnp.where(za_at == 0, mine, other), jnp.where(za_at == 0, other, mine)]


    member = jnp.arange(8, dtype=jnp.int32)
    member_y, member_za, member_core = y_at ^ (member % 2), za_at ^ (member // 2 % 2), core_at ^ (member // 4)
    group = jnp.arange(4, dtype=jnp.int32)
    span_table = jnp.arange(block_deal.shape[0], dtype=jnp.int32)

    def natural_tile(zb_of, x_of):
        entry = 2 * ((zb_of * 2 + member_za) * 2 + x_of) + member_y
        span = jnp.sum(jnp.where(entry[..., None] == span_table, block_deal, 0), axis=-1, dtype=jnp.int32)
        return span * 2 + member_core

    query_tile = natural_tile(zb_at, x_at)
    key_tile = natural_tile(zb_at ^ (group % 2)[:, None], x_at ^ (group // 2)[:, None]).reshape(-1)
    offsets, tiles, start_rows, start_cols, cosine, sine = places_of(query_tile, key_tile, seq_lengths, tok_dev)


    q_width, k_width = q_weight.shape[1] // 2, k_weight.shape[1] // 2
    qkv_width = q_width + 2 * k_width
    local_low, grad_local, qkv_keep, qkv_give = prologue(
        to_order,
        jnp.stack([za_at, (zb_at * 2 + za_at) * 2 + x_at]),
        tokens,
        out_grad,
        q_weight,
        k_weight,
        v_weight,
        (norm_gain[None], mlp_gain[None], q_gain[None], k_gain[None]),
    )
    local_rows = local_low.astype(F32)
    o_give = half_of(o_weight, 1 - za_at, 0)
    za_place = za_at[None].astype(jnp.int32)
    z_keep, qkv_far, x_keep = swap(qkv_keep, "zb"), swap(qkv_give, "za"), swap(qkv_keep, "x")
    tokens_y = swap(local_low, "y")
    (o_far,) = trade(qkv_keep, [(o_give, "za")])
    token, (qkv_far, z_keep, x_keep, tokens_y, o_far) = meet(token, (qkv_far, z_keep, x_keep, tokens_y, o_far))
    down_keep = half_of(down_weight, za_at, 0)
    tokens_z, z_far, xz_keep, x_far, down_xk = trade(
        token, [(local_low, "za"), (qkv_far, "zb"), (z_keep, "x"), (qkv_far, "x"), (down_keep, "x")]
    )
    o_pair = in_order(half_of(o_weight, za_at, 0), o_far, 1)
    token, (z_far, tokens_z, xz_keep, x_far, o_pair, down_xk) = meet(
        token, (z_far, tokens_z, xz_keep, x_far, o_pair, down_xk)
    )
    *fars, xz_far, o_x, o_z = trade(
        token, far(tokens_y, tokens_z, FAR) + [(z_far, "x"), (o_pair, "x"), (o_pair, "zb")]
    )
    gate_weight, up_weight, down_weight = after(token, (gate_weight, up_weight, down_weight))
    gate_keep, up_keep = half_of(gate_weight, za_at, 1), half_of(up_weight, za_at, 1)
    gate_give, up_give = half_of(gate_weight, 1 - za_at, 1), half_of(up_weight, 1 - za_at, 1)
    down_give = half_of(down_weight, 1 - za_at, 0)
    token, (xz_far, fars, o_x, o_z) = meet(token, (xz_far, fars, o_x, o_z))
    mine = mine_of(local_low, tokens_y, tokens_z, fars)
    theirs, gate_zk0, gate_far, gate_xk = trade(
        token, [(mine, "core"), (gate_keep[:KEEP_ROWS], "zb"), (gate_give, "za"), (gate_keep, "x")]
    )
    qkv_all = jnp.concatenate(
        [
            in_order(qkv_keep, qkv_far, 0),
            in_order(z_keep, z_far, 0),
            in_order(x_keep, x_far, 0),
            in_order(xz_keep, xz_far, 0),
        ],
        axis=0,
    ).reshape(8, blk_rows + 16, qkv_width)
    qkv_cols = qkv_all[:, :blk_rows].reshape(width, qkv_width)
    gains = qkv_all[:, blk_rows, : 2 * blk_rows].astype(F32)
    gain_one = gains[:, :blk_rows].reshape(1, width)
    gain_two = gains[:, blk_rows:].reshape(1, width)
    head_sum = jnp.sum(qkv_all[:, blk_rows + 1, : 2 * HEAD_SIZE].astype(F32), axis=0, keepdims=True)
    qk_gains = jnp.concatenate([head_sum[:, :HEAD_SIZE], head_sum[:, HEAD_SIZE:]], axis=0)


    input_rows = jnp.concatenate([mine, theirs], axis=0).astype(F32)
    input_rho = lax.rsqrt(jnp.mean(input_rows * input_rows, axis=-1, keepdims=True) + EPSILON)
    normed = (input_rows * input_rho * gain_one).astype(BF16)
    raw = matmul(normed, qkv_cols)
    queries, kv_own = shape_heads(raw, cosine, sine, qk_gains)
    token, (queries, kv_own, gate_zk0, gate_far, gate_xk) = meet(
        token, (queries, kv_own, gate_zk0, gate_far, gate_xk)
    )
    kv_z, kv_x, up_far, grads_y = trade(
        token, [(kv_own, "zb"), (kv_own, "x"), (up_give, "za"), (grad_local, "y")]
    )
    token, (kv_x,) = meet(token, (kv_x,))
    (o_xz,) = trade(token, [(o_z, "x")])
    (attn_part,) = attend(offsets[0], tiles, queries, start_cols, [kv_own, kv_x], last=False)
    gate_pair = in_order(gate_keep, gate_far, 0)
    token, (kv_z, attn_part, grads_y, o_xz, up_far, gate_pair) = meet(
        token, (kv_z, attn_part, grads_y, o_xz, up_far, gate_pair)
    )
    gate_rest = jnp.concatenate([gate_keep[KEEP_ROWS:], gate_far], axis=0)
    token, (gate_rest,) = meet(token, (gate_rest,))
    kv_xz, gate_zr, grads_z = trade(token, [(kv_z, "x"), (gate_rest, "zb"), (grad_local, "za")])
    o_cols = jnp.concatenate([o_pair, o_z, o_x, o_xz], axis=1)
    token, (kv_xz, o_cols) = meet(token, (kv_xz, o_cols))
    (gate_xf,) = trade(token, [(gate_far, "x")])
    attn_low, inverse = attend(offsets[1], tiles, queries, start_cols, [kv_z, kv_xz], before=attn_part)
    given = matmul(attn_low[middle:], o_cols).astype(BF16)
    token, (given, attn_low, gate_xf, gate_zr, grads_z) = meet(token, (given, attn_low, gate_xf, gate_zr, grads_z))
    up_pair = in_order(up_keep, up_far, 0)
    given, up_z0, up_x0, grads_far, down_far = trade(
        token,
        [(given, "core"), (up_pair[:UP_ROWS], "zb"), (up_pair[:blk_rows], "x"), (grads_z, "y"), (down_give, "za")],
    )
    kept = matmul(attn_low[:middle], o_cols)
    token, (given, kept, up_z0, up_x0, up_pair, grads_far, down_far) = meet(
        token, (given, kept, up_z0, up_x0, up_pair, grads_far, down_far)
    )
    grad_mine = mine_of(grad_local, grads_y, grads_z, [grads_far])
    kept = kept + given.astype(F32)
    from_y, up_z1, up_x1 = trade(
        token,
        far_sums(kept) + [(up_pair[UP_ROWS:blk_rows], "zb"), (up_pair[blk_rows:], "x")],
    )
    gate_z = assemble(
        za_place,
        [
            (gate_zk0, 0, 1),
            (gate_zr[: blk_rows - KEEP_ROWS], KEEP_ROWS, 1),
            (gate_zr[blk_rows - KEEP_ROWS :], 0, -1),
        ],
        0,
    )
    token, (from_y, kept, up_x1, gate_z, up_z1, grad_mine) = meet(
        token, (from_y, kept, up_x1, gate_z, up_z1, grad_mine)
    )
    *nears, gate_xz, up_z2, grad_theirs = trade(
        token, near_sums(kept, from_y) + [(gate_z, "x"), (up_pair[blk_rows:], "zb"), (grad_mine, "core")]
    )
    token, (nears, kept, gate_xz, up_z2, grad_theirs) = meet(token, (nears, kept, gate_xz, up_z2, grad_theirs))
    up_z01 = jnp.concatenate([up_z0, up_z1], axis=0)
    residual = local_rows + own_sum(kept, nears)


    rho_two = lax.rsqrt(jnp.mean(residual * residual, axis=-1, keepdims=True) + EPSILON)
    unit_two = residual * rho_two
    mlp_low = (unit_two * gain_two).astype(BF16)
    token, (mlp_low,) = meet(token, (mlp_low,))
    mlp_y, mlp_z, down_zk, down_xf, up_xz0 = trade(
        token, near(mlp_low) + [(down_keep, "zb"), (down_far, "x"), (up_z01, "x")]
    )
    gate_cols = assemble(
        za_place,
        [(gate_pair, 0, 0), (gate_z, quarter, 0), (gate_xk, half, 1), (gate_xf, half, -1)]
        + [(gate_xz, half + quarter, 0)],
        0,
    )
    grad_mine, grad_theirs = after(token, (grad_mine, grad_theirs))
    grad_rows = assemble(za_place, [(grad_mine, 0, 0), (grad_theirs, middle, 0)], 0)
    token, (mlp_y, mlp_z, down_xf, up_xz0, gate_cols, down_zk, grad_rows) = meet(
        token, (mlp_y, mlp_z, down_xf, up_xz0, gate_cols, down_zk, grad_rows)
    )
    *fars, up_xz1, down_zf0 = trade(token, far(mlp_y, mlp_z, FAR) + [(up_z2, "x"), (down_far[:400], "zb")])
    token, (fars, down_zf0, up_xz1) = meet(token, (fars, down_zf0, up_xz1))
    mlp_mine = mine_of(mlp_low, mlp_y, mlp_z, fars)
    mlp_theirs, down_zf1, down_xzk, down_xzf0 = trade(
        token, [(mlp_mine, "core"), (down_far[400:], "zb"), (down_zk, "x"), (down_zf0, "x")]
    )
    up_cols = assemble(
        za_place,
        [
            (up_pair, 0, 0),
            (up_z01, quarter, 0),
            (up_z2, quarter + blk_rows, 0),
            (up_x0, half, 0),
            (up_x1, half + blk_rows, 0),
            (up_xz0, half + quarter, 0),
            (up_xz1, half + quarter + blk_rows, 0),
        ],
        0,
    )
    token, (mlp_theirs, up_cols, down_zf1, down_xzk, down_xzf0) = meet(
        token, (mlp_theirs, up_cols, down_zf1, down_xzk, down_xzf0)
    )
    (down_xzf1,) = trade(token, [(down_zf1, "x")])
    mlp_rows = jnp.concatenate([mlp_mine, mlp_theirs], axis=0)
    gate_act = matmul(mlp_rows, gate_cols)
    token, (gate_act, up_cols, mlp_rows) = meet(token, (gate_act, up_cols, mlp_rows))
    sig = jax.nn.sigmoid(gate_act)
    silu = gate_act * sig
    slope = sig * (1.0 + gate_act * (1.0 - sig))
    up_slope = silu.astype(BF16)
    token, (silu, slope, up_slope, up_cols, mlp_rows) = meet(token, (silu, slope, up_slope, up_cols, mlp_rows))
    up_act = matmul(mlp_rows, up_cols)
    hidden = (silu * up_act).astype(BF16)
    gate_slope = (up_act * slope).astype(BF16)
    down_zf = jnp.concatenate([down_zf0, down_zf1], axis=0)
    token, (hidden, gate_slope, up_slope, grad_rows, down_xzf1, down_zf) = meet(
        token, (hidden, gate_slope, up_slope, grad_rows, down_xzf1, down_zf)
    )
    down_xzf = jnp.concatenate([down_xzf0, down_xzf1], axis=0)

    def columns_of(value, piece):
        return value[:, piece * quarter : (piece + 1) * quarter]

    down_cols = assemble(
        za_place,
        [
            (down_keep, 0, 1),
            (down_far, 0, -1),
            (down_zk, quarter, 1),
            (down_zf, quarter, -1),
            (down_xk, half, 1),
            (down_xf, half, -1),
            (down_xzk, half + quarter, 1),
            (down_xzf, half + quarter, -1),
        ],
        1,
    )
    down_3 = contract_rows(hidden, columns_of(grad_rows, 3)).astype(BF16)
    token, (down_3, down_cols) = meet(token, (down_3, down_cols))
    (down_3,) = trade(token, [(down_3, "x")])
    hidden_grad = contract_cols(grad_rows, down_cols)
    gate_low = (hidden_grad * gate_slope.astype(F32)).astype(BF16)
    up_low = (hidden_grad * up_slope.astype(F32)).astype(BF16)

    kept, given = two_terms(gate_low, up_low, gate_cols, up_cols)
    token, (kept, given, gate_low, up_low, down_3) = meet(token, (kept, given, gate_low, up_low, down_3))
    hidden, grad_rows = after(token, (hidden, grad_rows))
    down_1 = (contract_rows(hidden, columns_of(grad_rows, 1)) + down_3.astype(F32)).astype(BF16)
    given, down_1a = trade(token, [(given, "core"), (down_1[:144], "zb")])
    gate_3 = contract_rows(columns_of(mlp_rows, 3), gate_low).astype(BF16)
    token, (given, kept, down_1, down_1a, gate_3) = meet(token, (given, kept, down_1, down_1a, gate_3))
    kept = kept + given.astype(F32)
    token, (kept,) = meet(token, (kept,))
    from_y, down_1b, gate_3 = trade(token, far_sums(kept) + [(down_1[144:416], "zb"), (gate_3, "x")])
    down_2 = contract_rows(hidden, columns_of(grad_rows, 2)).astype(BF16)
    up_3 = contract_rows(columns_of(mlp_rows, 3), up_low).astype(BF16)
    gate_1 = contract_rows(columns_of(mlp_rows, 1), gate_low)
    token, (from_y, kept, down_1b, gate_3, down_2, up_3, gate_1) = meet(
        token, (from_y, kept, down_1b, gate_3, down_2, up_3, gate_1)
    )
    *nears, down_1c, up_3 = trade(token, near_sums(kept, from_y) + [(down_1[416:], "zb"), (up_3, "x")])
    gate_1 = (gate_1 + gate_3.astype(F32)).astype(BF16)
    gate_2 = contract_rows(columns_of(mlp_rows, 2), gate_low).astype(BF16)
    up_1 = contract_rows(columns_of(mlp_rows, 1), up_low)
    up_2 = contract_rows(columns_of(mlp_rows, 2), up_low).astype(BF16)
    token, (nears, kept, down_1c, up_3, gate_2, up_1, up_2, gate_1) = meet(
        token, (nears, kept, down_1c, up_3, gate_2, up_1, up_2, gate_1)
    )
    mlp_in_grad = own_sum(kept, nears)
    gain_two_part = jnp.sum(mlp_in_grad * unit_two, axis=0, keepdims=True)
    scaled = mlp_in_grad * gain_two
    inner = jnp.mean(scaled * unit_two, axis=-1, keepdims=True)
    residual_grad = grad_local.astype(F32) + rho_two * (scaled - unit_two * inner)


    branch_low = residual_grad.astype(BF16)
    token, (branch_low, residual_grad, gain_two_part, gate_1) = meet(
        token, (branch_low, residual_grad, gain_two_part, gate_1)
    )
    branch_y, branch_z, gate_1a, gate_2 = trade(
        token, near(branch_low) + [(gate_1[:blk_rows], "zb"), (gate_2, "x")]
    )
    hidden, down_cols = after(token, (hidden, down_cols))
    out_given = matmul(hidden[middle:], down_cols).astype(BF16)
    up_1 = (up_1 + up_3.astype(F32)).astype(BF16)
    down_0 = contract_rows(hidden, columns_of(grad_rows, 0)) + jnp.concatenate(
        [down_1a, down_1b, down_1c], axis=0
    ).astype(F32)
    token, (branch_y, branch_z, gate_1a, gate_2, out_given, up_1, down_0, gate_low, up_low) = meet(
        token, (branch_y, branch_z, gate_1a, gate_2, out_given, up_1, down_0, gate_low, up_low)
    )
    gate_0 = contract_rows(columns_of(mlp_rows, 0), gate_low) + gate_2.astype(F32)
    *fars, gate_1b, down_2a = trade(
        token, far(branch_y, branch_z, FAR) + [(gate_1[blk_rows:384], "zb"), (down_2[:384], "x")]
    )
    hidden, down_cols = after(token, (hidden, down_cols))
    out_kept = matmul(hidden[:middle], down_cols)
    token, (fars, out_kept, gate_1b, down_2a, gate_0) = meet(token, (fars, out_kept, gate_1b, down_2a, gate_0))
    branch_mine = mine_of(branch_low, branch_y, branch_z, fars)
    branch_theirs, gate_1c, down_2b, out_given = trade(
        token,
        [(branch_mine, "core"), (gate_1[384:464], "zb"), (down_2[384:512], "x"), (out_given, "core")],
    )
    grad_own = contract_cols(branch_mine, o_cols).astype(BF16)
    attn_grad = jnp.concatenate([grad_own, contract_cols(branch_theirs, o_cols).astype(BF16)], axis=0)
    mixed = jnp.concatenate([gate_1[464:], up_1[:144]], axis=0)
    token, (attn_grad, gate_1c, down_2b, mixed) = meet(token, (attn_grad, gate_1c, down_2b, mixed))
    mixed, up_2a, down_2c = trade(token, [(mixed, "zb"), (up_2[:blk_rows], "x"), (down_2[512:], "x")])
    query_part, kv_1, kv_3 = attend_back(
        offsets[1], tiles, queries, start_rows, inverse, attn_low, attn_grad, [kv_z, kv_xz], last=False
    )
    out_kept = out_kept + out_given.astype(F32)
    token, (query_part, kv_1, kv_3, mixed, up_2a, down_2c, out_kept) = meet(
        token, (query_part, kv_1, kv_3, mixed, up_2a, down_2c, out_kept)
    )
    gate_1d, up_1a = mixed[:48], mixed[48:]
    kv_3, up_1b, out_from = trade(token, [(kv_3, "x"), (up_1[144:336], "zb")] + far_sums(out_kept))
    query_grad, kv_0, kv_2 = attend_back(
        offsets[0],
        tiles,
        queries,
        start_rows,
        inverse,
        attn_low,
        attn_grad,
        [kv_own, kv_x],
        before=query_part,
    )
    token, (query_grad, kv_0, kv_2, kv_3, up_1b, out_from) = meet(
        token, (query_grad, kv_0, kv_2, kv_3, up_1b, out_from)
    )
    kv_1 = (kv_1.astype(F32) + kv_3.astype(F32)).astype(BF16)
    kv_1, kv_2, *out_nears = trade(token, [(kv_1, "zb"), (kv_2, "x")] + near_sums(out_kept, out_from))
    token, (kv_2, branch_mine, branch_theirs, up_low, query_grad, gate_0, down_0) = meet(
        token, (kv_2, branch_mine, branch_theirs, up_low, query_grad, gate_0, down_0)
    )
    q_low, q_gain_part = shape_back(raw, query_grad, cosine, sine, qk_gains, 2, 0, 0, HEAD_SIZE**-0.5)
    q_3 = swap(contract_rows(columns_of(normed, 3), q_low).astype(BF16), "x")
    branch_rows = jnp.concatenate([branch_mine, branch_theirs], axis=0)
    o_3 = contract_rows(attn_low, columns_of(branch_rows, 3)).astype(BF16)
    q_1 = contract_rows(columns_of(normed, 1), q_low)
    gate_part = gate_0 + jnp.concatenate([gate_1a, gate_1b, gate_1c, gate_1d], axis=0).astype(F32)
    gate_mine, gate_give = za_parts(gate_part, 0)
    down_part = down_0 + jnp.concatenate([down_2a, down_2b, down_2c], axis=0).astype(F32)
    down_mine, down_give = za_parts(down_part, 1)
    token, (kv_1, out_nears, q_low, q_gain_part, o_3, gate_mine, gate_give, down_mine, down_give, q_1) = meet(
        token, (kv_1, out_nears, q_low, q_gain_part, o_3, gate_mine, gate_give, down_mine, down_give, q_1)
    )
    gate_give, up_1c, down_give, up_2b = trade(
        token, [(gate_give, "za"), (up_1[336:], "zb"), (down_give, "za"), (up_2[blk_rows:], "x")]
    )
    kv_grad = (kv_0.astype(F32) + kv_1.astype(F32) + kv_2.astype(F32)).astype(BF16)
    kv_low, k_gain_part = shape_back(raw, kv_grad, cosine, sine, qk_gains, 1, 2, 1, 1.0)
    low = jnp.concatenate([q_low, kv_low], axis=1)
    given = contract_cols(low[middle:], qkv_cols).astype(BF16)
    w_3 = contract_rows(columns_of(normed, 3), kv_low).astype(BF16)
    q_1 = (q_1 + q_3.astype(F32)).astype(BF16)
    token, (given, low, kv_low, k_gain_part, w_3, q_1, gate_give, up_1c, up_2b) = meet(
        token, (given, low, kv_low, k_gain_part, w_3, q_1, gate_give, up_1c, up_2b)
    )
    given_low = given
    kv_late, normed, low = after(token, (kv_low, normed, low))
    given, q_1, w_3, o_3 = trade(token, [(given, "core"), (q_1, "zb"), (w_3, "x"), (o_3, "x")])
    terms = contract_cols(low[:middle], qkv_cols)
    w_1 = contract_rows(columns_of(normed, 1), kv_late)
    token, (given, terms, q_1, w_3, o_3, w_1, down_give, up_low, attn_low, branch_rows) = meet(
        token, (given, terms, q_1, w_3, o_3, w_1, down_give, up_low, attn_low, branch_rows)
    )
    kept = terms + given.astype(F32)
    w_1 = (w_1 + w_3.astype(F32)).astype(BF16)
    token, (kept, w_1) = meet(token, (kept, w_1))
    from_y, w_1 = trade(token, far_sums(kept) + [(w_1, "zb")])
    o_1 = (contract_rows(attn_low, columns_of(branch_rows, 1)) + o_3.astype(F32)).astype(BF16)
    o_2 = contract_rows(attn_low, columns_of(branch_rows, 2)).astype(BF16)
    terms_low, given_low, normed_low = after(token, (terms, given_low, normed))
    gain_one_part = (
        jnp.sum(
            terms_low * normed_low[:middle].astype(F32) + given_low.astype(F32) * normed_low[middle:].astype(F32),
            axis=0,
            keepdims=True,
        )
        / gain_one
    )
    gain_sum = jnp.concatenate(
        [
            *reorder(from_order, [gain_one_part, gain_two_part], [F32, F32]),
            jnp.sum(q_gain_part, axis=0, keepdims=True),
            jnp.sum(k_gain_part, axis=0, keepdims=True),
        ],
        axis=1,
    )
    qw_2 = contract_rows(columns_of(normed, 2), low).astype(BF16)
    token, (from_y, kept, w_1, o_1, qw_2, o_2, gain_sum, up_low, attn_low, branch_rows, low) = meet(
        token, (from_y, kept, w_1, o_1, qw_2, o_2, gain_sum, up_low, attn_low, branch_rows, low)
    )
    *nears, o_1, qw_2, gain_x = trade(
        token, near_sums(kept, from_y) + [(o_1, "zb"), (qw_2, "x"), (gain_sum, "core")]
    )
    gain_sum = gain_sum + gain_x
    gain_sum = gain_sum + swap(gain_sum, "zb")
    gate_mine, gate_give, down_mine, down_give = after(token, (gate_mine, gate_give, down_mine, down_give))
    up_part = (
        contract_rows(columns_of(mlp_rows, 0), up_low)
        + jnp.concatenate([up_2a, up_2b], axis=0).astype(F32)
        + jnp.concatenate([up_1a, up_1b, up_1c], axis=0).astype(F32)
    )
    up_mine, up_give = za_parts(up_part, 0)
    qw_0 = contract_rows(columns_of(normed, 0), low)
    o_0 = contract_rows(attn_low, columns_of(branch_rows, 0))
    block_out = residual + own_sum(out_kept, out_nears)
    token, (nears, kept, qw_2, qw_0, o_0, block_out, gain_sum, o_1, up_mine, up_give) = meet(
        token, (nears, kept, qw_2, qw_0, o_0, block_out, gain_sum, o_1, up_mine, up_give)
    )
    qkv_mine, qkv_give = za_parts(qw_0 + qw_2.astype(F32) + jnp.concatenate([q_1, w_1], axis=1).astype(F32), 0)
    token, (qkv_mine, qkv_give) = meet(token, (qkv_mine, qkv_give))
    gain_x, qkv_give, up_give, o_2 = trade(
        token, [(gain_sum, "za"), (qkv_give, "za"), (up_give, "za"), (o_2, "x")]
    )
    gain_sum = gain_sum + gain_x
    gain_x = swap(gain_sum, "y")
    o_mine, o_give = za_parts(o_0 + o_2.astype(F32) + o_1.astype(F32), 1)
    token, (gain_sum, o_mine, o_give) = meet(token, (gain_sum + gain_x, o_mine, o_give))
    gain_x, o_give = trade(token, [(gain_sum, "x"), (o_give, "za")])
    gain_sum = gain_sum + gain_x
    input_grad = own_sum(kept, nears)
    unit_one = local_rows * (rho_one := lax.rsqrt(jnp.mean(local_rows * local_rows, axis=-1, keepdims=True) + EPSILON))
    scaled = input_grad * gain_one
    inner = jnp.mean(scaled * unit_one, axis=-1, keepdims=True)
    in_grad = residual_grad + rho_one * (scaled - unit_one * inner)
    block_out, in_grad = reorder(from_order, [block_out, in_grad], [BF16, F32])
    device = (((y_at * 2 + core_at) * 2 + zb_at) * 2 + za_at) * 2 + x_at

    def own_slice(first, length):
        share = length // 32
        return lax.dynamic_slice_in_dim(gain_sum[0], first + device * share, share, axis=0)

    qkv_parts = za_join(qkv_mine, qkv_give)

    def columns(lo, hi):
        return jnp.concatenate([part[:, lo:hi] for part in qkv_parts], axis=1)

    return (
        block_out,
        in_grad,
        own_slice(0, width),
        columns(0, q_width),
        columns(q_width, q_width + k_width),
        columns(q_width + k_width, qkv_width),
        own_slice(2 * width, HEAD_SIZE),
        own_slice(2 * width + HEAD_SIZE, HEAD_SIZE),
        jnp.concatenate(za_join(o_mine, o_give), axis=0),
        own_slice(width, width),
        jnp.concatenate(za_join(gate_mine, gate_give), axis=1),
        jnp.concatenate(za_join(up_mine, up_give), axis=1),
        jnp.concatenate(za_join(down_mine, down_give), axis=0),
    )


def layer(
    sizes,
    tokens,
    out_grad,
    seq_lengths,
    block_deal,
    norm_gain,
    q_weight,
    k_weight,
    v_weight,
    q_gain,
    k_gain,
    o_weight,
    mlp_gain,
    gate_weight,
    up_weight,
    down_weight,
):
    y_count, core_count, zb_count, za_count, x_count = sizes
    pairwise = sizes == (2, 2, 2, 2, 2)
    all_axes = ("y", "core", "zb", "za", "x")
    y_at, core_at, zb_at, za_at, x_at = (lax.axis_index(name) for name in all_axes)
    tok_dev, width = tokens.shape
    blk_rows = q_weight.shape[0]
    group_count = zb_count * x_count
    member_count = y_count * core_count * za_count
    head_count = y_count * core_count
    rows = member_count * tok_dev
    piece = za_count * blk_rows


    def gather_rows(value):
        if not pairwise:
            return lax.all_gather(value, ("y", "core", "za"), axis=0, tiled=True)
        half = tok_dev // 2
        along_y = swap(value, "y")
        along_z = swap(value, "za")
        parts = [value, along_y, along_z, swap(along_z[:half], "y"), swap(along_y[half:], "za")]
        mine = jnp.concatenate(parts, axis=0)
        return jnp.concatenate([mine, swap(mine, "core")], axis=0)

    def scatter_rows(part_of):
        if not pairwise:
            full = part_of(slice(0, rows)).astype(BF16)
            return lax.psum_scatter(full, ("y", "core", "za"), scatter_dimension=0, tiled=True).astype(F32)
        middle = rows // 2
        half = tok_dev // 2
        given = swap(part_of(slice(middle, rows)).astype(BF16), "core")
        kept = part_of(slice(0, middle)) + given.astype(F32)
        own, to_y, to_z, far = (kept[i * tok_dev : (i + 1) * tok_dev] for i in range(4))
        far = far.astype(BF16)
        from_y = swap(far[:half], "y").astype(F32)
        from_z = swap(far[half:], "za").astype(F32)
        z_sum = jnp.concatenate([to_z[:half] + from_y, to_z[half:]], axis=0).astype(BF16)
        y_sum = jnp.concatenate([to_y[:half], to_y[half:] + from_z], axis=0).astype(BF16)
        return own + swap(y_sum, "y").astype(F32) + swap(z_sum, "za").astype(F32)


    def gather_pieces(own, axis):
        if not pairwise:
            return lax.all_gather(own, ("zb", "x"), axis=axis, tiled=True)
        along_z = swap(own, "zb")
        return jnp.concatenate([own, along_z, swap(own, "x"), swap(along_z, "x")], axis=axis)

    def scatter_pieces(part_of, length, axis):
        if not pairwise:
            full = part_of(0, length).astype(BF16)
            return lax.psum_scatter(full, ("zb", "x"), scatter_dimension=axis, tiled=True).astype(F32)
        half, quarter = length // 2, length // 4
        given = swap(part_of(half, length).astype(BF16), "x")
        kept = part_of(0, half) + given.astype(F32)
        given = swap(lax.slice_in_dim(kept, quarter, half, axis=axis).astype(BF16), "zb")
        return lax.slice_in_dim(kept, 0, quarter, axis=axis) + given.astype(F32)

    def in_order(mine, other, axis):
        first = jnp.where(za_at == 0, mine, other)
        second = jnp.where(za_at == 0, other, mine)
        return jnp.concatenate([first, second], axis=axis)

    def gather_weight(part_of, axis):
        mine = part_of(za_at)
        if za_count > 1:
            mine = in_order(mine, swap(part_of(1 - za_at), "za"), axis)
        return gather_pieces(mine, axis)

    def scatter_weight(part_of, axis):
        part = scatter_pieces(part_of, width, axis)
        if za_count == 1:
            return [part]
        first = lax.slice_in_dim(part, 0, blk_rows, axis=axis)
        second = lax.slice_in_dim(part, blk_rows, 2 * blk_rows, axis=axis)
        mine = jnp.where(za_at == 0, first, second)
        other = swap(jnp.where(za_at == 0, second, first).astype(BF16), "za").astype(F32)
        return [jnp.where(za_at == 0, mine, other), jnp.where(za_at == 0, other, mine)]

    def half_of(weight, at, axis):
        size = weight.shape[axis] // za_count
        return lax.dynamic_slice_in_dim(weight, at * size, size, axis=axis)


    def piece_group(index):
        if pairwise:
            return zb_at ^ (index % 2), x_at ^ (index // 2)
        return index // x_count, index % x_count

    def to_pieces(value):
        blocks = []
        for index in range(group_count):
            zb_of, x_of = piece_group(index)
            for za_of in range(za_count):
                block = (zb_of * za_count + za_of) * x_count + x_of
                blocks.append(lax.dynamic_slice_in_dim(value, block * blk_rows, blk_rows, axis=1))
        return jnp.concatenate(blocks, axis=1) if pairwise else value

    def from_pieces(value):
        if not pairwise:
            return value
        blocks = []
        for block in range(group_count * za_count):
            zb_of, za_of, x_of = block // 4, block // 2 % 2, block % 2
            index = (x_at ^ x_of) * 2 + (zb_at ^ zb_of)
            blocks.append(lax.dynamic_slice_in_dim(value, (index * 2 + za_of) * blk_rows, blk_rows, axis=1))
        return jnp.concatenate(blocks, axis=1)


    per_span = head_count // 2
    member = jnp.arange(member_count, dtype=jnp.int32)
    if pairwise:
        member_y, member_za, member_core = y_at ^ (member % 2), za_at ^ (member // 2 % 2), core_at ^ (member // 4)
    else:
        member_za = member % za_count
        member_core = member // za_count % core_count
        member_y = member // (za_count * core_count)
    group = jnp.arange(group_count, dtype=jnp.int32)
    group_zb, group_x = piece_group(group)
    member_head = member_y * core_count + member_core
    span_table = jnp.arange(block_deal.shape[0], dtype=jnp.int32)

    def natural_tile(zb_of, x_of):
        blk = (zb_of * za_count + member_za) * x_count + x_of
        entry = 2 * blk + member_head // per_span
        span = jnp.sum(
            jnp.where(entry[..., None] == span_table, block_deal, 0), axis=-1, dtype=jnp.int32
        )
        return span * per_span + member_head % per_span

    query_tile = natural_tile(zb_at, x_at)
    key_tile = natural_tile(group_zb[:, None], group_x[:, None]).reshape(-1)
    tile_ids = jnp.arange(key_tile.shape[0], dtype=jnp.int32)
    offsets = jnp.sum(
        jnp.where(key_tile[None, :] == tile_ids[:, None], tile_ids[None, :] * tok_dev, 0), axis=1, dtype=jnp.int32
    )
    natural = query_tile[:, None] * tok_dev + jnp.arange(tok_dev, dtype=jnp.int32)[None, :]
    seq_ids = jnp.arange(seq_lengths.shape[0], dtype=jnp.int32)
    seq_ends = jnp.sum(jnp.where(seq_ids[None, :] <= seq_ids[:, None], seq_lengths[None, :], 0), axis=1, dtype=jnp.int32)
    starts = jnp.max(jnp.where(seq_ends <= natural[..., None], seq_ends, 0), axis=-1)
    tiles = (query_tile, starts[:, 0] // (2 * tok_dev))
    start_rows = jnp.stack([starts, starts], axis=1)
    start_cols = jnp.broadcast_to(starts.reshape(rows, 1), (rows, 128))
    places = (natural - starts).reshape(rows)
    half_width = HEAD_SIZE // 2
    frequency = jnp.power(ROPE_BASE, -jnp.arange(half_width, dtype=F32) * (2.0 / HEAD_SIZE))
    angles = places.astype(F32)[:, None] * frequency[None, :]
    cosine = jnp.cos(angles)
    sine = jnp.sin(angles)
    cosine = jnp.concatenate([cosine, cosine], axis=1)
    sine = jnp.concatenate([-sine, sine], axis=1)


    q_width = q_weight.shape[1] // za_count
    k_width = k_weight.shape[1] // za_count
    qkv_width = q_width + 2 * k_width
    gain_pad = 16

    gain_row = jnp.concatenate([norm_gain, mlp_gain])
    head_gains = jnp.concatenate([q_gain, k_gain])

    def gain_rows():
        top = jnp.pad(gain_row, (0, qkv_width - gain_row.shape[0]))[None]
        bottom = jnp.pad(head_gains, (0, qkv_width - head_gains.shape[0]))[None]
        return jnp.concatenate([top, bottom, jnp.zeros((gain_pad - 2, qkv_width), BF16)], axis=0)

    def qkv_part(at):
        return jnp.concatenate(
            [half_of(q_weight, at, 1), half_of(k_weight, at, 1), half_of(v_weight, at, 1), ], axis=1
        )

    padded = blk_rows + gain_pad
    own_gain_rows = gain_rows()
    qkv_all = gather_weight(lambda at: jnp.concatenate([qkv_part(at), own_gain_rows], axis=0), 0)
    qkv_all = qkv_all.reshape(group_count * za_count, padded, qkv_width)
    qkv_cols = qkv_all[:, :blk_rows].reshape(width, qkv_width)
    gains = qkv_all[:, blk_rows, : 2 * blk_rows].astype(F32)
    gain_one = gains[:, :blk_rows].reshape(1, width)
    gain_two = gains[:, blk_rows:].reshape(1, width)
    small = q_gain.shape[0]
    head_parts = qkv_all[:, blk_rows + 1, : 2 * small].astype(F32).reshape(group_count * za_count, 2, small)

    def head_gain(which):
        return from_small(head_parts[:, which])

    def from_small(parts):
        if not pairwise:
            return parts.reshape(1, -1)
        rows_of = []
        for block in range(8):
            zb_of, za_of, x_of = block // 4, block // 2 % 2, block % 2
            index = ((x_at ^ x_of) * 2 + (zb_at ^ zb_of)) * 2 + za_of
            rows_of.append(lax.dynamic_slice_in_dim(parts, index, 1, axis=0))
        return jnp.concatenate(rows_of, axis=1)

    qk_gains = jnp.concatenate([head_gain(0), head_gain(1)], axis=0)


    local_low = to_pieces(tokens)
    local_rows = local_low.astype(F32)
    input_rows = gather_rows(local_low).astype(F32)
    o_cols = gather_weight(lambda at: half_of(o_weight, at, 0), 1)
    gu_cols = gather_weight(
        lambda at: jnp.concatenate([half_of(gate_weight, at, 1), half_of(up_weight, at, 1)], axis=1), 0
    )
    down_cols = gather_weight(lambda at: half_of(down_weight, at, 0), 1)
    grad_local = to_pieces(out_grad)
    grad_rows = gather_rows(grad_local)

    def unit_rows(value):
        return value * lax.rsqrt(jnp.mean(value * value, axis=-1, keepdims=True) + EPSILON)

    input_unit = unit_rows(input_rows)
    normed = (input_unit * gain_one).astype(BF16)
    raw = matmul(normed, qkv_cols)
    queries, kv_own = shape_heads(raw, cosine, sine, qk_gains)
    key_values = gather_pieces(kv_own, 0)
    attn_low, inverse = attend(offsets, tiles, queries, start_cols, [key_values])
    residual = local_rows + scatter_rows(lambda at: matmul(attn_low[at], o_cols))


    rho_two = lax.rsqrt(jnp.mean(residual * residual, axis=-1, keepdims=True) + EPSILON)
    unit_two = residual * rho_two
    mlp_rows = gather_rows((unit_two * gain_two).astype(BF16))
    ff = gu_cols.shape[1] // 2
    gate_up = matmul(mlp_rows, gu_cols)
    gate_act, up_act = gate_up[:, :ff], gate_up[:, ff:]
    sig = jax.nn.sigmoid(gate_act)
    silu = gate_act * sig
    hidden = (silu * up_act).astype(BF16)
    hidden_grad = contract_cols(grad_rows, down_cols)
    gate_low = (hidden_grad * up_act * (sig * (1.0 + gate_act * (1.0 - sig)))).astype(BF16)
    up_low = (hidden_grad * silu).astype(BF16)
    gu_low = jnp.concatenate([gate_low, up_low], axis=1)
    mlp_in_grad = scatter_rows(lambda at: contract_cols(gu_low[at], gu_cols))

    down_parts = scatter_weight(lambda lo, hi: contract_rows(hidden, grad_rows[:, lo:hi]), 1)
    gate_parts = scatter_weight(lambda lo, hi: contract_rows(mlp_rows[:, lo:hi], gate_low), 0)
    up_parts = scatter_weight(lambda lo, hi: contract_rows(mlp_rows[:, lo:hi], up_low), 0)
    block_out = residual + scatter_rows(lambda at: matmul(hidden[at], down_cols))

    gain_two_part = jnp.sum(mlp_in_grad * unit_two, axis=0, keepdims=True)
    scaled = mlp_in_grad * gain_two
    inner = jnp.mean(scaled * unit_two, axis=-1, keepdims=True)
    residual_grad = grad_local.astype(F32) + rho_two * (scaled - unit_two * inner)


    branch_rows = gather_rows(residual_grad.astype(BF16))
    attn_grad = contract_cols(branch_rows, o_cols).astype(BF16)
    query_grad, kv_grads = attend_back(
        offsets, tiles, queries, start_rows, inverse, attn_low, attn_grad, [key_values]
    )
    o_parts = scatter_weight(lambda lo, hi: contract_rows(attn_low, branch_rows[:, lo:hi]), 1)
    kv_grad = scatter_pieces(lambda lo, hi: kv_grads[lo:hi].astype(F32), kv_grads.shape[0], 0).astype(BF16)
    q_low, q_gain_part = shape_back(raw, query_grad, cosine, sine, qk_gains, 2, 0, 0, HEAD_SIZE**-0.5)
    kv_low, k_gain_part = shape_back(raw, kv_grad, cosine, sine, qk_gains, 1, 2, 1, 1.0)
    low = jnp.concatenate([q_low, kv_low], axis=1)

    gain_one_parts = []

    def input_terms(at):
        terms = contract_cols(low[at], qkv_cols)
        gain_one_parts.append(jnp.sum(terms * input_unit[at], axis=0, keepdims=True))
        return terms

    input_grad = scatter_rows(input_terms)
    qkv_parts = scatter_weight(lambda lo, hi: contract_rows(normed[:, lo:hi], low), 0)

    gain_sum = jnp.concatenate(
        [
            from_pieces(sum(gain_one_parts)),
            from_pieces(gain_two_part),
            jnp.sum(q_gain_part, axis=0, keepdims=True),
            jnp.sum(k_gain_part, axis=0, keepdims=True),
        ],
        axis=1,
    )
    if pairwise:
        for name in ("core", "y", "za", "x", "zb"):
            gain_sum = gain_sum + swap(gain_sum, name)
    else:
        gain_sum = lax.psum(gain_sum, all_axes)

    unit_one = local_rows * (rho_one := lax.rsqrt(jnp.mean(local_rows * local_rows, axis=-1, keepdims=True) + EPSILON))
    scaled = input_grad * gain_one
    inner = jnp.mean(scaled * unit_one, axis=-1, keepdims=True)
    in_grad = residual_grad + rho_one * (scaled - unit_one * inner)

    device = (((y_at * core_count + core_at) * zb_count + zb_at) * za_count + za_at) * x_count + x_at
    device_count = head_count * zb_count * za_count * x_count

    def own_slice(first, length):
        share = length // device_count
        return lax.dynamic_slice_in_dim(gain_sum[0], first + device * share, share, axis=0)

    def join(parts, lo, hi, axis):
        cut = [lax.slice_in_dim(part, lo, hi, axis=axis) for part in parts]
        return jnp.concatenate(cut, axis=axis)

    return (
        from_pieces(block_out).astype(BF16),
        from_pieces(in_grad),
        own_slice(0, width),
        join(qkv_parts, 0, q_width, 1),
        join(qkv_parts, q_width, q_width + k_width, 1),
        join(qkv_parts, q_width + k_width, qkv_width, 1),
        own_slice(2 * width, HEAD_SIZE),
        own_slice(2 * width + HEAD_SIZE, HEAD_SIZE),
        jnp.concatenate(o_parts, axis=0),
        own_slice(width, width),
        jnp.concatenate(gate_parts, axis=1),
        jnp.concatenate(up_parts, axis=1),
        jnp.concatenate(down_parts, axis=0),
    )


def solution(mesh):
    heads, blks = mesh.shape["head"], mesh.shape["blk"]
    za_count = KEY_VALUE_HEADS // heads
    side = math.isqrt(blks // za_count)
    sizes = (heads // 2, 2, side, za_count, side)
    names = ("y", "core", "zb", "za", "x")
    devices = mesh.devices.reshape(sizes)
    inner = Mesh(devices, names)
    head, blk = ("y", "core"), ("zb", "za", "x")
    rows, in_weight, out_weight, gain = P(names, None), P(blk, head), P(head, blk), P(blk)
    return jax.shard_map(
        paired_layer if sizes == (2, 2, 2, 2, 2) else functools.partial(layer, sizes),
        mesh=inner,
        in_specs=(
            rows,
            rows,
            P(),
            P(),
            gain,
            in_weight,
            in_weight,
            in_weight,
            gain,
            gain,
            out_weight,
            gain,
            in_weight,
            in_weight,
            out_weight,
        ),
        out_specs=(
            rows,
            rows,
            P(names),
            in_weight,
            in_weight,
            in_weight,
            P(names),
            P(names),
            out_weight,
            P(names),
            in_weight,
            in_weight,
            out_weight,
        ),
        check_vma=False,
    )
```

```python
import functools
import math

import jax
import jax.numpy as jnp
from jax import lax
from jax.experimental import pallas as pl
from jax.experimental.pallas import tpu as pltpu
from jax.sharding import Mesh
from jax.sharding import PartitionSpec as P

HEAD_SIZE = 128
KEY_VALUE_HEADS = 8
EPSILON = 1e-06
ROPE_BASE = 1000000.0
F32 = jnp.float32
BF16 = jnp.bfloat16
SWAP = [(0, 1), (1, 0)]
PAIRS_OF_ROWS = (((0,), (0,)), ((), ()))
PAIRS_OF_COLS = (((1,), (1,)), ((), ()))
VMEM = pltpu.MemorySpace.VMEM
LIGHT = pl.CostEstimate(flops=1000, bytes_accessed=1000, transcendentals=0)
SMEM = pltpu.MemorySpace.SMEM


def matmul(left, right):
    return jnp.dot(left, right, preferred_element_type=F32)


def contract_rows(left, right):
    return lax.dot_general(left, right, PAIRS_OF_ROWS, preferred_element_type=F32)


def contract_cols(left, right):
    return lax.dot_general(left, right, PAIRS_OF_COLS, preferred_element_type=F32)


def swap(value, axis):
    return lax.ppermute(value, axis, SWAP)


def attend_kernel(off_ref, tile_ref, low_ref, q_ref, start_ref, *refs, parts, first, last):
    half = 128
    kv_refs, refs = refs[:parts], refs[parts:]
    if not first:
        before_ref, refs = refs[0], refs[1:]
    if last:
        out_ref, inv_ref, kv_ref, acc_ref = refs
    else:
        after_ref, kv_ref, acc_ref = refs
    share = kv_refs[0].shape[0]
    for part, ref in enumerate(kv_refs):
        kv_ref[part * share : (part + 1) * share, :] = ref[...]
    lane = lax.broadcasted_iota(jnp.int32, (256, 256), 1)
    row = lax.broadcasted_iota(jnp.int32, (256, 256), 0) % half
    ones = jnp.ones((256, HEAD_SIZE), BF16)

    def tile(index, unused):
        rows = pl.ds(pl.multiple_of(index * half, half), half)
        queries = jnp.concatenate([q_ref[rows, :HEAD_SIZE], q_ref[rows, HEAD_SIZE:]], axis=0)
        start = start_ref[rows, :]
        start = jnp.concatenate([start, start], axis=1)
        start = jnp.concatenate([start, start], axis=0)
        places = tile_ref[index] * half + row
        acc_ref[...] = jnp.zeros_like(acc_ref) if first else before_ref[index]

        def step(block, unused_step):
            at = off_ref[2 * block]

            @pl.when(at >= 0)
            def _():
                low = pl.ds(pl.multiple_of(at, half), half)
                high = pl.ds(pl.multiple_of(off_ref[2 * block + 1], half), half)
                keys = jnp.concatenate([kv_ref[low, :HEAD_SIZE], kv_ref[high, :HEAD_SIZE]], axis=0)
                values = jnp.concatenate([kv_ref[low, HEAD_SIZE:], kv_ref[high, HEAD_SIZE:]], axis=0)
                scores = contract_cols(queries, keys)
                natural = block * 256 + lane
                allowed = (natural <= places) & (natural >= start)
                weights = jnp.where(allowed, jnp.exp(scores), 0.0).astype(BF16)
                acc_ref[...] += matmul(weights, jnp.concatenate([values, ones], axis=1))

            return unused_step

        lax.fori_loop(low_ref[index], tile_ref[index] // 2 + 1, step, 0)
        if last:
            inverse = 1.0 / acc_ref[:, HEAD_SIZE:]
            attended = (acc_ref[:, :HEAD_SIZE] * inverse).astype(BF16)
            out_ref[rows, :HEAD_SIZE] = attended[:half]
            out_ref[rows, HEAD_SIZE:] = attended[half:]
            inv_ref[index, 0:1, :] = jnp.transpose(inverse[:half])[0:1, :]
            inv_ref[index, 1:2, :] = jnp.transpose(inverse[half:])[0:1, :]
        else:
            after_ref[index] = acc_ref[...]
        return unused

    lax.fori_loop(0, q_ref.shape[0] // half, tile, 0)


def attend_back_kernel(
    off_ref, tile_ref, low_ref, q_ref, start_ref, inv_ref, out_ref, grad_ref, *refs, parts, first, last
):
    half = 128
    kv_refs, refs = refs[:parts], refs[parts:]
    if not first:
        before_ref, refs = refs[0], refs[1:]
    dq_ref, *dkv_refs = refs[: 1 + parts]
    kv_ref, dk_ref, dv_ref, acc_ref = refs[1 + parts :]
    share = kv_refs[0].shape[0]
    for part, ref in enumerate(kv_refs):
        kv_ref[part * share : (part + 1) * share, :] = ref[...]
    key_row = lax.broadcasted_iota(jnp.int32, (256, 256), 0)
    query_lane = lax.broadcasted_iota(jnp.int32, (1, 256), 1) % half

    def clear(index, unused):
        rows = pl.ds(pl.multiple_of(index * 256, 256), 256)
        dk_ref[rows, :] = jnp.zeros((256, HEAD_SIZE), F32)
        dv_ref[rows, :] = jnp.zeros((256, HEAD_SIZE), F32)
        return unused

    lax.fori_loop(0, dk_ref.shape[0] // 256, clear, 0)

    def tile(index, unused):
        rows = pl.ds(pl.multiple_of(index * half, half), half)

        def both(ref):
            return jnp.concatenate([ref[rows, :HEAD_SIZE], ref[rows, HEAD_SIZE:]], axis=0)

        def along(ref):
            return jnp.concatenate([ref[index, 0:1, :], ref[index, 1:2, :]], axis=1)

        queries = both(q_ref)
        grads = both(grad_ref)
        products = both(out_ref).astype(F32) * grads.astype(F32)
        deltas = jnp.sum(jnp.transpose(products), axis=0, keepdims=True)
        inverse = along(inv_ref)
        start = along(start_ref)
        places = tile_ref[index] * half + query_lane
        acc_ref[...] = jnp.zeros_like(acc_ref) if first else both(before_ref)

        def step(block, unused_step):
            at = off_ref[2 * block]

            @pl.when(at >= 0)
            def _():
                low = pl.ds(pl.multiple_of(at, half), half)
                high = pl.ds(pl.multiple_of(off_ref[2 * block + 1], half), half)
                keys = jnp.concatenate([kv_ref[low, :HEAD_SIZE], kv_ref[high, :HEAD_SIZE]], axis=0)
                values = jnp.concatenate([kv_ref[low, HEAD_SIZE:], kv_ref[high, HEAD_SIZE:]], axis=0)
                scores = contract_cols(keys, queries)
                natural = block * 256 + key_row
                allowed = (natural <= places) & (natural >= start)
                probs = jnp.where(allowed, jnp.exp(scores) * inverse, 0.0)
                prob_grad = contract_cols(values, grads)
                score_grad = (probs * (prob_grad - deltas)).astype(BF16)
                value_part = matmul(probs.astype(BF16), grads)
                key_part = matmul(score_grad, queries)
                dv_ref[low, :] += value_part[:half]
                dv_ref[high, :] += value_part[half:]
                dk_ref[low, :] += key_part[:half]
                dk_ref[high, :] += key_part[half:]
                acc_ref[...] += contract_rows(score_grad, keys)

            return unused_step

        lax.fori_loop(low_ref[index], tile_ref[index] // 2 + 1, step, 0)
        dq_ref[rows, :HEAD_SIZE] = acc_ref[:half, :].astype(dq_ref.dtype)
        dq_ref[rows, HEAD_SIZE:] = acc_ref[half:, :].astype(dq_ref.dtype)
        return unused

    lax.fori_loop(0, q_ref.shape[0] // half, tile, 0)

    for part, ref in enumerate(dkv_refs):

        def store(index, unused):
            target = pl.ds(pl.multiple_of(index * 256, 256), 256)
            source = pl.ds(pl.multiple_of(part * share + index * 256, 256), 256)
            ref[target, :HEAD_SIZE] = dk_ref[source, :].astype(BF16)
            ref[target, HEAD_SIZE:] = dv_ref[source, :].astype(BF16)
            return unused

        lax.fori_loop(0, share // 256, store, 0)


def attend(offsets, tiles, queries, start_cols, kv_parts, before=None, last=True):
    rows, width = queries.shape
    parts, share = len(kv_parts), kv_parts[0].shape[0]
    keys = parts * share
    first = before is None
    extra = () if first else (before,)
    whole = (
        (jax.ShapeDtypeStruct((rows, width), BF16), jax.ShapeDtypeStruct((rows // 128, 2, 128), F32))
        if last
        else (jax.ShapeDtypeStruct((rows // 128, 256, 256), F32),)
    )
    return pl.pallas_call(
        functools.partial(attend_kernel, parts=parts, first=first, last=last),
        name="attend",
        out_shape=whole,
        in_specs=[pl.BlockSpec(memory_space=SMEM)] * 3 + [pl.BlockSpec(memory_space=VMEM)] * (2 + parts + len(extra)),
        out_specs=[pl.BlockSpec(memory_space=VMEM)] * len(whole),
        scratch_shapes=[pltpu.VMEM((keys, width), BF16), pltpu.VMEM((256, 256), F32)],
        compiler_params=pltpu.CompilerParams(vmem_limit_bytes=12 * 2**20 + keys * 1536),
        cost_estimate=LIGHT,
    )(offsets, *tiles, queries, start_cols, *kv_parts, *extra)


def attend_back(offsets, tiles, queries, start_rows, inverse, attended, grads, kv_parts, before=None, last=True):
    rows, width = queries.shape
    parts, share = len(kv_parts), kv_parts[0].shape[0]
    keys = parts * share
    first = before is None
    extra = () if first else (before,)
    return pl.pallas_call(
        functools.partial(attend_back_kernel, parts=parts, first=first, last=last),
        name="attend_back",
        out_shape=(jax.ShapeDtypeStruct((rows, width), BF16 if last else F32),)
        + tuple(jax.ShapeDtypeStruct((share, width), BF16) for unused in kv_parts),
        in_specs=[pl.BlockSpec(memory_space=SMEM)] * 3 + [pl.BlockSpec(memory_space=VMEM)] * (5 + parts + len(extra)),
        out_specs=[pl.BlockSpec(memory_space=VMEM)] * (1 + parts),
        scratch_shapes=[
            pltpu.VMEM((keys, width), BF16),
            pltpu.VMEM((keys, HEAD_SIZE), F32),
            pltpu.VMEM((keys, HEAD_SIZE), F32),
            pltpu.VMEM((256, HEAD_SIZE), F32),
        ],
        compiler_params=pltpu.CompilerParams(vmem_limit_bytes=12 * 2**20 + keys * 2816),
        cost_estimate=LIGHT,
    )(offsets, *tiles, queries, start_rows, inverse, attended, grads, *kv_parts, *extra)


def shape_kernel(raw_ref, cos_ref, sin_ref, gain_ref, q_ref, kv_ref):
    cosine = cos_ref[...]
    sine = sin_ref[...]

    def shaped(first, gain):
        value = raw_ref[:, first : first + HEAD_SIZE]
        mean_square = jnp.mean(value * value, axis=-1, keepdims=True)
        value = value * lax.rsqrt(mean_square + EPSILON) * gain
        return value * cosine + pltpu.roll(value, HEAD_SIZE // 2, 1) * sine

    for head in range(2):
        columns = slice(head * HEAD_SIZE, (head + 1) * HEAD_SIZE)
        q_ref[:, columns] = (shaped(head * HEAD_SIZE, gain_ref[0:1, :]) * HEAD_SIZE**-0.5).astype(BF16)
    kv_ref[:, :HEAD_SIZE] = shaped(2 * HEAD_SIZE, gain_ref[1:2, :]).astype(BF16)
    kv_ref[:, HEAD_SIZE:] = raw_ref[:, 3 * HEAD_SIZE :].astype(BF16)


def shape_back_kernel(raw_ref, grad_ref, cos_ref, sin_ref, gain_ref, low_ref, gain_grad_ref, *, heads, gain_row, factor):
    @pl.when(pl.program_id(0) == 0)
    def _():
        gain_grad_ref[...] = jnp.zeros_like(gain_grad_ref)

    cosine = cos_ref[...]
    sine = sin_ref[...]
    gain = gain_ref[gain_row : gain_row + 1, :]
    total = jnp.zeros((8, HEAD_SIZE), F32)
    for head in range(heads):
        columns = slice(head * HEAD_SIZE, (head + 1) * HEAD_SIZE)
        value = raw_ref[:, columns]
        grad = grad_ref[:, columns].astype(F32) * factor
        grad = grad * cosine - pltpu.roll(grad, HEAD_SIZE // 2, 1) * sine
        rho = lax.rsqrt(jnp.mean(value * value, axis=-1, keepdims=True) + EPSILON)
        unit = value * rho
        total = total + jnp.sum((grad * unit).reshape(-1, 8, HEAD_SIZE), axis=0)
        scaled = grad * gain
        inner = jnp.mean(scaled * unit, axis=-1, keepdims=True)
        low_ref[:, columns] = (rho * (scaled - unit * inner)).astype(BF16)
    if heads == 1:
        low_ref[:, HEAD_SIZE:] = grad_ref[:, HEAD_SIZE:].astype(BF16)
    gain_grad_ref[...] += total


ROW_TILE = 256


def shape_heads(raw, cosine, sine, gains):
    rows = raw.shape[0]
    block = lambda width: pl.BlockSpec((ROW_TILE, width), lambda i: (i, 0))
    return pl.pallas_call(
        shape_kernel,
        name="shape_heads",
        grid=(rows // ROW_TILE,),
        out_shape=(jax.ShapeDtypeStruct((rows, 256), BF16), jax.ShapeDtypeStruct((rows, 256), BF16)),
        in_specs=[block(512), block(128), block(128), pl.BlockSpec((2, 128), lambda i: (0, 0))],
        out_specs=[block(256), block(256)],
        compiler_params=pltpu.CompilerParams(vmem_limit_bytes=8 * 2**20),
        cost_estimate=LIGHT,
    )(raw, cosine, sine, gains)


def shape_back(raw, grads, cosine, sine, gains, heads, column, gain_row, factor):
    rows = raw.shape[0]
    block = lambda width, at=0: pl.BlockSpec((ROW_TILE, width), lambda i: (i, at))
    return pl.pallas_call(
        functools.partial(shape_back_kernel, heads=heads, gain_row=gain_row, factor=factor),
        name="shape_back",
        grid=(rows // ROW_TILE,),
        out_shape=(jax.ShapeDtypeStruct((rows, 256), BF16), jax.ShapeDtypeStruct((8, 128), F32)),
        in_specs=[
            block(heads * 128, column),
            block(256),
            block(128),
            block(128),
            pl.BlockSpec((2, 128), lambda i: (0, 0)),
        ],
        out_specs=[block(256), pl.BlockSpec((8, 128), lambda i: (0, 0))],
        compiler_params=pltpu.CompilerParams(vmem_limit_bytes=8 * 2**20),
        cost_estimate=LIGHT,
    )(raw, grads, cosine, sine, gains)


def reorder_kernel(order_ref, *refs):
    half = len(refs) // 2
    for source, target in zip(refs[:half], refs[half:]):
        target[...] = source[...].astype(target.dtype)


def reorder(order, values, types):
    rows, width = values[0].shape
    blocks = order.shape[0]
    size = width // blocks
    taken = pl.BlockSpec((rows, size), lambda i, order_ref: (0, order_ref[i]))
    put = pl.BlockSpec((rows, size), lambda i, order_ref: (0, i))
    return pl.pallas_call(
        reorder_kernel,
        name="reorder",
        grid_spec=pltpu.PrefetchScalarGridSpec(
            num_scalar_prefetch=1,
            grid=(blocks,),
            in_specs=[taken] * len(values),
            out_specs=[put] * len(values),
        ),
        out_shape=[jax.ShapeDtypeStruct(value.shape, kind) for value, kind in zip(values, types)],
        compiler_params=pltpu.CompilerParams(vmem_limit_bytes=8 * 2**20),
        cost_estimate=LIGHT,
    )(order, *values)


def assemble_kernel(at_ref, *refs, entries, axis):
    out_ref = refs[-1]
    for source, (place, kind) in zip(refs[:-1], entries):
        size = source.shape[axis]
        if kind == 0:
            span = slice(place, place + size)
        else:
            at = at_ref[0] if kind > 0 else 1 - at_ref[0]
            span = pl.ds(pl.multiple_of(place + at * 256, 16 if axis == 0 else 128), size)
        if axis == 0:
            out_ref[span, :] = source[...]
        else:
            out_ref[:, span] = source[...]


def assemble(at, parts, axis):
    values = [value for value, unused, kind in parts]
    total = sum(value.shape[axis] for value in values)
    other = values[0].shape[1 - axis]
    shape = (total, other) if axis == 0 else (other, total)
    return pl.pallas_call(
        functools.partial(assemble_kernel, entries=tuple((place, kind) for unused, place, kind in parts), axis=axis),
        name="assemble",
        out_shape=jax.ShapeDtypeStruct(shape, BF16),
        in_specs=[pl.BlockSpec(memory_space=SMEM)] + [pl.BlockSpec(memory_space=VMEM)] * len(values),
        out_specs=pl.BlockSpec(memory_space=VMEM),
        compiler_params=pltpu.CompilerParams(vmem_limit_bytes=12 * 2**20),
        cost_estimate=LIGHT,
    )(at, *values)


def terms_kernel(left_ref, right_ref, left_cols_ref, right_cols_ref, kept_ref, given_ref):
    total = contract_cols(left_ref[...], left_cols_ref[...]) + contract_cols(right_ref[...], right_cols_ref[...])
    middle = kept_ref.shape[0]
    kept_ref[...] = total[:middle]
    given_ref[...] = total[middle:].astype(BF16)


def two_terms(left, right, left_cols, right_cols):
    rows, depth = left.shape
    width = left_cols.shape[0]
    tile = 512
    value = pl.BlockSpec((rows, depth), lambda i: (0, 0))
    cols = pl.BlockSpec((tile, depth), lambda i: (i, 0))
    half = pl.BlockSpec((rows // 2, tile), lambda i: (0, i))
    return pl.pallas_call(
        terms_kernel,
        name="two_terms",
        grid=(width // tile,),
        out_shape=(jax.ShapeDtypeStruct((rows // 2, width), F32), jax.ShapeDtypeStruct((rows // 2, width), BF16)),
        in_specs=[value, value, cols, cols],
        out_specs=(half, half),
        cost_estimate=LIGHT,
    )(left, right, left_cols, right_cols)


def hidden_kernel(mine_ref, theirs_ref, gate_ref, up_ref, hidden_ref, gate_slope_ref, up_slope_ref):
    middle = mine_ref.shape[0]
    for part, source in ((slice(0, middle), mine_ref), (slice(middle, 2 * middle), theirs_ref)):
        rows = source[...]
        gate = matmul(rows, gate_ref[...])
        up = matmul(rows, up_ref[...])
        sig = 1.0 / (1.0 + jnp.exp(-gate))
        silu = gate * sig
        hidden_ref[part, :] = (silu * up).astype(BF16)
        gate_slope_ref[part, :] = (up * (sig * (1.0 + gate * (1.0 - sig)))).astype(BF16)
        up_slope_ref[part, :] = silu.astype(BF16)


def hidden_units(mine, theirs, gate_cols, up_cols):
    middle, width = mine.shape
    units = gate_cols.shape[1]
    tile = 256
    whole = pl.BlockSpec((middle, width), lambda i: (0, 0))
    cols = pl.BlockSpec((width, tile), lambda i: (0, i))
    out = pl.BlockSpec((2 * middle, tile), lambda i: (0, i))
    return pl.pallas_call(
        hidden_kernel,
        name="hidden_units",
        grid=(units // tile,),
        out_shape=(jax.ShapeDtypeStruct((2 * middle, units), BF16),) * 3,
        in_specs=[whole, whole, cols, cols],
        out_specs=(out,) * 3,
        cost_estimate=LIGHT,
    )(mine, theirs, gate_cols, up_cols)


def prologue_kernel(
    order_ref, at_ref, tokens_ref, grad_ref, q_ref, k_ref, v_ref, norm_ref, mlp_ref, q_gain_ref, k_gain_ref,
    tokens_out, grad_out, keep_ref, give_ref
):
    size = tokens_ref.shape[1] // 8
    for block in range(8):
        source = pl.ds(pl.multiple_of(order_ref[block] * size, 128), size)
        tokens_out[:, block * size : (block + 1) * size] = tokens_ref[:, source]
        grad_out[:, block * size : (block + 1) * size] = grad_ref[:, source]

    rows, q_width = q_ref.shape[0], q_ref.shape[1] // 2
    k_width = k_ref.shape[1] // 2
    total = q_width + 2 * k_width
    small = q_gain_ref.shape[1]
    place = lax.broadcasted_iota(jnp.int32, (small, HEAD_SIZE), 1) - lax.broadcasted_iota(
        jnp.int32, (small, HEAD_SIZE), 0
    )
    put = (place == at_ref[1] * small).astype(BF16)
    extra = jnp.concatenate(
        [
            jnp.concatenate([norm_ref[...], mlp_ref[...]], axis=1),
            jnp.concatenate(
                [
                    matmul(q_gain_ref[...], put).astype(BF16),
                    matmul(k_gain_ref[...], put).astype(BF16),
                    jnp.zeros((1, total - 2 * HEAD_SIZE), BF16),
                ],
                axis=1,
            ),
            jnp.zeros((14, total), BF16),
        ],
        axis=0,
    )
    for target, at in ((keep_ref, at_ref[0]), (give_ref, 1 - at_ref[0])):
        target[:rows, :q_width] = q_ref[:, pl.ds(pl.multiple_of(at * q_width, 128), q_width)]
        target[:rows, q_width : q_width + k_width] = k_ref[:, pl.ds(pl.multiple_of(at * k_width, 128), k_width)]
        target[:rows, q_width + k_width :] = v_ref[:, pl.ds(pl.multiple_of(at * k_width, 128), k_width)]
        target[rows:, :] = extra


def prologue(order, at, tokens, out_grad, q_weight, k_weight, v_weight, gains):
    shape = jax.ShapeDtypeStruct((q_weight.shape[0] + 16, (q_weight.shape[1] + 2 * k_weight.shape[1]) // 2), BF16)
    whole = lambda value: pl.BlockSpec(value.shape, lambda i, order_ref, at_ref: (0, 0))
    fixed = (q_weight, k_weight, v_weight) + gains
    return pl.pallas_call(
        prologue_kernel,
        name="prologue",
        grid_spec=pltpu.PrefetchScalarGridSpec(
            num_scalar_prefetch=2,
            grid=(1,),
            in_specs=[whole(tokens), whole(out_grad)] + [whole(value) for value in fixed],
            out_specs=[whole(tokens), whole(tokens), whole(shape), whole(shape)],
        ),
        out_shape=(jax.ShapeDtypeStruct(tokens.shape, BF16),) * 2 + (shape, shape),
        cost_estimate=LIGHT,
    )(order, at, tokens, out_grad, *fixed)


def after(token, values):
    return lax.optimization_barrier((token, values))[1]


def meet(token, values):
    return lax.optimization_barrier((token, values))


def trade(token, sends):
    held = after(token, [value for value, unused in sends])
    return [swap(value, axis) for value, (unused, axis) in zip(held, sends)]


def places_of(query_tile, key_tile, seq_lengths, tok_dev):
    rows = query_tile.shape[0] * tok_dev
    tile_ids = jnp.arange(key_tile.shape[0], dtype=jnp.int32)
    shares = (tile_ids // 16) * 8 + tile_ids % 8
    found = key_tile[None, :] == tile_ids[:, None]

    def offsets_of(parity):
        mine = found & (tile_ids // 8 % 2 == parity)[None, :]
        return jnp.sum(jnp.where(mine, shares * tok_dev + 1, 0), axis=1, dtype=jnp.int32) - 1

    offsets = (offsets_of(0), offsets_of(1))
    natural = query_tile[:, None] * tok_dev + jnp.arange(tok_dev, dtype=jnp.int32)[None, :]
    seq_ids = jnp.arange(seq_lengths.shape[0], dtype=jnp.int32)
    seq_ends = jnp.sum(jnp.where(seq_ids[None, :] <= seq_ids[:, None], seq_lengths[None, :], 0), axis=1, dtype=jnp.int32)
    starts = jnp.max(jnp.where(seq_ends <= natural[..., None], seq_ends, 0), axis=-1)
    tiles = (query_tile, jnp.max(jnp.where(seq_ends <= (query_tile * tok_dev)[:, None], seq_ends, 0), axis=-1) // (2 * tok_dev))
    start_rows = jnp.stack([starts, starts], axis=1)
    start_cols = jnp.broadcast_to(starts.reshape(rows, 1), (rows, 128))
    places = (natural - starts).reshape(rows)
    half_width = HEAD_SIZE // 2
    frequency = jnp.power(ROPE_BASE, -jnp.arange(half_width, dtype=F32) * (2.0 / HEAD_SIZE))
    angles = places.astype(F32)[:, None] * frequency[None, :]
    cosine = jnp.cos(angles)
    sine = jnp.sin(angles)
    cosine = jnp.concatenate([cosine, cosine], axis=1)
    sine = jnp.concatenate([-sine, sine], axis=1)
    return offsets, tiles, start_rows, start_cols, cosine, sine


FAR = 96
KEEP_ROWS = 128
UP_ROWS = 96


def paired_layer(
    tokens,
    out_grad,
    seq_lengths,
    block_deal,
    norm_gain,
    q_weight,
    k_weight,
    v_weight,
    q_gain,
    k_gain,
    o_weight,
    mlp_gain,
    gate_weight,
    up_weight,
    down_weight,
):
    y_at, core_at, zb_at, za_at, x_at = (lax.axis_index(name) for name in ("y", "core", "zb", "za", "x"))
    tok_dev, width = tokens.shape
    blk_rows = q_weight.shape[0]
    rows = 8 * tok_dev
    middle = rows // 2
    half, quarter = width // 2, width // 4
    token = seq_lengths


    place_ids = jnp.arange(8, dtype=jnp.int32)
    to_order = ((zb_at ^ (place_ids // 2 % 2)) * 2 + place_ids % 2) * 2 + (x_at ^ (place_ids // 4))
    from_order = ((x_at ^ (place_ids % 2)) * 2 + (zb_at ^ (place_ids // 4))) * 2 + place_ids // 2 % 2

    def in_order(mine, other, axis):
        first = jnp.where(za_at == 0, mine, other)
        second = jnp.where(za_at == 0, other, mine)
        return jnp.concatenate([first, second], axis=axis)

    def half_of(weight, at, axis):
        size = weight.shape[axis] // 2
        return lax.dynamic_slice_in_dim(weight, at * size, size, axis=axis)


    def near(value):
        return [(value, "y"), (value, "za")]

    def far(from_y, from_z, rows_y):
        sends = [(from_z[:rows_y], "y")]
        return sends + ([(from_y[rows_y:], "za")] if rows_y < tok_dev else [])

    def mine_of(value, from_y, from_z, fars):
        return jnp.concatenate([value, from_y, from_z] + fars, axis=0)

    def far_sums(kept):
        return [(kept[3 * tok_dev :].astype(BF16), "y")]

    def near_sums(kept, from_y):
        to_y, to_z = kept[tok_dev : 2 * tok_dev], kept[2 * tok_dev : 3 * tok_dev] + from_y.astype(F32)
        return [(to_y.astype(BF16), "y"), (to_z.astype(BF16), "za")]

    def own_sum(kept, nears):
        return kept[:tok_dev] + nears[0].astype(F32) + nears[1].astype(F32)


    def za_parts(part, axis):
        first = lax.slice_in_dim(part, 0, blk_rows, axis=axis)
        second = lax.slice_in_dim(part, blk_rows, 2 * blk_rows, axis=axis)
        return jnp.where(za_at == 0, first, second), jnp.where(za_at == 0, second, first).astype(BF16)

    def za_join(mine, other):
        other = other.astype(F32)
        return [jnp.where(za_at == 0, mine, other), jnp.where(za_at == 0, other, mine)]


    member = jnp.arange(8, dtype=jnp.int32)
    member_y, member_za, member_core = y_at ^ (member % 2), za_at ^ (member // 2 % 2), core_at ^ (member // 4)
    group = jnp.arange(4, dtype=jnp.int32)
    span_table = jnp.arange(block_deal.shape[0], dtype=jnp.int32)

    def natural_tile(zb_of, x_of):
        entry = 2 * ((zb_of * 2 + member_za) * 2 + x_of) + member_y
        span = jnp.sum(jnp.where(entry[..., None] == span_table, block_deal, 0), axis=-1, dtype=jnp.int32)
        return span * 2 + member_core

    query_tile = natural_tile(zb_at, x_at)
    key_tile = natural_tile(zb_at ^ (group % 2)[:, None], x_at ^ (group // 2)[:, None]).reshape(-1)
    offsets, tiles, start_rows, start_cols, cosine, sine = places_of(query_tile, key_tile, seq_lengths, tok_dev)


    q_width, k_width = q_weight.shape[1] // 2, k_weight.shape[1] // 2
    qkv_width = q_width + 2 * k_width
    local_low, grad_local, qkv_keep, qkv_give = prologue(
        to_order,
        jnp.stack([za_at, (zb_at * 2 + za_at) * 2 + x_at]),
        tokens,
        out_grad,
        q_weight,
        k_weight,
        v_weight,
        (norm_gain[None], mlp_gain[None], q_gain[None], k_gain[None]),
    )
    local_rows = local_low.astype(F32)
    o_give = half_of(o_weight, 1 - za_at, 0)
    za_place = za_at[None].astype(jnp.int32)
    z_keep, qkv_far, x_keep = swap(qkv_keep, "zb"), swap(qkv_give, "za"), swap(qkv_keep, "x")
    tokens_y = swap(local_low, "y")
    (o_far,) = trade(qkv_keep, [(o_give, "za")])
    token, (qkv_far, z_keep, x_keep, tokens_y, o_far) = meet(token, (qkv_far, z_keep, x_keep, tokens_y, o_far))
    down_keep = half_of(down_weight, za_at, 0)
    tokens_z, z_far, xz_keep, x_far, down_xk = trade(
        token, [(local_low, "za"), (qkv_far, "zb"), (z_keep, "x"), (qkv_far, "x"), (down_keep, "x")]
    )
    o_pair = in_order(half_of(o_weight, za_at, 0), o_far, 1)
    token, (z_far, tokens_z, xz_keep, x_far, o_pair, down_xk) = meet(
        token, (z_far, tokens_z, xz_keep, x_far, o_pair, down_xk)
    )
    *fars, xz_far, o_x, o_z = trade(
        token, far(tokens_y, tokens_z, FAR) + [(z_far, "x"), (o_pair, "x"), (o_pair, "zb")]
    )
    gate_weight, up_weight, down_weight = after(token, (gate_weight, up_weight, down_weight))
    gate_keep, up_keep = half_of(gate_weight, za_at, 1), half_of(up_weight, za_at, 1)
    gate_give, up_give = half_of(gate_weight, 1 - za_at, 1), half_of(up_weight, 1 - za_at, 1)
    down_give = half_of(down_weight, 1 - za_at, 0)
    token, (xz_far, fars, o_x, o_z) = meet(token, (xz_far, fars, o_x, o_z))
    mine = mine_of(local_low, tokens_y, tokens_z, fars)
    theirs, gate_zk0, gate_far, gate_xk = trade(
        token, [(mine, "core"), (gate_keep[:KEEP_ROWS], "zb"), (gate_give, "za"), (gate_keep, "x")]
    )
    qkv_all = jnp.concatenate(
        [
            in_order(qkv_keep, qkv_far, 0),
            in_order(z_keep, z_far, 0),
            in_order(x_keep, x_far, 0),
            in_order(xz_keep, xz_far, 0),
        ],
        axis=0,
    ).reshape(8, blk_rows + 16, qkv_width)
    qkv_cols = qkv_all[:, :blk_rows].reshape(width, qkv_width)
    gains = qkv_all[:, blk_rows, : 2 * blk_rows].astype(F32)
    gain_one = gains[:, :blk_rows].reshape(1, width)
    gain_two = gains[:, blk_rows:].reshape(1, width)
    head_sum = jnp.sum(qkv_all[:, blk_rows + 1, : 2 * HEAD_SIZE].astype(F32), axis=0, keepdims=True)
    qk_gains = jnp.concatenate([head_sum[:, :HEAD_SIZE], head_sum[:, HEAD_SIZE:]], axis=0)


    input_rows = jnp.concatenate([mine, theirs], axis=0).astype(F32)
    input_rho = lax.rsqrt(jnp.mean(input_rows * input_rows, axis=-1, keepdims=True) + EPSILON)
    normed = (input_rows * input_rho * gain_one).astype(BF16)
    raw = matmul(normed, qkv_cols)
    queries, kv_own = shape_heads(raw, cosine, sine, qk_gains)
    token, (queries, kv_own, gate_zk0, gate_far, gate_xk) = meet(
        token, (queries, kv_own, gate_zk0, gate_far, gate_xk)
    )
    kv_z, kv_x, up_far, grads_y = trade(
        token, [(kv_own, "zb"), (kv_own, "x"), (up_give, "za"), (grad_local, "y")]
    )
    token, (kv_x,) = meet(token, (kv_x,))
    (o_xz,) = trade(token, [(o_z, "x")])
    (attn_part,) = attend(offsets[0], tiles, queries, start_cols, [kv_own, kv_x], last=False)
    gate_pair = in_order(gate_keep, gate_far, 0)
    token, (kv_z, attn_part, grads_y, o_xz, up_far, gate_pair) = meet(
        token, (kv_z, attn_part, grads_y, o_xz, up_far, gate_pair)
    )
    gate_rest = jnp.concatenate([gate_keep[KEEP_ROWS:], gate_far], axis=0)
    token, (gate_rest,) = meet(token, (gate_rest,))
    kv_xz, gate_zr, grads_z = trade(token, [(kv_z, "x"), (gate_rest, "zb"), (grad_local, "za")])
    o_cols = jnp.concatenate([o_pair, o_z, o_x, o_xz], axis=1)
    token, (kv_xz, o_cols) = meet(token, (kv_xz, o_cols))
    (gate_xf,) = trade(token, [(gate_far, "x")])
    attn_low, inverse = attend(offsets[1], tiles, queries, start_cols, [kv_z, kv_xz], before=attn_part)
    given = matmul(attn_low[middle:], o_cols).astype(BF16)
    token, (given, attn_low, gate_xf, gate_zr, grads_z) = meet(token, (given, attn_low, gate_xf, gate_zr, grads_z))
    up_pair = in_order(up_keep, up_far, 0)
    given, up_z0, up_x0, grads_far, down_far = trade(
        token,
        [(given, "core"), (up_pair[:UP_ROWS], "zb"), (up_pair[:blk_rows], "x"), (grads_z, "y"), (down_give, "za")],
    )
    kept = matmul(attn_low[:middle], o_cols)
    token, (given, kept, up_z0, up_x0, up_pair, grads_far, down_far) = meet(
        token, (given, kept, up_z0, up_x0, up_pair, grads_far, down_far)
    )
    grad_mine = mine_of(grad_local, grads_y, grads_z, [grads_far])
    kept = kept + given.astype(F32)
    from_y, up_z1, up_x1 = trade(
        token,
        far_sums(kept) + [(up_pair[UP_ROWS:blk_rows], "zb"), (up_pair[blk_rows:], "x")],
    )
    gate_z = assemble(
        za_place,
        [
            (gate_zk0, 0, 1),
            (gate_zr[: blk_rows - KEEP_ROWS], KEEP_ROWS, 1),
            (gate_zr[blk_rows - KEEP_ROWS :], 0, -1),
        ],
        0,
    )
    token, (from_y, kept, up_x1, gate_z, up_z1, grad_mine) = meet(
        token, (from_y, kept, up_x1, gate_z, up_z1, grad_mine)
    )
    *nears, gate_xz, up_z2, grad_theirs = trade(
        token, near_sums(kept, from_y) + [(gate_z, "x"), (up_pair[blk_rows:], "zb"), (grad_mine, "core")]
    )
    token, (nears, kept, gate_xz, up_z2, grad_theirs) = meet(token, (nears, kept, gate_xz, up_z2, grad_theirs))
    up_z01 = jnp.concatenate([up_z0, up_z1], axis=0)
    residual = local_rows + own_sum(kept, nears)


    rho_two = lax.rsqrt(jnp.mean(residual * residual, axis=-1, keepdims=True) + EPSILON)
    unit_two = residual * rho_two
    mlp_low = (unit_two * gain_two).astype(BF16)
    token, (mlp_low,) = meet(token, (mlp_low,))
    mlp_y, mlp_z, down_zk, down_xf, up_xz0 = trade(
        token, near(mlp_low) + [(down_keep, "zb"), (down_far, "x"), (up_z01, "x")]
    )
    gate_cols = assemble(
        za_place,
        [(gate_pair, 0, 0), (gate_z, quarter, 0), (gate_xk, half, 1), (gate_xf, half, -1)]
        + [(gate_xz, half + quarter, 0)],
        0,
    )
    grad_mine, grad_theirs = after(token, (grad_mine, grad_theirs))
    grad_rows = assemble(za_place, [(grad_mine, 0, 0), (grad_theirs, middle, 0)], 0)
    token, (mlp_y, mlp_z, down_xf, up_xz0, gate_cols, down_zk, grad_rows) = meet(
        token, (mlp_y, mlp_z, down_xf, up_xz0, gate_cols, down_zk, grad_rows)
    )
    *fars, up_xz1, down_zf0 = trade(token, far(mlp_y, mlp_z, FAR) + [(up_z2, "x"), (down_far[:400], "zb")])
    token, (fars, down_zf0, up_xz1) = meet(token, (fars, down_zf0, up_xz1))
    mlp_mine = mine_of(mlp_low, mlp_y, mlp_z, fars)
    mlp_theirs, down_zf1, down_xzk, down_xzf0 = trade(
        token, [(mlp_mine, "core"), (down_far[400:], "zb"), (down_zk, "x"), (down_zf0, "x")]
    )
    up_cols = assemble(
        za_place,
        [
            (up_pair, 0, 0),
            (up_z01, quarter, 0),
            (up_z2, quarter + blk_rows, 0),
            (up_x0, half, 0),
            (up_x1, half + blk_rows, 0),
            (up_xz0, half + quarter, 0),
            (up_xz1, half + quarter + blk_rows, 0),
        ],
        0,
    )
    token, (mlp_theirs, up_cols) = meet(token, (mlp_theirs, up_cols))
    mlp_rows = jnp.concatenate([mlp_mine, mlp_theirs], axis=0)
    gate_act = matmul(mlp_rows, gate_cols)
    token, (gate_act, up_cols, mlp_rows) = meet(token, (gate_act, up_cols, mlp_rows))
    sig = jax.nn.sigmoid(gate_act)
    silu = gate_act * sig
    slope = sig * (1.0 + gate_act * (1.0 - sig))
    up_slope = silu.astype(BF16)
    token, (silu, slope, up_slope, up_cols, mlp_rows) = meet(token, (silu, slope, up_slope, up_cols, mlp_rows))
    up_act = matmul(mlp_rows, up_cols)
    hidden = (silu * up_act).astype(BF16)
    gate_slope = (up_act * slope).astype(BF16)
    token, (hidden, gate_slope, up_slope, down_zf1, down_xzk, down_xzf0) = meet(
        token, (hidden, gate_slope, up_slope, down_zf1, down_xzk, down_xzf0)
    )
    (down_xzf1,) = trade(token, [(down_zf1, "x")])
    down_zf = jnp.concatenate([down_zf0, down_zf1], axis=0)
    down_3 = contract_rows(hidden, grad_rows[:, 3 * quarter :]).astype(BF16)
    token, (down_3, down_xzf1, down_zf) = meet(token, (down_3, down_xzf1, down_zf))
    down_xzf = jnp.concatenate([down_xzf0, down_xzf1], axis=0)

    def columns_of(value, piece):
        return value[:, piece * quarter : (piece + 1) * quarter]

    down_cols = assemble(
        za_place,
        [
            (down_keep, 0, 1),
            (down_far, 0, -1),
            (down_zk, quarter, 1),
            (down_zf, quarter, -1),
            (down_xk, half, 1),
            (down_xf, half, -1),
            (down_xzk, half + quarter, 1),
            (down_xzf, half + quarter, -1),
        ],
        1,
    )
    token, (down_cols,) = meet(token, (down_cols,))
    (down_3,) = trade(token, [(down_3, "x")])
    hidden_grad = contract_cols(grad_rows, down_cols)
    gate_low = (hidden_grad * gate_slope.astype(F32)).astype(BF16)
    up_low = (hidden_grad * up_slope.astype(F32)).astype(BF16)

    kept, given = two_terms(gate_low, up_low, gate_cols, up_cols)
    token, (kept, given, gate_low, up_low, down_3) = meet(token, (kept, given, gate_low, up_low, down_3))
    hidden, grad_rows = after(token, (hidden, grad_rows))
    down_1 = (contract_rows(hidden, columns_of(grad_rows, 1)) + down_3.astype(F32)).astype(BF16)
    given, down_1a = trade(token, [(given, "core"), (down_1[:144], "zb")])
    gate_3 = contract_rows(columns_of(mlp_rows, 3), gate_low).astype(BF16)
    token, (given, kept, down_1, down_1a, gate_3) = meet(token, (given, kept, down_1, down_1a, gate_3))
    kept = kept + given.astype(F32)
    token, (kept,) = meet(token, (kept,))
    from_y, down_1b, gate_3 = trade(token, far_sums(kept) + [(down_1[144:416], "zb"), (gate_3, "x")])
    down_2 = contract_rows(hidden, columns_of(grad_rows, 2)).astype(BF16)
    up_3 = contract_rows(columns_of(mlp_rows, 3), up_low).astype(BF16)
    gate_1 = contract_rows(columns_of(mlp_rows, 1), gate_low)
    token, (from_y, kept, down_1b, gate_3, down_2, up_3, gate_1) = meet(
        token, (from_y, kept, down_1b, gate_3, down_2, up_3, gate_1)
    )
    *nears, down_1c, up_3 = trade(token, near_sums(kept, from_y) + [(down_1[416:], "zb"), (up_3, "x")])
    gate_1 = (gate_1 + gate_3.astype(F32)).astype(BF16)
    gate_2 = contract_rows(columns_of(mlp_rows, 2), gate_low).astype(BF16)
    up_1 = contract_rows(columns_of(mlp_rows, 1), up_low)
    up_2 = contract_rows(columns_of(mlp_rows, 2), up_low).astype(BF16)
    token, (nears, kept, down_1c, up_3, gate_2, up_1, up_2, gate_1) = meet(
        token, (nears, kept, down_1c, up_3, gate_2, up_1, up_2, gate_1)
    )
    mlp_in_grad = own_sum(kept, nears)
    gain_two_part = jnp.sum(mlp_in_grad * unit_two, axis=0, keepdims=True)
    scaled = mlp_in_grad * gain_two
    inner = jnp.mean(scaled * unit_two, axis=-1, keepdims=True)
    residual_grad = grad_local.astype(F32) + rho_two * (scaled - unit_two * inner)


    branch_low = residual_grad.astype(BF16)
    token, (branch_low, residual_grad, gain_two_part, gate_1) = meet(
        token, (branch_low, residual_grad, gain_two_part, gate_1)
    )
    branch_y, branch_z, gate_1a, gate_2 = trade(
        token, near(branch_low) + [(gate_1[:blk_rows], "zb"), (gate_2, "x")]
    )
    hidden, down_cols = after(token, (hidden, down_cols))
    out_given = matmul(hidden[middle:], down_cols).astype(BF16)
    up_1 = (up_1 + up_3.astype(F32)).astype(BF16)
    down_0 = contract_rows(hidden, columns_of(grad_rows, 0)) + jnp.concatenate(
        [down_1a, down_1b, down_1c], axis=0
    ).astype(F32)
    token, (branch_y, branch_z, gate_1a, gate_2, out_given, up_1, down_0, gate_low, up_low) = meet(
        token, (branch_y, branch_z, gate_1a, gate_2, out_given, up_1, down_0, gate_low, up_low)
    )
    gate_0 = contract_rows(columns_of(mlp_rows, 0), gate_low) + gate_2.astype(F32)
    *fars, gate_1b, down_2a = trade(
        token, far(branch_y, branch_z, FAR) + [(gate_1[blk_rows:384], "zb"), (down_2[:384], "x")]
    )
    hidden, down_cols = after(token, (hidden, down_cols))
    out_kept = matmul(hidden[:middle], down_cols)
    token, (fars, out_kept, gate_1b, down_2a, gate_0) = meet(token, (fars, out_kept, gate_1b, down_2a, gate_0))
    branch_mine = mine_of(branch_low, branch_y, branch_z, fars)
    branch_theirs, gate_1c, down_2b, out_given = trade(
        token,
        [(branch_mine, "core"), (gate_1[384:464], "zb"), (down_2[384:512], "x"), (out_given, "core")],
    )
    grad_own = contract_cols(branch_mine, o_cols).astype(BF16)
    attn_grad = jnp.concatenate([grad_own, contract_cols(branch_theirs, o_cols).astype(BF16)], axis=0)
    mixed = jnp.concatenate([gate_1[464:], up_1[:144]], axis=0)
    token, (attn_grad, gate_1c, down_2b, mixed) = meet(token, (attn_grad, gate_1c, down_2b, mixed))
    mixed, up_2a, down_2c = trade(token, [(mixed, "zb"), (up_2[:blk_rows], "x"), (down_2[512:], "x")])
    query_part, kv_1, kv_3 = attend_back(
        offsets[1], tiles, queries, start_rows, inverse, attn_low, attn_grad, [kv_z, kv_xz], last=False
    )
    out_kept = out_kept + out_given.astype(F32)
    token, (query_part, kv_1, kv_3, mixed, up_2a, down_2c, out_kept) = meet(
        token, (query_part, kv_1, kv_3, mixed, up_2a, down_2c, out_kept)
    )
    gate_1d, up_1a = mixed[:48], mixed[48:]
    kv_3, up_1b, out_from = trade(token, [(kv_3, "x"), (up_1[144:336], "zb")] + far_sums(out_kept))
    query_grad, kv_0, kv_2 = attend_back(
        offsets[0],
        tiles,
        queries,
        start_rows,
        inverse,
        attn_low,
        attn_grad,
        [kv_own, kv_x],
        before=query_part,
    )
    token, (query_grad, kv_0, kv_2, kv_3, up_1b, out_from) = meet(
        token, (query_grad, kv_0, kv_2, kv_3, up_1b, out_from)
    )
    kv_1 = (kv_1.astype(F32) + kv_3.astype(F32)).astype(BF16)
    kv_1, kv_2, *out_nears = trade(token, [(kv_1, "zb"), (kv_2, "x")] + near_sums(out_kept, out_from))
    token, (kv_2, branch_mine, branch_theirs, up_low, query_grad, gate_0, down_0) = meet(
        token, (kv_2, branch_mine, branch_theirs, up_low, query_grad, gate_0, down_0)
    )
    q_low, q_gain_part = shape_back(raw, query_grad, cosine, sine, qk_gains, 2, 0, 0, HEAD_SIZE**-0.5)
    q_3 = swap(contract_rows(columns_of(normed, 3), q_low).astype(BF16), "x")
    branch_rows = jnp.concatenate([branch_mine, branch_theirs], axis=0)
    o_3 = contract_rows(attn_low, columns_of(branch_rows, 3)).astype(BF16)
    q_1 = contract_rows(columns_of(normed, 1), q_low)
    gate_part = gate_0 + jnp.concatenate([gate_1a, gate_1b, gate_1c, gate_1d], axis=0).astype(F32)
    gate_mine, gate_give = za_parts(gate_part, 0)
    down_part = down_0 + jnp.concatenate([down_2a, down_2b, down_2c], axis=0).astype(F32)
    down_mine, down_give = za_parts(down_part, 1)
    token, (kv_1, out_nears, q_low, q_gain_part, o_3, gate_mine, gate_give, down_mine, down_give, q_1) = meet(
        token, (kv_1, out_nears, q_low, q_gain_part, o_3, gate_mine, gate_give, down_mine, down_give, q_1)
    )
    gate_give, up_1c, down_give, up_2b = trade(
        token, [(gate_give, "za"), (up_1[336:], "zb"), (down_give, "za"), (up_2[blk_rows:], "x")]
    )
    kv_grad = (kv_0.astype(F32) + kv_1.astype(F32) + kv_2.astype(F32)).astype(BF16)
    kv_low, k_gain_part = shape_back(raw, kv_grad, cosine, sine, qk_gains, 1, 2, 1, 1.0)
    low = jnp.concatenate([q_low, kv_low], axis=1)
    given = contract_cols(low[middle:], qkv_cols).astype(BF16)
    w_3 = contract_rows(columns_of(normed, 3), kv_low).astype(BF16)
    q_1 = (q_1 + q_3.astype(F32)).astype(BF16)
    token, (given, low, kv_low, k_gain_part, w_3, q_1, gate_give, up_1c, up_2b) = meet(
        token, (given, low, kv_low, k_gain_part, w_3, q_1, gate_give, up_1c, up_2b)
    )
    given_low = given
    kv_late, normed, low = after(token, (kv_low, normed, low))
    given, q_1, w_3, o_3 = trade(token, [(given, "core"), (q_1, "zb"), (w_3, "x"), (o_3, "x")])
    terms = contract_cols(low[:middle], qkv_cols)
    w_1 = contract_rows(columns_of(normed, 1), kv_late)
    token, (given, terms, q_1, w_3, o_3, w_1, down_give, up_low, attn_low, branch_rows) = meet(
        token, (given, terms, q_1, w_3, o_3, w_1, down_give, up_low, attn_low, branch_rows)
    )
    kept = terms + given.astype(F32)
    w_1 = (w_1 + w_3.astype(F32)).astype(BF16)
    token, (kept, w_1) = meet(token, (kept, w_1))
    from_y, w_1 = trade(token, far_sums(kept) + [(w_1, "zb")])
    o_1 = (contract_rows(attn_low, columns_of(branch_rows, 1)) + o_3.astype(F32)).astype(BF16)
    o_2 = contract_rows(attn_low, columns_of(branch_rows, 2)).astype(BF16)
    terms_low, given_low, normed_low = after(token, (terms, given_low, normed))
    gain_one_part = (
        jnp.sum(
            terms_low * normed_low[:middle].astype(F32) + given_low.astype(F32) * normed_low[middle:].astype(F32),
            axis=0,
            keepdims=True,
        )
        / gain_one
    )
    gain_sum = jnp.concatenate(
        [
            *reorder(from_order, [gain_one_part, gain_two_part], [F32, F32]),
            jnp.sum(q_gain_part, axis=0, keepdims=True),
            jnp.sum(k_gain_part, axis=0, keepdims=True),
        ],
        axis=1,
    )
    qw_2 = contract_rows(columns_of(normed, 2), low).astype(BF16)
    token, (from_y, kept, w_1, o_1, qw_2, o_2, gain_sum, up_low, attn_low, branch_rows, low) = meet(
        token, (from_y, kept, w_1, o_1, qw_2, o_2, gain_sum, up_low, attn_low, branch_rows, low)
    )
    *nears, o_1, qw_2, gain_x = trade(
        token, near_sums(kept, from_y) + [(o_1, "zb"), (qw_2, "x"), (gain_sum, "core")]
    )
    gain_sum = gain_sum + gain_x
    gain_sum = gain_sum + swap(gain_sum, "zb")
    gate_mine, gate_give, down_mine, down_give = after(token, (gate_mine, gate_give, down_mine, down_give))
    up_part = (
        contract_rows(columns_of(mlp_rows, 0), up_low)
        + jnp.concatenate([up_2a, up_2b], axis=0).astype(F32)
        + jnp.concatenate([up_1a, up_1b, up_1c], axis=0).astype(F32)
    )
    up_mine, up_give = za_parts(up_part, 0)
    qw_0 = contract_rows(columns_of(normed, 0), low)
    o_0 = contract_rows(attn_low, columns_of(branch_rows, 0))
    block_out = residual + own_sum(out_kept, out_nears)
    token, (nears, kept, qw_2, qw_0, o_0, block_out, gain_sum, o_1, up_mine, up_give) = meet(
        token, (nears, kept, qw_2, qw_0, o_0, block_out, gain_sum, o_1, up_mine, up_give)
    )
    qkv_mine, qkv_give = za_parts(qw_0 + qw_2.astype(F32) + jnp.concatenate([q_1, w_1], axis=1).astype(F32), 0)
    token, (qkv_mine, qkv_give) = meet(token, (qkv_mine, qkv_give))
    gain_x, qkv_give, up_give, o_2 = trade(
        token, [(gain_sum, "za"), (qkv_give, "za"), (up_give, "za"), (o_2, "x")]
    )
    gain_sum = gain_sum + gain_x
    gain_x = swap(gain_sum, "y")
    o_mine, o_give = za_parts(o_0 + o_2.astype(F32) + o_1.astype(F32), 1)
    token, (gain_sum, o_mine, o_give) = meet(token, (gain_sum + gain_x, o_mine, o_give))
    gain_x, o_give = trade(token, [(gain_sum, "x"), (o_give, "za")])
    gain_sum = gain_sum + gain_x
    input_grad = own_sum(kept, nears)
    unit_one = local_rows * (rho_one := lax.rsqrt(jnp.mean(local_rows * local_rows, axis=-1, keepdims=True) + EPSILON))
    scaled = input_grad * gain_one
    inner = jnp.mean(scaled * unit_one, axis=-1, keepdims=True)
    in_grad = residual_grad + rho_one * (scaled - unit_one * inner)
    block_out, in_grad = reorder(from_order, [block_out, in_grad], [BF16, F32])
    device = (((y_at * 2 + core_at) * 2 + zb_at) * 2 + za_at) * 2 + x_at

    def own_slice(first, length):
        share = length // 32
        return lax.dynamic_slice_in_dim(gain_sum[0], first + device * share, share, axis=0)

    qkv_parts = za_join(qkv_mine, qkv_give)

    def columns(lo, hi):
        return jnp.concatenate([part[:, lo:hi] for part in qkv_parts], axis=1)

    return (
        block_out,
        in_grad,
        own_slice(0, width),
        columns(0, q_width),
        columns(q_width, q_width + k_width),
        columns(q_width + k_width, qkv_width),
        own_slice(2 * width, HEAD_SIZE),
        own_slice(2 * width + HEAD_SIZE, HEAD_SIZE),
        jnp.concatenate(za_join(o_mine, o_give), axis=0),
        own_slice(width, width),
        jnp.concatenate(za_join(gate_mine, gate_give), axis=1),
        jnp.concatenate(za_join(up_mine, up_give), axis=1),
        jnp.concatenate(za_join(down_mine, down_give), axis=0),
    )


def layer(
    sizes,
    tokens,
    out_grad,
    seq_lengths,
    block_deal,
    norm_gain,
    q_weight,
    k_weight,
    v_weight,
    q_gain,
    k_gain,
    o_weight,
    mlp_gain,
    gate_weight,
    up_weight,
    down_weight,
):
    y_count, core_count, zb_count, za_count, x_count = sizes
    pairwise = sizes == (2, 2, 2, 2, 2)
    all_axes = ("y", "core", "zb", "za", "x")
    y_at, core_at, zb_at, za_at, x_at = (lax.axis_index(name) for name in all_axes)
    tok_dev, width = tokens.shape
    blk_rows = q_weight.shape[0]
    group_count = zb_count * x_count
    member_count = y_count * core_count * za_count
    head_count = y_count * core_count
    rows = member_count * tok_dev
    piece = za_count * blk_rows


    def gather_rows(value):
        if not pairwise:
            return lax.all_gather(value, ("y", "core", "za"), axis=0, tiled=True)
        half = tok_dev // 2
        along_y = swap(value, "y")
        along_z = swap(value, "za")
        parts = [value, along_y, along_z, swap(along_z[:half], "y"), swap(along_y[half:], "za")]
        mine = jnp.concatenate(parts, axis=0)
        return jnp.concatenate([mine, swap(mine, "core")], axis=0)

    def scatter_rows(part_of):
        if not pairwise:
            full = part_of(slice(0, rows)).astype(BF16)
            return lax.psum_scatter(full, ("y", "core", "za"), scatter_dimension=0, tiled=True).astype(F32)
        middle = rows // 2
        half = tok_dev // 2
        given = swap(part_of(slice(middle, rows)).astype(BF16), "core")
        kept = part_of(slice(0, middle)) + given.astype(F32)
        own, to_y, to_z, far = (kept[i * tok_dev : (i + 1) * tok_dev] for i in range(4))
        far = far.astype(BF16)
        from_y = swap(far[:half], "y").astype(F32)
        from_z = swap(far[half:], "za").astype(F32)
        z_sum = jnp.concatenate([to_z[:half] + from_y, to_z[half:]], axis=0).astype(BF16)
        y_sum = jnp.concatenate([to_y[:half], to_y[half:] + from_z], axis=0).astype(BF16)
        return own + swap(y_sum, "y").astype(F32) + swap(z_sum, "za").astype(F32)


    def gather_pieces(own, axis):
        if not pairwise:
            return lax.all_gather(own, ("zb", "x"), axis=axis, tiled=True)
        along_z = swap(own, "zb")
        return jnp.concatenate([own, along_z, swap(own, "x"), swap(along_z, "x")], axis=axis)

    def scatter_pieces(part_of, length, axis):
        if not pairwise:
            full = part_of(0, length).astype(BF16)
            return lax.psum_scatter(full, ("zb", "x"), scatter_dimension=axis, tiled=True).astype(F32)
        half, quarter = length // 2, length // 4
        given = swap(part_of(half, length).astype(BF16), "x")
        kept = part_of(0, half) + given.astype(F32)
        given = swap(lax.slice_in_dim(kept, quarter, half, axis=axis).astype(BF16), "zb")
        return lax.slice_in_dim(kept, 0, quarter, axis=axis) + given.astype(F32)

    def in_order(mine, other, axis):
        first = jnp.where(za_at == 0, mine, other)
        second = jnp.where(za_at == 0, other, mine)
        return jnp.concatenate([first, second], axis=axis)

    def gather_weight(part_of, axis):
        mine = part_of(za_at)
        if za_count > 1:
            mine = in_order(mine, swap(part_of(1 - za_at), "za"), axis)
        return gather_pieces(mine, axis)

    def scatter_weight(part_of, axis):
        part = scatter_pieces(part_of, width, axis)
        if za_count == 1:
            return [part]
        first = lax.slice_in_dim(part, 0, blk_rows, axis=axis)
        second = lax.slice_in_dim(part, blk_rows, 2 * blk_rows, axis=axis)
        mine = jnp.where(za_at == 0, first, second)
        other = swap(jnp.where(za_at == 0, second, first).astype(BF16), "za").astype(F32)
        return [jnp.where(za_at == 0, mine, other), jnp.where(za_at == 0, other, mine)]

    def half_of(weight, at, axis):
        size = weight.shape[axis] // za_count
        return lax.dynamic_slice_in_dim(weight, at * size, size, axis=axis)


    def piece_group(index):
        if pairwise:
            return zb_at ^ (index % 2), x_at ^ (index // 2)
        return index // x_count, index % x_count

    def to_pieces(value):
        blocks = []
        for index in range(group_count):
            zb_of, x_of = piece_group(index)
            for za_of in range(za_count):
                block = (zb_of * za_count + za_of) * x_count + x_of
                blocks.append(lax.dynamic_slice_in_dim(value, block * blk_rows, blk_rows, axis=1))
        return jnp.concatenate(blocks, axis=1) if pairwise else value

    def from_pieces(value):
        if not pairwise:
            return value
        blocks = []
        for block in range(group_count * za_count):
            zb_of, za_of, x_of = block // 4, block // 2 % 2, block % 2
            index = (x_at ^ x_of) * 2 + (zb_at ^ zb_of)
            blocks.append(lax.dynamic_slice_in_dim(value, (index * 2 + za_of) * blk_rows, blk_rows, axis=1))
        return jnp.concatenate(blocks, axis=1)


    per_span = head_count // 2
    member = jnp.arange(member_count, dtype=jnp.int32)
    if pairwise:
        member_y, member_za, member_core = y_at ^ (member % 2), za_at ^ (member // 2 % 2), core_at ^ (member // 4)
    else:
        member_za = member % za_count
        member_core = member // za_count % core_count
        member_y = member // (za_count * core_count)
    group = jnp.arange(group_count, dtype=jnp.int32)
    group_zb, group_x = piece_group(group)
    member_head = member_y * core_count + member_core
    span_table = jnp.arange(block_deal.shape[0], dtype=jnp.int32)

    def natural_tile(zb_of, x_of):
        blk = (zb_of * za_count + member_za) * x_count + x_of
        entry = 2 * blk + member_head // per_span
        span = jnp.sum(
            jnp.where(entry[..., None] == span_table, block_deal, 0), axis=-1, dtype=jnp.int32
        )
        return span * per_span + member_head % per_span

    query_tile = natural_tile(zb_at, x_at)
    key_tile = natural_tile(group_zb[:, None], group_x[:, None]).reshape(-1)
    tile_ids = jnp.arange(key_tile.shape[0], dtype=jnp.int32)
    offsets = jnp.sum(
        jnp.where(key_tile[None, :] == tile_ids[:, None], tile_ids[None, :] * tok_dev, 0), axis=1, dtype=jnp.int32
    )
    natural = query_tile[:, None] * tok_dev + jnp.arange(tok_dev, dtype=jnp.int32)[None, :]
    seq_ids = jnp.arange(seq_lengths.shape[0], dtype=jnp.int32)
    seq_ends = jnp.sum(jnp.where(seq_ids[None, :] <= seq_ids[:, None], seq_lengths[None, :], 0), axis=1, dtype=jnp.int32)
    starts = jnp.max(jnp.where(seq_ends <= natural[..., None], seq_ends, 0), axis=-1)
    tiles = (query_tile, starts[:, 0] // (2 * tok_dev))
    start_rows = jnp.stack([starts, starts], axis=1)
    start_cols = jnp.broadcast_to(starts.reshape(rows, 1), (rows, 128))
    places = (natural - starts).reshape(rows)
    half_width = HEAD_SIZE // 2
    frequency = jnp.power(ROPE_BASE, -jnp.arange(half_width, dtype=F32) * (2.0 / HEAD_SIZE))
    angles = places.astype(F32)[:, None] * frequency[None, :]
    cosine = jnp.cos(angles)
    sine = jnp.sin(angles)
    cosine = jnp.concatenate([cosine, cosine], axis=1)
    sine = jnp.concatenate([-sine, sine], axis=1)


    q_width = q_weight.shape[1] // za_count
    k_width = k_weight.shape[1] // za_count
    qkv_width = q_width + 2 * k_width
    gain_pad = 16

    gain_row = jnp.concatenate([norm_gain, mlp_gain])
    head_gains = jnp.concatenate([q_gain, k_gain])

    def gain_rows():
        top = jnp.pad(gain_row, (0, qkv_width - gain_row.shape[0]))[None]
        bottom = jnp.pad(head_gains, (0, qkv_width - head_gains.shape[0]))[None]
        return jnp.concatenate([top, bottom, jnp.zeros((gain_pad - 2, qkv_width), BF16)], axis=0)

    def qkv_part(at):
        return jnp.concatenate(
            [half_of(q_weight, at, 1), half_of(k_weight, at, 1), half_of(v_weight, at, 1), ], axis=1
        )

    padded = blk_rows + gain_pad
    own_gain_rows = gain_rows()
    qkv_all = gather_weight(lambda at: jnp.concatenate([qkv_part(at), own_gain_rows], axis=0), 0)
    qkv_all = qkv_all.reshape(group_count * za_count, padded, qkv_width)
    qkv_cols = qkv_all[:, :blk_rows].reshape(width, qkv_width)
    gains = qkv_all[:, blk_rows, : 2 * blk_rows].astype(F32)
    gain_one = gains[:, :blk_rows].reshape(1, width)
    gain_two = gains[:, blk_rows:].reshape(1, width)
    small = q_gain.shape[0]
    head_parts = qkv_all[:, blk_rows + 1, : 2 * small].astype(F32).reshape(group_count * za_count, 2, small)

    def head_gain(which):
        return from_small(head_parts[:, which])

    def from_small(parts):
        if not pairwise:
            return parts.reshape(1, -1)
        rows_of = []
        for block in range(8):
            zb_of, za_of, x_of = block // 4, block // 2 % 2, block % 2
            index = ((x_at ^ x_of) * 2 + (zb_at ^ zb_of)) * 2 + za_of
            rows_of.append(lax.dynamic_slice_in_dim(parts, index, 1, axis=0))
        return jnp.concatenate(rows_of, axis=1)

    qk_gains = jnp.concatenate([head_gain(0), head_gain(1)], axis=0)


    local_low = to_pieces(tokens)
    local_rows = local_low.astype(F32)
    input_rows = gather_rows(local_low).astype(F32)
    o_cols = gather_weight(lambda at: half_of(o_weight, at, 0), 1)
    gu_cols = gather_weight(
        lambda at: jnp.concatenate([half_of(gate_weight, at, 1), half_of(up_weight, at, 1)], axis=1), 0
    )
    down_cols = gather_weight(lambda at: half_of(down_weight, at, 0), 1)
    grad_local = to_pieces(out_grad)
    grad_rows = gather_rows(grad_local)

    def unit_rows(value):
        return value * lax.rsqrt(jnp.mean(value * value, axis=-1, keepdims=True) + EPSILON)

    input_unit = unit_rows(input_rows)
    normed = (input_unit * gain_one).astype(BF16)
    raw = matmul(normed, qkv_cols)
    queries, kv_own = shape_heads(raw, cosine, sine, qk_gains)
    key_values = gather_pieces(kv_own, 0)
    attn_low, inverse = attend(offsets, tiles, queries, start_cols, [key_values])
    residual = local_rows + scatter_rows(lambda at: matmul(attn_low[at], o_cols))


    rho_two = lax.rsqrt(jnp.mean(residual * residual, axis=-1, keepdims=True) + EPSILON)
    unit_two = residual * rho_two
    mlp_rows = gather_rows((unit_two * gain_two).astype(BF16))
    ff = gu_cols.shape[1] // 2
    gate_up = matmul(mlp_rows, gu_cols)
    gate_act, up_act = gate_up[:, :ff], gate_up[:, ff:]
    sig = jax.nn.sigmoid(gate_act)
    silu = gate_act * sig
    hidden = (silu * up_act).astype(BF16)
    hidden_grad = contract_cols(grad_rows, down_cols)
    gate_low = (hidden_grad * up_act * (sig * (1.0 + gate_act * (1.0 - sig)))).astype(BF16)
    up_low = (hidden_grad * silu).astype(BF16)
    gu_low = jnp.concatenate([gate_low, up_low], axis=1)
    mlp_in_grad = scatter_rows(lambda at: contract_cols(gu_low[at], gu_cols))

    down_parts = scatter_weight(lambda lo, hi: contract_rows(hidden, grad_rows[:, lo:hi]), 1)
    gate_parts = scatter_weight(lambda lo, hi: contract_rows(mlp_rows[:, lo:hi], gate_low), 0)
    up_parts = scatter_weight(lambda lo, hi: contract_rows(mlp_rows[:, lo:hi], up_low), 0)
    block_out = residual + scatter_rows(lambda at: matmul(hidden[at], down_cols))

    gain_two_part = jnp.sum(mlp_in_grad * unit_two, axis=0, keepdims=True)
    scaled = mlp_in_grad * gain_two
    inner = jnp.mean(scaled * unit_two, axis=-1, keepdims=True)
    residual_grad = grad_local.astype(F32) + rho_two * (scaled - unit_two * inner)


    branch_rows = gather_rows(residual_grad.astype(BF16))
    attn_grad = contract_cols(branch_rows, o_cols).astype(BF16)
    query_grad, kv_grads = attend_back(
        offsets, tiles, queries, start_rows, inverse, attn_low, attn_grad, [key_values]
    )
    o_parts = scatter_weight(lambda lo, hi: contract_rows(attn_low, branch_rows[:, lo:hi]), 1)
    kv_grad = scatter_pieces(lambda lo, hi: kv_grads[lo:hi].astype(F32), kv_grads.shape[0], 0).astype(BF16)
    q_low, q_gain_part = shape_back(raw, query_grad, cosine, sine, qk_gains, 2, 0, 0, HEAD_SIZE**-0.5)
    kv_low, k_gain_part = shape_back(raw, kv_grad, cosine, sine, qk_gains, 1, 2, 1, 1.0)
    low = jnp.concatenate([q_low, kv_low], axis=1)

    gain_one_parts = []

    def input_terms(at):
        terms = contract_cols(low[at], qkv_cols)
        gain_one_parts.append(jnp.sum(terms * input_unit[at], axis=0, keepdims=True))
        return terms

    input_grad = scatter_rows(input_terms)
    qkv_parts = scatter_weight(lambda lo, hi: contract_rows(normed[:, lo:hi], low), 0)

    gain_sum = jnp.concatenate(
        [
            from_pieces(sum(gain_one_parts)),
            from_pieces(gain_two_part),
            jnp.sum(q_gain_part, axis=0, keepdims=True),
            jnp.sum(k_gain_part, axis=0, keepdims=True),
        ],
        axis=1,
    )
    if pairwise:
        for name in ("core", "y", "za", "x", "zb"):
            gain_sum = gain_sum + swap(gain_sum, name)
    else:
        gain_sum = lax.psum(gain_sum, all_axes)

    unit_one = local_rows * (rho_one := lax.rsqrt(jnp.mean(local_rows * local_rows, axis=-1, keepdims=True) + EPSILON))
    scaled = input_grad * gain_one
    inner = jnp.mean(scaled * unit_one, axis=-1, keepdims=True)
    in_grad = residual_grad + rho_one * (scaled - unit_one * inner)

    device = (((y_at * core_count + core_at) * zb_count + zb_at) * za_count + za_at) * x_count + x_at
    device_count = head_count * zb_count * za_count * x_count

    def own_slice(first, length):
        share = length // device_count
        return lax.dynamic_slice_in_dim(gain_sum[0], first + device * share, share, axis=0)

    def join(parts, lo, hi, axis):
        cut = [lax.slice_in_dim(part, lo, hi, axis=axis) for part in parts]
        return jnp.concatenate(cut, axis=axis)

    return (
        from_pieces(block_out).astype(BF16),
        from_pieces(in_grad),
        own_slice(0, width),
        join(qkv_parts, 0, q_width, 1),
        join(qkv_parts, q_width, q_width + k_width, 1),
        join(qkv_parts, q_width + k_width, qkv_width, 1),
        own_slice(2 * width, HEAD_SIZE),
        own_slice(2 * width + HEAD_SIZE, HEAD_SIZE),
        jnp.concatenate(o_parts, axis=0),
        own_slice(width, width),
        jnp.concatenate(gate_parts, axis=1),
        jnp.concatenate(up_parts, axis=1),
        jnp.concatenate(down_parts, axis=0),
    )


def solution(mesh):
    heads, blks = mesh.shape["head"], mesh.shape["blk"]
    za_count = KEY_VALUE_HEADS // heads
    side = math.isqrt(blks // za_count)
    sizes = (heads // 2, 2, side, za_count, side)
    names = ("y", "core", "zb", "za", "x")
    devices = mesh.devices.reshape(sizes)
    inner = Mesh(devices, names)
    head, blk = ("y", "core"), ("zb", "za", "x")
    rows, in_weight, out_weight, gain = P(names, None), P(blk, head), P(head, blk), P(blk)
    return jax.shard_map(
        paired_layer if sizes == (2, 2, 2, 2, 2) else functools.partial(layer, sizes),
        mesh=inner,
        in_specs=(
            rows,
            rows,
            P(),
            P(),
            gain,
            in_weight,
            in_weight,
            in_weight,
            gain,
            gain,
            out_weight,
            gain,
            in_weight,
            in_weight,
            out_weight,
        ),
        out_specs=(
            rows,
            rows,
            P(names),
            in_weight,
            in_weight,
            in_weight,
            P(names),
            P(names),
            out_weight,
            P(names),
            in_weight,
            in_weight,
            out_weight,
        ),
        check_vma=False,
    )
```

```python
import functools
import math

import jax
import jax.numpy as jnp
from jax import lax
from jax.experimental import pallas as pl
from jax.experimental.pallas import tpu as pltpu
from jax.sharding import Mesh
from jax.sharding import PartitionSpec as P

HEAD_SIZE = 128
KEY_VALUE_HEADS = 8
EPSILON = 1e-06
ROPE_BASE = 1000000.0
F32 = jnp.float32
BF16 = jnp.bfloat16
SWAP = [(0, 1), (1, 0)]
PAIRS_OF_ROWS = (((0,), (0,)), ((), ()))
PAIRS_OF_COLS = (((1,), (1,)), ((), ()))
VMEM = pltpu.MemorySpace.VMEM
LIGHT = pl.CostEstimate(flops=1000, bytes_accessed=1000, transcendentals=0)
SMEM = pltpu.MemorySpace.SMEM


def matmul(left, right):
    return jnp.dot(left, right, preferred_element_type=F32)


def contract_rows(left, right):
    return lax.dot_general(left, right, PAIRS_OF_ROWS, preferred_element_type=F32)


def contract_cols(left, right):
    return lax.dot_general(left, right, PAIRS_OF_COLS, preferred_element_type=F32)


def swap(value, axis):
    return lax.ppermute(value, axis, SWAP)


def attend_kernel(off_ref, tile_ref, low_ref, q_ref, start_ref, *refs, parts, first, last):
    half = 128
    kv_refs, refs = refs[:parts], refs[parts:]
    if not first:
        before_ref, refs = refs[0], refs[1:]
    if last:
        out_ref, inv_ref, kv_ref, acc_ref = refs
    else:
        after_ref, kv_ref, acc_ref = refs
    share = kv_refs[0].shape[0]
    for part, ref in enumerate(kv_refs):
        kv_ref[part * share : (part + 1) * share, :] = ref[...]
    lane = lax.broadcasted_iota(jnp.int32, (256, 256), 1)
    row = lax.broadcasted_iota(jnp.int32, (256, 256), 0) % half
    ones = jnp.ones((256, HEAD_SIZE), BF16)

    def tile(index, unused):
        rows = pl.ds(pl.multiple_of(index * half, half), half)
        queries = jnp.concatenate([q_ref[rows, :HEAD_SIZE], q_ref[rows, HEAD_SIZE:]], axis=0)
        start = start_ref[rows, :]
        start = jnp.concatenate([start, start], axis=1)
        start = jnp.concatenate([start, start], axis=0)
        places = tile_ref[index] * half + row
        acc_ref[...] = jnp.zeros_like(acc_ref) if first else before_ref[index]

        def step(block, unused_step):
            at = off_ref[2 * block]

            @pl.when(at >= 0)
            def _():
                low = pl.ds(pl.multiple_of(at, half), half)
                high = pl.ds(pl.multiple_of(off_ref[2 * block + 1], half), half)
                keys = jnp.concatenate([kv_ref[low, :HEAD_SIZE], kv_ref[high, :HEAD_SIZE]], axis=0)
                values = jnp.concatenate([kv_ref[low, HEAD_SIZE:], kv_ref[high, HEAD_SIZE:]], axis=0)
                scores = contract_cols(queries, keys)
                natural = block * 256 + lane
                allowed = (natural <= places) & (natural >= start)
                weights = jnp.where(allowed, jnp.exp(scores), 0.0).astype(BF16)
                acc_ref[...] += matmul(weights, jnp.concatenate([values, ones], axis=1))

            return unused_step

        lax.fori_loop(low_ref[index], tile_ref[index] // 2 + 1, step, 0)
        if last:
            inverse = 1.0 / acc_ref[:, HEAD_SIZE:]
            attended = (acc_ref[:, :HEAD_SIZE] * inverse).astype(BF16)
            out_ref[rows, :HEAD_SIZE] = attended[:half]
            out_ref[rows, HEAD_SIZE:] = attended[half:]
            inv_ref[index, 0:1, :] = jnp.transpose(inverse[:half])[0:1, :]
            inv_ref[index, 1:2, :] = jnp.transpose(inverse[half:])[0:1, :]
        else:
            after_ref[index] = acc_ref[...]
        return unused

    lax.fori_loop(0, q_ref.shape[0] // half, tile, 0)


def attend_back_kernel(
    off_ref, tile_ref, low_ref, q_ref, start_ref, inv_ref, out_ref, grad_ref, *refs, parts, first, last
):
    half = 128
    kv_refs, refs = refs[:parts], refs[parts:]
    if not first:
        before_ref, refs = refs[0], refs[1:]
    dq_ref, *dkv_refs = refs[: 1 + parts]
    kv_ref, dk_ref, dv_ref, acc_ref = refs[1 + parts :]
    share = kv_refs[0].shape[0]
    for part, ref in enumerate(kv_refs):
        kv_ref[part * share : (part + 1) * share, :] = ref[...]
    key_row = lax.broadcasted_iota(jnp.int32, (256, 256), 0)
    query_lane = lax.broadcasted_iota(jnp.int32, (1, 256), 1) % half

    def clear(index, unused):
        rows = pl.ds(pl.multiple_of(index * 256, 256), 256)
        dk_ref[rows, :] = jnp.zeros((256, HEAD_SIZE), F32)
        dv_ref[rows, :] = jnp.zeros((256, HEAD_SIZE), F32)
        return unused

    lax.fori_loop(0, dk_ref.shape[0] // 256, clear, 0)

    def tile(index, unused):
        rows = pl.ds(pl.multiple_of(index * half, half), half)

        def both(ref):
            return jnp.concatenate([ref[rows, :HEAD_SIZE], ref[rows, HEAD_SIZE:]], axis=0)

        def along(ref):
            return jnp.concatenate([ref[index, 0:1, :], ref[index, 1:2, :]], axis=1)

        queries = both(q_ref)
        grads = both(grad_ref)
        products = both(out_ref).astype(F32) * grads.astype(F32)
        deltas = jnp.sum(jnp.transpose(products), axis=0, keepdims=True)
        inverse = along(inv_ref)
        start = along(start_ref)
        places = tile_ref[index] * half + query_lane
        acc_ref[...] = jnp.zeros_like(acc_ref) if first else both(before_ref)

        def step(block, unused_step):
            at = off_ref[2 * block]

            @pl.when(at >= 0)
            def _():
                low = pl.ds(pl.multiple_of(at, half), half)
                high = pl.ds(pl.multiple_of(off_ref[2 * block + 1], half), half)
                keys = jnp.concatenate([kv_ref[low, :HEAD_SIZE], kv_ref[high, :HEAD_SIZE]], axis=0)
                values = jnp.concatenate([kv_ref[low, HEAD_SIZE:], kv_ref[high, HEAD_SIZE:]], axis=0)
                scores = contract_cols(keys, queries)
                natural = block * 256 + key_row
                allowed = (natural <= places) & (natural >= start)
                probs = jnp.where(allowed, jnp.exp(scores) * inverse, 0.0)
                prob_grad = contract_cols(values, grads)
                score_grad = (probs * (prob_grad - deltas)).astype(BF16)
                value_part = matmul(probs.astype(BF16), grads)
                key_part = matmul(score_grad, queries)
                dv_ref[low, :] += value_part[:half]
                dv_ref[high, :] += value_part[half:]
                dk_ref[low, :] += key_part[:half]
                dk_ref[high, :] += key_part[half:]
                acc_ref[...] += contract_rows(score_grad, keys)

            return unused_step

        lax.fori_loop(low_ref[index], tile_ref[index] // 2 + 1, step, 0)
        dq_ref[rows, :HEAD_SIZE] = acc_ref[:half, :].astype(dq_ref.dtype)
        dq_ref[rows, HEAD_SIZE:] = acc_ref[half:, :].astype(dq_ref.dtype)
        return unused

    lax.fori_loop(0, q_ref.shape[0] // half, tile, 0)

    for part, ref in enumerate(dkv_refs):

        def store(index, unused):
            target = pl.ds(pl.multiple_of(index * 256, 256), 256)
            source = pl.ds(pl.multiple_of(part * share + index * 256, 256), 256)
            ref[target, :HEAD_SIZE] = dk_ref[source, :].astype(BF16)
            ref[target, HEAD_SIZE:] = dv_ref[source, :].astype(BF16)
            return unused

        lax.fori_loop(0, share // 256, store, 0)


def attend(offsets, tiles, queries, start_cols, kv_parts, before=None, last=True):
    rows, width = queries.shape
    parts, share = len(kv_parts), kv_parts[0].shape[0]
    keys = parts * share
    first = before is None
    extra = () if first else (before,)
    whole = (
        (jax.ShapeDtypeStruct((rows, width), BF16), jax.ShapeDtypeStruct((rows // 128, 2, 128), F32))
        if last
        else (jax.ShapeDtypeStruct((rows // 128, 256, 256), F32),)
    )
    return pl.pallas_call(
        functools.partial(attend_kernel, parts=parts, first=first, last=last),
        name="attend",
        out_shape=whole,
        in_specs=[pl.BlockSpec(memory_space=SMEM)] * 3 + [pl.BlockSpec(memory_space=VMEM)] * (2 + parts + len(extra)),
        out_specs=[pl.BlockSpec(memory_space=VMEM)] * len(whole),
        scratch_shapes=[pltpu.VMEM((keys, width), BF16), pltpu.VMEM((256, 256), F32)],
        compiler_params=pltpu.CompilerParams(vmem_limit_bytes=12 * 2**20 + keys * 1536),
        cost_estimate=LIGHT,
    )(offsets, *tiles, queries, start_cols, *kv_parts, *extra)


def attend_back(offsets, tiles, queries, start_rows, inverse, attended, grads, kv_parts, before=None, last=True):
    rows, width = queries.shape
    parts, share = len(kv_parts), kv_parts[0].shape[0]
    keys = parts * share
    first = before is None
    extra = () if first else (before,)
    return pl.pallas_call(
        functools.partial(attend_back_kernel, parts=parts, first=first, last=last),
        name="attend_back",
        out_shape=(jax.ShapeDtypeStruct((rows, width), BF16 if last else F32),)
        + tuple(jax.ShapeDtypeStruct((share, width), BF16) for unused in kv_parts),
        in_specs=[pl.BlockSpec(memory_space=SMEM)] * 3 + [pl.BlockSpec(memory_space=VMEM)] * (5 + parts + len(extra)),
        out_specs=[pl.BlockSpec(memory_space=VMEM)] * (1 + parts),
        scratch_shapes=[
            pltpu.VMEM((keys, width), BF16),
            pltpu.VMEM((keys, HEAD_SIZE), F32),
            pltpu.VMEM((keys, HEAD_SIZE), F32),
            pltpu.VMEM((256, HEAD_SIZE), F32),
        ],
        compiler_params=pltpu.CompilerParams(vmem_limit_bytes=12 * 2**20 + keys * 2816),
        cost_estimate=LIGHT,
    )(offsets, *tiles, queries, start_rows, inverse, attended, grads, *kv_parts, *extra)


def shape_kernel(raw_ref, cos_ref, sin_ref, gain_ref, q_ref, kv_ref):
    cosine = cos_ref[...]
    sine = sin_ref[...]

    def shaped(first, gain):
        value = raw_ref[:, first : first + HEAD_SIZE]
        mean_square = jnp.mean(value * value, axis=-1, keepdims=True)
        value = value * lax.rsqrt(mean_square + EPSILON) * gain
        return value * cosine + pltpu.roll(value, HEAD_SIZE // 2, 1) * sine

    for head in range(2):
        columns = slice(head * HEAD_SIZE, (head + 1) * HEAD_SIZE)
        q_ref[:, columns] = (shaped(head * HEAD_SIZE, gain_ref[0:1, :]) * HEAD_SIZE**-0.5).astype(BF16)
    kv_ref[:, :HEAD_SIZE] = shaped(2 * HEAD_SIZE, gain_ref[1:2, :]).astype(BF16)
    kv_ref[:, HEAD_SIZE:] = raw_ref[:, 3 * HEAD_SIZE :].astype(BF16)


def shape_back_kernel(raw_ref, grad_ref, cos_ref, sin_ref, gain_ref, low_ref, gain_grad_ref, *, heads, gain_row, factor):
    @pl.when(pl.program_id(0) == 0)
    def _():
        gain_grad_ref[...] = jnp.zeros_like(gain_grad_ref)

    cosine = cos_ref[...]
    sine = sin_ref[...]
    gain = gain_ref[gain_row : gain_row + 1, :]
    total = jnp.zeros((8, HEAD_SIZE), F32)
    for head in range(heads):
        columns = slice(head * HEAD_SIZE, (head + 1) * HEAD_SIZE)
        value = raw_ref[:, columns]
        grad = grad_ref[:, columns].astype(F32) * factor
        grad = grad * cosine - pltpu.roll(grad, HEAD_SIZE // 2, 1) * sine
        rho = lax.rsqrt(jnp.mean(value * value, axis=-1, keepdims=True) + EPSILON)
        unit = value * rho
        total = total + jnp.sum((grad * unit).reshape(-1, 8, HEAD_SIZE), axis=0)
        scaled = grad * gain
        inner = jnp.mean(scaled * unit, axis=-1, keepdims=True)
        low_ref[:, columns] = (rho * (scaled - unit * inner)).astype(BF16)
    if heads == 1:
        low_ref[:, HEAD_SIZE:] = grad_ref[:, HEAD_SIZE:].astype(BF16)
    gain_grad_ref[...] += total


ROW_TILE = 256


def shape_heads(raw, cosine, sine, gains):
    rows = raw.shape[0]
    block = lambda width: pl.BlockSpec((ROW_TILE, width), lambda i: (i, 0))
    return pl.pallas_call(
        shape_kernel,
        name="shape_heads",
        grid=(rows // ROW_TILE,),
        out_shape=(jax.ShapeDtypeStruct((rows, 256), BF16), jax.ShapeDtypeStruct((rows, 256), BF16)),
        in_specs=[block(512), block(128), block(128), pl.BlockSpec((2, 128), lambda i: (0, 0))],
        out_specs=[block(256), block(256)],
        compiler_params=pltpu.CompilerParams(vmem_limit_bytes=8 * 2**20),
        cost_estimate=LIGHT,
    )(raw, cosine, sine, gains)


def shape_back(raw, grads, cosine, sine, gains, heads, column, gain_row, factor):
    rows = raw.shape[0]
    block = lambda width, at=0: pl.BlockSpec((ROW_TILE, width), lambda i: (i, at))
    return pl.pallas_call(
        functools.partial(shape_back_kernel, heads=heads, gain_row=gain_row, factor=factor),
        name="shape_back",
        grid=(rows // ROW_TILE,),
        out_shape=(jax.ShapeDtypeStruct((rows, 256), BF16), jax.ShapeDtypeStruct((8, 128), F32)),
        in_specs=[
            block(heads * 128, column),
            block(256),
            block(128),
            block(128),
            pl.BlockSpec((2, 128), lambda i: (0, 0)),
        ],
        out_specs=[block(256), pl.BlockSpec((8, 128), lambda i: (0, 0))],
        compiler_params=pltpu.CompilerParams(vmem_limit_bytes=8 * 2**20),
        cost_estimate=LIGHT,
    )(raw, grads, cosine, sine, gains)


def reorder_kernel(order_ref, *refs):
    half = len(refs) // 2
    for source, target in zip(refs[:half], refs[half:]):
        target[...] = source[...].astype(target.dtype)


def reorder(order, values, types):
    rows, width = values[0].shape
    blocks = order.shape[0]
    size = width // blocks
    taken = pl.BlockSpec((rows, size), lambda i, order_ref: (0, order_ref[i]))
    put = pl.BlockSpec((rows, size), lambda i, order_ref: (0, i))
    return pl.pallas_call(
        reorder_kernel,
        name="reorder",
        grid_spec=pltpu.PrefetchScalarGridSpec(
            num_scalar_prefetch=1,
            grid=(blocks,),
            in_specs=[taken] * len(values),
            out_specs=[put] * len(values),
        ),
        out_shape=[jax.ShapeDtypeStruct(value.shape, kind) for value, kind in zip(values, types)],
        compiler_params=pltpu.CompilerParams(vmem_limit_bytes=8 * 2**20),
        cost_estimate=LIGHT,
    )(order, *values)


def assemble_kernel(at_ref, *refs, entries, axis):
    out_ref = refs[-1]
    for source, (place, kind) in zip(refs[:-1], entries):
        size = source.shape[axis]
        if kind == 0:
            span = slice(place, place + size)
        else:
            at = at_ref[0] if kind > 0 else 1 - at_ref[0]
            span = pl.ds(pl.multiple_of(place + at * 256, 16 if axis == 0 else 128), size)
        if axis == 0:
            out_ref[span, :] = source[...]
        else:
            out_ref[:, span] = source[...]


def assemble(at, parts, axis):
    values = [value for value, unused, kind in parts]
    total = sum(value.shape[axis] for value in values)
    other = values[0].shape[1 - axis]
    shape = (total, other) if axis == 0 else (other, total)
    return pl.pallas_call(
        functools.partial(assemble_kernel, entries=tuple((place, kind) for unused, place, kind in parts), axis=axis),
        name="assemble",
        out_shape=jax.ShapeDtypeStruct(shape, BF16),
        in_specs=[pl.BlockSpec(memory_space=SMEM)] + [pl.BlockSpec(memory_space=VMEM)] * len(values),
        out_specs=pl.BlockSpec(memory_space=VMEM),
        compiler_params=pltpu.CompilerParams(vmem_limit_bytes=12 * 2**20),
        cost_estimate=LIGHT,
    )(at, *values)


def terms_kernel(left_ref, right_ref, left_cols_ref, right_cols_ref, kept_ref, given_ref):
    total = contract_cols(left_ref[...], left_cols_ref[...]) + contract_cols(right_ref[...], right_cols_ref[...])
    middle = kept_ref.shape[0]
    kept_ref[...] = total[:middle]
    given_ref[...] = total[middle:].astype(BF16)


def two_terms(left, right, left_cols, right_cols):
    rows, depth = left.shape
    width = left_cols.shape[0]
    tile = 512
    value = pl.BlockSpec((rows, depth), lambda i: (0, 0))
    cols = pl.BlockSpec((tile, depth), lambda i: (i, 0))
    half = pl.BlockSpec((rows // 2, tile), lambda i: (0, i))
    return pl.pallas_call(
        terms_kernel,
        name="two_terms",
        grid=(width // tile,),
        out_shape=(jax.ShapeDtypeStruct((rows // 2, width), F32), jax.ShapeDtypeStruct((rows // 2, width), BF16)),
        in_specs=[value, value, cols, cols],
        out_specs=(half, half),
        cost_estimate=LIGHT,
    )(left, right, left_cols, right_cols)


def hidden_kernel(mine_ref, theirs_ref, gate_ref, up_ref, hidden_ref, gate_slope_ref, up_slope_ref):
    middle = mine_ref.shape[0]
    for part, source in ((slice(0, middle), mine_ref), (slice(middle, 2 * middle), theirs_ref)):
        rows = source[...]
        gate = matmul(rows, gate_ref[...])
        up = matmul(rows, up_ref[...])
        sig = 1.0 / (1.0 + jnp.exp(-gate))
        silu = gate * sig
        hidden_ref[part, :] = (silu * up).astype(BF16)
        gate_slope_ref[part, :] = (up * (sig * (1.0 + gate * (1.0 - sig)))).astype(BF16)
        up_slope_ref[part, :] = silu.astype(BF16)


def hidden_units(mine, theirs, gate_cols, up_cols):
    middle, width = mine.shape
    units = gate_cols.shape[1]
    tile = 256
    whole = pl.BlockSpec((middle, width), lambda i: (0, 0))
    cols = pl.BlockSpec((width, tile), lambda i: (0, i))
    out = pl.BlockSpec((2 * middle, tile), lambda i: (0, i))
    return pl.pallas_call(
        hidden_kernel,
        name="hidden_units",
        grid=(units // tile,),
        out_shape=(jax.ShapeDtypeStruct((2 * middle, units), BF16),) * 3,
        in_specs=[whole, whole, cols, cols],
        out_specs=(out,) * 3,
        cost_estimate=LIGHT,
    )(mine, theirs, gate_cols, up_cols)


def prologue_kernel(
    order_ref, at_ref, tokens_ref, grad_ref, q_ref, k_ref, v_ref, norm_ref, mlp_ref, q_gain_ref, k_gain_ref,
    tokens_out, grad_out, keep_ref, give_ref
):
    size = tokens_ref.shape[1] // 8
    for block in range(8):
        source = pl.ds(pl.multiple_of(order_ref[block] * size, 128), size)
        tokens_out[:, block * size : (block + 1) * size] = tokens_ref[:, source]
        grad_out[:, block * size : (block + 1) * size] = grad_ref[:, source]

    rows, q_width = q_ref.shape[0], q_ref.shape[1] // 2
    k_width = k_ref.shape[1] // 2
    total = q_width + 2 * k_width
    small = q_gain_ref.shape[1]
    place = lax.broadcasted_iota(jnp.int32, (small, HEAD_SIZE), 1) - lax.broadcasted_iota(
        jnp.int32, (small, HEAD_SIZE), 0
    )
    put = (place == at_ref[1] * small).astype(BF16)
    extra = jnp.concatenate(
        [
            jnp.concatenate([norm_ref[...].reshape(1, rows), mlp_ref[...].reshape(1, rows)], axis=1),
            jnp.concatenate(
                [
                    matmul(q_gain_ref[...], put).astype(BF16),
                    matmul(k_gain_ref[...], put).astype(BF16),
                    jnp.zeros((1, total - 2 * HEAD_SIZE), BF16),
                ],
                axis=1,
            ),
            jnp.zeros((14, total), BF16),
        ],
        axis=0,
    )
    for target, at in ((keep_ref, at_ref[0]), (give_ref, 1 - at_ref[0])):
        target[:rows, :q_width] = q_ref[:, pl.ds(pl.multiple_of(at * q_width, 128), q_width)]
        target[:rows, q_width : q_width + k_width] = k_ref[:, pl.ds(pl.multiple_of(at * k_width, 128), k_width)]
        target[:rows, q_width + k_width :] = v_ref[:, pl.ds(pl.multiple_of(at * k_width, 128), k_width)]
        target[rows:, :] = extra


def prologue(order, at, tokens, out_grad, q_weight, k_weight, v_weight, gains):
    shape = jax.ShapeDtypeStruct((q_weight.shape[0] + 16, (q_weight.shape[1] + 2 * k_weight.shape[1]) // 2), BF16)
    whole = lambda value: pl.BlockSpec(value.shape, lambda i, order_ref, at_ref: (0,) * len(value.shape))
    fixed = (q_weight, k_weight, v_weight) + gains
    return pl.pallas_call(
        prologue_kernel,
        name="prologue",
        grid_spec=pltpu.PrefetchScalarGridSpec(
            num_scalar_prefetch=2,
            grid=(1,),
            in_specs=[whole(tokens), whole(out_grad)] + [whole(value) for value in fixed],
            out_specs=[whole(tokens), whole(tokens), whole(shape), whole(shape)],
        ),
        out_shape=(jax.ShapeDtypeStruct(tokens.shape, BF16),) * 2 + (shape, shape),
        cost_estimate=LIGHT,
    )(order, at, tokens, out_grad, *fixed)


def after(token, values):
    return lax.optimization_barrier((token, values))[1]


def meet(token, values):
    return lax.optimization_barrier((token, values))


def trade(token, sends):
    held = after(token, [value for value, unused in sends])
    return [swap(value, axis) for value, (unused, axis) in zip(held, sends)]


def places_of(query_tile, key_tile, seq_lengths, tok_dev):
    rows = query_tile.shape[0] * tok_dev
    tile_ids = jnp.arange(key_tile.shape[0], dtype=jnp.int32)
    shares = (tile_ids // 16) * 8 + tile_ids % 8
    found = key_tile[None, :] == tile_ids[:, None]

    def offsets_of(parity):
        mine = found & (tile_ids // 8 % 2 == parity)[None, :]
        return jnp.sum(jnp.where(mine, shares * tok_dev + 1, 0), axis=1, dtype=jnp.int32) - 1

    offsets = (offsets_of(0), offsets_of(1))
    natural = query_tile[:, None] * tok_dev + jnp.arange(tok_dev, dtype=jnp.int32)[None, :]
    seq_ids = jnp.arange(seq_lengths.shape[0], dtype=jnp.int32)
    seq_ends = jnp.sum(jnp.where(seq_ids[None, :] <= seq_ids[:, None], seq_lengths[None, :], 0), axis=1, dtype=jnp.int32)
    starts = jnp.max(jnp.where(seq_ends <= natural[..., None], seq_ends, 0), axis=-1)
    tiles = (query_tile, jnp.max(jnp.where(seq_ends <= (query_tile * tok_dev)[:, None], seq_ends, 0), axis=-1) // (2 * tok_dev))
    start_rows = jnp.stack([starts, starts], axis=1)
    start_cols = jnp.broadcast_to(starts.reshape(rows, 1), (rows, 128))
    places = (natural - starts).reshape(rows)
    half_width = HEAD_SIZE // 2
    frequency = jnp.power(ROPE_BASE, -jnp.arange(half_width, dtype=F32) * (2.0 / HEAD_SIZE))
    angles = places.astype(F32)[:, None] * frequency[None, :]
    cosine = jnp.cos(angles)
    sine = jnp.sin(angles)
    cosine = jnp.concatenate([cosine, cosine], axis=1)
    sine = jnp.concatenate([-sine, sine], axis=1)
    return offsets, tiles, start_rows, start_cols, cosine, sine


FAR = 96
KEEP_ROWS = 128
UP_ROWS = 96


def paired_layer(
    tokens,
    out_grad,
    seq_lengths,
    block_deal,
    norm_gain,
    q_weight,
    k_weight,
    v_weight,
    q_gain,
    k_gain,
    o_weight,
    mlp_gain,
    gate_weight,
    up_weight,
    down_weight,
):
    y_at, core_at, zb_at, za_at, x_at = (lax.axis_index(name) for name in ("y", "core", "zb", "za", "x"))
    tok_dev, width = tokens.shape
    blk_rows = q_weight.shape[0]
    rows = 8 * tok_dev
    middle = rows // 2
    half, quarter = width // 2, width // 4
    token = seq_lengths


    place_ids = jnp.arange(8, dtype=jnp.int32)
    to_order = ((zb_at ^ (place_ids // 2 % 2)) * 2 + place_ids % 2) * 2 + (x_at ^ (place_ids // 4))
    from_order = ((x_at ^ (place_ids % 2)) * 2 + (zb_at ^ (place_ids // 4))) * 2 + place_ids // 2 % 2

    def in_order(mine, other, axis):
        first = jnp.where(za_at == 0, mine, other)
        second = jnp.where(za_at == 0, other, mine)
        return jnp.concatenate([first, second], axis=axis)

    def half_of(weight, at, axis):
        size = weight.shape[axis] // 2
        return lax.dynamic_slice_in_dim(weight, at * size, size, axis=axis)


    def near(value):
        return [(value, "y"), (value, "za")]

    def far(from_y, from_z, rows_y):
        sends = [(from_z[:rows_y], "y")]
        return sends + ([(from_y[rows_y:], "za")] if rows_y < tok_dev else [])

    def mine_of(value, from_y, from_z, fars):
        return jnp.concatenate([value, from_y, from_z] + fars, axis=0)

    def far_sums(kept):
        return [(kept[3 * tok_dev :].astype(BF16), "y")]

    def near_sums(kept, from_y):
        to_y, to_z = kept[tok_dev : 2 * tok_dev], kept[2 * tok_dev : 3 * tok_dev] + from_y.astype(F32)
        return [(to_y.astype(BF16), "y"), (to_z.astype(BF16), "za")]

    def own_sum(kept, nears):
        return kept[:tok_dev] + nears[0].astype(F32) + nears[1].astype(F32)


    def za_parts(part, axis):
        first = lax.slice_in_dim(part, 0, blk_rows, axis=axis)
        second = lax.slice_in_dim(part, blk_rows, 2 * blk_rows, axis=axis)
        return jnp.where(za_at == 0, first, second), jnp.where(za_at == 0, second, first).astype(BF16)

    def za_join(mine, other):
        other = other.astype(F32)
        return [jnp.where(za_at == 0, mine, other), jnp.where(za_at == 0, other, mine)]


    member = jnp.arange(8, dtype=jnp.int32)
    member_y, member_za, member_core = y_at ^ (member % 2), za_at ^ (member // 2 % 2), core_at ^ (member // 4)
    group = jnp.arange(4, dtype=jnp.int32)
    span_table = jnp.arange(block_deal.shape[0], dtype=jnp.int32)

    def natural_tile(zb_of, x_of):
        entry = 2 * ((zb_of * 2 + member_za) * 2 + x_of) + member_y
        span = jnp.sum(jnp.where(entry[..., None] == span_table, block_deal, 0), axis=-1, dtype=jnp.int32)
        return span * 2 + member_core

    query_tile = natural_tile(zb_at, x_at)
    key_tile = natural_tile(zb_at ^ (group % 2)[:, None], x_at ^ (group // 2)[:, None]).reshape(-1)
    offsets, tiles, start_rows, start_cols, cosine, sine = places_of(query_tile, key_tile, seq_lengths, tok_dev)


    q_width, k_width = q_weight.shape[1] // 2, k_weight.shape[1] // 2
    qkv_width = q_width + 2 * k_width
    local_low, grad_local, qkv_keep, qkv_give = prologue(
        to_order,
        jnp.stack([za_at, (zb_at * 2 + za_at) * 2 + x_at]),
        tokens,
        out_grad,
        q_weight,
        k_weight,
        v_weight,
        (norm_gain, mlp_gain, q_gain[None], k_gain[None]),
    )
    local_rows = local_low.astype(F32)
    o_give = half_of(o_weight, 1 - za_at, 0)
    za_place = za_at[None].astype(jnp.int32)
    z_keep, qkv_far, x_keep = swap(qkv_keep, "zb"), swap(qkv_give, "za"), swap(qkv_keep, "x")
    tokens_y = swap(local_low, "y")
    (o_far,) = trade(qkv_keep, [(o_give, "za")])
    token, (qkv_far, z_keep, x_keep, tokens_y, o_far) = meet(token, (qkv_far, z_keep, x_keep, tokens_y, o_far))
    down_keep = half_of(down_weight, za_at, 0)
    tokens_z, z_far, xz_keep, x_far, down_xk = trade(
        token, [(local_low, "za"), (qkv_far, "zb"), (z_keep, "x"), (qkv_far, "x"), (down_keep, "x")]
    )
    o_pair = in_order(half_of(o_weight, za_at, 0), o_far, 1)
    token, (z_far, tokens_z, xz_keep, x_far, o_pair, down_xk) = meet(
        token, (z_far, tokens_z, xz_keep, x_far, o_pair, down_xk)
    )
    *fars, xz_far, o_x, o_z = trade(
        token, far(tokens_y, tokens_z, FAR) + [(z_far, "x"), (o_pair, "x"), (o_pair, "zb")]
    )
    gate_weight, up_weight, down_weight = after(token, (gate_weight, up_weight, down_weight))
    gate_keep, up_keep = half_of(gate_weight, za_at, 1), half_of(up_weight, za_at, 1)
    gate_give, up_give = half_of(gate_weight, 1 - za_at, 1), half_of(up_weight, 1 - za_at, 1)
    down_give = half_of(down_weight, 1 - za_at, 0)
    token, (xz_far, fars, o_x, o_z) = meet(token, (xz_far, fars, o_x, o_z))
    mine = mine_of(local_low, tokens_y, tokens_z, fars)
    theirs, gate_zk0, gate_far, gate_xk = trade(
        token, [(mine, "core"), (gate_keep[:KEEP_ROWS], "zb"), (gate_give, "za"), (gate_keep, "x")]
    )
    qkv_all = jnp.concatenate(
        [
            in_order(qkv_keep, qkv_far, 0),
            in_order(z_keep, z_far, 0),
            in_order(x_keep, x_far, 0),
            in_order(xz_keep, xz_far, 0),
        ],
        axis=0,
    ).reshape(8, blk_rows + 16, qkv_width)
    qkv_cols = qkv_all[:, :blk_rows].reshape(width, qkv_width)
    gains = qkv_all[:, blk_rows, : 2 * blk_rows].astype(F32)
    gain_one = gains[:, :blk_rows].reshape(1, width)
    gain_two = gains[:, blk_rows:].reshape(1, width)
    head_sum = jnp.sum(qkv_all[:, blk_rows + 1, : 2 * HEAD_SIZE].astype(F32), axis=0, keepdims=True)
    qk_gains = jnp.concatenate([head_sum[:, :HEAD_SIZE], head_sum[:, HEAD_SIZE:]], axis=0)


    input_rows = jnp.concatenate([mine, theirs], axis=0).astype(F32)
    input_rho = lax.rsqrt(jnp.mean(input_rows * input_rows, axis=-1, keepdims=True) + EPSILON)
    normed = (input_rows * input_rho * gain_one).astype(BF16)
    raw = matmul(normed, qkv_cols)
    queries, kv_own = shape_heads(raw, cosine, sine, qk_gains)
    token, (queries, kv_own, gate_zk0, gate_far, gate_xk) = meet(
        token, (queries, kv_own, gate_zk0, gate_far, gate_xk)
    )
    kv_z, kv_x, up_far, grads_y = trade(
        token, [(kv_own, "zb"), (kv_own, "x"), (up_give, "za"), (grad_local, "y")]
    )
    token, (kv_x,) = meet(token, (kv_x,))
    (o_xz,) = trade(token, [(o_z, "x")])
    (attn_part,) = attend(offsets[0], tiles, queries, start_cols, [kv_own, kv_x], last=False)
    gate_pair = in_order(gate_keep, gate_far, 0)
    token, (kv_z, attn_part, grads_y, o_xz, up_far, gate_pair) = meet(
        token, (kv_z, attn_part, grads_y, o_xz, up_far, gate_pair)
    )
    gate_rest = jnp.concatenate([gate_keep[KEEP_ROWS:], gate_far], axis=0)
    token, (gate_rest,) = meet(token, (gate_rest,))
    kv_xz, gate_zr, grads_z = trade(token, [(kv_z, "x"), (gate_rest, "zb"), (grad_local, "za")])
    o_cols = jnp.concatenate([o_pair, o_z, o_x, o_xz], axis=1)
    token, (kv_xz, o_cols) = meet(token, (kv_xz, o_cols))
    (gate_xf,) = trade(token, [(gate_far, "x")])
    attn_low, inverse = attend(offsets[1], tiles, queries, start_cols, [kv_z, kv_xz], before=attn_part)
    given = matmul(attn_low[middle:], o_cols).astype(BF16)
    token, (given, attn_low, gate_xf, gate_zr, grads_z) = meet(token, (given, attn_low, gate_xf, gate_zr, grads_z))
    up_pair = in_order(up_keep, up_far, 0)
    given, up_z0, up_x0, grads_far, down_far = trade(
        token,
        [(given, "core"), (up_pair[:UP_ROWS], "zb"), (up_pair[:blk_rows], "x"), (grads_z, "y"), (down_give, "za")],
    )
    kept = matmul(attn_low[:middle], o_cols)
    token, (given, kept, up_z0, up_x0, up_pair, grads_far, down_far) = meet(
        token, (given, kept, up_z0, up_x0, up_pair, grads_far, down_far)
    )
    grad_mine = mine_of(grad_local, grads_y, grads_z, [grads_far])
    kept = kept + given.astype(F32)
    from_y, up_z1, up_x1 = trade(
        token,
        far_sums(kept) + [(up_pair[UP_ROWS:blk_rows], "zb"), (up_pair[blk_rows:], "x")],
    )
    gate_z = assemble(
        za_place,
        [
            (gate_zk0, 0, 1),
            (gate_zr[: blk_rows - KEEP_ROWS], KEEP_ROWS, 1),
            (gate_zr[blk_rows - KEEP_ROWS :], 0, -1),
        ],
        0,
    )
    token, (from_y, kept, up_x1, gate_z, up_z1, grad_mine) = meet(
        token, (from_y, kept, up_x1, gate_z, up_z1, grad_mine)
    )
    *nears, gate_xz, up_z2, grad_theirs = trade(
        token, near_sums(kept, from_y) + [(gate_z, "x"), (up_pair[blk_rows:], "zb"), (grad_mine, "core")]
    )
    token, (nears, kept, gate_xz, up_z2, grad_theirs) = meet(token, (nears, kept, gate_xz, up_z2, grad_theirs))
    up_z01 = jnp.concatenate([up_z0, up_z1], axis=0)
    residual = local_rows + own_sum(kept, nears)


    rho_two = lax.rsqrt(jnp.mean(residual * residual, axis=-1, keepdims=True) + EPSILON)
    unit_two = residual * rho_two
    mlp_low = (unit_two * gain_two).astype(BF16)
    token, (mlp_low,) = meet(token, (mlp_low,))
    mlp_y, mlp_z, down_zk, down_xf, up_xz0 = trade(
        token, near(mlp_low) + [(down_keep, "zb"), (down_far, "x"), (up_z01, "x")]
    )
    gate_cols = assemble(
        za_place,
        [(gate_pair, 0, 0), (gate_z, quarter, 0), (gate_xk, half, 1), (gate_xf, half, -1)]
        + [(gate_xz, half + quarter, 0)],
        0,
    )
    grad_mine, grad_theirs = after(token, (grad_mine, grad_theirs))
    grad_rows = assemble(za_place, [(grad_mine, 0, 0), (grad_theirs, middle, 0)], 0)
    token, (mlp_y, mlp_z, down_xf, up_xz0, gate_cols, down_zk, grad_rows) = meet(
        token, (mlp_y, mlp_z, down_xf, up_xz0, gate_cols, down_zk, grad_rows)
    )
    *fars, up_xz1, down_zf0 = trade(token, far(mlp_y, mlp_z, FAR) + [(up_z2, "x"), (down_far[:400], "zb")])
    token, (fars, down_zf0, up_xz1) = meet(token, (fars, down_zf0, up_xz1))
    mlp_mine = mine_of(mlp_low, mlp_y, mlp_z, fars)
    mlp_theirs, down_zf1, down_xzk, down_xzf0 = trade(
        token, [(mlp_mine, "core"), (down_far[400:], "zb"), (down_zk, "x"), (down_zf0, "x")]
    )
    up_cols = assemble(
        za_place,
        [
            (up_pair, 0, 0),
            (up_z01, quarter, 0),
            (up_z2, quarter + blk_rows, 0),
            (up_x0, half, 0),
            (up_x1, half + blk_rows, 0),
            (up_xz0, half + quarter, 0),
            (up_xz1, half + quarter + blk_rows, 0),
        ],
        0,
    )
    token, (mlp_theirs, up_cols) = meet(token, (mlp_theirs, up_cols))
    mlp_rows = jnp.concatenate([mlp_mine, mlp_theirs], axis=0)
    gate_act = matmul(mlp_rows, gate_cols)
    token, (gate_act, up_cols, mlp_rows) = meet(token, (gate_act, up_cols, mlp_rows))
    sig = jax.nn.sigmoid(gate_act)
    silu = gate_act * sig
    slope = sig * (1.0 + gate_act * (1.0 - sig))
    up_slope = silu.astype(BF16)
    token, (silu, slope, up_slope, up_cols, mlp_rows) = meet(token, (silu, slope, up_slope, up_cols, mlp_rows))
    up_act = matmul(mlp_rows, up_cols)
    hidden = (silu * up_act).astype(BF16)
    gate_slope = (up_act * slope).astype(BF16)
    token, (hidden, gate_slope, up_slope, down_zf1, down_xzk, down_xzf0) = meet(
        token, (hidden, gate_slope, up_slope, down_zf1, down_xzk, down_xzf0)
    )
    (down_xzf1,) = trade(token, [(down_zf1, "x")])
    down_zf = jnp.concatenate([down_zf0, down_zf1], axis=0)
    down_3 = contract_rows(hidden, grad_rows[:, 3 * quarter :]).astype(BF16)
    token, (down_3, down_xzf1, down_zf) = meet(token, (down_3, down_xzf1, down_zf))
    down_xzf = jnp.concatenate([down_xzf0, down_xzf1], axis=0)

    def columns_of(value, piece):
        return value[:, piece * quarter : (piece + 1) * quarter]

    down_cols = assemble(
        za_place,
        [
            (down_keep, 0, 1),
            (down_far, 0, -1),
            (down_zk, quarter, 1),
            (down_zf, quarter, -1),
            (down_xk, half, 1),
            (down_xf, half, -1),
            (down_xzk, half + quarter, 1),
            (down_xzf, half + quarter, -1),
        ],
        1,
    )
    token, (down_cols,) = meet(token, (down_cols,))
    (down_3,) = trade(token, [(down_3, "x")])
    hidden_grad = contract_cols(grad_rows, down_cols)
    gate_low = (hidden_grad * gate_slope.astype(F32)).astype(BF16)
    up_low = (hidden_grad * up_slope.astype(F32)).astype(BF16)

    kept, given = two_terms(gate_low, up_low, gate_cols, up_cols)
    token, (kept, given, gate_low, up_low, down_3) = meet(token, (kept, given, gate_low, up_low, down_3))
    hidden, grad_rows = after(token, (hidden, grad_rows))
    down_1 = (contract_rows(hidden, columns_of(grad_rows, 1)) + down_3.astype(F32)).astype(BF16)
    given, down_1a = trade(token, [(given, "core"), (down_1[:144], "zb")])
    gate_3 = contract_rows(columns_of(mlp_rows, 3), gate_low).astype(BF16)
    token, (given, kept, down_1, down_1a, gate_3) = meet(token, (given, kept, down_1, down_1a, gate_3))
    kept = kept + given.astype(F32)
    token, (kept,) = meet(token, (kept,))
    from_y, down_1b, gate_3 = trade(token, far_sums(kept) + [(down_1[144:416], "zb"), (gate_3, "x")])
    down_2 = contract_rows(hidden, columns_of(grad_rows, 2)).astype(BF16)
    up_3 = contract_rows(columns_of(mlp_rows, 3), up_low).astype(BF16)
    gate_1 = contract_rows(columns_of(mlp_rows, 1), gate_low)
    token, (from_y, kept, down_1b, gate_3, down_2, up_3, gate_1) = meet(
        token, (from_y, kept, down_1b, gate_3, down_2, up_3, gate_1)
    )
    *nears, down_1c, up_3 = trade(token, near_sums(kept, from_y) + [(down_1[416:], "zb"), (up_3, "x")])
    gate_1 = (gate_1 + gate_3.astype(F32)).astype(BF16)
    gate_2 = contract_rows(columns_of(mlp_rows, 2), gate_low).astype(BF16)
    up_1 = contract_rows(columns_of(mlp_rows, 1), up_low)
    up_2 = contract_rows(columns_of(mlp_rows, 2), up_low).astype(BF16)
    token, (nears, kept, down_1c, up_3, gate_2, up_1, up_2, gate_1) = meet(
        token, (nears, kept, down_1c, up_3, gate_2, up_1, up_2, gate_1)
    )
    mlp_in_grad = own_sum(kept, nears)
    gain_two_part = jnp.sum(mlp_in_grad * unit_two, axis=0, keepdims=True)
    scaled = mlp_in_grad * gain_two
    inner = jnp.mean(scaled * unit_two, axis=-1, keepdims=True)
    residual_grad = grad_local.astype(F32) + rho_two * (scaled - unit_two * inner)


    branch_low = residual_grad.astype(BF16)
    token, (branch_low, residual_grad, gain_two_part, gate_1) = meet(
        token, (branch_low, residual_grad, gain_two_part, gate_1)
    )
    branch_y, branch_z, gate_1a, gate_2 = trade(
        token, near(branch_low) + [(gate_1[:blk_rows], "zb"), (gate_2, "x")]
    )
    hidden, down_cols = after(token, (hidden, down_cols))
    out_given = matmul(hidden[middle:], down_cols).astype(BF16)
    up_1 = (up_1 + up_3.astype(F32)).astype(BF16)
    down_0 = contract_rows(hidden, columns_of(grad_rows, 0)) + jnp.concatenate(
        [down_1a, down_1b, down_1c], axis=0
    ).astype(F32)
    token, (branch_y, branch_z, gate_1a, gate_2, out_given, up_1, down_0, gate_low, up_low) = meet(
        token, (branch_y, branch_z, gate_1a, gate_2, out_given, up_1, down_0, gate_low, up_low)
    )
    gate_0 = contract_rows(columns_of(mlp_rows, 0), gate_low) + gate_2.astype(F32)
    *fars, gate_1b, down_2a = trade(
        token, far(branch_y, branch_z, FAR) + [(gate_1[blk_rows:384], "zb"), (down_2[:384], "x")]
    )
    hidden, down_cols = after(token, (hidden, down_cols))
    out_kept = matmul(hidden[:middle], down_cols)
    token, (fars, out_kept, gate_1b, down_2a, gate_0) = meet(token, (fars, out_kept, gate_1b, down_2a, gate_0))
    branch_mine = mine_of(branch_low, branch_y, branch_z, fars)
    branch_theirs, gate_1c, down_2b, out_given = trade(
        token,
        [(branch_mine, "core"), (gate_1[384:464], "zb"), (down_2[384:512], "x"), (out_given, "core")],
    )
    grad_own = contract_cols(branch_mine, o_cols).astype(BF16)
    attn_grad = jnp.concatenate([grad_own, contract_cols(branch_theirs, o_cols).astype(BF16)], axis=0)
    mixed = jnp.concatenate([gate_1[464:], up_1[:144]], axis=0)
    token, (attn_grad, gate_1c, down_2b, mixed) = meet(token, (attn_grad, gate_1c, down_2b, mixed))
    mixed, up_2a, down_2c = trade(token, [(mixed, "zb"), (up_2[:blk_rows], "x"), (down_2[512:], "x")])
    query_part, kv_1, kv_3 = attend_back(
        offsets[1], tiles, queries, start_rows, inverse, attn_low, attn_grad, [kv_z, kv_xz], last=False
    )
    out_kept = out_kept + out_given.astype(F32)
    token, (query_part, kv_1, kv_3, mixed, up_2a, down_2c, out_kept) = meet(
        token, (query_part, kv_1, kv_3, mixed, up_2a, down_2c, out_kept)
    )
    gate_1d, up_1a = mixed[:48], mixed[48:]
    kv_3, up_1b, out_from = trade(token, [(kv_3, "x"), (up_1[144:336], "zb")] + far_sums(out_kept))
    query_grad, kv_0, kv_2 = attend_back(
        offsets[0],
        tiles,
        queries,
        start_rows,
        inverse,
        attn_low,
        attn_grad,
        [kv_own, kv_x],
        before=query_part,
    )
    token, (query_grad, kv_0, kv_2, kv_3, up_1b, out_from) = meet(
        token, (query_grad, kv_0, kv_2, kv_3, up_1b, out_from)
    )
    kv_1 = (kv_1.astype(F32) + kv_3.astype(F32)).astype(BF16)
    kv_1, kv_2, *out_nears = trade(token, [(kv_1, "zb"), (kv_2, "x")] + near_sums(out_kept, out_from))
    token, (kv_2, branch_mine, branch_theirs, up_low, query_grad, gate_0, down_0) = meet(
        token, (kv_2, branch_mine, branch_theirs, up_low, query_grad, gate_0, down_0)
    )
    q_low, q_gain_part = shape_back(raw, query_grad, cosine, sine, qk_gains, 2, 0, 0, HEAD_SIZE**-0.5)
    q_3 = swap(contract_rows(columns_of(normed, 3), q_low).astype(BF16), "x")
    branch_rows = jnp.concatenate([branch_mine, branch_theirs], axis=0)
    o_3 = contract_rows(attn_low, columns_of(branch_rows, 3)).astype(BF16)
    q_1 = contract_rows(columns_of(normed, 1), q_low)
    gate_part = gate_0 + jnp.concatenate([gate_1a, gate_1b, gate_1c, gate_1d], axis=0).astype(F32)
    gate_mine, gate_give = za_parts(gate_part, 0)
    down_part = down_0 + jnp.concatenate([down_2a, down_2b, down_2c], axis=0).astype(F32)
    down_mine, down_give = za_parts(down_part, 1)
    token, (kv_1, out_nears, q_low, q_gain_part, o_3, gate_mine, gate_give, down_mine, down_give, q_1) = meet(
        token, (kv_1, out_nears, q_low, q_gain_part, o_3, gate_mine, gate_give, down_mine, down_give, q_1)
    )
    gate_give, up_1c, down_give, up_2b = trade(
        token, [(gate_give, "za"), (up_1[336:], "zb"), (down_give, "za"), (up_2[blk_rows:], "x")]
    )
    kv_grad = (kv_0.astype(F32) + kv_1.astype(F32) + kv_2.astype(F32)).astype(BF16)
    kv_low, k_gain_part = shape_back(raw, kv_grad, cosine, sine, qk_gains, 1, 2, 1, 1.0)
    low = jnp.concatenate([q_low, kv_low], axis=1)
    given = contract_cols(low[middle:], qkv_cols).astype(BF16)
    w_3 = contract_rows(columns_of(normed, 3), kv_low).astype(BF16)
    q_1 = (q_1 + q_3.astype(F32)).astype(BF16)
    token, (given, low, kv_low, k_gain_part, w_3, q_1, gate_give, up_1c, up_2b) = meet(
        token, (given, low, kv_low, k_gain_part, w_3, q_1, gate_give, up_1c, up_2b)
    )
    given_low = given
    kv_late, normed, low = after(token, (kv_low, normed, low))
    given, q_1, w_3, o_3 = trade(token, [(given, "core"), (q_1, "zb"), (w_3, "x"), (o_3, "x")])
    terms = contract_cols(low[:middle], qkv_cols)
    w_1 = contract_rows(columns_of(normed, 1), kv_late)
    token, (given, terms, q_1, w_3, o_3, w_1, down_give, up_low, attn_low, branch_rows) = meet(
        token, (given, terms, q_1, w_3, o_3, w_1, down_give, up_low, attn_low, branch_rows)
    )
    kept = terms + given.astype(F32)
    w_1 = (w_1 + w_3.astype(F32)).astype(BF16)
    token, (kept, w_1) = meet(token, (kept, w_1))
    from_y, w_1 = trade(token, far_sums(kept) + [(w_1, "zb")])
    o_1 = (contract_rows(attn_low, columns_of(branch_rows, 1)) + o_3.astype(F32)).astype(BF16)
    o_2 = contract_rows(attn_low, columns_of(branch_rows, 2)).astype(BF16)
    terms_low, given_low, normed_low = after(token, (terms, given_low, normed))
    gain_one_part = (
        jnp.sum(
            terms_low * normed_low[:middle].astype(F32) + given_low.astype(F32) * normed_low[middle:].astype(F32),
            axis=0,
            keepdims=True,
        )
        / gain_one
    )
    gain_sum = jnp.concatenate(
        [
            *reorder(from_order, [gain_one_part, gain_two_part], [F32, F32]),
            jnp.sum(q_gain_part, axis=0, keepdims=True),
            jnp.sum(k_gain_part, axis=0, keepdims=True),
        ],
        axis=1,
    )
    qw_2 = contract_rows(columns_of(normed, 2), low).astype(BF16)
    token, (from_y, kept, w_1, o_1, qw_2, o_2, gain_sum, up_low, attn_low, branch_rows, low) = meet(
        token, (from_y, kept, w_1, o_1, qw_2, o_2, gain_sum, up_low, attn_low, branch_rows, low)
    )
    *nears, o_1, qw_2, gain_x = trade(
        token, near_sums(kept, from_y) + [(o_1, "zb"), (qw_2, "x"), (gain_sum, "core")]
    )
    gain_sum = gain_sum + gain_x
    gain_sum = gain_sum + swap(gain_sum, "zb")
    gate_mine, gate_give, down_mine, down_give = after(token, (gate_mine, gate_give, down_mine, down_give))
    up_part = (
        contract_rows(columns_of(mlp_rows, 0), up_low)
        + jnp.concatenate([up_2a, up_2b], axis=0).astype(F32)
        + jnp.concatenate([up_1a, up_1b, up_1c], axis=0).astype(F32)
    )
    up_mine, up_give = za_parts(up_part, 0)
    qw_0 = contract_rows(columns_of(normed, 0), low)
    o_0 = contract_rows(attn_low, columns_of(branch_rows, 0))
    block_out = residual + own_sum(out_kept, out_nears)
    token, (nears, kept, qw_2, qw_0, o_0, block_out, gain_sum, o_1, up_mine, up_give) = meet(
        token, (nears, kept, qw_2, qw_0, o_0, block_out, gain_sum, o_1, up_mine, up_give)
    )
    qkv_mine, qkv_give = za_parts(qw_0 + qw_2.astype(F32) + jnp.concatenate([q_1, w_1], axis=1).astype(F32), 0)
    token, (qkv_mine, qkv_give) = meet(token, (qkv_mine, qkv_give))
    gain_x, qkv_give, up_give, o_2 = trade(
        token, [(gain_sum, "za"), (qkv_give, "za"), (up_give, "za"), (o_2, "x")]
    )
    gain_sum = gain_sum + gain_x
    gain_x = swap(gain_sum, "y")
    o_mine, o_give = za_parts(o_0 + o_2.astype(F32) + o_1.astype(F32), 1)
    token, (gain_sum, o_mine, o_give) = meet(token, (gain_sum + gain_x, o_mine, o_give))
    gain_x, o_give = trade(token, [(gain_sum, "x"), (o_give, "za")])
    gain_sum = gain_sum + gain_x
    input_grad = own_sum(kept, nears)
    unit_one = local_rows * (rho_one := lax.rsqrt(jnp.mean(local_rows * local_rows, axis=-1, keepdims=True) + EPSILON))
    scaled = input_grad * gain_one
    inner = jnp.mean(scaled * unit_one, axis=-1, keepdims=True)
    in_grad = residual_grad + rho_one * (scaled - unit_one * inner)
    block_out, in_grad = reorder(from_order, [block_out, in_grad], [BF16, F32])
    device = (((y_at * 2 + core_at) * 2 + zb_at) * 2 + za_at) * 2 + x_at

    def own_slice(first, length):
        share = length // 32
        return lax.dynamic_slice_in_dim(gain_sum[0], first + device * share, share, axis=0)

    qkv_parts = za_join(qkv_mine, qkv_give)

    def columns(lo, hi):
        return jnp.concatenate([part[:, lo:hi] for part in qkv_parts], axis=1)

    return (
        block_out,
        in_grad,
        own_slice(0, width),
        columns(0, q_width),
        columns(q_width, q_width + k_width),
        columns(q_width + k_width, qkv_width),
        own_slice(2 * width, HEAD_SIZE),
        own_slice(2 * width + HEAD_SIZE, HEAD_SIZE),
        jnp.concatenate(za_join(o_mine, o_give), axis=0),
        own_slice(width, width),
        jnp.concatenate(za_join(gate_mine, gate_give), axis=1),
        jnp.concatenate(za_join(up_mine, up_give), axis=1),
        jnp.concatenate(za_join(down_mine, down_give), axis=0),
    )


def layer(
    sizes,
    tokens,
    out_grad,
    seq_lengths,
    block_deal,
    norm_gain,
    q_weight,
    k_weight,
    v_weight,
    q_gain,
    k_gain,
    o_weight,
    mlp_gain,
    gate_weight,
    up_weight,
    down_weight,
):
    y_count, core_count, zb_count, za_count, x_count = sizes
    pairwise = sizes == (2, 2, 2, 2, 2)
    all_axes = ("y", "core", "zb", "za", "x")
    y_at, core_at, zb_at, za_at, x_at = (lax.axis_index(name) for name in all_axes)
    tok_dev, width = tokens.shape
    blk_rows = q_weight.shape[0]
    group_count = zb_count * x_count
    member_count = y_count * core_count * za_count
    head_count = y_count * core_count
    rows = member_count * tok_dev
    piece = za_count * blk_rows


    def gather_rows(value):
        if not pairwise:
            return lax.all_gather(value, ("y", "core", "za"), axis=0, tiled=True)
        half = tok_dev // 2
        along_y = swap(value, "y")
        along_z = swap(value, "za")
        parts = [value, along_y, along_z, swap(along_z[:half], "y"), swap(along_y[half:], "za")]
        mine = jnp.concatenate(parts, axis=0)
        return jnp.concatenate([mine, swap(mine, "core")], axis=0)

    def scatter_rows(part_of):
        if not pairwise:
            full = part_of(slice(0, rows)).astype(BF16)
            return lax.psum_scatter(full, ("y", "core", "za"), scatter_dimension=0, tiled=True).astype(F32)
        middle = rows // 2
        half = tok_dev // 2
        given = swap(part_of(slice(middle, rows)).astype(BF16), "core")
        kept = part_of(slice(0, middle)) + given.astype(F32)
        own, to_y, to_z, far = (kept[i * tok_dev : (i + 1) * tok_dev] for i in range(4))
        far = far.astype(BF16)
        from_y = swap(far[:half], "y").astype(F32)
        from_z = swap(far[half:], "za").astype(F32)
        z_sum = jnp.concatenate([to_z[:half] + from_y, to_z[half:]], axis=0).astype(BF16)
        y_sum = jnp.concatenate([to_y[:half], to_y[half:] + from_z], axis=0).astype(BF16)
        return own + swap(y_sum, "y").astype(F32) + swap(z_sum, "za").astype(F32)


    def gather_pieces(own, axis):
        if not pairwise:
            return lax.all_gather(own, ("zb", "x"), axis=axis, tiled=True)
        along_z = swap(own, "zb")
        return jnp.concatenate([own, along_z, swap(own, "x"), swap(along_z, "x")], axis=axis)

    def scatter_pieces(part_of, length, axis):
        if not pairwise:
            full = part_of(0, length).astype(BF16)
            return lax.psum_scatter(full, ("zb", "x"), scatter_dimension=axis, tiled=True).astype(F32)
        half, quarter = length // 2, length // 4
        given = swap(part_of(half, length).astype(BF16), "x")
        kept = part_of(0, half) + given.astype(F32)
        given = swap(lax.slice_in_dim(kept, quarter, half, axis=axis).astype(BF16), "zb")
        return lax.slice_in_dim(kept, 0, quarter, axis=axis) + given.astype(F32)

    def in_order(mine, other, axis):
        first = jnp.where(za_at == 0, mine, other)
        second = jnp.where(za_at == 0, other, mine)
        return jnp.concatenate([first, second], axis=axis)

    def gather_weight(part_of, axis):
        mine = part_of(za_at)
        if za_count > 1:
            mine = in_order(mine, swap(part_of(1 - za_at), "za"), axis)
        return gather_pieces(mine, axis)

    def scatter_weight(part_of, axis):
        part = scatter_pieces(part_of, width, axis)
        if za_count == 1:
            return [part]
        first = lax.slice_in_dim(part, 0, blk_rows, axis=axis)
        second = lax.slice_in_dim(part, blk_rows, 2 * blk_rows, axis=axis)
        mine = jnp.where(za_at == 0, first, second)
        other = swap(jnp.where(za_at == 0, second, first).astype(BF16), "za").astype(F32)
        return [jnp.where(za_at == 0, mine, other), jnp.where(za_at == 0, other, mine)]

    def half_of(weight, at, axis):
        size = weight.shape[axis] // za_count
        return lax.dynamic_slice_in_dim(weight, at * size, size, axis=axis)


    def piece_group(index):
        if pairwise:
            return zb_at ^ (index % 2), x_at ^ (index // 2)
        return index // x_count, index % x_count

    def to_pieces(value):
        blocks = []
        for index in range(group_count):
            zb_of, x_of = piece_group(index)
            for za_of in range(za_count):
                block = (zb_of * za_count + za_of) * x_count + x_of
                blocks.append(lax.dynamic_slice_in_dim(value, block * blk_rows, blk_rows, axis=1))
        return jnp.concatenate(blocks, axis=1) if pairwise else value

    def from_pieces(value):
        if not pairwise:
            return value
        blocks = []
        for block in range(group_count * za_count):
            zb_of, za_of, x_of = block // 4, block // 2 % 2, block % 2
            index = (x_at ^ x_of) * 2 + (zb_at ^ zb_of)
            blocks.append(lax.dynamic_slice_in_dim(value, (index * 2 + za_of) * blk_rows, blk_rows, axis=1))
        return jnp.concatenate(blocks, axis=1)


    per_span = head_count // 2
    member = jnp.arange(member_count, dtype=jnp.int32)
    if pairwise:
        member_y, member_za, member_core = y_at ^ (member % 2), za_at ^ (member // 2 % 2), core_at ^ (member // 4)
    else:
        member_za = member % za_count
        member_core = member // za_count % core_count
        member_y = member // (za_count * core_count)
    group = jnp.arange(group_count, dtype=jnp.int32)
    group_zb, group_x = piece_group(group)
    member_head = member_y * core_count + member_core
    span_table = jnp.arange(block_deal.shape[0], dtype=jnp.int32)

    def natural_tile(zb_of, x_of):
        blk = (zb_of * za_count + member_za) * x_count + x_of
        entry = 2 * blk + member_head // per_span
        span = jnp.sum(
            jnp.where(entry[..., None] == span_table, block_deal, 0), axis=-1, dtype=jnp.int32
        )
        return span * per_span + member_head % per_span

    query_tile = natural_tile(zb_at, x_at)
    key_tile = natural_tile(group_zb[:, None], group_x[:, None]).reshape(-1)
    tile_ids = jnp.arange(key_tile.shape[0], dtype=jnp.int32)
    offsets = jnp.sum(
        jnp.where(key_tile[None, :] == tile_ids[:, None], tile_ids[None, :] * tok_dev, 0), axis=1, dtype=jnp.int32
    )
    natural = query_tile[:, None] * tok_dev + jnp.arange(tok_dev, dtype=jnp.int32)[None, :]
    seq_ids = jnp.arange(seq_lengths.shape[0], dtype=jnp.int32)
    seq_ends = jnp.sum(jnp.where(seq_ids[None, :] <= seq_ids[:, None], seq_lengths[None, :], 0), axis=1, dtype=jnp.int32)
    starts = jnp.max(jnp.where(seq_ends <= natural[..., None], seq_ends, 0), axis=-1)
    tiles = (query_tile, starts[:, 0] // (2 * tok_dev))
    start_rows = jnp.stack([starts, starts], axis=1)
    start_cols = jnp.broadcast_to(starts.reshape(rows, 1), (rows, 128))
    places = (natural - starts).reshape(rows)
    half_width = HEAD_SIZE // 2
    frequency = jnp.power(ROPE_BASE, -jnp.arange(half_width, dtype=F32) * (2.0 / HEAD_SIZE))
    angles = places.astype(F32)[:, None] * frequency[None, :]
    cosine = jnp.cos(angles)
    sine = jnp.sin(angles)
    cosine = jnp.concatenate([cosine, cosine], axis=1)
    sine = jnp.concatenate([-sine, sine], axis=1)


    q_width = q_weight.shape[1] // za_count
    k_width = k_weight.shape[1] // za_count
    qkv_width = q_width + 2 * k_width
    gain_pad = 16

    gain_row = jnp.concatenate([norm_gain, mlp_gain])
    head_gains = jnp.concatenate([q_gain, k_gain])

    def gain_rows():
        top = jnp.pad(gain_row, (0, qkv_width - gain_row.shape[0]))[None]
        bottom = jnp.pad(head_gains, (0, qkv_width - head_gains.shape[0]))[None]
        return jnp.concatenate([top, bottom, jnp.zeros((gain_pad - 2, qkv_width), BF16)], axis=0)

    def qkv_part(at):
        return jnp.concatenate(
            [half_of(q_weight, at, 1), half_of(k_weight, at, 1), half_of(v_weight, at, 1), ], axis=1
        )

    padded = blk_rows + gain_pad
    own_gain_rows = gain_rows()
    qkv_all = gather_weight(lambda at: jnp.concatenate([qkv_part(at), own_gain_rows], axis=0), 0)
    qkv_all = qkv_all.reshape(group_count * za_count, padded, qkv_width)
    qkv_cols = qkv_all[:, :blk_rows].reshape(width, qkv_width)
    gains = qkv_all[:, blk_rows, : 2 * blk_rows].astype(F32)
    gain_one = gains[:, :blk_rows].reshape(1, width)
    gain_two = gains[:, blk_rows:].reshape(1, width)
    small = q_gain.shape[0]
    head_parts = qkv_all[:, blk_rows + 1, : 2 * small].astype(F32).reshape(group_count * za_count, 2, small)

    def head_gain(which):
        return from_small(head_parts[:, which])

    def from_small(parts):
        if not pairwise:
            return parts.reshape(1, -1)
        rows_of = []
        for block in range(8):
            zb_of, za_of, x_of = block // 4, block // 2 % 2, block % 2
            index = ((x_at ^ x_of) * 2 + (zb_at ^ zb_of)) * 2 + za_of
            rows_of.append(lax.dynamic_slice_in_dim(parts, index, 1, axis=0))
        return jnp.concatenate(rows_of, axis=1)

    qk_gains = jnp.concatenate([head_gain(0), head_gain(1)], axis=0)


    local_low = to_pieces(tokens)
    local_rows = local_low.astype(F32)
    input_rows = gather_rows(local_low).astype(F32)
    o_cols = gather_weight(lambda at: half_of(o_weight, at, 0), 1)
    gu_cols = gather_weight(
        lambda at: jnp.concatenate([half_of(gate_weight, at, 1), half_of(up_weight, at, 1)], axis=1), 0
    )
    down_cols = gather_weight(lambda at: half_of(down_weight, at, 0), 1)
    grad_local = to_pieces(out_grad)
    grad_rows = gather_rows(grad_local)

    def unit_rows(value):
        return value * lax.rsqrt(jnp.mean(value * value, axis=-1, keepdims=True) + EPSILON)

    input_unit = unit_rows(input_rows)
    normed = (input_unit * gain_one).astype(BF16)
    raw = matmul(normed, qkv_cols)
    queries, kv_own = shape_heads(raw, cosine, sine, qk_gains)
    key_values = gather_pieces(kv_own, 0)
    attn_low, inverse = attend(offsets, tiles, queries, start_cols, [key_values])
    residual = local_rows + scatter_rows(lambda at: matmul(attn_low[at], o_cols))


    rho_two = lax.rsqrt(jnp.mean(residual * residual, axis=-1, keepdims=True) + EPSILON)
    unit_two = residual * rho_two
    mlp_rows = gather_rows((unit_two * gain_two).astype(BF16))
    ff = gu_cols.shape[1] // 2
    gate_up = matmul(mlp_rows, gu_cols)
    gate_act, up_act = gate_up[:, :ff], gate_up[:, ff:]
    sig = jax.nn.sigmoid(gate_act)
    silu = gate_act * sig
    hidden = (silu * up_act).astype(BF16)
    hidden_grad = contract_cols(grad_rows, down_cols)
    gate_low = (hidden_grad * up_act * (sig * (1.0 + gate_act * (1.0 - sig)))).astype(BF16)
    up_low = (hidden_grad * silu).astype(BF16)
    gu_low = jnp.concatenate([gate_low, up_low], axis=1)
    mlp_in_grad = scatter_rows(lambda at: contract_cols(gu_low[at], gu_cols))

    down_parts = scatter_weight(lambda lo, hi: contract_rows(hidden, grad_rows[:, lo:hi]), 1)
    gate_parts = scatter_weight(lambda lo, hi: contract_rows(mlp_rows[:, lo:hi], gate_low), 0)
    up_parts = scatter_weight(lambda lo, hi: contract_rows(mlp_rows[:, lo:hi], up_low), 0)
    block_out = residual + scatter_rows(lambda at: matmul(hidden[at], down_cols))

    gain_two_part = jnp.sum(mlp_in_grad * unit_two, axis=0, keepdims=True)
    scaled = mlp_in_grad * gain_two
    inner = jnp.mean(scaled * unit_two, axis=-1, keepdims=True)
    residual_grad = grad_local.astype(F32) + rho_two * (scaled - unit_two * inner)


    branch_rows = gather_rows(residual_grad.astype(BF16))
    attn_grad = contract_cols(branch_rows, o_cols).astype(BF16)
    query_grad, kv_grads = attend_back(
        offsets, tiles, queries, start_rows, inverse, attn_low, attn_grad, [key_values]
    )
    o_parts = scatter_weight(lambda lo, hi: contract_rows(attn_low, branch_rows[:, lo:hi]), 1)
    kv_grad = scatter_pieces(lambda lo, hi: kv_grads[lo:hi].astype(F32), kv_grads.shape[0], 0).astype(BF16)
    q_low, q_gain_part = shape_back(raw, query_grad, cosine, sine, qk_gains, 2, 0, 0, HEAD_SIZE**-0.5)
    kv_low, k_gain_part = shape_back(raw, kv_grad, cosine, sine, qk_gains, 1, 2, 1, 1.0)
    low = jnp.concatenate([q_low, kv_low], axis=1)

    gain_one_parts = []

    def input_terms(at):
        terms = contract_cols(low[at], qkv_cols)
        gain_one_parts.append(jnp.sum(terms * input_unit[at], axis=0, keepdims=True))
        return terms

    input_grad = scatter_rows(input_terms)
    qkv_parts = scatter_weight(lambda lo, hi: contract_rows(normed[:, lo:hi], low), 0)

    gain_sum = jnp.concatenate(
        [
            from_pieces(sum(gain_one_parts)),
            from_pieces(gain_two_part),
            jnp.sum(q_gain_part, axis=0, keepdims=True),
            jnp.sum(k_gain_part, axis=0, keepdims=True),
        ],
        axis=1,
    )
    if pairwise:
        for name in ("core", "y", "za", "x", "zb"):
            gain_sum = gain_sum + swap(gain_sum, name)
    else:
        gain_sum = lax.psum(gain_sum, all_axes)

    unit_one = local_rows * (rho_one := lax.rsqrt(jnp.mean(local_rows * local_rows, axis=-1, keepdims=True) + EPSILON))
    scaled = input_grad * gain_one
    inner = jnp.mean(scaled * unit_one, axis=-1, keepdims=True)
    in_grad = residual_grad + rho_one * (scaled - unit_one * inner)

    device = (((y_at * core_count + core_at) * zb_count + zb_at) * za_count + za_at) * x_count + x_at
    device_count = head_count * zb_count * za_count * x_count

    def own_slice(first, length):
        share = length // device_count
        return lax.dynamic_slice_in_dim(gain_sum[0], first + device * share, share, axis=0)

    def join(parts, lo, hi, axis):
        cut = [lax.slice_in_dim(part, lo, hi, axis=axis) for part in parts]
        return jnp.concatenate(cut, axis=axis)

    return (
        from_pieces(block_out).astype(BF16),
        from_pieces(in_grad),
        own_slice(0, width),
        join(qkv_parts, 0, q_width, 1),
        join(qkv_parts, q_width, q_width + k_width, 1),
        join(qkv_parts, q_width + k_width, qkv_width, 1),
        own_slice(2 * width, HEAD_SIZE),
        own_slice(2 * width + HEAD_SIZE, HEAD_SIZE),
        jnp.concatenate(o_parts, axis=0),
        own_slice(width, width),
        jnp.concatenate(gate_parts, axis=1),
        jnp.concatenate(up_parts, axis=1),
        jnp.concatenate(down_parts, axis=0),
    )


def solution(mesh):
    heads, blks = mesh.shape["head"], mesh.shape["blk"]
    za_count = KEY_VALUE_HEADS // heads
    side = math.isqrt(blks // za_count)
    sizes = (heads // 2, 2, side, za_count, side)
    names = ("y", "core", "zb", "za", "x")
    devices = mesh.devices.reshape(sizes)
    inner = Mesh(devices, names)
    head, blk = ("y", "core"), ("zb", "za", "x")
    rows, in_weight, out_weight, gain = P(names, None), P(blk, head), P(head, blk), P(blk)
    return jax.shard_map(
        paired_layer if sizes == (2, 2, 2, 2, 2) else functools.partial(layer, sizes),
        mesh=inner,
        in_specs=(
            rows,
            rows,
            P(),
            P(),
            gain,
            in_weight,
            in_weight,
            in_weight,
            gain,
            gain,
            out_weight,
            gain,
            in_weight,
            in_weight,
            out_weight,
        ),
        out_specs=(
            rows,
            rows,
            P(names),
            in_weight,
            in_weight,
            in_weight,
            P(names),
            P(names),
            out_weight,
            P(names),
            in_weight,
            in_weight,
            out_weight,
        ),
        check_vma=False,
    )
```

```python
import functools
import math

import jax
import jax.numpy as jnp
from jax import lax
from jax.experimental import pallas as pl
from jax.experimental.pallas import tpu as pltpu
from jax.sharding import Mesh
from jax.sharding import PartitionSpec as P

HEAD_SIZE = 128
KEY_VALUE_HEADS = 8
EPSILON = 1e-06
ROPE_BASE = 1000000.0
F32 = jnp.float32
BF16 = jnp.bfloat16
SWAP = [(0, 1), (1, 0)]
PAIRS_OF_ROWS = (((0,), (0,)), ((), ()))
PAIRS_OF_COLS = (((1,), (1,)), ((), ()))
VMEM = pltpu.MemorySpace.VMEM
LIGHT = pl.CostEstimate(flops=1000, bytes_accessed=1000, transcendentals=0)
SMEM = pltpu.MemorySpace.SMEM


def matmul(left, right):
    return jnp.dot(left, right, preferred_element_type=F32)


def contract_rows(left, right):
    return lax.dot_general(left, right, PAIRS_OF_ROWS, preferred_element_type=F32)


def contract_cols(left, right):
    return lax.dot_general(left, right, PAIRS_OF_COLS, preferred_element_type=F32)


def swap(value, axis):
    return lax.ppermute(value, axis, SWAP)


def attend_kernel(off_ref, tile_ref, low_ref, q_ref, start_ref, *refs, parts, first, last):
    half = 128
    kv_refs, refs = refs[:parts], refs[parts:]
    if not first:
        before_ref, refs = refs[0], refs[1:]
    if last:
        out_ref, inv_ref, kv_ref, acc_ref = refs
    else:
        after_ref, kv_ref, acc_ref = refs
    share = kv_refs[0].shape[0]
    for part, ref in enumerate(kv_refs):
        kv_ref[part * share : (part + 1) * share, :] = ref[...]
    lane = lax.broadcasted_iota(jnp.int32, (256, 256), 1)
    row = lax.broadcasted_iota(jnp.int32, (256, 256), 0) % half
    ones = jnp.ones((256, HEAD_SIZE), BF16)

    def tile(index, unused):
        rows = pl.ds(pl.multiple_of(index * half, half), half)
        queries = jnp.concatenate([q_ref[rows, :HEAD_SIZE], q_ref[rows, HEAD_SIZE:]], axis=0)
        start = start_ref[rows, :]
        start = jnp.concatenate([start, start], axis=1)
        start = jnp.concatenate([start, start], axis=0)
        places = tile_ref[index] * half + row
        acc_ref[...] = jnp.zeros_like(acc_ref) if first else before_ref[index]

        def step(block, unused_step):
            at = off_ref[2 * block]

            @pl.when(at >= 0)
            def _():
                low = pl.ds(pl.multiple_of(at, half), half)
                high = pl.ds(pl.multiple_of(off_ref[2 * block + 1], half), half)
                keys = jnp.concatenate([kv_ref[low, :HEAD_SIZE], kv_ref[high, :HEAD_SIZE]], axis=0)
                values = jnp.concatenate([kv_ref[low, HEAD_SIZE:], kv_ref[high, HEAD_SIZE:]], axis=0)
                scores = contract_cols(queries, keys)
                natural = block * 256 + lane
                allowed = (natural <= places) & (natural >= start)
                weights = jnp.where(allowed, jnp.exp(scores), 0.0).astype(BF16)
                acc_ref[...] += matmul(weights, jnp.concatenate([values, ones], axis=1))

            return unused_step

        lax.fori_loop(low_ref[index], tile_ref[index] // 2 + 1, step, 0)
        if last:
            inverse = 1.0 / acc_ref[:, HEAD_SIZE:]
            attended = (acc_ref[:, :HEAD_SIZE] * inverse).astype(BF16)
            out_ref[rows, :HEAD_SIZE] = attended[:half]
            out_ref[rows, HEAD_SIZE:] = attended[half:]
            inv_ref[index, 0:1, :] = jnp.transpose(inverse[:half])[0:1, :]
            inv_ref[index, 1:2, :] = jnp.transpose(inverse[half:])[0:1, :]
        else:
            after_ref[index] = acc_ref[...]
        return unused

    lax.fori_loop(0, q_ref.shape[0] // half, tile, 0)


def attend_back_kernel(
    off_ref, tile_ref, low_ref, q_ref, start_ref, inv_ref, out_ref, grad_ref, *refs, parts, first, last
):
    half = 128
    kv_refs, refs = refs[:parts], refs[parts:]
    if not first:
        before_ref, refs = refs[0], refs[1:]
    dq_ref, *dkv_refs = refs[: 1 + parts]
    kv_ref, dk_ref, dv_ref, acc_ref = refs[1 + parts :]
    share = kv_refs[0].shape[0]
    for part, ref in enumerate(kv_refs):
        kv_ref[part * share : (part + 1) * share, :] = ref[...]
    key_row = lax.broadcasted_iota(jnp.int32, (256, 256), 0)
    query_lane = lax.broadcasted_iota(jnp.int32, (1, 256), 1) % half

    def clear(index, unused):
        rows = pl.ds(pl.multiple_of(index * 256, 256), 256)
        dk_ref[rows, :] = jnp.zeros((256, HEAD_SIZE), F32)
        dv_ref[rows, :] = jnp.zeros((256, HEAD_SIZE), F32)
        return unused

    lax.fori_loop(0, dk_ref.shape[0] // 256, clear, 0)

    def tile(index, unused):
        rows = pl.ds(pl.multiple_of(index * half, half), half)

        def both(ref):
            return jnp.concatenate([ref[rows, :HEAD_SIZE], ref[rows, HEAD_SIZE:]], axis=0)

        def along(ref):
            return jnp.concatenate([ref[index, 0:1, :], ref[index, 1:2, :]], axis=1)

        queries = both(q_ref)
        grads = both(grad_ref)
        products = both(out_ref).astype(F32) * grads.astype(F32)
        deltas = jnp.sum(jnp.transpose(products), axis=0, keepdims=True)
        inverse = along(inv_ref)
        start = along(start_ref)
        places = tile_ref[index] * half + query_lane
        acc_ref[...] = jnp.zeros_like(acc_ref) if first else both(before_ref)

        def step(block, unused_step):
            at = off_ref[2 * block]

            @pl.when(at >= 0)
            def _():
                low = pl.ds(pl.multiple_of(at, half), half)
                high = pl.ds(pl.multiple_of(off_ref[2 * block + 1], half), half)
                keys = jnp.concatenate([kv_ref[low, :HEAD_SIZE], kv_ref[high, :HEAD_SIZE]], axis=0)
                values = jnp.concatenate([kv_ref[low, HEAD_SIZE:], kv_ref[high, HEAD_SIZE:]], axis=0)
                scores = contract_cols(keys, queries)
                natural = block * 256 + key_row
                allowed = (natural <= places) & (natural >= start)
                probs = jnp.where(allowed, jnp.exp(scores) * inverse, 0.0)
                prob_grad = contract_cols(values, grads)
                score_grad = (probs * (prob_grad - deltas)).astype(BF16)
                value_part = matmul(probs.astype(BF16), grads)
                key_part = matmul(score_grad, queries)
                dv_ref[low, :] += value_part[:half]
                dv_ref[high, :] += value_part[half:]
                dk_ref[low, :] += key_part[:half]
                dk_ref[high, :] += key_part[half:]
                acc_ref[...] += contract_rows(score_grad, keys)

            return unused_step

        lax.fori_loop(low_ref[index], tile_ref[index] // 2 + 1, step, 0)
        dq_ref[rows, :HEAD_SIZE] = acc_ref[:half, :].astype(dq_ref.dtype)
        dq_ref[rows, HEAD_SIZE:] = acc_ref[half:, :].astype(dq_ref.dtype)
        return unused

    lax.fori_loop(0, q_ref.shape[0] // half, tile, 0)

    for part, ref in enumerate(dkv_refs):

        def store(index, unused):
            target = pl.ds(pl.multiple_of(index * 256, 256), 256)
            source = pl.ds(pl.multiple_of(part * share + index * 256, 256), 256)
            ref[target, :HEAD_SIZE] = dk_ref[source, :].astype(BF16)
            ref[target, HEAD_SIZE:] = dv_ref[source, :].astype(BF16)
            return unused

        lax.fori_loop(0, share // 256, store, 0)


def attend(offsets, tiles, queries, start_cols, kv_parts, before=None, last=True):
    rows, width = queries.shape
    parts, share = len(kv_parts), kv_parts[0].shape[0]
    keys = parts * share
    first = before is None
    extra = () if first else (before,)
    whole = (
        (jax.ShapeDtypeStruct((rows, width), BF16), jax.ShapeDtypeStruct((rows // 128, 2, 128), F32))
        if last
        else (jax.ShapeDtypeStruct((rows // 128, 256, 256), F32),)
    )
    return pl.pallas_call(
        functools.partial(attend_kernel, parts=parts, first=first, last=last),
        name="attend",
        out_shape=whole,
        in_specs=[pl.BlockSpec(memory_space=SMEM)] * 3 + [pl.BlockSpec(memory_space=VMEM)] * (2 + parts + len(extra)),
        out_specs=[pl.BlockSpec(memory_space=VMEM)] * len(whole),
        scratch_shapes=[pltpu.VMEM((keys, width), BF16), pltpu.VMEM((256, 256), F32)],
        compiler_params=pltpu.CompilerParams(vmem_limit_bytes=12 * 2**20 + keys * 1536),
        cost_estimate=LIGHT,
    )(offsets, *tiles, queries, start_cols, *kv_parts, *extra)


def attend_back(offsets, tiles, queries, start_rows, inverse, attended, grads, kv_parts, before=None, last=True):
    rows, width = queries.shape
    parts, share = len(kv_parts), kv_parts[0].shape[0]
    keys = parts * share
    first = before is None
    extra = () if first else (before,)
    return pl.pallas_call(
        functools.partial(attend_back_kernel, parts=parts, first=first, last=last),
        name="attend_back",
        out_shape=(jax.ShapeDtypeStruct((rows, width), BF16 if last else F32),)
        + tuple(jax.ShapeDtypeStruct((share, width), BF16) for unused in kv_parts),
        in_specs=[pl.BlockSpec(memory_space=SMEM)] * 3 + [pl.BlockSpec(memory_space=VMEM)] * (5 + parts + len(extra)),
        out_specs=[pl.BlockSpec(memory_space=VMEM)] * (1 + parts),
        scratch_shapes=[
            pltpu.VMEM((keys, width), BF16),
            pltpu.VMEM((keys, HEAD_SIZE), F32),
            pltpu.VMEM((keys, HEAD_SIZE), F32),
            pltpu.VMEM((256, HEAD_SIZE), F32),
        ],
        compiler_params=pltpu.CompilerParams(vmem_limit_bytes=12 * 2**20 + keys * 2816),
        cost_estimate=LIGHT,
    )(offsets, *tiles, queries, start_rows, inverse, attended, grads, *kv_parts, *extra)


def shape_kernel(raw_ref, cos_ref, sin_ref, gain_ref, q_ref, kv_ref):
    cosine = cos_ref[...]
    sine = sin_ref[...]

    def shaped(first, gain):
        value = raw_ref[:, first : first + HEAD_SIZE]
        mean_square = jnp.mean(value * value, axis=-1, keepdims=True)
        value = value * lax.rsqrt(mean_square + EPSILON) * gain
        return value * cosine + pltpu.roll(value, HEAD_SIZE // 2, 1) * sine

    for head in range(2):
        columns = slice(head * HEAD_SIZE, (head + 1) * HEAD_SIZE)
        q_ref[:, columns] = (shaped(head * HEAD_SIZE, gain_ref[0:1, :]) * HEAD_SIZE**-0.5).astype(BF16)
    kv_ref[:, :HEAD_SIZE] = shaped(2 * HEAD_SIZE, gain_ref[1:2, :]).astype(BF16)
    kv_ref[:, HEAD_SIZE:] = raw_ref[:, 3 * HEAD_SIZE :].astype(BF16)


def shape_back_kernel(raw_ref, grad_ref, cos_ref, sin_ref, gain_ref, low_ref, gain_grad_ref, *, heads, gain_row, factor):
    @pl.when(pl.program_id(0) == 0)
    def _():
        gain_grad_ref[...] = jnp.zeros_like(gain_grad_ref)

    cosine = cos_ref[...]
    sine = sin_ref[...]
    gain = gain_ref[gain_row : gain_row + 1, :]
    total = jnp.zeros((8, HEAD_SIZE), F32)
    for head in range(heads):
        columns = slice(head * HEAD_SIZE, (head + 1) * HEAD_SIZE)
        value = raw_ref[:, columns]
        grad = grad_ref[:, columns].astype(F32) * factor
        grad = grad * cosine - pltpu.roll(grad, HEAD_SIZE // 2, 1) * sine
        rho = lax.rsqrt(jnp.mean(value * value, axis=-1, keepdims=True) + EPSILON)
        unit = value * rho
        total = total + jnp.sum((grad * unit).reshape(-1, 8, HEAD_SIZE), axis=0)
        scaled = grad * gain
        inner = jnp.mean(scaled * unit, axis=-1, keepdims=True)
        low_ref[:, columns] = (rho * (scaled - unit * inner)).astype(BF16)
    if heads == 1:
        low_ref[:, HEAD_SIZE:] = grad_ref[:, HEAD_SIZE:].astype(BF16)
    gain_grad_ref[...] += total


ROW_TILE = 256


def shape_heads(raw, cosine, sine, gains):
    rows = raw.shape[0]
    block = lambda width: pl.BlockSpec((ROW_TILE, width), lambda i: (i, 0))
    return pl.pallas_call(
        shape_kernel,
        name="shape_heads",
        grid=(rows // ROW_TILE,),
        out_shape=(jax.ShapeDtypeStruct((rows, 256), BF16), jax.ShapeDtypeStruct((rows, 256), BF16)),
        in_specs=[block(512), block(128), block(128), pl.BlockSpec((2, 128), lambda i: (0, 0))],
        out_specs=[block(256), block(256)],
        compiler_params=pltpu.CompilerParams(vmem_limit_bytes=8 * 2**20),
        cost_estimate=LIGHT,
    )(raw, cosine, sine, gains)


def shape_back(raw, grads, cosine, sine, gains, heads, column, gain_row, factor):
    rows = raw.shape[0]
    block = lambda width, at=0: pl.BlockSpec((ROW_TILE, width), lambda i: (i, at))
    return pl.pallas_call(
        functools.partial(shape_back_kernel, heads=heads, gain_row=gain_row, factor=factor),
        name="shape_back",
        grid=(rows // ROW_TILE,),
        out_shape=(jax.ShapeDtypeStruct((rows, 256), BF16), jax.ShapeDtypeStruct((8, 128), F32)),
        in_specs=[
            block(heads * 128, column),
            block(256),
            block(128),
            block(128),
            pl.BlockSpec((2, 128), lambda i: (0, 0)),
        ],
        out_specs=[block(256), pl.BlockSpec((8, 128), lambda i: (0, 0))],
        compiler_params=pltpu.CompilerParams(vmem_limit_bytes=8 * 2**20),
        cost_estimate=LIGHT,
    )(raw, grads, cosine, sine, gains)


def reorder_kernel(order_ref, *refs):
    half = len(refs) // 2
    for source, target in zip(refs[:half], refs[half:]):
        target[...] = source[...].astype(target.dtype)


def reorder(order, values, types):
    rows, width = values[0].shape
    blocks = order.shape[0]
    size = width // blocks
    taken = pl.BlockSpec((rows, size), lambda i, order_ref: (0, order_ref[i]))
    put = pl.BlockSpec((rows, size), lambda i, order_ref: (0, i))
    return pl.pallas_call(
        reorder_kernel,
        name="reorder",
        grid_spec=pltpu.PrefetchScalarGridSpec(
            num_scalar_prefetch=1,
            grid=(blocks,),
            in_specs=[taken] * len(values),
            out_specs=[put] * len(values),
        ),
        out_shape=[jax.ShapeDtypeStruct(value.shape, kind) for value, kind in zip(values, types)],
        compiler_params=pltpu.CompilerParams(vmem_limit_bytes=8 * 2**20),
        cost_estimate=LIGHT,
    )(order, *values)


def assemble_kernel(at_ref, *refs, entries, axis):
    out_ref = refs[-1]
    for source, (place, kind) in zip(refs[:-1], entries):
        size = source.shape[axis]
        if kind == 0:
            span = slice(place, place + size)
        else:
            at = at_ref[0] if kind > 0 else 1 - at_ref[0]
            span = pl.ds(pl.multiple_of(place + at * 256, 16 if axis == 0 else 128), size)
        if axis == 0:
            out_ref[span, :] = source[...]
        else:
            out_ref[:, span] = source[...]


def assemble(at, parts, axis):
    values = [value for value, unused, kind in parts]
    total = sum(value.shape[axis] for value in values)
    other = values[0].shape[1 - axis]
    shape = (total, other) if axis == 0 else (other, total)
    return pl.pallas_call(
        functools.partial(assemble_kernel, entries=tuple((place, kind) for unused, place, kind in parts), axis=axis),
        name="assemble",
        out_shape=jax.ShapeDtypeStruct(shape, BF16),
        in_specs=[pl.BlockSpec(memory_space=SMEM)] + [pl.BlockSpec(memory_space=VMEM)] * len(values),
        out_specs=pl.BlockSpec(memory_space=VMEM),
        compiler_params=pltpu.CompilerParams(vmem_limit_bytes=12 * 2**20),
        cost_estimate=LIGHT,
    )(at, *values)


def terms_kernel(left_ref, right_ref, left_cols_ref, right_cols_ref, kept_ref, given_ref):
    total = contract_cols(left_ref[...], left_cols_ref[...]) + contract_cols(right_ref[...], right_cols_ref[...])
    middle = kept_ref.shape[0]
    kept_ref[...] = total[:middle]
    given_ref[...] = total[middle:].astype(BF16)


def two_terms(left, right, left_cols, right_cols):
    rows, depth = left.shape
    width = left_cols.shape[0]
    tile = 512
    value = pl.BlockSpec((rows, depth), lambda i: (0, 0))
    cols = pl.BlockSpec((tile, depth), lambda i: (i, 0))
    half = pl.BlockSpec((rows // 2, tile), lambda i: (0, i))
    return pl.pallas_call(
        terms_kernel,
        name="two_terms",
        grid=(width // tile,),
        out_shape=(jax.ShapeDtypeStruct((rows // 2, width), F32), jax.ShapeDtypeStruct((rows // 2, width), BF16)),
        in_specs=[value, value, cols, cols],
        out_specs=(half, half),
        cost_estimate=LIGHT,
    )(left, right, left_cols, right_cols)


def hidden_kernel(mine_ref, theirs_ref, gate_ref, up_ref, hidden_ref, gate_slope_ref, up_slope_ref):
    middle = mine_ref.shape[0]
    for part, source in ((slice(0, middle), mine_ref), (slice(middle, 2 * middle), theirs_ref)):
        rows = source[...]
        gate = matmul(rows, gate_ref[...])
        up = matmul(rows, up_ref[...])
        sig = 1.0 / (1.0 + jnp.exp(-gate))
        silu = gate * sig
        hidden_ref[part, :] = (silu * up).astype(BF16)
        gate_slope_ref[part, :] = (up * (sig * (1.0 + gate * (1.0 - sig)))).astype(BF16)
        up_slope_ref[part, :] = silu.astype(BF16)


def hidden_units(mine, theirs, gate_cols, up_cols):
    middle, width = mine.shape
    units = gate_cols.shape[1]
    tile = 256
    whole = pl.BlockSpec((middle, width), lambda i: (0, 0))
    cols = pl.BlockSpec((width, tile), lambda i: (0, i))
    out = pl.BlockSpec((2 * middle, tile), lambda i: (0, i))
    return pl.pallas_call(
        hidden_kernel,
        name="hidden_units",
        grid=(units // tile,),
        out_shape=(jax.ShapeDtypeStruct((2 * middle, units), BF16),) * 3,
        in_specs=[whole, whole, cols, cols],
        out_specs=(out,) * 3,
        cost_estimate=LIGHT,
    )(mine, theirs, gate_cols, up_cols)


def prologue_kernel(
    order_ref, at_ref, tokens_ref, grad_ref, q_ref, k_ref, v_ref, norm_ref, mlp_ref, q_gain_ref, k_gain_ref,
    tokens_out, grad_out, keep_ref, give_ref
):
    size = tokens_ref.shape[1] // 8
    for block in range(8):
        source = pl.ds(pl.multiple_of(order_ref[block] * size, 128), size)
        tokens_out[:, block * size : (block + 1) * size] = tokens_ref[:, source]
        grad_out[:, block * size : (block + 1) * size] = grad_ref[:, source]

    rows, q_width = q_ref.shape[0], q_ref.shape[1] // 2
    k_width = k_ref.shape[1] // 2
    total = q_width + 2 * k_width
    small = q_gain_ref.shape[1]
    place = lax.broadcasted_iota(jnp.int32, (small, HEAD_SIZE), 1) - lax.broadcasted_iota(
        jnp.int32, (small, HEAD_SIZE), 0
    )
    put = (place == at_ref[1] * small).astype(BF16)
    extra = jnp.concatenate(
        [
            jnp.concatenate([norm_ref[...].reshape(1, rows), mlp_ref[...].reshape(1, rows)], axis=1),
            jnp.concatenate(
                [
                    matmul(q_gain_ref[...], put).astype(BF16),
                    matmul(k_gain_ref[...], put).astype(BF16),
                    jnp.zeros((1, total - 2 * HEAD_SIZE), BF16),
                ],
                axis=1,
            ),
            jnp.zeros((14, total), BF16),
        ],
        axis=0,
    )
    for target, at in ((keep_ref, at_ref[0]), (give_ref, 1 - at_ref[0])):
        target[:rows, :q_width] = q_ref[:, pl.ds(pl.multiple_of(at * q_width, 128), q_width)]
        target[:rows, q_width : q_width + k_width] = k_ref[:, pl.ds(pl.multiple_of(at * k_width, 128), k_width)]
        target[:rows, q_width + k_width :] = v_ref[:, pl.ds(pl.multiple_of(at * k_width, 128), k_width)]
        target[rows:, :] = extra


def prologue(order, at, tokens, out_grad, q_weight, k_weight, v_weight, gains):
    shape = jax.ShapeDtypeStruct((q_weight.shape[0] + 16, (q_weight.shape[1] + 2 * k_weight.shape[1]) // 2), BF16)
    whole = lambda value: pl.BlockSpec(value.shape, lambda i, order_ref, at_ref: (0,) * len(value.shape))
    fixed = (q_weight, k_weight, v_weight) + gains
    return pl.pallas_call(
        prologue_kernel,
        name="prologue",
        grid_spec=pltpu.PrefetchScalarGridSpec(
            num_scalar_prefetch=2,
            grid=(1,),
            in_specs=[whole(tokens), whole(out_grad)] + [whole(value) for value in fixed],
            out_specs=[whole(tokens), whole(tokens), whole(shape), whole(shape)],
        ),
        out_shape=(jax.ShapeDtypeStruct(tokens.shape, BF16),) * 2 + (shape, shape),
        cost_estimate=LIGHT,
    )(order, at, tokens, out_grad, *fixed)


def after(token, values):
    return lax.optimization_barrier((token, values))[1]


def meet(token, values):
    return lax.optimization_barrier((token, values))


def trade(token, sends):
    held = after(token, [value for value, unused in sends])
    return [swap(value, axis) for value, (unused, axis) in zip(held, sends)]


def places_of(query_tile, key_tile, seq_lengths, tok_dev):
    rows = query_tile.shape[0] * tok_dev
    tile_ids = jnp.arange(key_tile.shape[0], dtype=jnp.int32)
    shares = (tile_ids // 16) * 8 + tile_ids % 8
    found = key_tile[None, :] == tile_ids[:, None]

    def offsets_of(parity):
        mine = found & (tile_ids // 8 % 2 == parity)[None, :]
        return jnp.sum(jnp.where(mine, shares * tok_dev + 1, 0), axis=1, dtype=jnp.int32) - 1

    offsets = (offsets_of(0), offsets_of(1))
    natural = query_tile[:, None] * tok_dev + jnp.arange(tok_dev, dtype=jnp.int32)[None, :]
    seq_ids = jnp.arange(seq_lengths.shape[0], dtype=jnp.int32)
    seq_ends = jnp.sum(jnp.where(seq_ids[None, :] <= seq_ids[:, None], seq_lengths[None, :], 0), axis=1, dtype=jnp.int32)
    starts = jnp.max(jnp.where(seq_ends <= natural[..., None], seq_ends, 0), axis=-1)
    tiles = (query_tile, jnp.max(jnp.where(seq_ends <= (query_tile * tok_dev)[:, None], seq_ends, 0), axis=-1) // (2 * tok_dev))
    start_rows = jnp.stack([starts, starts], axis=1)
    start_cols = jnp.broadcast_to(starts.reshape(rows, 1), (rows, 128))
    places = (natural - starts).reshape(rows)
    half_width = HEAD_SIZE // 2
    frequency = jnp.power(ROPE_BASE, -jnp.arange(half_width, dtype=F32) * (2.0 / HEAD_SIZE))
    angles = places.astype(F32)[:, None] * frequency[None, :]
    cosine = jnp.cos(angles)
    sine = jnp.sin(angles)
    cosine = jnp.concatenate([cosine, cosine], axis=1)
    sine = jnp.concatenate([-sine, sine], axis=1)
    return offsets, tiles, start_rows, start_cols, cosine, sine


FAR = 96
KEEP_ROWS = 128
UP_ROWS = 96


def paired_layer(
    tokens,
    out_grad,
    seq_lengths,
    block_deal,
    norm_gain,
    q_weight,
    k_weight,
    v_weight,
    q_gain,
    k_gain,
    o_weight,
    mlp_gain,
    gate_weight,
    up_weight,
    down_weight,
):
    y_at, core_at, zb_at, za_at, x_at = (lax.axis_index(name) for name in ("y", "core", "zb", "za", "x"))
    tok_dev, width = tokens.shape
    blk_rows = q_weight.shape[0]
    rows = 8 * tok_dev
    middle = rows // 2
    half, quarter = width // 2, width // 4
    token = seq_lengths


    place_ids = jnp.arange(8, dtype=jnp.int32)
    to_order = ((zb_at ^ (place_ids // 2 % 2)) * 2 + place_ids % 2) * 2 + (x_at ^ (place_ids // 4))
    from_order = ((x_at ^ (place_ids % 2)) * 2 + (zb_at ^ (place_ids // 4))) * 2 + place_ids // 2 % 2

    def in_order(mine, other, axis):
        first = jnp.where(za_at == 0, mine, other)
        second = jnp.where(za_at == 0, other, mine)
        return jnp.concatenate([first, second], axis=axis)

    def half_of(weight, at, axis):
        size = weight.shape[axis] // 2
        return lax.dynamic_slice_in_dim(weight, at * size, size, axis=axis)


    def near(value):
        return [(value, "y"), (value, "za")]

    def far(from_y, from_z, rows_y):
        sends = [(from_z[:rows_y], "y")]
        return sends + ([(from_y[rows_y:], "za")] if rows_y < tok_dev else [])

    def mine_of(value, from_y, from_z, fars):
        return jnp.concatenate([value, from_y, from_z] + fars, axis=0)

    def far_sums(kept):
        return [(kept[3 * tok_dev :].astype(BF16), "y")]

    def near_sums(kept, from_y):
        to_y, to_z = kept[tok_dev : 2 * tok_dev], kept[2 * tok_dev : 3 * tok_dev] + from_y.astype(F32)
        return [(to_y.astype(BF16), "y"), (to_z.astype(BF16), "za")]

    def own_sum(kept, nears):
        return kept[:tok_dev] + nears[0].astype(F32) + nears[1].astype(F32)


    def za_parts(part, axis):
        first = lax.slice_in_dim(part, 0, blk_rows, axis=axis)
        second = lax.slice_in_dim(part, blk_rows, 2 * blk_rows, axis=axis)
        return jnp.where(za_at == 0, first, second), jnp.where(za_at == 0, second, first).astype(BF16)

    def za_join(mine, other):
        other = other.astype(F32)
        return [jnp.where(za_at == 0, mine, other), jnp.where(za_at == 0, other, mine)]


    member = jnp.arange(8, dtype=jnp.int32)
    member_y, member_za, member_core = y_at ^ (member % 2), za_at ^ (member // 2 % 2), core_at ^ (member // 4)
    group = jnp.arange(4, dtype=jnp.int32)
    span_table = jnp.arange(block_deal.shape[0], dtype=jnp.int32)

    def natural_tile(zb_of, x_of):
        entry = 2 * ((zb_of * 2 + member_za) * 2 + x_of) + member_y
        span = jnp.sum(jnp.where(entry[..., None] == span_table, block_deal, 0), axis=-1, dtype=jnp.int32)
        return span * 2 + member_core

    query_tile = natural_tile(zb_at, x_at)
    key_tile = natural_tile(zb_at ^ (group % 2)[:, None], x_at ^ (group // 2)[:, None]).reshape(-1)
    offsets, tiles, start_rows, start_cols, cosine, sine = places_of(query_tile, key_tile, seq_lengths, tok_dev)


    q_width, k_width = q_weight.shape[1] // 2, k_weight.shape[1] // 2
    qkv_width = q_width + 2 * k_width
    local_low, grad_local, qkv_keep, qkv_give = prologue(
        to_order,
        jnp.stack([za_at, (zb_at * 2 + za_at) * 2 + x_at]),
        tokens,
        out_grad,
        q_weight,
        k_weight,
        v_weight,
        (norm_gain, mlp_gain, q_gain[None], k_gain[None]),
    )
    local_rows = local_low.astype(F32)
    o_give = half_of(o_weight, 1 - za_at, 0)
    za_place = za_at[None].astype(jnp.int32)
    z_keep, qkv_far, x_keep = swap(qkv_keep, "zb"), swap(qkv_give, "za"), swap(qkv_keep, "x")
    tokens_y = swap(local_low, "y")
    (o_far,) = trade(qkv_keep, [(o_give, "za")])
    token, (qkv_far, z_keep, x_keep, tokens_y, o_far) = meet(token, (qkv_far, z_keep, x_keep, tokens_y, o_far))
    down_keep = half_of(down_weight, za_at, 0)
    tokens_z, z_far, xz_keep, x_far, down_xk = trade(
        token, [(local_low, "za"), (qkv_far, "zb"), (z_keep, "x"), (qkv_far, "x"), (down_keep, "x")]
    )
    o_pair = in_order(half_of(o_weight, za_at, 0), o_far, 1)
    token, (z_far, tokens_z, xz_keep, x_far, o_pair, down_xk) = meet(
        token, (z_far, tokens_z, xz_keep, x_far, o_pair, down_xk)
    )
    *fars, xz_far, o_x, o_z = trade(
        token, far(tokens_y, tokens_z, FAR) + [(z_far, "x"), (o_pair, "x"), (o_pair, "zb")]
    )
    gate_weight, up_weight, down_weight = after(token, (gate_weight, up_weight, down_weight))
    gate_keep, up_keep = half_of(gate_weight, za_at, 1), half_of(up_weight, za_at, 1)
    gate_give, up_give = half_of(gate_weight, 1 - za_at, 1), half_of(up_weight, 1 - za_at, 1)
    down_give = half_of(down_weight, 1 - za_at, 0)
    token, (xz_far, fars, o_x, o_z) = meet(token, (xz_far, fars, o_x, o_z))
    mine = mine_of(local_low, tokens_y, tokens_z, fars)
    theirs, gate_zk0, gate_far, gate_xk = trade(
        token, [(mine, "core"), (gate_keep[:KEEP_ROWS], "zb"), (gate_give, "za"), (gate_keep, "x")]
    )
    qkv_all = jnp.concatenate(
        [
            in_order(qkv_keep, qkv_far, 0),
            in_order(z_keep, z_far, 0),
            in_order(x_keep, x_far, 0),
            in_order(xz_keep, xz_far, 0),
        ],
        axis=0,
    ).reshape(8, blk_rows + 16, qkv_width)
    qkv_cols = qkv_all[:, :blk_rows].reshape(width, qkv_width)
    gains = qkv_all[:, blk_rows, : 2 * blk_rows].astype(F32)
    gain_one = gains[:, :blk_rows].reshape(1, width)
    gain_two = gains[:, blk_rows:].reshape(1, width)
    head_sum = jnp.sum(qkv_all[:, blk_rows + 1, : 2 * HEAD_SIZE].astype(F32), axis=0, keepdims=True)
    qk_gains = jnp.concatenate([head_sum[:, :HEAD_SIZE], head_sum[:, HEAD_SIZE:]], axis=0)


    input_rows = jnp.concatenate([mine, theirs], axis=0).astype(F32)
    input_rho = lax.rsqrt(jnp.mean(input_rows * input_rows, axis=-1, keepdims=True) + EPSILON)
    normed = (input_rows * input_rho * gain_one).astype(BF16)
    raw = matmul(normed, qkv_cols)
    queries, kv_own = shape_heads(raw, cosine, sine, qk_gains)
    token, (queries, kv_own, gate_zk0, gate_far, gate_xk) = meet(
        token, (queries, kv_own, gate_zk0, gate_far, gate_xk)
    )
    kv_z, kv_x, up_far, grads_y = trade(
        token, [(kv_own, "zb"), (kv_own, "x"), (up_give, "za"), (grad_local, "y")]
    )
    token, (kv_x,) = meet(token, (kv_x,))
    (o_xz,) = trade(token, [(o_z, "x")])
    (attn_part,) = attend(offsets[0], tiles, queries, start_cols, [kv_own, kv_x], last=False)
    gate_pair = in_order(gate_keep, gate_far, 0)
    token, (kv_z, attn_part, grads_y, o_xz, up_far, gate_pair) = meet(
        token, (kv_z, attn_part, grads_y, o_xz, up_far, gate_pair)
    )
    gate_rest = jnp.concatenate([gate_keep[KEEP_ROWS:], gate_far], axis=0)
    token, (gate_rest,) = meet(token, (gate_rest,))
    kv_xz, gate_zr, grads_z = trade(token, [(kv_z, "x"), (gate_rest, "zb"), (grad_local, "za")])
    o_cols = jnp.concatenate([o_pair, o_z, o_x, o_xz], axis=1)
    token, (kv_xz, o_cols) = meet(token, (kv_xz, o_cols))
    (gate_xf,) = trade(token, [(gate_far, "x")])
    attn_low, inverse = attend(offsets[1], tiles, queries, start_cols, [kv_z, kv_xz], before=attn_part)
    given = matmul(attn_low[middle:], o_cols).astype(BF16)
    token, (given, attn_low, gate_xf, gate_zr, grads_z) = meet(token, (given, attn_low, gate_xf, gate_zr, grads_z))
    up_pair = in_order(up_keep, up_far, 0)
    given, up_z0, up_x0, grads_far, down_far = trade(
        token,
        [(given, "core"), (up_pair[:UP_ROWS], "zb"), (up_pair[:blk_rows], "x"), (grads_z, "y"), (down_give, "za")],
    )
    kept = matmul(attn_low[:middle], o_cols)
    token, (given, kept, up_z0, up_x0, up_pair, grads_far, down_far) = meet(
        token, (given, kept, up_z0, up_x0, up_pair, grads_far, down_far)
    )
    grad_mine = mine_of(grad_local, grads_y, grads_z, [grads_far])
    kept = kept + given.astype(F32)
    from_y, up_z1, up_x1 = trade(
        token,
        far_sums(kept) + [(up_pair[UP_ROWS:blk_rows], "zb"), (up_pair[blk_rows:], "x")],
    )
    gate_z = assemble(
        za_place,
        [
            (gate_zk0, 0, 1),
            (gate_zr[: blk_rows - KEEP_ROWS], KEEP_ROWS, 1),
            (gate_zr[blk_rows - KEEP_ROWS :], 0, -1),
        ],
        0,
    )
    token, (from_y, kept, up_x1, gate_z, up_z1, grad_mine) = meet(
        token, (from_y, kept, up_x1, gate_z, up_z1, grad_mine)
    )
    *nears, gate_xz, up_z2, grad_theirs = trade(
        token, near_sums(kept, from_y) + [(gate_z, "x"), (up_pair[blk_rows:], "zb"), (grad_mine, "core")]
    )
    token, (nears, kept, gate_xz, up_z2, grad_theirs) = meet(token, (nears, kept, gate_xz, up_z2, grad_theirs))
    up_z01 = jnp.concatenate([up_z0, up_z1], axis=0)
    residual = local_rows + own_sum(kept, nears)


    rho_two = lax.rsqrt(jnp.mean(residual * residual, axis=-1, keepdims=True) + EPSILON)
    unit_two = residual * rho_two
    mlp_low = (unit_two * gain_two).astype(BF16)
    token, (mlp_low,) = meet(token, (mlp_low,))
    mlp_y, mlp_z, down_zk, down_xf, up_xz0 = trade(
        token, near(mlp_low) + [(down_keep, "zb"), (down_far, "x"), (up_z01, "x")]
    )
    gate_cols = assemble(
        za_place,
        [(gate_pair, 0, 0), (gate_z, quarter, 0), (gate_xk, half, 1), (gate_xf, half, -1)]
        + [(gate_xz, half + quarter, 0)],
        0,
    )
    grad_mine, grad_theirs = after(token, (grad_mine, grad_theirs))
    grad_rows = assemble(za_place, [(grad_mine, 0, 0), (grad_theirs, middle, 0)], 0)
    token, (mlp_y, mlp_z, down_xf, up_xz0, gate_cols, down_zk, grad_rows) = meet(
        token, (mlp_y, mlp_z, down_xf, up_xz0, gate_cols, down_zk, grad_rows)
    )
    *fars, up_xz1, down_zf0 = trade(token, far(mlp_y, mlp_z, FAR) + [(up_z2, "x"), (down_far[:400], "zb")])
    token, (fars, down_zf0, up_xz1) = meet(token, (fars, down_zf0, up_xz1))
    mlp_mine = mine_of(mlp_low, mlp_y, mlp_z, fars)
    mlp_theirs, down_zf1, down_xzk, down_xzf0 = trade(
        token, [(mlp_mine, "core"), (down_far[400:], "zb"), (down_zk, "x"), (down_zf0, "x")]
    )
    up_cols = assemble(
        za_place,
        [
            (up_pair, 0, 0),
            (up_z01, quarter, 0),
            (up_z2, quarter + blk_rows, 0),
            (up_x0, half, 0),
            (up_x1, half + blk_rows, 0),
            (up_xz0, half + quarter, 0),
            (up_xz1, half + quarter + blk_rows, 0),
        ],
        0,
    )
    token, (mlp_theirs, up_cols) = meet(token, (mlp_theirs, up_cols))
    mlp_rows = jnp.concatenate([mlp_mine, mlp_theirs], axis=0)
    gate_act = matmul(mlp_rows, gate_cols)
    token, (gate_act, up_cols, mlp_rows) = meet(token, (gate_act, up_cols, mlp_rows))
    sig = jax.nn.sigmoid(gate_act)
    silu = gate_act * sig
    slope = sig * (1.0 + gate_act * (1.0 - sig))
    up_slope = silu.astype(BF16)
    token, (silu, slope, up_slope, up_cols, mlp_rows) = meet(token, (silu, slope, up_slope, up_cols, mlp_rows))
    up_act = matmul(mlp_rows, up_cols)
    hidden = (silu * up_act).astype(BF16)
    gate_slope = (up_act * slope).astype(BF16)
    token, (hidden, gate_slope, up_slope, down_zf1, down_xzk, down_xzf0) = meet(
        token, (hidden, gate_slope, up_slope, down_zf1, down_xzk, down_xzf0)
    )
    (down_xzf1,) = trade(token, [(down_zf1, "x")])
    down_zf = jnp.concatenate([down_zf0, down_zf1], axis=0)
    down_3 = contract_rows(hidden, grad_rows[:, 3 * quarter :]).astype(BF16)
    token, (down_3, down_xzf1, down_zf) = meet(token, (down_3, down_xzf1, down_zf))
    down_xzf = jnp.concatenate([down_xzf0, down_xzf1], axis=0)

    def columns_of(value, piece):
        return value[:, piece * quarter : (piece + 1) * quarter]

    down_cols = assemble(
        za_place,
        [
            (down_keep, 0, 1),
            (down_far, 0, -1),
            (down_zk, quarter, 1),
            (down_zf, quarter, -1),
            (down_xk, half, 1),
            (down_xf, half, -1),
            (down_xzk, half + quarter, 1),
            (down_xzf, half + quarter, -1),
        ],
        1,
    )
    token, (down_cols,) = meet(token, (down_cols,))
    (down_3,) = trade(token, [(down_3, "x")])
    hidden_grad = contract_cols(grad_rows, down_cols)
    gate_low = (hidden_grad * gate_slope.astype(F32)).astype(BF16)
    up_low = (hidden_grad * up_slope.astype(F32)).astype(BF16)

    kept, given = two_terms(gate_low, up_low, gate_cols, up_cols)
    token, (kept, given, gate_low, up_low, down_3) = meet(token, (kept, given, gate_low, up_low, down_3))
    hidden, grad_rows = after(token, (hidden, grad_rows))
    down_1 = (contract_rows(hidden, columns_of(grad_rows, 1)) + down_3.astype(F32)).astype(BF16)
    given, down_1a = trade(token, [(given, "core"), (down_1[:144], "zb")])
    gate_3 = contract_rows(columns_of(mlp_rows, 3), gate_low).astype(BF16)
    token, (given, kept, down_1, down_1a, gate_3) = meet(token, (given, kept, down_1, down_1a, gate_3))
    kept = kept + given.astype(F32)
    token, (kept,) = meet(token, (kept,))
    from_y, down_1b, gate_3 = trade(token, far_sums(kept) + [(down_1[144:416], "zb"), (gate_3, "x")])
    down_2 = contract_rows(hidden, columns_of(grad_rows, 2)).astype(BF16)
    up_3 = contract_rows(columns_of(mlp_rows, 3), up_low).astype(BF16)
    gate_1 = contract_rows(columns_of(mlp_rows, 1), gate_low)
    token, (from_y, kept, down_1b, gate_3, down_2, up_3, gate_1) = meet(
        token, (from_y, kept, down_1b, gate_3, down_2, up_3, gate_1)
    )
    *nears, down_1c, up_3 = trade(token, near_sums(kept, from_y) + [(down_1[416:], "zb"), (up_3, "x")])
    gate_1 = (gate_1 + gate_3.astype(F32)).astype(BF16)
    gate_2 = contract_rows(columns_of(mlp_rows, 2), gate_low).astype(BF16)
    up_1 = contract_rows(columns_of(mlp_rows, 1), up_low)
    up_2 = contract_rows(columns_of(mlp_rows, 2), up_low).astype(BF16)
    token, (nears, kept, down_1c, up_3, gate_2, up_1, up_2, gate_1) = meet(
        token, (nears, kept, down_1c, up_3, gate_2, up_1, up_2, gate_1)
    )
    mlp_in_grad = own_sum(kept, nears)
    gain_two_part = jnp.sum(mlp_in_grad * unit_two, axis=0, keepdims=True)
    scaled = mlp_in_grad * gain_two
    inner = jnp.mean(scaled * unit_two, axis=-1, keepdims=True)
    residual_grad = grad_local.astype(F32) + rho_two * (scaled - unit_two * inner)


    branch_low = residual_grad.astype(BF16)
    token, (branch_low, residual_grad, gain_two_part, gate_1) = meet(
        token, (branch_low, residual_grad, gain_two_part, gate_1)
    )
    branch_y, branch_z, gate_1a, gate_2 = trade(
        token, near(branch_low) + [(gate_1[:blk_rows], "zb"), (gate_2, "x")]
    )
    hidden, down_cols = after(token, (hidden, down_cols))
    out_given = matmul(hidden[middle:], down_cols).astype(BF16)
    up_1 = (up_1 + up_3.astype(F32)).astype(BF16)
    down_0 = contract_rows(hidden, columns_of(grad_rows, 0)) + jnp.concatenate(
        [down_1a, down_1b, down_1c], axis=0
    ).astype(F32)
    token, (branch_y, branch_z, gate_1a, gate_2, out_given, up_1, down_0, gate_low, up_low) = meet(
        token, (branch_y, branch_z, gate_1a, gate_2, out_given, up_1, down_0, gate_low, up_low)
    )
    gate_0 = contract_rows(columns_of(mlp_rows, 0), gate_low) + gate_2.astype(F32)
    *fars, gate_1b, down_2a = trade(
        token, far(branch_y, branch_z, FAR) + [(gate_1[blk_rows:384], "zb"), (down_2[:384], "x")]
    )
    hidden, down_cols = after(token, (hidden, down_cols))
    out_kept = matmul(hidden[:middle], down_cols)
    token, (fars, out_kept, gate_1b, down_2a, gate_0) = meet(token, (fars, out_kept, gate_1b, down_2a, gate_0))
    branch_mine = mine_of(branch_low, branch_y, branch_z, fars)
    branch_theirs, gate_1c, down_2b, out_given = trade(
        token,
        [(branch_mine, "core"), (gate_1[384:464], "zb"), (down_2[384:512], "x"), (out_given, "core")],
    )
    grad_own = contract_cols(branch_mine, o_cols).astype(BF16)
    attn_grad = jnp.concatenate([grad_own, contract_cols(branch_theirs, o_cols).astype(BF16)], axis=0)
    mixed = jnp.concatenate([gate_1[464:], up_1[:144]], axis=0)
    token, (attn_grad, gate_1c, down_2b, mixed) = meet(token, (attn_grad, gate_1c, down_2b, mixed))
    mixed, up_2a, down_2c = trade(token, [(mixed, "zb"), (up_2[:blk_rows], "x"), (down_2[512:], "x")])
    query_part, kv_1, kv_3 = attend_back(
        offsets[1], tiles, queries, start_rows, inverse, attn_low, attn_grad, [kv_z, kv_xz], last=False
    )
    out_kept = out_kept + out_given.astype(F32)
    token, (query_part, kv_1, kv_3, mixed, up_2a, down_2c, out_kept) = meet(
        token, (query_part, kv_1, kv_3, mixed, up_2a, down_2c, out_kept)
    )
    gate_1d, up_1a = mixed[:48], mixed[48:]
    kv_3, up_1b, out_from = trade(token, [(kv_3, "x"), (up_1[144:336], "zb")] + far_sums(out_kept))
    query_grad, kv_0, kv_2 = attend_back(
        offsets[0],
        tiles,
        queries,
        start_rows,
        inverse,
        attn_low,
        attn_grad,
        [kv_own, kv_x],
        before=query_part,
    )
    token, (query_grad, kv_0, kv_2, kv_3, up_1b, out_from) = meet(
        token, (query_grad, kv_0, kv_2, kv_3, up_1b, out_from)
    )
    kv_1 = (kv_1.astype(F32) + kv_3.astype(F32)).astype(BF16)
    kv_1, kv_2, *out_nears = trade(token, [(kv_1, "zb"), (kv_2, "x")] + near_sums(out_kept, out_from))
    token, (kv_2, branch_mine, branch_theirs, up_low, query_grad, gate_0, down_0) = meet(
        token, (kv_2, branch_mine, branch_theirs, up_low, query_grad, gate_0, down_0)
    )
    q_low, q_gain_part = shape_back(raw, query_grad, cosine, sine, qk_gains, 2, 0, 0, HEAD_SIZE**-0.5)
    q_3 = swap(contract_rows(columns_of(normed, 3), q_low).astype(BF16), "x")
    branch_rows = jnp.concatenate([branch_mine, branch_theirs], axis=0)
    o_3 = contract_rows(attn_low, columns_of(branch_rows, 3)).astype(BF16)
    q_1 = contract_rows(columns_of(normed, 1), q_low)
    gate_part = gate_0 + jnp.concatenate([gate_1a, gate_1b, gate_1c, gate_1d], axis=0).astype(F32)
    gate_mine, gate_give = za_parts(gate_part, 0)
    down_part = down_0 + jnp.concatenate([down_2a, down_2b, down_2c], axis=0).astype(F32)
    down_mine, down_give = za_parts(down_part, 1)
    token, (kv_1, out_nears, q_low, q_gain_part, o_3, gate_mine, gate_give, down_mine, down_give, q_1) = meet(
        token, (kv_1, out_nears, q_low, q_gain_part, o_3, gate_mine, gate_give, down_mine, down_give, q_1)
    )
    gate_give, up_1c, down_give, up_2b = trade(
        token, [(gate_give, "za"), (up_1[336:], "zb"), (down_give, "za"), (up_2[blk_rows:], "x")]
    )
    kv_grad = (kv_0.astype(F32) + kv_1.astype(F32) + kv_2.astype(F32)).astype(BF16)
    kv_low, k_gain_part = shape_back(raw, kv_grad, cosine, sine, qk_gains, 1, 2, 1, 1.0)
    low = jnp.concatenate([q_low, kv_low], axis=1)
    given = contract_cols(low[middle:], qkv_cols).astype(BF16)
    w_3 = contract_rows(columns_of(normed, 3), kv_low).astype(BF16)
    q_1 = (q_1 + q_3.astype(F32)).astype(BF16)
    token, (given, low, kv_low, k_gain_part, w_3, q_1, gate_give, up_1c, up_2b) = meet(
        token, (given, low, kv_low, k_gain_part, w_3, q_1, gate_give, up_1c, up_2b)
    )
    given_low = given
    kv_late, normed, low, up_low = after(token, (kv_low, normed, low, up_low))
    up_part = (
        contract_rows(columns_of(mlp_rows, 0), up_low)
        + jnp.concatenate([up_2a, up_2b], axis=0).astype(F32)
        + jnp.concatenate([up_1a, up_1b, up_1c], axis=0).astype(F32)
    )
    up_mine, up_give = za_parts(up_part, 0)
    given, q_1, w_3, o_3 = trade(token, [(given, "core"), (q_1, "zb"), (w_3, "x"), (o_3, "x")])
    terms = contract_cols(low[:middle], qkv_cols)
    w_1 = contract_rows(columns_of(normed, 1), kv_late)
    token, (given, terms, q_1, w_3, o_3, w_1, down_give, up_mine, up_give, attn_low, branch_rows) = meet(
        token, (given, terms, q_1, w_3, o_3, w_1, down_give, up_mine, up_give, attn_low, branch_rows)
    )
    kept = terms + given.astype(F32)
    w_1 = (w_1 + w_3.astype(F32)).astype(BF16)
    token, (kept, w_1) = meet(token, (kept, w_1))
    from_y, w_1, up_give = trade(token, far_sums(kept) + [(w_1, "zb"), (up_give, "za")])
    o_1 = (contract_rows(attn_low, columns_of(branch_rows, 1)) + o_3.astype(F32)).astype(BF16)
    o_2 = contract_rows(attn_low, columns_of(branch_rows, 2)).astype(BF16)
    terms_low, given_low, normed_low = after(token, (terms, given_low, normed))
    gain_one_part = (
        jnp.sum(
            terms_low * normed_low[:middle].astype(F32) + given_low.astype(F32) * normed_low[middle:].astype(F32),
            axis=0,
            keepdims=True,
        )
        / gain_one
    )
    gain_sum = jnp.concatenate(
        [
            *reorder(from_order, [gain_one_part, gain_two_part], [F32, F32]),
            jnp.sum(q_gain_part, axis=0, keepdims=True),
            jnp.sum(k_gain_part, axis=0, keepdims=True),
        ],
        axis=1,
    )
    qw_2 = contract_rows(columns_of(normed, 2), low).astype(BF16)
    token, (from_y, kept, w_1, o_1, qw_2, o_2, gain_sum, up_give, attn_low, branch_rows, low) = meet(
        token, (from_y, kept, w_1, o_1, qw_2, o_2, gain_sum, up_give, attn_low, branch_rows, low)
    )
    *nears, o_1, qw_2, gain_x = trade(
        token, near_sums(kept, from_y) + [(o_1, "zb"), (qw_2, "x"), (gain_sum, "core")]
    )
    gain_sum = gain_sum + gain_x
    gain_sum = gain_sum + swap(gain_sum, "zb")
    gate_mine, gate_give, down_mine, down_give = after(token, (gate_mine, gate_give, down_mine, down_give))
    qw_0 = contract_rows(columns_of(normed, 0), low)
    o_0 = contract_rows(attn_low, columns_of(branch_rows, 0))
    block_out = residual + own_sum(out_kept, out_nears)
    token, (nears, kept, qw_2, qw_0, o_0, block_out, gain_sum, o_1) = meet(
        token, (nears, kept, qw_2, qw_0, o_0, block_out, gain_sum, o_1)
    )
    qkv_mine, qkv_give = za_parts(qw_0 + qw_2.astype(F32) + jnp.concatenate([q_1, w_1], axis=1).astype(F32), 0)
    token, (qkv_mine, qkv_give) = meet(token, (qkv_mine, qkv_give))
    gain_x, qkv_give, o_2 = trade(
        token, [(gain_sum, "za"), (qkv_give, "za"), (o_2, "x")]
    )
    gain_sum = gain_sum + gain_x
    gain_x = swap(gain_sum, "y")
    o_mine, o_give = za_parts(o_0 + o_2.astype(F32) + o_1.astype(F32), 1)
    token, (gain_sum, o_mine, o_give) = meet(token, (gain_sum + gain_x, o_mine, o_give))
    gain_x, o_give = trade(token, [(gain_sum, "x"), (o_give, "za")])
    gain_sum = gain_sum + gain_x
    input_grad = own_sum(kept, nears)
    unit_one = local_rows * (rho_one := lax.rsqrt(jnp.mean(local_rows * local_rows, axis=-1, keepdims=True) + EPSILON))
    scaled = input_grad * gain_one
    inner = jnp.mean(scaled * unit_one, axis=-1, keepdims=True)
    in_grad = residual_grad + rho_one * (scaled - unit_one * inner)
    block_out, in_grad = reorder(from_order, [block_out, in_grad], [BF16, F32])
    device = (((y_at * 2 + core_at) * 2 + zb_at) * 2 + za_at) * 2 + x_at

    def own_slice(first, length):
        share = length // 32
        return lax.dynamic_slice_in_dim(gain_sum[0], first + device * share, share, axis=0)

    qkv_parts = za_join(qkv_mine, qkv_give)

    def columns(lo, hi):
        return jnp.concatenate([part[:, lo:hi] for part in qkv_parts], axis=1)

    return (
        block_out,
        in_grad,
        own_slice(0, width),
        columns(0, q_width),
        columns(q_width, q_width + k_width),
        columns(q_width + k_width, qkv_width),
        own_slice(2 * width, HEAD_SIZE),
        own_slice(2 * width + HEAD_SIZE, HEAD_SIZE),
        jnp.concatenate(za_join(o_mine, o_give), axis=0),
        own_slice(width, width),
        jnp.concatenate(za_join(gate_mine, gate_give), axis=1),
        jnp.concatenate(za_join(up_mine, up_give), axis=1),
        jnp.concatenate(za_join(down_mine, down_give), axis=0),
    )


def layer(
    sizes,
    tokens,
    out_grad,
    seq_lengths,
    block_deal,
    norm_gain,
    q_weight,
    k_weight,
    v_weight,
    q_gain,
    k_gain,
    o_weight,
    mlp_gain,
    gate_weight,
    up_weight,
    down_weight,
):
    y_count, core_count, zb_count, za_count, x_count = sizes
    pairwise = sizes == (2, 2, 2, 2, 2)
    all_axes = ("y", "core", "zb", "za", "x")
    y_at, core_at, zb_at, za_at, x_at = (lax.axis_index(name) for name in all_axes)
    tok_dev, width = tokens.shape
    blk_rows = q_weight.shape[0]
    group_count = zb_count * x_count
    member_count = y_count * core_count * za_count
    head_count = y_count * core_count
    rows = member_count * tok_dev
    piece = za_count * blk_rows


    def gather_rows(value):
        if not pairwise:
            return lax.all_gather(value, ("y", "core", "za"), axis=0, tiled=True)
        half = tok_dev // 2
        along_y = swap(value, "y")
        along_z = swap(value, "za")
        parts = [value, along_y, along_z, swap(along_z[:half], "y"), swap(along_y[half:], "za")]
        mine = jnp.concatenate(parts, axis=0)
        return jnp.concatenate([mine, swap(mine, "core")], axis=0)

    def scatter_rows(part_of):
        if not pairwise:
            full = part_of(slice(0, rows)).astype(BF16)
            return lax.psum_scatter(full, ("y", "core", "za"), scatter_dimension=0, tiled=True).astype(F32)
        middle = rows // 2
        half = tok_dev // 2
        given = swap(part_of(slice(middle, rows)).astype(BF16), "core")
        kept = part_of(slice(0, middle)) + given.astype(F32)
        own, to_y, to_z, far = (kept[i * tok_dev : (i + 1) * tok_dev] for i in range(4))
        far = far.astype(BF16)
        from_y = swap(far[:half], "y").astype(F32)
        from_z = swap(far[half:], "za").astype(F32)
        z_sum = jnp.concatenate([to_z[:half] + from_y, to_z[half:]], axis=0).astype(BF16)
        y_sum = jnp.concatenate([to_y[:half], to_y[half:] + from_z], axis=0).astype(BF16)
        return own + swap(y_sum, "y").astype(F32) + swap(z_sum, "za").astype(F32)


    def gather_pieces(own, axis):
        if not pairwise:
            return lax.all_gather(own, ("zb", "x"), axis=axis, tiled=True)
        along_z = swap(own, "zb")
        return jnp.concatenate([own, along_z, swap(own, "x"), swap(along_z, "x")], axis=axis)

    def scatter_pieces(part_of, length, axis):
        if not pairwise:
            full = part_of(0, length).astype(BF16)
            return lax.psum_scatter(full, ("zb", "x"), scatter_dimension=axis, tiled=True).astype(F32)
        half, quarter = length // 2, length // 4
        given = swap(part_of(half, length).astype(BF16), "x")
        kept = part_of(0, half) + given.astype(F32)
        given = swap(lax.slice_in_dim(kept, quarter, half, axis=axis).astype(BF16), "zb")
        return lax.slice_in_dim(kept, 0, quarter, axis=axis) + given.astype(F32)

    def in_order(mine, other, axis):
        first = jnp.where(za_at == 0, mine, other)
        second = jnp.where(za_at == 0, other, mine)
        return jnp.concatenate([first, second], axis=axis)

    def gather_weight(part_of, axis):
        mine = part_of(za_at)
        if za_count > 1:
            mine = in_order(mine, swap(part_of(1 - za_at), "za"), axis)
        return gather_pieces(mine, axis)

    def scatter_weight(part_of, axis):
        part = scatter_pieces(part_of, width, axis)
        if za_count == 1:
            return [part]
        first = lax.slice_in_dim(part, 0, blk_rows, axis=axis)
        second = lax.slice_in_dim(part, blk_rows, 2 * blk_rows, axis=axis)
        mine = jnp.where(za_at == 0, first, second)
        other = swap(jnp.where(za_at == 0, second, first).astype(BF16), "za").astype(F32)
        return [jnp.where(za_at == 0, mine, other), jnp.where(za_at == 0, other, mine)]

    def half_of(weight, at, axis):
        size = weight.shape[axis] // za_count
        return lax.dynamic_slice_in_dim(weight, at * size, size, axis=axis)


    def piece_group(index):
        if pairwise:
            return zb_at ^ (index % 2), x_at ^ (index // 2)
        return index // x_count, index % x_count

    def to_pieces(value):
        blocks = []
        for index in range(group_count):
            zb_of, x_of = piece_group(index)
            for za_of in range(za_count):
                block = (zb_of * za_count + za_of) * x_count + x_of
                blocks.append(lax.dynamic_slice_in_dim(value, block * blk_rows, blk_rows, axis=1))
        return jnp.concatenate(blocks, axis=1) if pairwise else value

    def from_pieces(value):
        if not pairwise:
            return value
        blocks = []
        for block in range(group_count * za_count):
            zb_of, za_of, x_of = block // 4, block // 2 % 2, block % 2
            index = (x_at ^ x_of) * 2 + (zb_at ^ zb_of)
            blocks.append(lax.dynamic_slice_in_dim(value, (index * 2 + za_of) * blk_rows, blk_rows, axis=1))
        return jnp.concatenate(blocks, axis=1)


    per_span = head_count // 2
    member = jnp.arange(member_count, dtype=jnp.int32)
    if pairwise:
        member_y, member_za, member_core = y_at ^ (member % 2), za_at ^ (member // 2 % 2), core_at ^ (member // 4)
    else:
        member_za = member % za_count
        member_core = member // za_count % core_count
        member_y = member // (za_count * core_count)
    group = jnp.arange(group_count, dtype=jnp.int32)
    group_zb, group_x = piece_group(group)
    member_head = member_y * core_count + member_core
    span_table = jnp.arange(block_deal.shape[0], dtype=jnp.int32)

    def natural_tile(zb_of, x_of):
        blk = (zb_of * za_count + member_za) * x_count + x_of
        entry = 2 * blk + member_head // per_span
        span = jnp.sum(
            jnp.where(entry[..., None] == span_table, block_deal, 0), axis=-1, dtype=jnp.int32
        )
        return span * per_span + member_head % per_span

    query_tile = natural_tile(zb_at, x_at)
    key_tile = natural_tile(group_zb[:, None], group_x[:, None]).reshape(-1)
    tile_ids = jnp.arange(key_tile.shape[0], dtype=jnp.int32)
    offsets = jnp.sum(
        jnp.where(key_tile[None, :] == tile_ids[:, None], tile_ids[None, :] * tok_dev, 0), axis=1, dtype=jnp.int32
    )
    natural = query_tile[:, None] * tok_dev + jnp.arange(tok_dev, dtype=jnp.int32)[None, :]
    seq_ids = jnp.arange(seq_lengths.shape[0], dtype=jnp.int32)
    seq_ends = jnp.sum(jnp.where(seq_ids[None, :] <= seq_ids[:, None], seq_lengths[None, :], 0), axis=1, dtype=jnp.int32)
    starts = jnp.max(jnp.where(seq_ends <= natural[..., None], seq_ends, 0), axis=-1)
    tiles = (query_tile, starts[:, 0] // (2 * tok_dev))
    start_rows = jnp.stack([starts, starts], axis=1)
    start_cols = jnp.broadcast_to(starts.reshape(rows, 1), (rows, 128))
    places = (natural - starts).reshape(rows)
    half_width = HEAD_SIZE // 2
    frequency = jnp.power(ROPE_BASE, -jnp.arange(half_width, dtype=F32) * (2.0 / HEAD_SIZE))
    angles = places.astype(F32)[:, None] * frequency[None, :]
    cosine = jnp.cos(angles)
    sine = jnp.sin(angles)
    cosine = jnp.concatenate([cosine, cosine], axis=1)
    sine = jnp.concatenate([-sine, sine], axis=1)


    q_width = q_weight.shape[1] // za_count
    k_width = k_weight.shape[1] // za_count
    qkv_width = q_width + 2 * k_width
    gain_pad = 16

    gain_row = jnp.concatenate([norm_gain, mlp_gain])
    head_gains = jnp.concatenate([q_gain, k_gain])

    def gain_rows():
        top = jnp.pad(gain_row, (0, qkv_width - gain_row.shape[0]))[None]
        bottom = jnp.pad(head_gains, (0, qkv_width - head_gains.shape[0]))[None]
        return jnp.concatenate([top, bottom, jnp.zeros((gain_pad - 2, qkv_width), BF16)], axis=0)

    def qkv_part(at):
        return jnp.concatenate(
            [half_of(q_weight, at, 1), half_of(k_weight, at, 1), half_of(v_weight, at, 1), ], axis=1
        )

    padded = blk_rows + gain_pad
    own_gain_rows = gain_rows()
    qkv_all = gather_weight(lambda at: jnp.concatenate([qkv_part(at), own_gain_rows], axis=0), 0)
    qkv_all = qkv_all.reshape(group_count * za_count, padded, qkv_width)
    qkv_cols = qkv_all[:, :blk_rows].reshape(width, qkv_width)
    gains = qkv_all[:, blk_rows, : 2 * blk_rows].astype(F32)
    gain_one = gains[:, :blk_rows].reshape(1, width)
    gain_two = gains[:, blk_rows:].reshape(1, width)
    small = q_gain.shape[0]
    head_parts = qkv_all[:, blk_rows + 1, : 2 * small].astype(F32).reshape(group_count * za_count, 2, small)

    def head_gain(which):
        return from_small(head_parts[:, which])

    def from_small(parts):
        if not pairwise:
            return parts.reshape(1, -1)
        rows_of = []
        for block in range(8):
            zb_of, za_of, x_of = block // 4, block // 2 % 2, block % 2
            index = ((x_at ^ x_of) * 2 + (zb_at ^ zb_of)) * 2 + za_of
            rows_of.append(lax.dynamic_slice_in_dim(parts, index, 1, axis=0))
        return jnp.concatenate(rows_of, axis=1)

    qk_gains = jnp.concatenate([head_gain(0), head_gain(1)], axis=0)


    local_low = to_pieces(tokens)
    local_rows = local_low.astype(F32)
    input_rows = gather_rows(local_low).astype(F32)
    o_cols = gather_weight(lambda at: half_of(o_weight, at, 0), 1)
    gu_cols = gather_weight(
        lambda at: jnp.concatenate([half_of(gate_weight, at, 1), half_of(up_weight, at, 1)], axis=1), 0
    )
    down_cols = gather_weight(lambda at: half_of(down_weight, at, 0), 1)
    grad_local = to_pieces(out_grad)
    grad_rows = gather_rows(grad_local)

    def unit_rows(value):
        return value * lax.rsqrt(jnp.mean(value * value, axis=-1, keepdims=True) + EPSILON)

    input_unit = unit_rows(input_rows)
    normed = (input_unit * gain_one).astype(BF16)
    raw = matmul(normed, qkv_cols)
    queries, kv_own = shape_heads(raw, cosine, sine, qk_gains)
    key_values = gather_pieces(kv_own, 0)
    attn_low, inverse = attend(offsets, tiles, queries, start_cols, [key_values])
    residual = local_rows + scatter_rows(lambda at: matmul(attn_low[at], o_cols))


    rho_two = lax.rsqrt(jnp.mean(residual * residual, axis=-1, keepdims=True) + EPSILON)
    unit_two = residual * rho_two
    mlp_rows = gather_rows((unit_two * gain_two).astype(BF16))
    ff = gu_cols.shape[1] // 2
    gate_up = matmul(mlp_rows, gu_cols)
    gate_act, up_act = gate_up[:, :ff], gate_up[:, ff:]
    sig = jax.nn.sigmoid(gate_act)
    silu = gate_act * sig
    hidden = (silu * up_act).astype(BF16)
    hidden_grad = contract_cols(grad_rows, down_cols)
    gate_low = (hidden_grad * up_act * (sig * (1.0 + gate_act * (1.0 - sig)))).astype(BF16)
    up_low = (hidden_grad * silu).astype(BF16)
    gu_low = jnp.concatenate([gate_low, up_low], axis=1)
    mlp_in_grad = scatter_rows(lambda at: contract_cols(gu_low[at], gu_cols))

    down_parts = scatter_weight(lambda lo, hi: contract_rows(hidden, grad_rows[:, lo:hi]), 1)
    gate_parts = scatter_weight(lambda lo, hi: contract_rows(mlp_rows[:, lo:hi], gate_low), 0)
    up_parts = scatter_weight(lambda lo, hi: contract_rows(mlp_rows[:, lo:hi], up_low), 0)
    block_out = residual + scatter_rows(lambda at: matmul(hidden[at], down_cols))

    gain_two_part = jnp.sum(mlp_in_grad * unit_two, axis=0, keepdims=True)
    scaled = mlp_in_grad * gain_two
    inner = jnp.mean(scaled * unit_two, axis=-1, keepdims=True)
    residual_grad = grad_local.astype(F32) + rho_two * (scaled - unit_two * inner)


    branch_rows = gather_rows(residual_grad.astype(BF16))
    attn_grad = contract_cols(branch_rows, o_cols).astype(BF16)
    query_grad, kv_grads = attend_back(
        offsets, tiles, queries, start_rows, inverse, attn_low, attn_grad, [key_values]
    )
    o_parts = scatter_weight(lambda lo, hi: contract_rows(attn_low, branch_rows[:, lo:hi]), 1)
    kv_grad = scatter_pieces(lambda lo, hi: kv_grads[lo:hi].astype(F32), kv_grads.shape[0], 0).astype(BF16)
    q_low, q_gain_part = shape_back(raw, query_grad, cosine, sine, qk_gains, 2, 0, 0, HEAD_SIZE**-0.5)
    kv_low, k_gain_part = shape_back(raw, kv_grad, cosine, sine, qk_gains, 1, 2, 1, 1.0)
    low = jnp.concatenate([q_low, kv_low], axis=1)

    gain_one_parts = []

    def input_terms(at):
        terms = contract_cols(low[at], qkv_cols)
        gain_one_parts.append(jnp.sum(terms * input_unit[at], axis=0, keepdims=True))
        return terms

    input_grad = scatter_rows(input_terms)
    qkv_parts = scatter_weight(lambda lo, hi: contract_rows(normed[:, lo:hi], low), 0)

    gain_sum = jnp.concatenate(
        [
            from_pieces(sum(gain_one_parts)),
            from_pieces(gain_two_part),
            jnp.sum(q_gain_part, axis=0, keepdims=True),
            jnp.sum(k_gain_part, axis=0, keepdims=True),
        ],
        axis=1,
    )
    if pairwise:
        for name in ("core", "y", "za", "x", "zb"):
            gain_sum = gain_sum + swap(gain_sum, name)
    else:
        gain_sum = lax.psum(gain_sum, all_axes)

    unit_one = local_rows * (rho_one := lax.rsqrt(jnp.mean(local_rows * local_rows, axis=-1, keepdims=True) + EPSILON))
    scaled = input_grad * gain_one
    inner = jnp.mean(scaled * unit_one, axis=-1, keepdims=True)
    in_grad = residual_grad + rho_one * (scaled - unit_one * inner)

    device = (((y_at * core_count + core_at) * zb_count + zb_at) * za_count + za_at) * x_count + x_at
    device_count = head_count * zb_count * za_count * x_count

    def own_slice(first, length):
        share = length // device_count
        return lax.dynamic_slice_in_dim(gain_sum[0], first + device * share, share, axis=0)

    def join(parts, lo, hi, axis):
        cut = [lax.slice_in_dim(part, lo, hi, axis=axis) for part in parts]
        return jnp.concatenate(cut, axis=axis)

    return (
        from_pieces(block_out).astype(BF16),
        from_pieces(in_grad),
        own_slice(0, width),
        join(qkv_parts, 0, q_width, 1),
        join(qkv_parts, q_width, q_width + k_width, 1),
        join(qkv_parts, q_width + k_width, qkv_width, 1),
        own_slice(2 * width, HEAD_SIZE),
        own_slice(2 * width + HEAD_SIZE, HEAD_SIZE),
        jnp.concatenate(o_parts, axis=0),
        own_slice(width, width),
        jnp.concatenate(gate_parts, axis=1),
        jnp.concatenate(up_parts, axis=1),
        jnp.concatenate(down_parts, axis=0),
    )


def solution(mesh):
    heads, blks = mesh.shape["head"], mesh.shape["blk"]
    za_count = KEY_VALUE_HEADS // heads
    side = math.isqrt(blks // za_count)
    sizes = (heads // 2, 2, side, za_count, side)
    names = ("y", "core", "zb", "za", "x")
    devices = mesh.devices.reshape(sizes)
    inner = Mesh(devices, names)
    head, blk = ("y", "core"), ("zb", "za", "x")
    rows, in_weight, out_weight, gain = P(names, None), P(blk, head), P(head, blk), P(blk)
    return jax.shard_map(
        paired_layer if sizes == (2, 2, 2, 2, 2) else functools.partial(layer, sizes),
        mesh=inner,
        in_specs=(
            rows,
            rows,
            P(),
            P(),
            gain,
            in_weight,
            in_weight,
            in_weight,
            gain,
            gain,
            out_weight,
            gain,
            in_weight,
            in_weight,
            out_weight,
        ),
        out_specs=(
            rows,
            rows,
            P(names),
            in_weight,
            in_weight,
            in_weight,
            P(names),
            P(names),
            out_weight,
            P(names),
            in_weight,
            in_weight,
            out_weight,
        ),
        check_vma=False,
    )
```
